32 devices in a mesh: dp: 2 (over x), vocab: 16 (over z, y, core).
Axes of the slice: x: 2, y: 2, z: 4, core: 2. Of those that a mesh axis runs over, the one named last changes fastest.
Arguments:
- token_ids: int32 [32, 256], P(('dp', 'vocab')), may hold values from 0 to 30526
- pred_mask: int32 [32, 256], P(('dp', 'vocab')), may hold values from 0 to 1, as said below
- fact_order: int32 [32, 256], P(('dp', 'vocab')), may hold values from 0 to 255, each once within a row
- corpus: int32 [32], P(('dp', 'vocab')), may hold values from 0 to 3, as said below
- embed_table: float32 [30720, 768], P('vocab'), may hold values from -0.42 to 0.42
- table_moment: float32 [30720, 768], P('vocab'), may hold values from -1.1444092e-05 to 1.1444092e-05
- table_square: float32 [30720, 768], P('vocab'), may hold values from 1.6192649e-13 to 2.5908238e-12
- layer_weights: float32 [3, 768, 3072], P(None, ('dp', 'vocab'))
- layer_moment: float32 [3, 768, 3072], P(None, ('dp', 'vocab')), may hold values from -1.1444092e-05 to 1.1444092e-05
- layer_square: float32 [3, 768, 3072], P(None, ('dp', 'vocab')), may hold values from 1.6192649e-13 to 2.5908238e-12
- position_table: float32 [256, 768], P(None, ('dp', 'vocab')), may hold values from -0.42 to 0.42
- position_moment: float32 [256, 768], P(None, ('dp', 'vocab')), may hold values from -1.1444092e-05 to 1.1444092e-05
- position_square: float32 [256, 768], P(None, ('dp', 'vocab')), may hold values from 1.6192649e-13 to 2.5908238e-12
- small_params: float32 [14, 768], P(None, ('dp', 'vocab'))
- small_moment: float32 [14, 768], P(None, ('dp', 'vocab')), may hold values from -1.1444092e-05 to 1.1444092e-05
- small_square: float32 [14, 768], P(None, ('dp', 'vocab')), may hold values from 1.6192649e-13 to 2.5908238e-12
Outputs:
- loss_value: float32 [], replicated
- grad_norm: float32 [], replicated
- table_next: float32 [30720, 768], P('vocab')
- table_moments: float32 [30720, 768], P('vocab')
- table_squares: float32 [30720, 768], P('vocab')
- layer_next: float32 [3, 768, 3072], P(None, ('dp', 'vocab'))
- layer_moments: float32 [3, 768, 3072], P(None, ('dp', 'vocab'))
- layer_squares: float32 [3, 768, 3072], P(None, ('dp', 'vocab'))
- position_next: float32 [256, 768], P(None, ('dp', 'vocab'))
- position_moments: float32 [256, 768], P(None, ('dp', 'vocab'))
- position_squares: float32 [256, 768], P(None, ('dp', 'vocab'))
- small_next: float32 [14, 768], P(None, ('dp', 'vocab'))
- small_moments: float32 [14, 768], P(None, ('dp', 'vocab'))
- small_squares: float32 [14, 768], P(None, ('dp', 'vocab'))
- trust_norms: float32 [6, 2], replicated
The draws below stay inside these ranges and needn't reach their ends.
Inputs may be any that keep to these rules, and one draw needn't show every extreme that they name: `pred_mask`: every sequence has between 256 // 10 and 64 masked tokens, and some sequence has exactly 64. Every corpus holds exactly 8 sequences.
All inputs are finite; a program needn't handle non-finite values.
Results may differ from the reference program's by a relative error of at most 0.0055.
The reference program's roundings to bfloat16 on the way count: a program that leaves them out, or rounds other values in their place, can miss the bound.
Values may be sent and summed in bfloat16 or wider, within the bound.
No kernel may reach another device: no remote copies, remote signals or barrier semaphores. Data moves between devices by JAX's collectives and lax.ppermute only.
A program may use at most 256 MiB of HBM per device.

```python
import math
import jax
import jax.numpy as jnp
import numpy as np
from jax import lax

D = 768
HEADS = 12
HD = 64
FF = 3072
VLIVE = 30527
VOCAB = 30720
MASK_ID = 103
NCORP = 4
STEP = 5
LEN = 256
CAP = 64
SEQS = 32


def draw_pred_mask(key, part):
    key_count, key_pick, key_order = jax.random.split(key, 3)
    least = LEN // 10
    most = LEN // 4
    counts = jax.random.randint(key_count, (SEQS,), least, most + 1)
    chosen = jax.random.randint(key_pick, (), 0, SEQS)
    counts = jnp.where(jnp.arange(SEQS) == chosen, most, counts)
    seq_keys = jax.random.split(key_order, SEQS)
    scores = jax.vmap(lambda seq_key: jax.random.permutation(seq_key, LEN))(seq_keys)
    return (scores < counts[:, None]).astype(jnp.int32)


def draw_corpus(key, part):
    return (jax.random.permutation(key, SEQS) % NCORP).astype(jnp.int32)


def draw_layer_weights(key, part):
    base = jax.random.normal(key, (3, D, FF), jnp.float32)
    column = jnp.arange(FF)
    first_row = jnp.where(column < 3 * D, D ** (-0.5), 4.0 * D ** (-0.5))
    scales = jnp.stack([first_row, jnp.full((FF,), D ** (-0.5)), jnp.full((FF,), FF ** (-0.5))])
    return (base * scales[:, None, :]).astype(jnp.float32)


def draw_small_params(key, part):
    key_gain, key_bias = jax.random.split(key)
    gains = jax.random.uniform(key_gain, (14, D), jnp.float32, 0.6, 1.4)
    biases = 0.3 * jax.random.normal(key_bias, (14, D), jnp.float32)
    row_index = jnp.arange(14)
    is_gain = (row_index == 0) | (row_index == 5) | (row_index == 12)
    return jnp.where(is_gain[:, None], gains, biases).astype(jnp.float32)


def with_ends(array, own_key, low, top_value):
    place = [jax.random.randint(jax.random.fold_in(own_key, axis), (), 0, length) for axis, length in enumerate(array.shape)]
    main_axis = array.shape.index(max(array.shape))
    beside = place[:main_axis] + [(place[main_axis] + 1) % array.shape[main_axis]] + place[main_axis + 1:]
    return array.at[tuple(place)].set(low).at[tuple(beside)].set(top_value)


def shard_levels(rng, extent, shards, low, largest):
    def one(axis_at, parts):
        steps = jax.random.uniform(jax.random.fold_in(jax.random.fold_in(rng, 6), axis_at), (parts,), jnp.float32, low / len(shards), largest / len(shards))
        return jnp.repeat(jnp.exp(steps), extent[axis_at] // parts).reshape((-1,) + (1,) * (len(extent) - axis_at - 1))

    level = one(*shards[0])
    for cut in shards[1:]:
        level = level * one(*cut)
    return level


def cumulative_ranks(amount, slope):
    weights = [(1 << 20) // math.isqrt(grade ** slope) + 1 for grade in range(1, amount + 1)]
    width = 1 + sum(weights) // (1 << 30)
    return np.cumsum(np.array([max(1, weight // width) for weight in weights]))


def ranked_ids(own_key, extent, number_of, lean):
    grid = cumulative_ranks(number_of, lean)
    lot = jax.random.randint(jax.random.fold_in(own_key, 1), extent, 0, int(grid[number_of - 1]))
    rank = jnp.searchsorted(jnp.asarray(grid, jnp.int32), lot, side="right")
    return jax.random.permutation(jax.random.fold_in(own_key, 2), number_of)[rank].astype(jnp.int32)


def scatter_about(key, dims, scale, bound, pieces=(), kind=jnp.bfloat16):
    factor_of = shard_levels(key, dims, pieces, -0.22, 0.18) if pieces else 1.0
    entries = jax.random.normal(key, dims, jnp.float32) * scale * factor_of
    return jnp.minimum(jnp.maximum(entries, -bound), bound).astype(kind)


def setup_inputs(seed: int = 0) -> dict:
    seeds = jax.random.split(jax.random.key(seed), 17)
    token_ids = with_ends(ranked_ids(seeds[0], (SEQS, LEN), VLIVE, 2), jax.random.fold_in(seeds[0], 3), 0, VLIVE - 1).astype(jnp.int32)
    pred_mask = draw_pred_mask(jax.random.fold_in(seeds[16], 71), 0)
    fact_order = jax.vmap(lambda own: jax.random.permutation(own, LEN))(jax.random.split(seeds[2], SEQS)).reshape((SEQS, LEN)).astype(jnp.int32)
    corpus = draw_corpus(jax.random.fold_in(seeds[16], 71), 0)
    embed_table = scatter_about(seeds[4], (VOCAB, D), 0.07, 0.42, ((0, 16),), jnp.float32)
    table_moment = scatter_about(seeds[5], (VOCAB, D), (0.011 * (VOCAB * D + 3 * D * FF + LEN * D + 14 * D) ** -0.5), 1.1444091796875e-05, ((0, 16),), jnp.float32)
    table_square = jnp.clip(jnp.exp(math.log(2.5908238228400382e-12) - 2.7725887 * jax.random.uniform(seeds[6], (VOCAB, D), jnp.float32) ** shard_levels(seeds[6], (VOCAB, D), ((0, 16),), -0.2, 0.2)), 1.619264889275024e-13, 2.5908238228400382e-12)
    layer_weights = draw_layer_weights(jax.random.fold_in(seeds[16], 71), 0)
    layer_moment = scatter_about(seeds[8], (3, D, FF), (0.011 * (VOCAB * D + 3 * D * FF + LEN * D + 14 * D) ** -0.5), 1.1444091796875e-05, ((1, 32),), jnp.float32)
    layer_square = jnp.clip(jnp.exp(math.log(2.5908238228400382e-12) - 2.7725887 * jax.random.uniform(seeds[9], (3, D, FF), jnp.float32) ** shard_levels(seeds[9], (3, D, FF), ((1, 32),), -0.2, 0.2)), 1.619264889275024e-13, 2.5908238228400382e-12)
    position_table = scatter_about(seeds[10], (LEN, D), 0.07, 0.42, ((1, 32),), jnp.float32)
    position_moment = scatter_about(seeds[11], (LEN, D), (0.011 * (VOCAB * D + 3 * D * FF + LEN * D + 14 * D) ** -0.5), 1.1444091796875e-05, ((1, 32),), jnp.float32)
    position_square = jnp.clip(jnp.exp(math.log(2.5908238228400382e-12) - 2.7725887 * jax.random.uniform(seeds[12], (LEN, D), jnp.float32) ** shard_levels(seeds[12], (LEN, D), ((1, 32),), -0.2, 0.2)), 1.619264889275024e-13, 2.5908238228400382e-12)
    small_params = draw_small_params(jax.random.fold_in(seeds[16], 71), 0)
    small_moment = scatter_about(seeds[14], (14, D), (0.011 * (VOCAB * D + 3 * D * FF + LEN * D + 14 * D) ** -0.5), 1.1444091796875e-05, ((1, 32),), jnp.float32)
    small_square = jnp.clip(jnp.exp(math.log(2.5908238228400382e-12) - 2.7725887 * jax.random.uniform(seeds[15], (14, D), jnp.float32) ** shard_levels(seeds[15], (14, D), ((1, 32),), -0.2, 0.2)), 1.619264889275024e-13, 2.5908238228400382e-12)
    return dict(token_ids=token_ids, pred_mask=pred_mask, fact_order=fact_order, corpus=corpus, embed_table=embed_table, table_moment=table_moment, table_square=table_square, layer_weights=layer_weights, layer_moment=layer_moment, layer_square=layer_square, position_table=position_table, position_moment=position_moment, position_square=position_square, small_params=small_params, small_moment=small_moment, small_square=small_square)


clip_norm = 0.1
learn_rate = 0.3
beta_first = 0.9
beta_second = 0.999
adam_eps = 1e-06
weight_decay = 0.01
norm_eps = 1e-05
masked_score = -1e+30

@jax.custom_vjp
def low(v):
    return lax.optimization_barrier(v.astype(jnp.bfloat16)).astype(jnp.float32)

@jax.custom_vjp
def low_back(v):
    return v

def low_keep(v):
    return (low(v), None)

def low_pass(kept, grad):
    return (grad,)

def back_keep(v):
    return (v, None)

def back_low(kept, grad):
    return (low(grad),)
low.defvjp(low_keep, low_pass)
low_back.defvjp(back_keep, back_low)

def matmul(left_op, right_op):
    return jnp.dot(left_op, right_op, precision=lax.Precision.HIGHEST)

def trans_mul(left_op, right_op):
    return lax.dot_general(left_op, right_op, (((1,), (1,)), ((), ())), precision=lax.Precision.HIGHEST)

def norm_rows(values, gain_row, bias_row):
    center = values - lax.optimization_barrier(jnp.mean(values, axis=-1, keepdims=True))
    spread = lax.optimization_barrier(jnp.mean(center * center, axis=-1, keepdims=True))
    return center * lax.rsqrt(spread + norm_eps) * gain_row + bias_row

def one_sequence(table_w, layer_w, position_w, small_w, token_row, pred_row, order_row, seq_weight):
    content = jnp.where(pred_row == 1, MASK_ID, token_row).astype(jnp.int32)
    rank_row = jnp.argsort(order_row).astype(jnp.int32)
    slot_pos = jnp.argsort(1 - pred_row, stable=True)[:CAP].astype(jnp.int32)
    live_slots = (jnp.arange(CAP) < jnp.sum(pred_row)).astype(jnp.float32)
    embed_rows = low_back(table_w[content])
    stream = low(norm_rows(embed_rows + position_w, small_w[0], small_w[1]))
    query_proj = layer_w[0, :, :D]
    key_proj = layer_w[0, :, D:2 * D]
    value_proj = layer_w[0, :, 2 * D:3 * D]
    out_proj = layer_w[0, :, 3 * D:]
    key_rows = low_back(low(matmul(stream, key_proj)))
    value_rows = low_back(low(matmul(stream, value_proj) + small_w[3]))
    query_init = norm_rows(position_w[slot_pos], small_w[0], small_w[1])
    query_rows = low_back(low(matmul(low(query_init), query_proj) + small_w[2]))
    query_heads = query_rows.reshape(CAP, HEADS, HD)
    key_heads = key_rows.reshape(LEN, HEADS, HD)
    value_heads = value_rows.reshape(LEN, HEADS, HD)
    scores = jnp.einsum('qhd,khd->hqk', query_heads, key_heads, precision=lax.Precision.HIGHEST) * HD ** (-0.5)
    scores = low_back(scores)
    allowed = rank_row[None, :] <= rank_row[slot_pos][:, None]
    scores = jnp.where(allowed[None], scores, masked_score)
    attn_b = low(jax.nn.softmax(scores, axis=-1))
    mixed_rows = jnp.einsum('hqk,khd->qhd', attn_b, value_heads, precision=lax.Precision.HIGHEST).reshape(CAP, D)
    mixed_rows = low_back(low(mixed_rows))
    attend = low_back(matmul(mixed_rows, out_proj) + small_w[4])
    middle = norm_rows(query_init + attend, small_w[5], small_w[6])
    hidden = low_back(matmul(low(middle), layer_w[1]) + small_w[7:11].reshape(FF))
    active = low(jax.nn.gelu(hidden, approximate=False))
    branch = low_back(trans_mul(active, layer_w[2]) + small_w[11])
    output_rows = low(norm_rows(middle + branch, small_w[12], small_w[13]))
    logits = low_back(trans_mul(output_rows, table_w))
    log_total = jax.nn.logsumexp(logits, axis=-1)
    target = jnp.take_along_axis(logits, token_row[slot_pos][:, None], axis=1)[:, 0]
    return jnp.sum((log_total - target) * live_slots) * seq_weight

def adam_moments(weight_arr, first_mom, second_mom, gradient, factor):
    clipped = gradient * factor
    new_first = beta_first * first_mom + (1.0 - beta_first) * clipped
    new_second = beta_second * second_mom + (1.0 - beta_second) * clipped * clipped
    direction = new_first / (1.0 - beta_first ** STEP) / (jnp.sqrt(new_second / (1.0 - beta_second ** STEP)) + adam_eps) + weight_decay * weight_arr
    return (new_first, new_second, direction)

def reference(token_ids, pred_mask, fact_order, corpus, embed_table, table_moment, table_square, layer_weights, layer_moment, layer_square, position_table, position_moment, position_square, small_params, small_moment, small_square):
    per_seq = lax.optimization_barrier(jnp.sum(pred_mask, axis=1)).astype(jnp.float32)
    corpus_hot = (corpus[:, None] == jnp.arange(NCORP)[None, :]).astype(jnp.float32)
    counts = lax.optimization_barrier(jnp.sum(corpus_hot * per_seq[:, None], axis=0))
    seq_weights = 1.0 / (NCORP * lax.optimization_barrier(jnp.sum(corpus_hot * counts[None, :], axis=1)))

    def total_loss(params):
        table_w, layer_w, position_w, small_w = [low(tensor) for tensor in params]

        def add_one(running, row_data):
            seq_term = jax.checkpoint(one_sequence)(table_w, layer_w, position_w, small_w, *row_data)
            return (running + seq_term, None)
        loss_sum, _ = lax.scan(add_one, jnp.zeros((), jnp.float32), (token_ids, pred_mask, fact_order, seq_weights))
        return loss_sum
    params = (embed_table, layer_weights, position_table, small_params)
    loss_value, pullback = jax.vjp(total_loss, params)
    gradients = pullback(jnp.ones((), jnp.float32))[0]
    total_square = sum((jnp.sum(grad_arr * grad_arr) for grad_arr in gradients))
    grad_norm = jnp.sqrt(total_square)
    factor = jnp.minimum(1.0, clip_norm / grad_norm)
    olds = ((embed_table, table_moment, table_square, (0, 1)), (layer_weights, layer_moment, layer_square, (1, 2)), (position_table, position_moment, position_square, (0, 1)), (small_params, small_moment, small_square, (0, 1)))
    results = []
    weight_norms = []
    update_norms = []
    directions = []
    for (weight_arr, first_mom, second_mom, axes), grad_arr in zip(olds, gradients):
        new_first, new_second, direction = adam_moments(weight_arr, first_mom, second_mom, grad_arr, factor)
        results.append((new_first, new_second))
        directions.append(direction)
        weight_norms.append(jnp.sqrt(lax.optimization_barrier(jnp.sum(weight_arr * weight_arr, axis=axes))).reshape(-1))
        update_norms.append(jnp.sqrt(lax.optimization_barrier(jnp.sum(direction * direction, axis=axes))).reshape(-1))
    trust_norms = jnp.stack([jnp.concatenate(weight_norms), jnp.concatenate(update_norms)], axis=1)
    ratio = trust_norms[:, 0] / trust_norms[:, 1]
    table_next = embed_table - learn_rate * ratio[0] * directions[0]
    layer_next = layer_weights - learn_rate * ratio[1:4][:, None, None] * directions[1]
    position_next = position_table - learn_rate * ratio[4] * directions[2]
    small_next = small_params - learn_rate * ratio[5] * directions[3]
    return (loss_value, grad_norm, table_next, results[0][0], results[0][1], layer_next, results[1][0], results[1][1], position_next, results[2][0], results[2][1], small_next, results[3][0], results[3][1], trust_norms)
```

```python
from functools import partial

import jax
import jax.numpy as jnp
from jax import lax
from jax.sharding import Mesh
from jax.sharding import PartitionSpec as P

HEADS = 12
HD = 64
MASK_ID = 103
NCORP = 4
STEP = 5
CAP = 64


clip_norm = 0.1
learn_rate = 0.3
beta_first = 0.9
beta_second = 0.999
adam_eps = 1e-06
weight_decay = 0.01
norm_eps = 1e-05
masked_score = -1e30
BUCKET = 32
ALL = ("dp", "hi", "mid", "core")
VOC = ("hi", "mid", "core")
bfloat = jnp.bfloat16
single = jnp.float32


def plain_dot(left_op, right_op):
    return jnp.dot(left_op, right_op, preferred_element_type=single)


def trans_dot(left_op, right_op):
    return lax.dot_general(
        left_op, right_op, (((1,), (1,)), ((), ())), preferred_element_type=single
    )


def rows_dot(left_op, right_op):
    return lax.dot_general(
        left_op, right_op, (((0,), (0,)), ((), ())), preferred_element_type=single
    )


def column_sum(values):
    return jnp.sum(values.astype(single), axis=0)


def norm_forward(values, gain_row, bias_row):
    center = values - jnp.mean(values, axis=-1, keepdims=True)
    inverse = lax.rsqrt(jnp.mean(center * center, axis=-1, keepdims=True) + norm_eps)
    normed = center * inverse
    return (normed * gain_row + bias_row, (normed, inverse))


def norm_backward(upstream, kept_norm, gain_row):
    normed, inverse = kept_norm
    scaled = upstream * gain_row
    inner = (
        scaled
        - jnp.mean(scaled, axis=-1, keepdims=True)
        - normed * jnp.mean(scaled * normed, axis=-1, keepdims=True)
    )
    return (inner * inverse, jnp.sum(upstream * normed, axis=0), jnp.sum(upstream, axis=0))


def split_heads(rows):
    return rows.reshape(rows.shape[0], HEADS, HD)


def attention_probs(query_rows, key_rows, allowed, log_total):
    scores = jnp.einsum(
        "qhd,khd->hqk",
        split_heads(query_rows),
        split_heads(key_rows),
        preferred_element_type=single,
    ) * HD ** (-0.5)
    scores = jnp.where(allowed[None], scores, masked_score)
    if log_total is None:
        row_top = jnp.max(scores, axis=-1, keepdims=True)
        log_total = row_top + jnp.log(jnp.sum(jnp.exp(scores - row_top), axis=-1, keepdims=True))
    return (jnp.exp(scores - log_total), log_total)


def layer_forward(layer_b, small_full, stream_b, query_init, allowed):
    width = stream_b.shape[1]
    key_rows = plain_dot(stream_b, layer_b[0][:, width : 2 * width]).astype(bfloat)
    value_rows = (plain_dot(stream_b, layer_b[0][:, 2 * width : 3 * width]) + small_full[3]).astype(
        bfloat
    )
    init_b = query_init.astype(bfloat)
    query_rows = (plain_dot(init_b, layer_b[0][:, :width]) + small_full[2]).astype(bfloat)
    attn_probs, log_total = attention_probs(query_rows, key_rows, allowed, None)
    mixed_b = jnp.einsum(
        "hqk,khd->qhd",
        attn_probs.astype(bfloat),
        split_heads(value_rows),
        preferred_element_type=single,
    )
    mixed_b = mixed_b.reshape(-1, width).astype(bfloat)
    attend = plain_dot(mixed_b, layer_b[0][:, 3 * width :]) + small_full[4]
    middle, middle_kept = norm_forward(query_init + attend, small_full[5], small_full[6])
    middle_b = middle.astype(bfloat)
    hidden = plain_dot(middle_b, layer_b[1]) + small_full[7:11].reshape(-1)
    active_b = jax.nn.gelu(hidden, approximate=False).astype(bfloat)
    branch = trans_dot(active_b, layer_b[2]) + small_full[11]
    output_rows, final_kept = norm_forward(middle + branch, small_full[12], small_full[13])
    kept_state = (
        key_rows,
        value_rows,
        init_b,
        query_rows,
        log_total,
        mixed_b,
        middle_kept,
        middle_b,
        hidden,
        active_b,
        final_kept,
    )
    return (output_rows, kept_state)


def layer_backward(layer_b, small_full, stream_b, allowed, kept_state, d_output):
    (
        key_rows,
        value_rows,
        init_b,
        query_rows,
        log_total,
        mixed_b,
        middle_kept,
        middle_b,
        hidden,
        active_b,
        final_kept,
    ) = kept_state
    width = stream_b.shape[1]
    d_sum, gain_three, bias_three = norm_backward(d_output, final_kept, small_full[12])
    d_branch = d_sum.astype(bfloat)
    grad_down = rows_dot(d_branch, active_b)
    _, gelu_pull = jax.vjp(partial(jax.nn.gelu, approximate=False), hidden)
    d_hidden = gelu_pull(plain_dot(d_branch, layer_b[2]))[0].astype(bfloat)
    grad_up = rows_dot(middle_b, d_hidden)
    d_middle = d_sum + trans_dot(d_hidden, layer_b[1])
    d_pre, gain_two, bias_two = norm_backward(d_middle, middle_kept, small_full[5])
    d_attend = d_pre.astype(bfloat)
    grad_out = rows_dot(mixed_b, d_attend)
    d_mixed = trans_dot(d_attend, layer_b[0][:, 3 * width :]).astype(bfloat)
    attn_probs, _ = attention_probs(query_rows, key_rows, allowed, log_total)
    mixed_heads = split_heads(d_mixed)
    d_probs = jnp.einsum(
        "qhd,khd->hqk", mixed_heads, split_heads(value_rows), preferred_element_type=single
    )
    d_value = jnp.einsum(
        "hqk,qhd->khd", attn_probs.astype(bfloat), mixed_heads, preferred_element_type=single
    )
    d_value = d_value.reshape(-1, width).astype(bfloat)
    d_scores = (
        attn_probs * (d_probs - jnp.sum(attn_probs * d_probs, axis=-1, keepdims=True))
    ).astype(bfloat)
    scale = HD ** (-0.5)
    d_query = (
        jnp.einsum("hqk,khd->qhd", d_scores, split_heads(key_rows), preferred_element_type=single)
        * scale
    )
    d_query = d_query.reshape(-1, width).astype(bfloat)
    d_key = (
        jnp.einsum("hqk,qhd->khd", d_scores, split_heads(query_rows), preferred_element_type=single)
        * scale
    )
    d_key = d_key.reshape(-1, width).astype(bfloat)
    grad_query = rows_dot(init_b, d_query)
    d_init = d_pre + trans_dot(d_query, layer_b[0][:, :width])
    grad_key = rows_dot(stream_b, d_key)
    grad_value = rows_dot(stream_b, d_value)
    d_stream = trans_dot(d_key, layer_b[0][:, width : 2 * width]) + trans_dot(
        d_value, layer_b[0][:, 2 * width : 3 * width]
    )
    grad_layer = (
        jnp.concatenate([grad_query, grad_key, grad_value, grad_out], axis=1),
        grad_up,
        grad_down,
    )
    grad_mid = jnp.concatenate(
        [
            column_sum(d_query)[None],
            column_sum(d_value)[None],
            column_sum(d_attend)[None],
            gain_two[None],
            bias_two[None],
            column_sum(d_hidden).reshape(4, width),
            column_sum(d_branch)[None],
            gain_three[None],
            bias_three[None],
        ]
    )
    return (grad_layer, grad_mid, d_init, d_stream)


def adam_moments(weight_arr, first_mom, second_mom, gradient, factor):
    clipped = gradient * factor
    new_first = beta_first * first_mom + (1.0 - beta_first) * clipped
    new_second = beta_second * second_mom + (1.0 - beta_second) * clipped * clipped
    direction = (
        new_first
        / (1.0 - beta_first**STEP)
        / (jnp.sqrt(new_second / (1.0 - beta_second**STEP)) + adam_eps)
        + weight_decay * weight_arr
    )
    return (new_first, new_second, direction)


def norm_pair(weight_arr, direction, axes):
    return jnp.stack(
        [jnp.sum(weight_arr * weight_arr, axis=axes), jnp.sum(direction * direction, axis=axes)],
        axis=-1,
    )


def copies_to(values, axes, count):
    return lax.all_to_all(
        jnp.broadcast_to(values[None], (count,) + values.shape), axes, 0, 0, tiled=True
    )


def total_over(values, axes, count):
    return jnp.sum(copies_to(values, axes, count), axis=0)


def masked_total(mask, values):
    return jnp.sum(jnp.where(mask, values, 0), axis=-1)


def slot_layout(pred_row, order_row, token_row):
    length = pred_row.shape[0]
    index = jnp.arange(length)
    before = index[None, :] <= index[:, None]
    seen = masked_total(before, pred_row[None, :])
    masked = jnp.sum(pred_row)
    place = jnp.where(pred_row == 1, seen - 1, masked + index - seen)
    slot_hot = place[None, :] == jnp.arange(CAP)[:, None]
    rank_row = masked_total(order_row[None, :] == index[:, None], index[None, :])
    slot_rank = masked_total(slot_hot, rank_row[None, :])
    slot_target = masked_total(slot_hot, token_row[None, :])
    allowed = rank_row[None, :] <= slot_rank[:, None]
    return slot_hot, slot_target, allowed, masked


def bucket_layout(content, vrows):
    index = jnp.arange(content.shape[0])
    same = content[None, :] == content[:, None]
    first = jnp.min(jnp.where(same, index[None, :], content.shape[0]), axis=1)
    is_first = first == index
    owner = content // vrows
    ahead = (owner[None, :] == owner[:, None]) & is_first[None, :] & (index[None, :] < first[:, None])
    return owner, jnp.sum(ahead.astype(jnp.int32), axis=1)


def bucket_round(content, owner, place, turn, owners, vrows):
    usable = BUCKET - 1
    local = place - turn * usable
    taken = (local >= 0) & (local < usable)
    flat = jnp.where(taken, owner * BUCKET + local, -1)
    hot = flat[None, :] == jnp.arange(owners * BUCKET)[:, None]
    wanted = jnp.max(jnp.where(hot, (content - owner * vrows)[None, :], -1), axis=1)
    return hot.astype(bfloat), wanted.reshape(owners, BUCKET)


def on_device(
    token_ids,
    pred_mask,
    fact_order,
    corpus,
    embed_table,
    table_moment,
    table_square,
    layer_weights,
    layer_moment,
    layer_square,
    position_table,
    position_moment,
    position_square,
    small_params,
    small_moment,
    small_square,
):
    dp_devs = lax.axis_size("dp")
    owners = lax.axis_size(VOC)
    devices = dp_devs * owners
    vrows, width = embed_table.shape
    length = token_ids.shape[1]
    attn_b, feed_b = (
        lax.all_gather(layer_weights[:1].astype(bfloat), ALL, axis=1, tiled=True),
        lax.all_gather(layer_weights[1:].astype(bfloat), ALL, axis=1, tiled=True),
    )
    layer_b = (attn_b[0], feed_b[0], feed_b[1])
    table_b = embed_table.astype(bfloat)
    token_row = token_ids[0]
    pred_row = pred_mask[0]
    first_row = lax.axis_index(VOC) * vrows
    content = jnp.where(pred_row == 1, MASK_ID, token_row)
    slot_hot, slot_target, allowed, masked = slot_layout(pred_row, fact_order[0], token_row)
    owner, place = bucket_layout(content, vrows)
    hot, wanted = bucket_round(content, owner, place, 0, owners, vrows)
    note = jnp.concatenate([slot_target, jnp.stack([masked, corpus[0], jnp.max(place)])])
    packet = jnp.concatenate(
        [wanted, jnp.broadcast_to(note[None], (owners, note.shape[0]))], axis=1
    )
    packet = jnp.pad(packet, ((0, 0), (0, 128 - packet.shape[1])))
    packet = jnp.broadcast_to(packet[None], (dp_devs,) + packet.shape)
    packet = lax.all_to_all(
        packet.reshape(devices, packet.shape[-1]), ALL, 0, 0, tiled=True
    )
    asked = packet[:, :BUCKET]
    counts_all = packet[:, BUCKET + CAP]
    corpus_all = packet[:, BUCKET + CAP + 1]
    rounds = jnp.max(packet[:, BUCKET + CAP + 2]) // (BUCKET - 1) + 1
    group = lax.axis_index("dp") * owners
    group_asked = lax.dynamic_slice_in_dim(asked, group, owners, 0)
    group_target = lax.dynamic_slice_in_dim(
        packet[:, BUCKET : BUCKET + CAP], group, owners, 0
    ).reshape(-1)
    corpus_hot = corpus_all[:, None] == jnp.arange(NCORP)[None, :]
    corpus_counts = jnp.sum(jnp.where(corpus_hot, counts_all[:, None], 0), axis=0)
    seq_count = masked_total(corpus_hot, corpus_counts[None, :])
    seq_weight = 1.0 / (NCORP * seq_count.astype(single))
    slot_weight = jnp.where(
        jnp.arange(CAP)[None, :] < counts_all[:, None], seq_weight[:, None], 0.0
    )
    group_weight = lax.dynamic_slice_in_dim(slot_weight, group, owners, 0).reshape(-1)

    def fetch(asked_rows, hot_rows):
        served = jnp.take(table_b, jnp.maximum(asked_rows, 0).reshape(-1), axis=0)
        arrived = lax.all_to_all(
            served.reshape(owners, BUCKET, width), VOC, 0, 0, tiled=True
        )
        return rows_dot(hot_rows, arrived.reshape(-1, width))

    embed_rows = fetch(group_asked, hot)

    def more_rows(state):
        turn, rows = state
        hot_t, wanted_t = bucket_round(content, owner, place, turn, owners, vrows)
        asked_t = lax.all_to_all(wanted_t, VOC, 0, 0, tiled=True)
        return turn + 1, rows + fetch(asked_t, hot_t)

    _, embed_rows = lax.while_loop(
        lambda state: state[0] < rounds, more_rows, (jnp.ones((), rounds.dtype), embed_rows)
    )
    shared_t = jnp.concatenate([position_table, small_params]).astype(bfloat).T
    shared = copies_to(shared_t, ALL, devices).reshape(width, -1).T
    position_b = shared[:length]
    position_full = position_b.astype(single)
    small_full = shared[length:].astype(single)
    stream, stream_kept = norm_forward(embed_rows + position_full, small_full[0], small_full[1])
    stream_b = stream.astype(bfloat)
    slot_b = slot_hot.astype(bfloat)
    query_init, init_kept = norm_forward(
        plain_dot(slot_b, position_b), small_full[0], small_full[1]
    )
    output_rows, kept_state = layer_forward(layer_b, small_full, stream_b, query_init, allowed)
    output_b = output_rows.astype(bfloat)
    group_rows = lax.all_gather(output_b, VOC, axis=0, tiled=True)
    logits = trans_dot(group_rows, table_b)
    local_target = group_target - first_row
    target_hit = jnp.arange(vrows)[None, :] == local_target[:, None]
    row_top = jnp.max(logits, axis=1)
    row_total = jnp.sum(jnp.exp(logits - row_top[:, None]), axis=1)
    row_target = jnp.sum(jnp.where(target_hit, logits, 0.0), axis=1)
    stats = copies_to(jnp.stack([row_top, row_total]), VOC, owners)
    top_all = jnp.max(stats[:, 0], axis=0)
    total_all = jnp.sum(stats[:, 1] * jnp.exp(stats[:, 0] - top_all[None]), axis=0)
    log_total = top_all + jnp.log(total_all)
    own_total = lax.dynamic_slice_in_dim(
        log_total * group_weight, lax.axis_index(VOC) * CAP, CAP, 0
    )
    loss_part = jnp.sum(own_total) - jnp.sum(row_target * group_weight)
    d_logits = (
        group_weight[:, None] * (jnp.exp(logits - log_total[:, None]) - target_hit.astype(single))
    ).astype(bfloat)
    d_output = lax.psum_scatter(
        plain_dot(d_logits, table_b), VOC, scatter_dimension=0, tiled=True
    )
    grad_head = rows_dot(d_logits, group_rows)
    if dp_devs == 2:
        grad_other = lax.ppermute(grad_head, "dp", [(0, 1), (1, 0)])
        grad_head = grad_head + grad_other
    else:
        grad_head = lax.psum(grad_head, "dp")
    grad_layer, grad_mid, d_init, d_stream = layer_backward(
        layer_b, small_full, stream_b, allowed, kept_state, d_output
    )
    d_start, gain_init, bias_init = norm_backward(d_init, init_kept, small_full[0])
    d_embed, gain_stream, bias_stream = norm_backward(d_stream, stream_kept, small_full[0])
    grad_position = d_embed + lax.dot_general(
        slot_hot.astype(single),
        d_start,
        (((0,), (0,)), ((), ())),
        precision=lax.Precision.HIGHEST,
        preferred_element_type=single,
    )
    grad_small = jnp.concatenate(
        [(gain_init + gain_stream)[None], (bias_init + bias_stream)[None], grad_mid]
    )
    embed_back = d_embed.astype(bfloat)
    mask_sum = jnp.sum(
        jnp.where((content == MASK_ID)[:, None], embed_back.astype(single), 0.0), axis=0
    )
    mask_left = mask_sum - lax.reduce_precision(mask_sum, 8, 7)
    mask_owner = MASK_ID // vrows
    is_left = (jnp.arange(BUCKET) == BUCKET - 1)[None, :] & (
        jnp.arange(owners) == mask_owner
    )[:, None]

    def give(hot_rows, extra):
        rows = plain_dot(hot_rows, embed_back).reshape(owners, BUCKET, width)
        rows = jnp.where(is_left[:, :, None] & extra, mask_left[None, None, :], rows)
        rows = jnp.broadcast_to(rows.astype(bfloat)[None], (dp_devs,) + rows.shape)
        return lax.all_to_all(
            rows.reshape(devices, BUCKET, width), ALL, 0, 0, tiled=True
        ).reshape(-1, width)

    def into_rows(asked_rows, given):
        flat = asked_rows.reshape(-1)
        row_hot = flat[None, :] == jnp.arange(vrows)[:, None]
        return plain_dot(row_hot.astype(bfloat), given)

    last = (jnp.arange(BUCKET) == BUCKET - 1)[None, :]
    left_row = jnp.where(lax.axis_index(VOC) == mask_owner, MASK_ID - first_row, -1)
    table_grad = grad_head + into_rows(jnp.where(last, left_row, asked), give(hot, True))

    def more_grads(state):
        turn, grads = state
        hot_t, wanted_t = bucket_round(content, owner, place, turn, owners, vrows)
        wanted_t = jnp.broadcast_to(wanted_t[None], (dp_devs,) + wanted_t.shape)
        asked_t = lax.all_to_all(
            wanted_t.reshape(devices, BUCKET), ALL, 0, 0, tiled=True
        )
        return turn + 1, grads + into_rows(asked_t, give(hot_t, False))

    _, table_grad = lax.while_loop(
        lambda state: state[0] < rounds, more_grads, (jnp.ones((), rounds.dtype), table_grad)
    )
    layer_grad = jnp.stack(
        [lax.psum_scatter(part, ALL, scatter_dimension=0, tiled=True) for part in grad_layer[::-1]][
            ::-1
        ]
    )
    shared_grad = jnp.concatenate([grad_position, grad_small]).T.reshape(
        devices, width // devices, -1
    )
    shared_grad = jnp.sum(lax.all_to_all(shared_grad, ALL, 0, 0, tiled=True), axis=0).T
    position_grad, small_grad = shared_grad[:length], shared_grad[length:]
    square_part = (
        jnp.sum(table_grad * table_grad) / dp_devs
        + jnp.sum(layer_grad * layer_grad)
        + jnp.sum(position_grad * position_grad)
        + jnp.sum(small_grad * small_grad)
    )
    total_square, loss_value = total_over(jnp.stack([square_part, loss_part]), ALL, devices)
    grad_norm = jnp.sqrt(total_square)
    factor = jnp.minimum(1.0, clip_norm / grad_norm)
    table_first, table_second, table_dir = adam_moments(
        embed_table, table_moment, table_square, table_grad, factor
    )
    layer_first, layer_second, layer_dir = adam_moments(
        layer_weights, layer_moment, layer_square, layer_grad, factor
    )
    position_first, position_second, position_dir = adam_moments(
        position_table, position_moment, position_square, position_grad, factor
    )
    small_first, small_second, small_dir = adam_moments(
        small_params, small_moment, small_square, small_grad, factor
    )
    partial_norms = jnp.concatenate(
        [
            norm_pair(embed_table, table_dir, (0, 1))[None] / dp_devs,
            norm_pair(layer_weights, layer_dir, (1, 2)),
            norm_pair(position_table, position_dir, (0, 1))[None],
            norm_pair(small_params, small_dir, (0, 1))[None],
        ]
    )
    trust_square = total_over(partial_norms, ALL, devices)
    trust_norms = jnp.sqrt(trust_square)
    ratio = trust_norms[:, 0] / trust_norms[:, 1]
    table_next = embed_table - learn_rate * ratio[0] * table_dir
    layer_next = layer_weights - learn_rate * ratio[1:4][:, None, None] * layer_dir
    position_next = position_table - learn_rate * ratio[4] * position_dir
    small_next = small_params - learn_rate * ratio[5] * small_dir
    return (
        loss_value,
        grad_norm,
        table_next,
        table_first,
        table_second,
        layer_next,
        layer_first,
        layer_second,
        position_next,
        position_first,
        position_second,
        small_next,
        small_first,
        small_second,
        trust_norms,
    )


def solution(mesh):
    dp_devs, owners = mesh.devices.shape
    fine = Mesh(mesh.devices.reshape(dp_devs, owners // 4, 2, 2), ALL)
    rows, inner = P(ALL, None), P(None, ALL)
    table, layer = P(VOC, None), P(None, ALL, None)
    return jax.shard_map(
        on_device,
        mesh=fine,
        in_specs=(rows,) * 3 + (P(ALL),) + (table,) * 3 + (layer,) * 3 + (inner,) * 6,
        out_specs=(P(), P()) + (table,) * 3 + (layer,) * 3 + (inner,) * 6 + (P(),),
        check_vma=False,
    )
```

```python
from functools import partial

import jax
import jax.numpy as jnp
from jax import lax
from jax.sharding import Mesh
from jax.sharding import PartitionSpec as P

HEADS = 12
HD = 64
MASK_ID = 103
NCORP = 4
STEP = 5
CAP = 64


clip_norm = 0.1
learn_rate = 0.3
beta_first = 0.9
beta_second = 0.999
adam_eps = 1e-06
weight_decay = 0.01
norm_eps = 1e-05
masked_score = -1e30
BUCKET = 32
ALL = ("dp", "hi", "mid", "core")
VOC = ("hi", "mid", "core")
NEAR = ("dp", "mid", "core")
bfloat = jnp.bfloat16
single = jnp.float32


def plain_dot(left_op, right_op):
    return jnp.dot(left_op, right_op, preferred_element_type=single)


def trans_dot(left_op, right_op):
    return lax.dot_general(
        left_op, right_op, (((1,), (1,)), ((), ())), preferred_element_type=single
    )


def rows_dot(left_op, right_op):
    return lax.dot_general(
        left_op, right_op, (((0,), (0,)), ((), ())), preferred_element_type=single
    )


def column_sum(values):
    return jnp.sum(values.astype(single), axis=0)


def norm_forward(values, gain_row, bias_row):
    center = values - jnp.mean(values, axis=-1, keepdims=True)
    inverse = lax.rsqrt(jnp.mean(center * center, axis=-1, keepdims=True) + norm_eps)
    normed = center * inverse
    return (normed * gain_row + bias_row, (normed, inverse))


def norm_backward(upstream, kept_norm, gain_row):
    normed, inverse = kept_norm
    scaled = upstream * gain_row
    inner = (
        scaled
        - jnp.mean(scaled, axis=-1, keepdims=True)
        - normed * jnp.mean(scaled * normed, axis=-1, keepdims=True)
    )
    return (inner * inverse, jnp.sum(upstream * normed, axis=0), jnp.sum(upstream, axis=0))


def split_heads(rows):
    return rows.reshape(rows.shape[0], HEADS, HD)


def attention_probs(query_rows, key_rows, allowed, log_total):
    scores = jnp.einsum(
        "qhd,khd->hqk",
        split_heads(query_rows),
        split_heads(key_rows),
        preferred_element_type=single,
    ) * HD ** (-0.5)
    scores = jnp.where(allowed[None], scores, masked_score)
    if log_total is None:
        row_top = jnp.max(scores, axis=-1, keepdims=True)
        log_total = row_top + jnp.log(jnp.sum(jnp.exp(scores - row_top), axis=-1, keepdims=True))
    return (jnp.exp(scores - log_total), log_total)


def layer_forward(layer_b, small_full, stream_b, query_init, allowed):
    width = stream_b.shape[1]
    key_rows = plain_dot(stream_b, layer_b[0][:, width : 2 * width]).astype(bfloat)
    value_rows = (plain_dot(stream_b, layer_b[0][:, 2 * width : 3 * width]) + small_full[3]).astype(
        bfloat
    )
    init_b = query_init.astype(bfloat)
    query_rows = (plain_dot(init_b, layer_b[0][:, :width]) + small_full[2]).astype(bfloat)
    attn_probs, log_total = attention_probs(query_rows, key_rows, allowed, None)
    mixed_b = jnp.einsum(
        "hqk,khd->qhd",
        attn_probs.astype(bfloat),
        split_heads(value_rows),
        preferred_element_type=single,
    )
    mixed_b = mixed_b.reshape(-1, width).astype(bfloat)
    attend = plain_dot(mixed_b, layer_b[0][:, 3 * width :]) + small_full[4]
    middle, middle_kept = norm_forward(query_init + attend, small_full[5], small_full[6])
    middle_b = middle.astype(bfloat)
    hidden = plain_dot(middle_b, layer_b[1]) + small_full[7:11].reshape(-1)
    active_b = jax.nn.gelu(hidden, approximate=False).astype(bfloat)
    branch = trans_dot(active_b, layer_b[2]) + small_full[11]
    output_rows, final_kept = norm_forward(middle + branch, small_full[12], small_full[13])
    kept_state = (
        key_rows,
        value_rows,
        init_b,
        query_rows,
        log_total,
        mixed_b,
        middle_kept,
        middle_b,
        hidden,
        active_b,
        final_kept,
    )
    return (output_rows, kept_state)


def feed_backward(layer_b, small_full, kept_state, d_output):
    hidden, final_kept, middle_kept = kept_state[8], kept_state[10], kept_state[6]
    d_sum, gain_three, bias_three = norm_backward(d_output, final_kept, small_full[12])
    d_branch = d_sum.astype(bfloat)
    _, gelu_pull = jax.vjp(partial(jax.nn.gelu, approximate=False), hidden)
    d_hidden = gelu_pull(plain_dot(d_branch, layer_b[2]))[0].astype(bfloat)
    d_middle = d_sum + trans_dot(d_hidden, layer_b[1])
    d_pre, gain_two, bias_two = norm_backward(d_middle, middle_kept, small_full[5])
    grad_mid = jnp.concatenate(
        [
            gain_two[None],
            bias_two[None],
            column_sum(d_hidden).reshape(4, -1),
            column_sum(d_branch)[None],
            gain_three[None],
            bias_three[None],
        ]
    )
    return d_branch, d_hidden, d_pre, grad_mid


def attention_backward(layer_b, allowed, kept_state, d_pre):
    key_rows, value_rows, _, query_rows, log_total = kept_state[:5]
    width = d_pre.shape[1]
    d_attend = d_pre.astype(bfloat)
    d_mixed = trans_dot(d_attend, layer_b[0][:, 3 * width :]).astype(bfloat)
    attn_probs, _ = attention_probs(query_rows, key_rows, allowed, log_total)
    mixed_heads = split_heads(d_mixed)
    d_probs = jnp.einsum(
        "qhd,khd->hqk", mixed_heads, split_heads(value_rows), preferred_element_type=single
    )
    d_value = jnp.einsum(
        "hqk,qhd->khd", attn_probs.astype(bfloat), mixed_heads, preferred_element_type=single
    )
    d_value = d_value.reshape(-1, width).astype(bfloat)
    d_scores = (
        attn_probs * (d_probs - jnp.sum(attn_probs * d_probs, axis=-1, keepdims=True))
    ).astype(bfloat)
    scale = HD ** (-0.5)
    d_query = (
        jnp.einsum("hqk,khd->qhd", d_scores, split_heads(key_rows), preferred_element_type=single)
        * scale
    )
    d_query = d_query.reshape(-1, width).astype(bfloat)
    d_key = (
        jnp.einsum("hqk,qhd->khd", d_scores, split_heads(query_rows), preferred_element_type=single)
        * scale
    )
    d_key = d_key.reshape(-1, width).astype(bfloat)
    d_init = d_pre + trans_dot(d_query, layer_b[0][:, :width])
    d_stream = trans_dot(d_key, layer_b[0][:, width : 2 * width]) + trans_dot(
        d_value, layer_b[0][:, 2 * width : 3 * width]
    )
    grad_mid = jnp.concatenate(
        [column_sum(d_query)[None], column_sum(d_value)[None], column_sum(d_attend)[None]]
    )
    return d_attend, d_query, d_key, d_value, d_init, d_stream, grad_mid


def adam_moments(weight_arr, first_mom, second_mom, gradient, factor):
    clipped = gradient * factor
    new_first = beta_first * first_mom + (1.0 - beta_first) * clipped
    new_second = beta_second * second_mom + (1.0 - beta_second) * clipped * clipped
    direction = (
        new_first
        / (1.0 - beta_first**STEP)
        / (jnp.sqrt(new_second / (1.0 - beta_second**STEP)) + adam_eps)
        + weight_decay * weight_arr
    )
    return (new_first, new_second, direction)


def norm_pair(weight_arr, direction, axes):
    return jnp.stack(
        [jnp.sum(weight_arr * weight_arr, axis=axes), jnp.sum(direction * direction, axis=axes)],
        axis=-1,
    )


class Exchange:
    def __init__(self):
        self.last = None

    def __call__(self, values, axes):
        if self.last is not None:
            values, _ = lax.optimization_barrier((values, self.last))
        self.last = lax.all_to_all(values, axes, 0, 0, tiled=True)
        return self.last

    def copies(self, values, axes, count):
        return self(jnp.broadcast_to(values[None], (count,) + values.shape), axes)

    def total(self, values, axes, count):
        return jnp.sum(self.copies(values, axes, count), axis=0)

    def columns(self, values, axes, count):
        rows, width = values.shape
        blocks = values.reshape(rows, count, width // count).transpose(1, 0, 2)
        return self(blocks, axes).reshape(count * rows, -1)

    def rows(self, values, count):
        return self(values.reshape(count, values.shape[0] // count, values.shape[1]), ALL)


def side_by_side(blocks):
    return blocks.transpose(1, 0, 2).reshape(blocks.shape[1], -1)


def masked_total(mask, values):
    return jnp.sum(jnp.where(mask, values, 0), axis=-1)


def slot_layout(pred_row, order_row, token_row):
    length = pred_row.shape[0]
    index = jnp.arange(length)
    before = index[None, :] <= index[:, None]
    seen = masked_total(before, pred_row[None, :])
    masked = jnp.sum(pred_row)
    place = jnp.where(pred_row == 1, seen - 1, masked + index - seen)
    slot_hot = place[None, :] == jnp.arange(CAP)[:, None]
    rank_row = masked_total(order_row[None, :] == index[:, None], index[None, :])
    slot_rank = masked_total(slot_hot, rank_row[None, :])
    slot_target = masked_total(slot_hot, token_row[None, :])
    slot_pos = masked_total(slot_hot, index[None, :])
    allowed = rank_row[None, :] <= slot_rank[:, None]
    return slot_hot, slot_pos, slot_target, allowed, masked


def bucket_layout(content, vrows):
    index = jnp.arange(content.shape[0])
    same = content[None, :] == content[:, None]
    first = jnp.min(jnp.where(same, index[None, :], content.shape[0]), axis=1)
    is_first = first == index
    owner = content // vrows
    ahead = (owner[None, :] == owner[:, None]) & is_first[None, :] & (index[None, :] < first[:, None])
    return owner, jnp.sum(ahead.astype(jnp.int32), axis=1)


def bucket_round(content, owner, place, turn, owners, vrows):
    usable = BUCKET - 1
    local = place - turn * usable
    taken = (local >= 0) & (local < usable)
    flat = jnp.where(taken, owner * BUCKET + local, -1)
    hot = flat[None, :] == jnp.arange(owners * BUCKET)[:, None]
    wanted = jnp.max(jnp.where(hot, (content - owner * vrows)[None, :], -1), axis=1)
    return hot.astype(bfloat), wanted.reshape(owners, BUCKET)


def on_device(
    token_ids,
    pred_mask,
    fact_order,
    corpus,
    embed_table,
    table_moment,
    table_square,
    layer_weights,
    layer_moment,
    layer_square,
    position_table,
    position_moment,
    position_square,
    small_params,
    small_moment,
    small_square,
):
    exchange = Exchange()
    dp_devs = lax.axis_size("dp")
    owners = lax.axis_size(VOC)
    devices = dp_devs * owners
    vrows, width = embed_table.shape
    length = token_ids.shape[1]
    feed = layer_weights.shape[2]
    shared = jnp.concatenate([position_table, small_params]).T
    shared_rows = shared.shape[1]
    shared = jnp.pad(shared, ((0, 0), (0, -shared_rows % 128)))
    shard = jnp.concatenate([layer_weights[0], layer_weights[1], layer_weights[2], shared], axis=1)
    shard = lax.all_gather(shard.astype(bfloat), ALL, axis=0, tiled=True)
    layer_b = tuple(shard[:, part * feed : (part + 1) * feed] for part in range(3))
    shared = shard[:, 3 * feed : 3 * feed + shared_rows].T
    table_b = embed_table.astype(bfloat)
    token_row = token_ids[0]
    pred_row = pred_mask[0]
    first_row = lax.axis_index(VOC) * vrows
    content = jnp.where(pred_row == 1, MASK_ID, token_row)
    slot_hot, slot_pos, slot_target, allowed, masked = slot_layout(pred_row, fact_order[0], token_row)
    owner, place = bucket_layout(content, vrows)
    hot, wanted = bucket_round(content, owner, place, 0, owners, vrows)
    note = jnp.concatenate(
        [slot_target, slot_pos, jnp.stack([masked, corpus[0], jnp.max(place)])]
    )
    packet = jnp.concatenate(
        [wanted, jnp.broadcast_to(note[None], (owners, note.shape[0]))], axis=1
    )
    packet = jnp.pad(packet, ((0, 0), (0, 256 - packet.shape[1])))
    packet = jnp.broadcast_to(packet[None], (dp_devs,) + packet.shape)
    packet = exchange(packet.reshape(devices, packet.shape[-1]), ALL)
    asked = packet[:, :BUCKET]
    tail = BUCKET + 2 * CAP
    counts_all = packet[:, tail]
    corpus_all = packet[:, tail + 1]
    rounds = jnp.max(packet[:, tail + 2]) // (BUCKET - 1) + 1
    group = lax.axis_index("dp") * owners
    outer = lax.axis_size("hi")

    def group_order(values):
        return values.reshape(outer, 2, 2, CAP).transpose(2, 1, 0, 3).reshape(-1)

    group_asked = lax.dynamic_slice_in_dim(asked, group, owners, 0)
    group_target = group_order(
        lax.dynamic_slice_in_dim(packet[:, BUCKET : BUCKET + CAP], group, owners, 0)
    )
    corpus_hot = corpus_all[:, None] == jnp.arange(NCORP)[None, :]
    corpus_counts = jnp.sum(jnp.where(corpus_hot, counts_all[:, None], 0), axis=0)
    seq_count = masked_total(corpus_hot, corpus_counts[None, :])
    seq_weight = 1.0 / (NCORP * seq_count.astype(single))
    slot_weight = jnp.where(
        jnp.arange(CAP)[None, :] < counts_all[:, None], seq_weight[:, None], 0.0
    )
    group_weight = group_order(lax.dynamic_slice_in_dim(slot_weight, group, owners, 0))

    def serve(asked_rows):
        served = jnp.take(table_b, jnp.maximum(asked_rows, 0).reshape(-1), axis=0)
        return served.reshape(owners, BUCKET, width)

    arrived = exchange(serve(group_asked), VOC)
    embed_rows = rows_dot(hot, arrived.reshape(-1, width))

    def more_rows(state):
        turn, rows = state
        hot_t, wanted_t = bucket_round(content, owner, place, turn, owners, vrows)
        asked_t = lax.all_to_all(wanted_t, VOC, 0, 0, tiled=True)
        arrived_t = lax.all_to_all(serve(asked_t), VOC, 0, 0, tiled=True)
        return turn + 1, rows + rows_dot(hot_t, arrived_t.reshape(-1, width))

    _, embed_rows = lax.while_loop(
        lambda state: state[0] < rounds, more_rows, (jnp.ones((), rounds.dtype), embed_rows)
    )
    position_b = shared[:length]
    position_full = position_b.astype(single)
    small_full = shared[length:].astype(single)
    stream, stream_kept = norm_forward(embed_rows + position_full, small_full[0], small_full[1])
    stream_b = stream.astype(bfloat)
    slot_b = slot_hot.astype(bfloat)
    query_init, init_kept = norm_forward(
        plain_dot(slot_b, position_b), small_full[0], small_full[1]
    )
    few = devices <= 32
    near = dp_devs * 4
    if few:
        stream_all = lax.all_gather(stream_b, NEAR, axis=0, tiled=True)
    output_rows, kept_state = layer_forward(layer_b, small_full, stream_b, query_init, allowed)
    output_b = output_rows.astype(bfloat)
    init_b, mixed_b, middle_b, active_b = (kept_state[2], kept_state[5], kept_state[7], kept_state[9])
    if few:
        kept_rows = jnp.concatenate([mixed_b, middle_b], axis=1)
        kept_rows, stream_all = lax.optimization_barrier((kept_rows, stream_all))
        kept_all = lax.all_gather(kept_rows, ALL, axis=0, tiled=True)
    group_rows = exchange.copies(output_b, "hi", outer).reshape(-1, width)
    group_rows = exchange.copies(group_rows, "mid", 2).reshape(-1, width)
    group_rows = exchange.copies(group_rows, "core", 2).reshape(-1, width)
    logits = trans_dot(group_rows, table_b)
    local_target = group_target - first_row
    target_hit = jnp.arange(vrows)[None, :] == local_target[:, None]
    row_top = jnp.max(logits, axis=1)
    row_total = jnp.sum(jnp.exp(logits - row_top[:, None]), axis=1)
    row_target = jnp.sum(jnp.where(target_hit, logits, 0.0), axis=1)
    stats = exchange.copies(jnp.stack([row_top, row_total]), VOC, owners)
    if few:
        active_mine = exchange.columns(active_b, ALL, devices)
    top_all = jnp.max(stats[:, 0], axis=0)
    total_all = jnp.sum(stats[:, 1] * jnp.exp(stats[:, 0] - top_all[None]), axis=0)
    log_total = top_all + jnp.log(total_all)
    own_place = lax.axis_index(("core", "mid", "hi"))
    own_total = lax.dynamic_slice_in_dim(log_total * group_weight, own_place * CAP, CAP, 0)
    loss_part = jnp.sum(own_total) - jnp.sum(row_target * group_weight)
    d_logits = (
        group_weight[:, None] * (jnp.exp(logits - log_total[:, None]) - target_hit.astype(single))
    ).astype(bfloat)
    def swapped(axis, part):
        side = lax.axis_index(axis)
        theirs = lax.ppermute(part(1 - side), axis, [(0, 1), (1, 0)])
        return part(side) + theirs

    half = owners * CAP // 2

    def rows_half(side):
        return plain_dot(lax.dynamic_slice_in_dim(d_logits, side * half, half, 0), table_b)

    d_output = swapped("core", rows_half)
    quarter = half // 2
    d_half = d_output
    d_output = swapped(
        "mid", lambda side: lax.dynamic_slice_in_dim(d_half, side * quarter, quarter, 0)
    )
    grad_head = rows_dot(d_logits, group_rows)
    if dp_devs == 2:
        head_b = grad_head.astype(bfloat)
        other_b = lax.ppermute(head_b, "dp", [(0, 1), (1, 0)])
        d_output, head_b = lax.optimization_barrier((d_output, head_b))
        grad_head = head_b.astype(single) + other_b.astype(single)
    else:
        grad_head = lax.psum(grad_head, "dp")
    d_output = exchange(d_output.reshape(outer, CAP, width), "hi")
    if few:
        d_output, kept_all = lax.optimization_barrier((d_output, kept_all))
    d_output = jnp.sum(d_output, axis=0)
    d_branch, d_hidden, d_pre, mid_feed = feed_backward(layer_b, small_full, kept_state, d_output)
    if few:
        wide = feed // devices
        both = jnp.concatenate(
            [
                d_hidden.reshape(CAP, devices, -1),
                d_pre.astype(bfloat).reshape(CAP, devices, -1),
            ],
            axis=2,
        ).reshape(CAP, -1)
        both = exchange.columns(both, ALL, devices)
        branch_all = lax.all_gather(d_branch, ALL, axis=0, tiled=True)
    d_attend, d_query, d_key, d_value, d_init, d_stream, mid_attn = attention_backward(
        layer_b, allowed, kept_state, d_pre
    )
    grad_mid = jnp.concatenate([mid_attn, mid_feed])
    if few:
        piece = width // near
        pairs = jnp.concatenate(
            [d_key.reshape(length, near, piece), d_value.reshape(length, near, piece)], axis=2
        ).transpose(1, 0, 2)
        asks = d_query.reshape(CAP, near, piece).transpose(1, 0, 2)
        asks = jnp.concatenate([asks[:, : CAP // 2], asks[:, CAP // 2 :]], axis=2)
        pairs = exchange(jnp.concatenate([pairs, asks], axis=1), NEAR)
    d_start, gain_init, bias_init = norm_backward(d_init, init_kept, small_full[0])
    d_embed, gain_stream, bias_stream = norm_backward(d_stream, stream_kept, small_full[0])
    grad_position = d_embed + lax.dot_general(
        slot_hot.astype(single),
        d_start,
        (((0,), (0,)), ((), ())),
        precision=lax.Precision.HIGHEST,
        preferred_element_type=single,
    )
    grad_small = jnp.concatenate(
        [(gain_init + gain_stream)[None], (bias_init + bias_stream)[None], grad_mid]
    )
    embed_back = d_embed.astype(bfloat)
    mask_sum = jnp.sum(
        jnp.where((content == MASK_ID)[:, None], embed_back.astype(single), 0.0), axis=0
    )
    mask_left = mask_sum - lax.reduce_precision(mask_sum, 8, 7)
    mask_owner = MASK_ID // vrows
    is_left = (jnp.arange(BUCKET) == BUCKET - 1)[None, :] & (
        jnp.arange(owners) == mask_owner
    )[:, None]

    def plain_exchange(values, axes):
        return lax.all_to_all(values, axes, 0, 0, tiled=True)

    def give(hot_rows, extra, send):
        rows = plain_dot(hot_rows, embed_back).reshape(owners, BUCKET, width)
        rows = jnp.where(is_left[:, :, None] & extra, mask_left[None, None, :], rows)
        rows = send(rows.astype(bfloat), VOC).reshape(-1, width)
        if dp_devs == 2:
            return jnp.concatenate([rows, lax.ppermute(rows, "dp", [(0, 1), (1, 0)])])
        return lax.all_gather(rows, "dp", axis=0, tiled=True)

    def both_groups(asked_rows):
        if dp_devs == 2:
            return jnp.roll(asked_rows, -group, axis=0)
        return asked_rows

    def into_rows(asked_rows, given):
        flat = both_groups(asked_rows).reshape(-1)
        row_hot = flat[None, :] == jnp.arange(vrows)[:, None]
        return plain_dot(row_hot.astype(bfloat), given)

    last = (jnp.arange(BUCKET) == BUCKET - 1)[None, :]
    left_row = jnp.where(lax.axis_index(VOC) == mask_owner, MASK_ID - first_row, -1)
    table_grad = grad_head + into_rows(jnp.where(last, left_row, asked), give(hot, True, exchange))

    def more_grads(state):
        turn, grads = state
        hot_t, wanted_t = bucket_round(content, owner, place, turn, owners, vrows)
        wanted_t = jnp.broadcast_to(wanted_t[None], (dp_devs,) + wanted_t.shape)
        asked_t = lax.all_to_all(
            wanted_t.reshape(devices, BUCKET), ALL, 0, 0, tiled=True
        )
        return turn + 1, grads + into_rows(asked_t, give(hot_t, False, plain_exchange))

    _, table_grad = lax.while_loop(
        lambda state: state[0] < rounds, more_grads, (jnp.ones((), rounds.dtype), table_grad)
    )
    if few:
        near_pos = packet[:, BUCKET + CAP : tail].reshape(dp_devs, outer, 4 * CAP)
        near_pos = lax.dynamic_index_in_dim(near_pos, lax.axis_index("hi"), 1, False).reshape(-1)
        init_rows = norm_forward(position_full, small_full[0], small_full[1])[0].astype(bfloat)
        init_hot = near_pos[:, None] == jnp.arange(length)[None, :]
        init_all = plain_dot(init_hot.astype(bfloat), init_rows).astype(bfloat)
        asks = pairs[:, length:]
        asks = jnp.concatenate([asks[..., :piece], asks[..., piece:]], axis=1)
        grad_pair = rows_dot(stream_all, pairs[:, :length].reshape(near * length, -1))
        grad_ask = rows_dot(init_all, asks.reshape(near * CAP, piece))
        share = width // devices
        grad_up = rows_dot(kept_all[:, width:], both[:, :wide])
        grad_out = rows_dot(kept_all[:, :width], both[:, wide:])
        grad_down = rows_dot(branch_all, active_mine)
        shared_grad = jnp.concatenate([grad_position, grad_small]).T
        results = jnp.concatenate(
            [grad_pair, grad_ask, grad_up, grad_down, grad_out, shared_grad], axis=1
        )
        results = exchange.rows(results.astype(bfloat), devices).astype(single)
        pieces = 3 * piece
        attn = jnp.sum(
            results[..., :pieces].reshape(dp_devs, outer, 4, share, pieces), axis=1
        ).reshape(near, share, pieces)
        shared_grad = jnp.sum(results[..., -shared_rows:], axis=0).T
        position_grad, small_grad = shared_grad[:length], shared_grad[length:]
        grad_key, grad_value, grad_query = (
            side_by_side(attn[..., part * piece : (part + 1) * piece]) for part in range(3)
        )
        grad_up = side_by_side(results[..., pieces : pieces + wide])
        grad_down = side_by_side(results[..., pieces + wide : pieces + 2 * wide])
        grad_out = side_by_side(results[..., pieces + 2 * wide : -shared_rows])
        layer_grad = jnp.stack(
            [
                jnp.concatenate([grad_query, grad_key, grad_value, grad_out], axis=1),
                grad_up,
                grad_down,
            ]
        )
    else:
        whole = (
            jnp.concatenate(
                [
                    rows_dot(init_b, d_query),
                    rows_dot(stream_b, d_key),
                    rows_dot(stream_b, d_value),
                    rows_dot(mixed_b, d_attend),
                ],
                axis=1,
            ),
            rows_dot(middle_b, d_hidden),
            rows_dot(d_branch, active_b),
        )
        layer_grad = jnp.stack(
            [lax.psum_scatter(part, ALL, scatter_dimension=0, tiled=True) for part in whole]
        )
        shared_grad = jnp.concatenate([grad_position, grad_small]).T
        shared_grad = lax.psum_scatter(shared_grad, ALL, scatter_dimension=0, tiled=True).T
        position_grad, small_grad = shared_grad[:length], shared_grad[length:]
    square_part = (
        jnp.sum(table_grad * table_grad) / dp_devs
        + jnp.sum(layer_grad * layer_grad)
        + jnp.sum(position_grad * position_grad)
        + jnp.sum(small_grad * small_grad)
    )
    total_square, loss_value = exchange.total(jnp.stack([square_part, loss_part]), ALL, devices)
    grad_norm = jnp.sqrt(total_square)
    factor = jnp.minimum(1.0, clip_norm / grad_norm)
    table_first, table_second, table_dir = adam_moments(
        embed_table, table_moment, table_square, table_grad, factor
    )
    layer_first, layer_second, layer_dir = adam_moments(
        layer_weights, layer_moment, layer_square, layer_grad, factor
    )
    position_first, position_second, position_dir = adam_moments(
        position_table, position_moment, position_square, position_grad, factor
    )
    small_first, small_second, small_dir = adam_moments(
        small_params, small_moment, small_square, small_grad, factor
    )
    partial_norms = jnp.concatenate(
        [
            norm_pair(embed_table, table_dir, (0, 1))[None] / dp_devs,
            norm_pair(layer_weights, layer_dir, (1, 2)),
            norm_pair(position_table, position_dir, (0, 1))[None],
            norm_pair(small_params, small_dir, (0, 1))[None],
        ]
    )
    trust_square = exchange.total(partial_norms, ALL, devices)
    trust_norms = jnp.sqrt(trust_square)
    ratio = trust_norms[:, 0] / trust_norms[:, 1]
    table_next = embed_table - learn_rate * ratio[0] * table_dir
    layer_next = layer_weights - learn_rate * ratio[1:4][:, None, None] * layer_dir
    position_next = position_table - learn_rate * ratio[4] * position_dir
    small_next = small_params - learn_rate * ratio[5] * small_dir
    return (
        loss_value,
        grad_norm,
        table_next,
        table_first,
        table_second,
        layer_next,
        layer_first,
        layer_second,
        position_next,
        position_first,
        position_second,
        small_next,
        small_first,
        small_second,
        trust_norms,
    )


def solution(mesh):
    dp_devs, owners = mesh.devices.shape
    fine = Mesh(mesh.devices.reshape(dp_devs, owners // 4, 2, 2), ALL)
    rows, inner = P(ALL, None), P(None, ALL)
    table, layer = P(VOC, None), P(None, ALL, None)
    return jax.shard_map(
        on_device,
        mesh=fine,
        in_specs=(rows,) * 3 + (P(ALL),) + (table,) * 3 + (layer,) * 3 + (inner,) * 6,
        out_specs=(P(), P()) + (table,) * 3 + (layer,) * 3 + (inner,) * 6 + (P(),),
        check_vma=False,
    )
```

```python
from functools import partial

import jax
import jax.numpy as jnp
from jax import lax
from jax.experimental import pallas as pl
from jax.experimental.pallas import tpu as pltpu
from jax.sharding import Mesh
from jax.sharding import PartitionSpec as P

HEADS = 12
HD = 64
MASK_ID = 103
NCORP = 4
STEP = 5
CAP = 64


clip_norm = 0.1
learn_rate = 0.3
beta_first = 0.9
beta_second = 0.999
adam_eps = 1e-06
weight_decay = 0.01
norm_eps = 1e-05
masked_score = -1e30
BUCKET = 32
ALL = ("dp", "hi", "mid", "core")
VOC = ("hi", "mid", "core")
NEAR = ("dp", "mid", "core")
bfloat = jnp.bfloat16
single = jnp.float32


def plain_dot(left_op, right_op):
    return jnp.dot(left_op, right_op, preferred_element_type=single)


def trans_dot(left_op, right_op):
    return lax.dot_general(
        left_op, right_op, (((1,), (1,)), ((), ())), preferred_element_type=single
    )


def rows_dot(left_op, right_op):
    return lax.dot_general(
        left_op, right_op, (((0,), (0,)), ((), ())), preferred_element_type=single
    )


def column_sum(values):
    return jnp.sum(values.astype(single), axis=0)


def norm_forward(values, gain_row, bias_row):
    center = values - jnp.mean(values, axis=-1, keepdims=True)
    inverse = lax.rsqrt(jnp.mean(center * center, axis=-1, keepdims=True) + norm_eps)
    normed = center * inverse
    return (normed * gain_row + bias_row, (normed, inverse))


def norm_backward(upstream, kept_norm, gain_row):
    normed, inverse = kept_norm
    scaled = upstream * gain_row
    inner = (
        scaled
        - jnp.mean(scaled, axis=-1, keepdims=True)
        - normed * jnp.mean(scaled * normed, axis=-1, keepdims=True)
    )
    return (inner * inverse, jnp.sum(upstream * normed, axis=0), jnp.sum(upstream, axis=0))


def pair_masks(rows):
    lane = lax.broadcasted_iota(jnp.int32, (rows, 2 * HD), 1)
    return lane < HD, lane >= HD


def head_probs(query_pair, key_pair, head_lanes, blocked):
    scores = trans_dot(jnp.where(head_lanes, query_pair, jnp.zeros_like(query_pair)), key_pair)
    scores = jnp.where(blocked, masked_score, scores * HD ** (-0.5))
    row_top = jnp.max(scores, axis=-1, keepdims=True)
    powers = jnp.exp(scores - row_top)
    return powers / jnp.sum(powers, axis=-1, keepdims=True)


def attend_kernel(
    stream_ref, init_ref, small_ref, allowed_ref, weight_ref,
    key_ref, value_ref, query_ref, mixed_ref, middle_ref, normed_ref, inverse_ref,
):
    step = pl.program_id(0)

    @pl.when(step == 0)
    def _():
        key_ref[...] = plain_dot(stream_ref[...], weight_ref[...]).astype(bfloat)

    @pl.when(step == 1)
    def _():
        value_ref[...] = (
            plain_dot(stream_ref[...], weight_ref[...]) + small_ref[pl.ds(3, 1), :]
        ).astype(bfloat)

    @pl.when(step == 2)
    def _():
        query_ref[...] = (
            plain_dot(init_ref[...].astype(bfloat), weight_ref[...]) + small_ref[pl.ds(2, 1), :]
        ).astype(bfloat)
        blocked = allowed_ref[...] == 0.0
        low, high = pair_masks(query_ref.shape[0])

        def one_pair(pair, carry):
            lanes = pl.ds(pl.multiple_of(pair * 2 * HD, 2 * HD), 2 * HD)
            query_pair, key_pair, value_pair = query_ref[:, lanes], key_ref[:, lanes], value_ref[:, lanes]
            left, right = (
                plain_dot(
                    head_probs(query_pair, key_pair, head_lanes, blocked).astype(bfloat), value_pair
                )
                for head_lanes in (low, high)
            )
            mixed_ref[:, lanes] = jnp.where(low, left, right).astype(bfloat)
            return carry

        lax.fori_loop(0, query_ref.shape[1] // (2 * HD), one_pair, 0)

    @pl.when(step == 3)
    def _():
        attend = plain_dot(mixed_ref[...], weight_ref[...]) + small_ref[pl.ds(4, 1), :]
        middle, (normed, inverse) = norm_forward(
            init_ref[...] + attend, small_ref[pl.ds(5, 1), :], small_ref[pl.ds(6, 1), :]
        )
        middle_ref[...] = middle
        normed_ref[...] = normed
        inverse_ref[...] = jnp.broadcast_to(inverse, inverse_ref.shape)


def attend_forward(stream_b, query_init, small_full, allowed, weights):
    length, width = stream_b.shape
    slots = query_init.shape[0]
    out = lambda rows, kind, columns=width: jax.ShapeDtypeStruct((rows, columns), kind)
    whole = lambda shape: pl.BlockSpec(shape, lambda step: (0, 0))
    shapes = (
        out(length, bfloat), out(length, bfloat), out(slots, bfloat), out(slots, bfloat),
        out(slots, single), out(slots, single), out(slots, single, 128),
    )
    return pl.pallas_call(
        attend_kernel,
        grid=(4,),
        in_specs=[
            whole(stream_b.shape),
            whole(query_init.shape),
            whole(small_full.shape),
            whole(allowed.shape),
            pl.BlockSpec(
                (width, width), lambda step: (0, jnp.where(step == 3, 3, (step + 1) % 3))
            ),
        ],
        out_specs=[whole(shape.shape) for shape in shapes],
        out_shape=shapes,
        cost_estimate=pl.CostEstimate(
            flops=4 * length * width * width + 8 * slots * length * width,
            bytes_accessed=8 * width * width,
            transcendentals=HEADS * slots * length,
        ),
        name="attention_forward",
    )(stream_b, query_init, small_full, allowed, weights)


def attend_back_kernel(
    d_attend_ref, key_ref, value_ref, query_ref, allowed_ref, weight_ref,
    d_query_ref, d_key_ref, d_value_ref, d_mixed_ref,
):
    d_mixed_ref[...] = trans_dot(d_attend_ref[...], weight_ref[...]).astype(bfloat)
    blocked = allowed_ref[...] == 0.0
    slots, length = blocked.shape
    low, high = pair_masks(slots)
    low_long, _ = pair_masks(length)
    scale = HD ** (-0.5)

    def one_pair(pair, carry):
        lanes = pl.ds(pl.multiple_of(pair * 2 * HD, 2 * HD), 2 * HD)
        query_pair, key_pair, value_pair = query_ref[:, lanes], key_ref[:, lanes], value_ref[:, lanes]
        mixed_pair = d_mixed_ref[:, lanes]
        found = []
        for head_lanes in (low, high):
            probs = head_probs(query_pair, key_pair, head_lanes, blocked)
            d_probs = trans_dot(
                jnp.where(head_lanes, mixed_pair, jnp.zeros_like(mixed_pair)), value_pair
            )
            inner = jnp.sum(probs * d_probs, axis=-1, keepdims=True)
            d_scores = (probs * (d_probs - inner)).astype(bfloat)
            found.append(
                (
                    plain_dot(d_scores, key_pair) * scale,
                    rows_dot(d_scores, query_pair) * scale,
                    rows_dot(probs.astype(bfloat), mixed_pair),
                )
            )
        d_query_ref[:, lanes] = jnp.where(low, found[0][0], found[1][0]).astype(bfloat)
        d_key_ref[:, lanes] = jnp.where(low_long, found[0][1], found[1][1]).astype(bfloat)
        d_value_ref[:, lanes] = jnp.where(low_long, found[0][2], found[1][2]).astype(bfloat)
        return carry

    lax.fori_loop(0, query_ref.shape[1] // (2 * HD), one_pair, 0)


def attend_backward(d_attend, key_rows, value_rows, query_rows, allowed, weights):
    length, width = key_rows.shape
    slots = d_attend.shape[0]
    whole = lambda shape: pl.BlockSpec(shape, lambda step: (0, 0))
    shapes = tuple(
        jax.ShapeDtypeStruct((rows, width), bfloat) for rows in (slots, length, length)
    )
    return pl.pallas_call(
        attend_back_kernel,
        grid=(1,),
        in_specs=[
            whole(d_attend.shape),
            whole(key_rows.shape),
            whole(value_rows.shape),
            whole(query_rows.shape),
            whole(allowed.shape),
            pl.BlockSpec((width, width), lambda step: (0, 3)),
        ],
        out_specs=[whole(shape.shape) for shape in shapes],
        out_shape=shapes,
        scratch_shapes=[pltpu.VMEM((slots, width), bfloat)],
        cost_estimate=pl.CostEstimate(
            flops=2 * slots * width * width + 20 * slots * length * width,
            bytes_accessed=2 * width * width,
            transcendentals=HEADS * slots * length,
        ),
        name="attention_backward",
    )(d_attend, key_rows, value_rows, query_rows, allowed, weights)


def feed_forward(layer_b, small_full, middle):
    middle_b = middle.astype(bfloat)
    hidden = plain_dot(middle_b, layer_b[1]) + small_full[7:11].reshape(-1)
    active_b = jax.nn.gelu(hidden, approximate=False).astype(bfloat)
    branch = trans_dot(active_b, layer_b[2]) + small_full[11]
    output_rows, final_kept = norm_forward(middle + branch, small_full[12], small_full[13])
    return output_rows, (middle_b, hidden, active_b, final_kept)


def feed_backward(layer_b, small_full, hidden, final_kept, middle_kept, d_output):
    d_sum, gain_three, bias_three = norm_backward(d_output, final_kept, small_full[12])
    d_branch = d_sum.astype(bfloat)
    _, gelu_pull = jax.vjp(partial(jax.nn.gelu, approximate=False), hidden)
    d_hidden = gelu_pull(plain_dot(d_branch, layer_b[2]))[0].astype(bfloat)
    d_middle = d_sum + trans_dot(d_hidden, layer_b[1])
    d_pre, gain_two, bias_two = norm_backward(d_middle, middle_kept, small_full[5])
    grad_mid = jnp.concatenate(
        [
            gain_two[None],
            bias_two[None],
            column_sum(d_hidden).reshape(4, -1),
            column_sum(d_branch)[None],
            gain_three[None],
            bias_three[None],
        ]
    )
    return d_branch, d_hidden, d_pre, grad_mid


def project_backward(layer_b, d_pre, d_query, d_key, d_value):
    width = d_pre.shape[1]
    d_init = d_pre + trans_dot(d_query, layer_b[0][:, :width])
    d_stream = trans_dot(d_key, layer_b[0][:, width : 2 * width]) + trans_dot(
        d_value, layer_b[0][:, 2 * width : 3 * width]
    )
    grad_mid = jnp.concatenate(
        [
            column_sum(d_query)[None],
            column_sum(d_value)[None],
            column_sum(d_pre.astype(bfloat))[None],
        ]
    )
    return d_init, d_stream, grad_mid


def adam_moments(weight_arr, first_mom, second_mom, gradient, factor):
    clipped = gradient * factor
    new_first = beta_first * first_mom + (1.0 - beta_first) * clipped
    new_second = beta_second * second_mom + (1.0 - beta_second) * clipped * clipped
    direction = (
        new_first
        / (1.0 - beta_first**STEP)
        / (jnp.sqrt(new_second / (1.0 - beta_second**STEP)) + adam_eps)
        + weight_decay * weight_arr
    )
    return (new_first, new_second, direction)


def norm_pair(weight_arr, direction, axes):
    return jnp.stack(
        [jnp.sum(weight_arr * weight_arr, axis=axes), jnp.sum(direction * direction, axis=axes)],
        axis=-1,
    )


class Exchange:
    def __init__(self):
        self.last = None

    def __call__(self, values, axes):
        if self.last is not None:
            values, _ = lax.optimization_barrier((values, self.last))
        self.last = lax.all_to_all(values, axes, 0, 0, tiled=True)
        return self.last

    def copies(self, values, axes, count):
        return self(jnp.broadcast_to(values[None], (count,) + values.shape), axes)

    def total(self, values, axes, count):
        return jnp.sum(self.copies(values, axes, count), axis=0)

    def columns(self, values, axes, count):
        rows, width = values.shape
        blocks = values.reshape(rows, count, width // count).transpose(1, 0, 2)
        return self(blocks, axes).reshape(count * rows, -1)

    def rows(self, values, count):
        return self(values.reshape(count, values.shape[0] // count, values.shape[1]), ALL)


def side_by_side(blocks):
    return blocks.transpose(1, 0, 2).reshape(blocks.shape[1], -1)


def masked_total(mask, values):
    return jnp.sum(jnp.where(mask, values, 0), axis=-1)


def slot_layout(pred_row, order_row, token_row):
    length = pred_row.shape[0]
    index = jnp.arange(length)
    before = index[None, :] <= index[:, None]
    seen = masked_total(before, pred_row[None, :])
    masked = jnp.sum(pred_row)
    place = jnp.where(pred_row == 1, seen - 1, masked + index - seen)
    slot_hot = place[None, :] == jnp.arange(CAP)[:, None]
    rank_row = masked_total(order_row[None, :] == index[:, None], index[None, :])
    slot_rank = masked_total(slot_hot, rank_row[None, :])
    slot_target = masked_total(slot_hot, token_row[None, :])
    slot_pos = masked_total(slot_hot, index[None, :])
    allowed = rank_row[None, :] <= slot_rank[:, None]
    return slot_hot, slot_pos, slot_target, allowed, masked


def bucket_layout(content, vrows):
    index = jnp.arange(content.shape[0])
    same = content[None, :] == content[:, None]
    first = jnp.min(jnp.where(same, index[None, :], content.shape[0]), axis=1)
    is_first = first == index
    owner = content // vrows
    ahead = (owner[None, :] == owner[:, None]) & is_first[None, :] & (index[None, :] < first[:, None])
    return owner, jnp.sum(ahead.astype(jnp.int32), axis=1)


def bucket_round(content, owner, place, turn, owners, vrows):
    usable = BUCKET - 1
    local = place - turn * usable
    taken = (local >= 0) & (local < usable)
    flat = jnp.where(taken, owner * BUCKET + local, -1)
    hot = flat[None, :] == jnp.arange(owners * BUCKET)[:, None]
    wanted = jnp.max(jnp.where(hot, (content - owner * vrows)[None, :], -1), axis=1)
    return hot.astype(bfloat), wanted.reshape(owners, BUCKET)


def on_device(
    token_ids,
    pred_mask,
    fact_order,
    corpus,
    embed_table,
    table_moment,
    table_square,
    layer_weights,
    layer_moment,
    layer_square,
    position_table,
    position_moment,
    position_square,
    small_params,
    small_moment,
    small_square,
):
    exchange = Exchange()
    dp_devs = lax.axis_size("dp")
    owners = lax.axis_size(VOC)
    devices = dp_devs * owners
    vrows, width = embed_table.shape
    length = token_ids.shape[1]
    feed = layer_weights.shape[2]
    shared = jnp.concatenate([position_table, small_params]).T
    shared_rows = shared.shape[1]
    shared = jnp.pad(shared, ((0, 0), (0, -shared_rows % 128)))
    shard = jnp.concatenate([layer_weights[0], layer_weights[1], layer_weights[2], shared], axis=1)
    shard = lax.all_gather(shard.astype(bfloat), ALL, axis=0, tiled=True)
    layer_b = tuple(shard[:, part * feed : (part + 1) * feed] for part in range(3))
    shared = shard[:, 3 * feed : 3 * feed + shared_rows].T
    table_b = embed_table.astype(bfloat)
    token_row = token_ids[0]
    pred_row = pred_mask[0]
    first_row = lax.axis_index(VOC) * vrows
    content = jnp.where(pred_row == 1, MASK_ID, token_row)
    slot_hot, slot_pos, slot_target, allowed, masked = slot_layout(pred_row, fact_order[0], token_row)
    owner, place = bucket_layout(content, vrows)
    hot, wanted = bucket_round(content, owner, place, 0, owners, vrows)
    note = jnp.concatenate(
        [slot_target, slot_pos, jnp.stack([masked, corpus[0], jnp.max(place)])]
    )
    packet = jnp.concatenate(
        [wanted, jnp.broadcast_to(note[None], (owners, note.shape[0]))], axis=1
    )
    packet = jnp.pad(packet, ((0, 0), (0, 256 - packet.shape[1])))
    packet = jnp.broadcast_to(packet[None], (dp_devs,) + packet.shape)
    packet = exchange(packet.reshape(devices, packet.shape[-1]), ALL)
    asked = packet[:, :BUCKET]
    tail = BUCKET + 2 * CAP
    counts_all = packet[:, tail]
    corpus_all = packet[:, tail + 1]
    rounds = jnp.max(packet[:, tail + 2]) // (BUCKET - 1) + 1
    group = lax.axis_index("dp") * owners
    outer = lax.axis_size("hi")

    def group_order(values):
        return values.reshape(outer, 2, 2, CAP).transpose(2, 1, 0, 3).reshape(-1)

    group_asked = lax.dynamic_slice_in_dim(asked, group, owners, 0)
    group_target = group_order(
        lax.dynamic_slice_in_dim(packet[:, BUCKET : BUCKET + CAP], group, owners, 0)
    )
    corpus_hot = corpus_all[:, None] == jnp.arange(NCORP)[None, :]
    corpus_counts = jnp.sum(jnp.where(corpus_hot, counts_all[:, None], 0), axis=0)
    seq_count = masked_total(corpus_hot, corpus_counts[None, :])
    seq_weight = 1.0 / (NCORP * seq_count.astype(single))
    slot_weight = jnp.where(
        jnp.arange(CAP)[None, :] < counts_all[:, None], seq_weight[:, None], 0.0
    )
    group_weight = group_order(lax.dynamic_slice_in_dim(slot_weight, group, owners, 0))

    def serve(asked_rows):
        served = jnp.take(table_b, jnp.maximum(asked_rows, 0).reshape(-1), axis=0)
        return served.reshape(owners, BUCKET, width)

    arrived = exchange(serve(group_asked), VOC)
    embed_rows = rows_dot(hot, arrived.reshape(-1, width))

    def more_rows(state):
        turn, rows = state
        hot_t, wanted_t = bucket_round(content, owner, place, turn, owners, vrows)
        asked_t = lax.all_to_all(wanted_t, VOC, 0, 0, tiled=True)
        arrived_t = lax.all_to_all(serve(asked_t), VOC, 0, 0, tiled=True)
        return turn + 1, rows + rows_dot(hot_t, arrived_t.reshape(-1, width))

    _, embed_rows = lax.while_loop(
        lambda state: state[0] < rounds, more_rows, (jnp.ones((), rounds.dtype), embed_rows)
    )
    position_b = shared[:length]
    position_full = position_b.astype(single)
    small_full = shared[length:].astype(single)
    stream, stream_kept = norm_forward(embed_rows + position_full, small_full[0], small_full[1])
    stream_b = stream.astype(bfloat)
    slot_b = slot_hot.astype(bfloat)
    query_init, init_kept = norm_forward(
        plain_dot(slot_b, position_b), small_full[0], small_full[1]
    )
    few = devices <= 32
    near = dp_devs * 4
    if few:
        stream_all = lax.all_gather(stream_b, NEAR, axis=0, tiled=True)
    allowed = allowed.astype(single)
    key_rows, value_rows, query_rows, mixed_b, middle, normed, inverse = attend_forward(
        stream_b, query_init, small_full, allowed, shard
    )
    output_rows, (middle_b, hidden, active_b, final_kept) = feed_forward(
        layer_b, small_full, middle
    )
    output_b = output_rows.astype(bfloat)
    if few:
        kept_rows = jnp.concatenate([mixed_b, middle_b], axis=1)
        kept_rows, stream_all = lax.optimization_barrier((kept_rows, stream_all))
        kept_all = lax.all_gather(kept_rows, ALL, axis=0, tiled=True)
    group_rows = exchange.copies(output_b, "hi", outer).reshape(-1, width)
    group_rows = exchange.copies(group_rows, "mid", 2).reshape(-1, width)
    group_rows = exchange.copies(group_rows, "core", 2).reshape(-1, width)
    logits = trans_dot(group_rows, table_b)
    local_target = group_target - first_row
    target_hit = jnp.arange(vrows)[None, :] == local_target[:, None]
    row_top = jnp.max(logits, axis=1)
    row_total = jnp.sum(jnp.exp(logits - row_top[:, None]), axis=1)
    row_target = jnp.sum(jnp.where(target_hit, logits, 0.0), axis=1)
    stats = exchange.copies(jnp.stack([row_top, row_total]), VOC, owners)
    if few:
        active_mine = exchange.columns(active_b, ALL, devices)
    top_all = jnp.max(stats[:, 0], axis=0)
    total_all = jnp.sum(stats[:, 1] * jnp.exp(stats[:, 0] - top_all[None]), axis=0)
    log_total = top_all + jnp.log(total_all)
    own_place = lax.axis_index(("core", "mid", "hi"))
    own_total = lax.dynamic_slice_in_dim(log_total * group_weight, own_place * CAP, CAP, 0)
    loss_part = jnp.sum(own_total) - jnp.sum(row_target * group_weight)
    d_logits = (
        group_weight[:, None] * (jnp.exp(logits - log_total[:, None]) - target_hit.astype(single))
    ).astype(bfloat)
    def swapped(axis, part):
        side = lax.axis_index(axis)
        theirs = lax.ppermute(part(1 - side), axis, [(0, 1), (1, 0)])
        return part(side) + theirs

    half = owners * CAP // 2

    def rows_half(side):
        return plain_dot(lax.dynamic_slice_in_dim(d_logits, side * half, half, 0), table_b)

    d_output = swapped("core", rows_half)
    quarter = half // 2
    d_half = d_output
    d_output = swapped(
        "mid", lambda side: lax.dynamic_slice_in_dim(d_half, side * quarter, quarter, 0)
    )
    grad_head = rows_dot(d_logits, group_rows)
    if dp_devs == 2:
        head_b = grad_head.astype(bfloat)
        other_b = lax.ppermute(head_b, "dp", [(0, 1), (1, 0)])
        d_output, head_b = lax.optimization_barrier((d_output, head_b))
        grad_head = head_b.astype(single) + other_b.astype(single)
    else:
        grad_head = lax.psum(grad_head, "dp")
    d_output = exchange(d_output.reshape(outer, CAP, width), "hi")
    if few:
        d_output, kept_all = lax.optimization_barrier((d_output, kept_all))
    d_output = jnp.sum(d_output, axis=0)
    d_branch, d_hidden, d_pre, mid_feed = feed_backward(
        layer_b, small_full, hidden, final_kept, (normed, inverse[:, :1]), d_output
    )
    d_attend = d_pre.astype(bfloat)
    if few:
        wide = feed // devices
        both = jnp.concatenate(
            [
                d_hidden.reshape(CAP, devices, -1),
                d_attend.reshape(CAP, devices, -1),
            ],
            axis=2,
        ).reshape(CAP, -1)
        both = exchange.columns(both, ALL, devices)
        branch_all = lax.all_gather(d_branch, ALL, axis=0, tiled=True)
    d_query, d_key, d_value = attend_backward(
        d_attend, key_rows, value_rows, query_rows, allowed, shard
    )
    d_init, d_stream, mid_attn = project_backward(layer_b, d_pre, d_query, d_key, d_value)
    grad_mid = jnp.concatenate([mid_attn, mid_feed])
    if few:
        piece = width // near
        pairs = jnp.concatenate(
            [d_key.reshape(length, near, piece), d_value.reshape(length, near, piece)], axis=2
        ).transpose(1, 0, 2)
        asks = d_query.reshape(CAP, near, piece).transpose(1, 0, 2)
        asks = jnp.concatenate([asks[:, : CAP // 2], asks[:, CAP // 2 :]], axis=2)
        pairs = exchange(jnp.concatenate([pairs, asks], axis=1), NEAR)
    d_start, gain_init, bias_init = norm_backward(d_init, init_kept, small_full[0])
    d_embed, gain_stream, bias_stream = norm_backward(d_stream, stream_kept, small_full[0])
    grad_position = d_embed + lax.dot_general(
        slot_hot.astype(single),
        d_start,
        (((0,), (0,)), ((), ())),
        precision=lax.Precision.HIGHEST,
        preferred_element_type=single,
    )
    grad_small = jnp.concatenate(
        [(gain_init + gain_stream)[None], (bias_init + bias_stream)[None], grad_mid]
    )
    embed_back = d_embed.astype(bfloat)
    mask_sum = jnp.sum(
        jnp.where((content == MASK_ID)[:, None], embed_back.astype(single), 0.0), axis=0
    )
    mask_left = mask_sum - lax.reduce_precision(mask_sum, 8, 7)
    mask_owner = MASK_ID // vrows
    is_left = (jnp.arange(BUCKET) == BUCKET - 1)[None, :] & (
        jnp.arange(owners) == mask_owner
    )[:, None]

    def plain_exchange(values, axes):
        return lax.all_to_all(values, axes, 0, 0, tiled=True)

    def give(hot_rows, extra, send):
        rows = plain_dot(hot_rows, embed_back).reshape(owners, BUCKET, width)
        rows = jnp.where(is_left[:, :, None] & extra, mask_left[None, None, :], rows)
        return send(rows.astype(bfloat), VOC).reshape(-1, width)

    def of_both(rows):
        if dp_devs == 2:
            return rows, lax.ppermute(rows, "dp", [(0, 1), (1, 0)])
        return (lax.all_gather(rows, "dp", axis=0, tiled=True),)

    def both_groups(asked_rows):
        if dp_devs == 2:
            return jnp.roll(asked_rows, -group, axis=0)
        return asked_rows

    def into_rows(asked_rows, given):
        flat = both_groups(asked_rows).reshape(-1)
        row_hot = flat[None, :] == jnp.arange(vrows)[:, None]
        return plain_dot(row_hot.astype(bfloat), jnp.concatenate(given))

    last = (jnp.arange(BUCKET) == BUCKET - 1)[None, :]
    left_row = jnp.where(lax.axis_index(VOC) == mask_owner, MASK_ID - first_row, -1)
    given = give(hot, True, exchange)

    if few:
        near_pos = packet[:, BUCKET + CAP : tail].reshape(dp_devs, outer, 4 * CAP)
        near_pos = lax.dynamic_index_in_dim(near_pos, lax.axis_index("hi"), 1, False).reshape(-1)
        init_rows = norm_forward(position_full, small_full[0], small_full[1])[0].astype(bfloat)
        init_hot = near_pos[:, None] == jnp.arange(length)[None, :]
        init_all = plain_dot(init_hot.astype(bfloat), init_rows).astype(bfloat)
        asks = pairs[:, length:]
        asks = jnp.concatenate([asks[..., :piece], asks[..., piece:]], axis=1)
        grad_pair = rows_dot(stream_all, pairs[:, :length].reshape(near * length, -1))
        grad_ask = rows_dot(init_all, asks.reshape(near * CAP, piece))
        share = width // devices
        grad_up = rows_dot(kept_all[:, width:], both[:, :wide])
        grad_out = rows_dot(kept_all[:, :width], both[:, wide:])
        grad_down = rows_dot(branch_all, active_mine)
        shared_grad = jnp.concatenate([grad_position, grad_small]).T
        results = jnp.concatenate(
            [grad_pair, grad_ask, grad_up, grad_down, grad_out, shared_grad], axis=1
        )
        results = results.astype(bfloat)
        given, _ = lax.optimization_barrier((given, results))
        results = exchange.rows(results, devices).astype(single)
        pieces = 3 * piece
        attn = jnp.sum(
            results[..., :pieces].reshape(dp_devs, outer, 4, share, pieces), axis=1
        ).reshape(near, share, pieces)
        shared_grad = jnp.sum(results[..., -shared_rows:], axis=0).T
        position_grad, small_grad = shared_grad[:length], shared_grad[length:]
        grad_key, grad_value, grad_query = (
            side_by_side(attn[..., part * piece : (part + 1) * piece]) for part in range(3)
        )
        grad_up = side_by_side(results[..., pieces : pieces + wide])
        grad_down = side_by_side(results[..., pieces + wide : pieces + 2 * wide])
        grad_out = side_by_side(results[..., pieces + 2 * wide : -shared_rows])
        layer_grad = jnp.stack(
            [
                jnp.concatenate([grad_query, grad_key, grad_value, grad_out], axis=1),
                grad_up,
                grad_down,
            ]
        )
    else:
        whole = (
            jnp.concatenate(
                [
                    rows_dot(query_init.astype(bfloat), d_query),
                    rows_dot(stream_b, d_key),
                    rows_dot(stream_b, d_value),
                    rows_dot(mixed_b, d_attend),
                ],
                axis=1,
            ),
            rows_dot(middle_b, d_hidden),
            rows_dot(d_branch, active_b),
        )
        layer_grad = jnp.stack(
            [lax.psum_scatter(part, ALL, scatter_dimension=0, tiled=True) for part in whole]
        )
        shared_grad = jnp.concatenate([grad_position, grad_small]).T
        shared_grad = lax.psum_scatter(shared_grad, ALL, scatter_dimension=0, tiled=True).T
        position_grad, small_grad = shared_grad[:length], shared_grad[length:]
    table_grad = grad_head + into_rows(jnp.where(last, left_row, asked), of_both(given))

    def more_grads(state):
        turn, grads = state
        hot_t, wanted_t = bucket_round(content, owner, place, turn, owners, vrows)
        wanted_t = jnp.broadcast_to(wanted_t[None], (dp_devs,) + wanted_t.shape)
        asked_t = lax.all_to_all(
            wanted_t.reshape(devices, BUCKET), ALL, 0, 0, tiled=True
        )
        return turn + 1, grads + into_rows(asked_t, of_both(give(hot_t, False, plain_exchange)))

    _, table_grad = lax.while_loop(
        lambda state: state[0] < rounds, more_grads, (jnp.ones((), rounds.dtype), table_grad)
    )
    split = vrows // dp_devs

    def own_part(values):
        return lax.dynamic_slice_in_dim(values, lax.axis_index("dp") * split, split, 0)

    grad_part = own_part(table_grad)
    square_part = (
        jnp.sum(grad_part * grad_part)
        + jnp.sum(layer_grad * layer_grad)
        + jnp.sum(position_grad * position_grad)
        + jnp.sum(small_grad * small_grad)
    )
    total_square, loss_value = exchange.total(jnp.stack([square_part, loss_part]), ALL, devices)
    grad_norm = jnp.sqrt(total_square)
    factor = jnp.minimum(1.0, clip_norm / grad_norm)
    weight_part = own_part(embed_table)
    _, _, part_dir = adam_moments(
        weight_part, own_part(table_moment), own_part(table_square), grad_part, factor
    )
    layer_first, layer_second, layer_dir = adam_moments(
        layer_weights, layer_moment, layer_square, layer_grad, factor
    )
    position_first, position_second, position_dir = adam_moments(
        position_table, position_moment, position_square, position_grad, factor
    )
    small_first, small_second, small_dir = adam_moments(
        small_params, small_moment, small_square, small_grad, factor
    )
    partial_norms = jnp.concatenate(
        [
            norm_pair(weight_part, part_dir, (0, 1))[None],
            norm_pair(layer_weights, layer_dir, (1, 2)),
            norm_pair(position_table, position_dir, (0, 1))[None],
            norm_pair(small_params, small_dir, (0, 1))[None],
        ]
    )
    factor_late, _ = lax.optimization_barrier((factor, partial_norms))
    table_first, table_second, table_dir = adam_moments(
        embed_table, table_moment, table_square, table_grad, factor_late
    )
    table_dir = lax.optimization_barrier(table_dir)
    trust_square = exchange.total(partial_norms, ALL, devices)
    trust_norms = jnp.sqrt(trust_square)
    ratio = trust_norms[:, 0] / trust_norms[:, 1]
    table_next = embed_table - learn_rate * ratio[0] * table_dir
    layer_next = layer_weights - learn_rate * ratio[1:4][:, None, None] * layer_dir
    position_next = position_table - learn_rate * ratio[4] * position_dir
    small_next = small_params - learn_rate * ratio[5] * small_dir
    return (
        loss_value,
        grad_norm,
        table_next,
        table_first,
        table_second,
        layer_next,
        layer_first,
        layer_second,
        position_next,
        position_first,
        position_second,
        small_next,
        small_first,
        small_second,
        trust_norms,
    )


def solution(mesh):
    dp_devs, owners = mesh.devices.shape
    fine = Mesh(mesh.devices.reshape(dp_devs, owners // 4, 2, 2), ALL)
    rows, inner = P(ALL, None), P(None, ALL)
    table, layer = P(VOC, None), P(None, ALL, None)
    return jax.shard_map(
        on_device,
        mesh=fine,
        in_specs=(rows,) * 3 + (P(ALL),) + (table,) * 3 + (layer,) * 3 + (inner,) * 6,
        out_specs=(P(), P()) + (table,) * 3 + (layer,) * 3 + (inner,) * 6 + (P(),),
        check_vma=False,
    )
```

```python
import jax
import jax.numpy as jnp
from jax import lax
from jax.experimental import pallas as pl
from jax.experimental.pallas import tpu as pltpu
from jax.sharding import Mesh
from jax.sharding import PartitionSpec as P

HEADS = 12
HD = 64
MASK_ID = 103
NCORP = 4
STEP = 5
CAP = 64


clip_norm = 0.1
learn_rate = 0.3
beta_first = 0.9
beta_second = 0.999
adam_eps = 1e-06
weight_decay = 0.01
norm_eps = 1e-05
masked_score = -1e30
BUCKET = 32
ALL = ("dp", "hi", "mid", "core")
VOC = ("hi", "mid", "core")
NEAR = ("dp", "mid", "core")
bfloat = jnp.bfloat16
single = jnp.float32


def plain_dot(left_op, right_op):
    return jnp.dot(left_op, right_op, preferred_element_type=single)


def trans_dot(left_op, right_op):
    return lax.dot_general(
        left_op, right_op, (((1,), (1,)), ((), ())), preferred_element_type=single
    )


def rows_dot(left_op, right_op):
    return lax.dot_general(
        left_op, right_op, (((0,), (0,)), ((), ())), preferred_element_type=single
    )


def column_sum(values):
    return jnp.sum(values.astype(single), axis=0)


def norm_forward(values, gain_row, bias_row):
    center = values - jnp.mean(values, axis=-1, keepdims=True)
    inverse = lax.rsqrt(jnp.mean(center * center, axis=-1, keepdims=True) + norm_eps)
    normed = center * inverse
    return (normed * gain_row + bias_row, (normed, inverse))


def norm_backward(upstream, kept_norm, gain_row):
    normed, inverse = kept_norm
    scaled = upstream * gain_row
    inner = (
        scaled
        - jnp.mean(scaled, axis=-1, keepdims=True)
        - normed * jnp.mean(scaled * normed, axis=-1, keepdims=True)
    )
    return (inner * inverse, jnp.sum(upstream * normed, axis=0), jnp.sum(upstream, axis=0))


def pair_masks(rows):
    lane = lax.broadcasted_iota(jnp.int32, (rows, 2 * HD), 1)
    return lane < HD, lane >= HD


def head_probs(query_pair, key_pair, head_lanes, blocked):
    scores = trans_dot(jnp.where(head_lanes, query_pair, jnp.zeros_like(query_pair)), key_pair)
    scores = jnp.where(blocked, masked_score, scores * HD ** (-0.5))
    row_top = jnp.max(scores, axis=-1, keepdims=True)
    powers = jnp.exp(scores - row_top)
    return powers / jnp.sum(powers, axis=-1, keepdims=True)


def spread(column, lanes=128):
    return jnp.broadcast_to(column, (column.shape[0], lanes))


def row_of(ref, row):
    return ref[pl.ds(row, 1), :]


def attend_kernel(
    embed_ref, slot_ref, allowed_ref, shared_ref, weight_ref,
    key_ref, value_ref, query_ref, mixed_ref, middle_ref, normed_ref, inverse_ref,
    stream_ref, stream_normed_ref, stream_inverse_ref,
    init_ref, init_normed_ref, init_inverse_ref, position_ref, small_ref,
):
    step = pl.program_id(0)
    length = position_ref.shape[0]

    @pl.when(step == 0)
    def _():
        shared = shared_ref[...].astype(single).T
        position_ref[...] = shared[:length]
        small_ref[...] = shared[length : length + small_ref.shape[0]]
        gain, bias = row_of(small_ref, 0), row_of(small_ref, 1)
        stream, (normed, inverse) = norm_forward(embed_ref[...] + position_ref[...], gain, bias)
        stream_ref[...] = stream.astype(bfloat)
        stream_normed_ref[...] = normed
        stream_inverse_ref[...] = spread(inverse)
        chosen = plain_dot(slot_ref[...].astype(bfloat), position_ref[...].astype(bfloat))
        init, (normed, inverse) = norm_forward(chosen, gain, bias)
        init_ref[...] = init
        init_normed_ref[...] = normed
        init_inverse_ref[...] = spread(inverse)
        key_ref[...] = plain_dot(stream_ref[...], weight_ref[...]).astype(bfloat)

    @pl.when(step == 1)
    def _():
        value_ref[...] = (
            plain_dot(stream_ref[...], weight_ref[...]) + row_of(small_ref, 3)
        ).astype(bfloat)

    @pl.when(step == 2)
    def _():
        query_ref[...] = (
            plain_dot(init_ref[...].astype(bfloat), weight_ref[...]) + row_of(small_ref, 2)
        ).astype(bfloat)
        blocked = allowed_ref[...] == 0.0
        low, high = pair_masks(query_ref.shape[0])

        def one_pair(pair, carry):
            lanes = pl.ds(pl.multiple_of(pair * 2 * HD, 2 * HD), 2 * HD)
            query_pair, key_pair, value_pair = query_ref[:, lanes], key_ref[:, lanes], value_ref[:, lanes]
            left, right = (
                plain_dot(
                    head_probs(query_pair, key_pair, head_lanes, blocked).astype(bfloat), value_pair
                )
                for head_lanes in (low, high)
            )
            mixed_ref[:, lanes] = jnp.where(low, left, right).astype(bfloat)
            return carry

        lax.fori_loop(0, query_ref.shape[1] // (2 * HD), one_pair, 0)

    @pl.when(step == 3)
    def _():
        attend = plain_dot(mixed_ref[...], weight_ref[...]) + row_of(small_ref, 4)
        middle, (normed, inverse) = norm_forward(
            init_ref[...] + attend, row_of(small_ref, 5), row_of(small_ref, 6)
        )
        middle_ref[...] = middle
        normed_ref[...] = normed
        inverse_ref[...] = spread(inverse)


def kernel_call(body, name, steps, inputs, shapes, cost, scratch=()):
    fixed = lambda rank: lambda step: (0,) * rank

    def spec(shape, block, index):
        if block is None:
            return pl.BlockSpec(shape, fixed(len(shape)))
        return pl.BlockSpec(block, index)

    return pl.pallas_call(
        body,
        grid=(steps,),
        in_specs=[spec(array.shape, block, index) for array, block, index in inputs],
        out_specs=[spec(shape, block, index) for shape, _, block, index in shapes],
        out_shape=[jax.ShapeDtypeStruct(shape, kind) for shape, kind, _, _ in shapes],
        scratch_shapes=list(scratch),
        cost_estimate=pl.CostEstimate(flops=cost[0], bytes_accessed=cost[1], transcendentals=cost[2]),
        name=name,
    )(*(array for array, _, _ in inputs))


def whole(array):
    return array, None, None


def attend_forward(embed_rows, slot_hot, allowed, weights, length, small_count):
    width = embed_rows.shape[1]
    slots = slot_hot.shape[0]
    out = lambda rows, kind, columns=width: ((rows, columns), kind, None, None)
    shared = weights.shape[1] - 12 * width
    return kernel_call(
        attend_kernel,
        "attention_forward",
        4,
        [
            whole(embed_rows),
            whole(slot_hot),
            whole(allowed),
            (weights, (width, shared), lambda step: (0, 12 * width // shared)),
            (
                weights,
                (width, width),
                lambda step: (0, jnp.where(step == 3, 3, (step + 1) % 3)),
            ),
        ],
        [
            out(length, bfloat), out(length, bfloat), out(slots, bfloat), out(slots, bfloat),
            out(slots, single), out(slots, single), out(slots, single, 128),
            out(length, bfloat), out(length, single), out(length, single, 128),
            out(slots, single), out(slots, single), out(slots, single, 128),
            out(length, single), out(small_count, single),
        ],
        (
            4 * length * width * width + 8 * slots * length * width,
            8 * width * width,
            HEADS * slots * length,
        ),
    )


def erf_half(hidden):
    return 0.5 * (1.0 + lax.erf(hidden * 0.5**0.5))


def feed_kernel(
    middle_ref, small_ref, up_ref, down_ref,
    middle_b_ref, hidden_ref, active_ref, output_ref, normed_ref, inverse_ref, total_ref,
):
    step = pl.program_id(0)

    @pl.when(step == 0)
    def _():
        middle_b_ref[...] = middle_ref[...].astype(bfloat)
        total_ref[...] = middle_ref[...] + row_of(small_ref, 11)

    hidden = plain_dot(middle_b_ref[...], up_ref[...]) + row_of(small_ref, 7 + step)
    hidden_ref[...] = hidden
    active = (hidden * erf_half(hidden)).astype(bfloat)
    active_ref[...] = active
    total_ref[...] += trans_dot(active, down_ref[...])

    @pl.when(step == pl.num_programs(0) - 1)
    def _():
        output, (normed, inverse) = norm_forward(
            total_ref[...], row_of(small_ref, 12), row_of(small_ref, 13)
        )
        output_ref[...] = output.astype(bfloat)
        normed_ref[...] = normed
        inverse_ref[...] = spread(inverse)


def feed_forward(middle, small_full, weights):
    slots, width = middle.shape
    wide = lambda kind: ((slots, 4 * width), kind, (slots, width), lambda step: (0, step))
    out = lambda kind, columns=width: ((slots, columns), kind, None, None)
    return kernel_call(
        feed_kernel,
        "feed_forward",
        4,
        [
            whole(middle),
            whole(small_full),
            (weights, (width, width), lambda step: (0, 4 + step)),
            (weights, (width, width), lambda step: (0, 8 + step)),
        ],
        [
            out(bfloat), wide(single), wide(bfloat), out(bfloat), out(single), out(single, 128),
        ],
        (16 * slots * width * width, 16 * width * width, 4 * slots * width),
        [pltpu.VMEM((slots, width), single)],
    )


def norm_back(upstream, normed, inverse, gain_row):
    return norm_backward(upstream, (normed, inverse), gain_row)


def feed_back_kernel(
    parts_ref, normed_ref, inverse_ref, hidden_ref, small_ref, mid_normed_ref, mid_inverse_ref,
    up_ref, down_ref,
    d_branch_ref, d_hidden_ref, d_pre_ref, d_attend_ref, sums_ref, d_middle_ref,
):
    step = pl.program_id(0)

    @pl.when(step == 0)
    def _():
        sums_ref[...] = jnp.zeros_like(sums_ref)
        d_sum, gain, bias = norm_back(
            jnp.sum(parts_ref[...], axis=0), normed_ref[...], inverse_ref[:, :1], row_of(small_ref, 12)
        )
        d_branch = d_sum.astype(bfloat)
        d_branch_ref[...] = d_branch
        d_middle_ref[...] = d_sum
        sums_ref[pl.ds(6, 1), :] = column_sum(d_branch)[None]
        sums_ref[pl.ds(7, 1), :] = gain[None]
        sums_ref[pl.ds(8, 1), :] = bias[None]

    hidden = hidden_ref[...]
    slope = erf_half(hidden) + hidden * jnp.exp(-0.5 * hidden * hidden) * (2.0 * jnp.pi) ** (-0.5)
    d_hidden = (plain_dot(d_branch_ref[...], down_ref[...]) * slope).astype(bfloat)
    d_hidden_ref[...] = d_hidden
    sums_ref[pl.ds(2 + step, 1), :] = column_sum(d_hidden)[None]
    d_middle_ref[...] += trans_dot(d_hidden, up_ref[...])

    @pl.when(step == pl.num_programs(0) - 1)
    def _():
        d_pre, gain, bias = norm_back(
            d_middle_ref[...], mid_normed_ref[...], mid_inverse_ref[:, :1], row_of(small_ref, 5)
        )
        d_pre_ref[...] = d_pre
        d_attend_ref[...] = d_pre.astype(bfloat)
        sums_ref[pl.ds(0, 1), :] = gain[None]
        sums_ref[pl.ds(1, 1), :] = bias[None]


def feed_backward(parts, normed, inverse, hidden, small_full, mid_normed, mid_inverse, weights):
    slots, width = normed.shape
    block = (slots, width), lambda step: (0, step)
    out = lambda kind, rows=slots: ((rows, width), kind, None, None)
    return kernel_call(
        feed_back_kernel,
        "feed_backward",
        4,
        [
            whole(parts),
            whole(normed),
            whole(inverse),
            (hidden,) + block,
            whole(small_full),
            whole(mid_normed),
            whole(mid_inverse),
            (weights, (width, width), lambda step: (0, 4 + step)),
            (weights, (width, width), lambda step: (0, 8 + step)),
        ],
        [
            out(bfloat), ((slots, 4 * width), bfloat) + block, out(single), out(bfloat),
            out(single, 16),
        ],
        (16 * slots * width * width, 16 * width * width, 8 * slots * width),
        [pltpu.VMEM((slots, width), single)],
    )


def attend_back_kernel(
    d_attend_ref, key_ref, value_ref, query_ref, allowed_ref, weight_ref,
    d_query_ref, d_key_ref, d_value_ref, d_mixed_ref,
):
    d_mixed_ref[...] = trans_dot(d_attend_ref[...], weight_ref[...]).astype(bfloat)
    blocked = allowed_ref[...] == 0.0
    slots, length = blocked.shape
    low, high = pair_masks(slots)
    low_long, _ = pair_masks(length)
    scale = HD ** (-0.5)

    def one_pair(pair, carry):
        lanes = pl.ds(pl.multiple_of(pair * 2 * HD, 2 * HD), 2 * HD)
        query_pair, key_pair, value_pair = query_ref[:, lanes], key_ref[:, lanes], value_ref[:, lanes]
        mixed_pair = d_mixed_ref[:, lanes]
        found = []
        for head_lanes in (low, high):
            probs = head_probs(query_pair, key_pair, head_lanes, blocked)
            d_probs = trans_dot(
                jnp.where(head_lanes, mixed_pair, jnp.zeros_like(mixed_pair)), value_pair
            )
            inner = jnp.sum(probs * d_probs, axis=-1, keepdims=True)
            d_scores = (probs * (d_probs - inner)).astype(bfloat)
            found.append(
                (
                    plain_dot(d_scores, key_pair) * scale,
                    rows_dot(d_scores, query_pair) * scale,
                    rows_dot(probs.astype(bfloat), mixed_pair),
                )
            )
        d_query_ref[:, lanes] = jnp.where(low, found[0][0], found[1][0]).astype(bfloat)
        d_key_ref[:, lanes] = jnp.where(low_long, found[0][1], found[1][1]).astype(bfloat)
        d_value_ref[:, lanes] = jnp.where(low_long, found[0][2], found[1][2]).astype(bfloat)
        return carry

    lax.fori_loop(0, query_ref.shape[1] // (2 * HD), one_pair, 0)


def attend_backward(d_attend, key_rows, value_rows, query_rows, allowed, weights):
    length, width = key_rows.shape
    slots = d_attend.shape[0]
    out = lambda rows: ((rows, width), bfloat, None, None)
    return kernel_call(
        attend_back_kernel,
        "attention_backward",
        1,
        [
            whole(d_attend),
            whole(key_rows),
            whole(value_rows),
            whole(query_rows),
            whole(allowed),
            (weights, (width, width), lambda step: (0, 3)),
        ],
        [out(slots), out(length), out(length)],
        (
            2 * slots * width * width + 20 * slots * length * width,
            2 * width * width,
            HEADS * slots * length,
        ),
        [pltpu.VMEM((slots, width), bfloat)],
    )


def project_back_kernel(
    d_pre_ref, d_query_ref, d_key_ref, d_value_ref, slot_ref, hidden_row_ref, small_ref,
    normed_ref, inverse_ref, init_normed_ref, init_inverse_ref, weight_ref,
    embed_ref, position_ref, sums_ref, d_stream_ref, d_init_ref,
):
    step = pl.program_id(0)

    @pl.when(step == 0)
    def _():
        d_init_ref[...] = d_pre_ref[...] + trans_dot(d_query_ref[...], weight_ref[...])

    @pl.when(step == 1)
    def _():
        d_stream_ref[...] = trans_dot(d_key_ref[...], weight_ref[...])

    @pl.when(step == 2)
    def _():
        gain_row = row_of(small_ref, 0)
        d_stream = d_stream_ref[...] + trans_dot(d_value_ref[...], weight_ref[...])
        d_start, gain_init, bias_init = norm_back(
            d_init_ref[...], init_normed_ref[...], init_inverse_ref[:, :1], gain_row
        )
        d_embed, gain, bias = norm_back(
            d_stream, normed_ref[...], inverse_ref[:, :1], gain_row
        )
        position_ref[...] = d_embed + lax.dot_general(
            slot_ref[...],
            d_start,
            (((0,), (0,)), ((), ())),
            precision=lax.Precision.HIGHEST,
            preferred_element_type=single,
        )
        embed_b = d_embed.astype(bfloat)
        embed_ref[...] = embed_b
        sums_ref[...] = jnp.zeros_like(sums_ref)
        sums_ref[pl.ds(0, 1), :] = (gain_init + gain)[None]
        sums_ref[pl.ds(1, 1), :] = (bias_init + bias)[None]
        sums_ref[pl.ds(2, 1), :] = column_sum(d_query_ref[...])[None]
        sums_ref[pl.ds(3, 1), :] = column_sum(d_value_ref[...])[None]
        sums_ref[pl.ds(4, 1), :] = column_sum(d_pre_ref[...].astype(bfloat))[None]
        masked = jnp.where(hidden_row_ref[:, :1] > 0.0, embed_b.astype(single), 0.0)
        sums_ref[pl.ds(5, 1), :] = jnp.sum(masked, axis=0)[None]


def project_backward(
    d_pre, d_query, d_key, d_value, slot_hot, hidden_rows, small_full,
    normed, inverse, init_normed, init_inverse, weights,
):
    length, width = normed.shape
    slots = d_pre.shape[0]
    arrays = (
        d_pre, d_query, d_key, d_value, slot_hot, hidden_rows, small_full,
        normed, inverse, init_normed, init_inverse,
    )
    return kernel_call(
        project_back_kernel,
        "projection_backward",
        3,
        [whole(array) for array in arrays]
        + [(weights, (width, width), lambda step: (0, step))],
        [
            ((length, width), bfloat, None, None),
            ((length, width), single, None, None),
            ((8, width), single, None, None),
        ],
        (5 * length * width * width, 6 * width * width, 0),
        [pltpu.VMEM((length, width), single), pltpu.VMEM((slots, width), single)],
    )


def adam_moments(weight_arr, first_mom, second_mom, gradient, factor):
    clipped = gradient * factor
    new_first = beta_first * first_mom + (1.0 - beta_first) * clipped
    new_second = beta_second * second_mom + (1.0 - beta_second) * clipped * clipped
    direction = (
        new_first
        / (1.0 - beta_first**STEP)
        / (jnp.sqrt(new_second / (1.0 - beta_second**STEP)) + adam_eps)
        + weight_decay * weight_arr
    )
    return (new_first, new_second, direction)


def norm_pair(weight_arr, direction, axes):
    return jnp.stack(
        [jnp.sum(weight_arr * weight_arr, axis=axes), jnp.sum(direction * direction, axis=axes)],
        axis=-1,
    )


class Exchange:
    def __init__(self):
        self.last = None

    def __call__(self, values, axes):
        if self.last is not None:
            values, _ = lax.optimization_barrier((values, self.last))
        self.last = lax.all_to_all(values, axes, 0, 0, tiled=True)
        return self.last

    def copies(self, values, axes, count):
        return self(jnp.broadcast_to(values[None], (count,) + values.shape), axes)

    def total(self, values, axes, count):
        return jnp.sum(self.copies(values, axes, count), axis=0)

    def columns(self, values, axes, count):
        rows, width = values.shape
        blocks = values.reshape(rows, count, width // count).transpose(1, 0, 2)
        return self(blocks, axes).reshape(count * rows, -1)

    def rows(self, values, count):
        return self(values.reshape(count, values.shape[0] // count, values.shape[1]), ALL)


def side_by_side(blocks):
    return blocks.transpose(1, 0, 2).reshape(blocks.shape[1], -1)


def masked_total(mask, values):
    return jnp.sum(jnp.where(mask, values, 0), axis=-1)


def slot_layout(pred_row, order_row, token_row):
    length = pred_row.shape[0]
    index = jnp.arange(length)
    before = index[None, :] <= index[:, None]
    seen = masked_total(before, pred_row[None, :])
    masked = jnp.sum(pred_row)
    place = jnp.where(pred_row == 1, seen - 1, masked + index - seen)
    slot_hot = place[None, :] == jnp.arange(CAP)[:, None]
    rank_row = masked_total(order_row[None, :] == index[:, None], index[None, :])
    slot_rank = masked_total(slot_hot, rank_row[None, :])
    slot_target = masked_total(slot_hot, token_row[None, :])
    slot_pos = masked_total(slot_hot, index[None, :])
    allowed = rank_row[None, :] <= slot_rank[:, None]
    return slot_hot, slot_pos, slot_target, allowed, masked


def bucket_layout(content, vrows):
    index = jnp.arange(content.shape[0])
    same = content[None, :] == content[:, None]
    first = jnp.min(jnp.where(same, index[None, :], content.shape[0]), axis=1)
    is_first = first == index
    owner = content // vrows
    ahead = (owner[None, :] == owner[:, None]) & is_first[None, :] & (index[None, :] < first[:, None])
    return owner, jnp.sum(ahead.astype(jnp.int32), axis=1)


def bucket_round(content, owner, place, turn, owners, vrows):
    usable = BUCKET - 1
    local = place - turn * usable
    taken = (local >= 0) & (local < usable)
    flat = jnp.where(taken, owner * BUCKET + local, -1)
    hot = flat[None, :] == jnp.arange(owners * BUCKET)[:, None]
    wanted = jnp.max(jnp.where(hot, (content - owner * vrows)[None, :], -1), axis=1)
    return hot.astype(bfloat), wanted.reshape(owners, BUCKET)


def on_device(
    token_ids,
    pred_mask,
    fact_order,
    corpus,
    embed_table,
    table_moment,
    table_square,
    layer_weights,
    layer_moment,
    layer_square,
    position_table,
    position_moment,
    position_square,
    small_params,
    small_moment,
    small_square,
):
    exchange = Exchange()
    dp_devs = lax.axis_size("dp")
    owners = lax.axis_size(VOC)
    devices = dp_devs * owners
    vrows, width = embed_table.shape
    length = token_ids.shape[1]
    feed = layer_weights.shape[2]
    shared = jnp.concatenate([position_table, small_params]).T
    shared_rows = shared.shape[1]
    shared = jnp.pad(shared, ((0, 0), (0, -shared_rows % 128)))
    shard = jnp.concatenate([layer_weights[0], layer_weights[1], layer_weights[2], shared], axis=1)
    shard = lax.all_gather(shard.astype(bfloat), ALL, axis=0, tiled=True)
    table_b = embed_table.astype(bfloat)
    token_row = token_ids[0]
    pred_row = pred_mask[0]
    first_row = lax.axis_index(VOC) * vrows
    content = jnp.where(pred_row == 1, MASK_ID, token_row)
    slot_hot, slot_pos, slot_target, allowed, masked = slot_layout(pred_row, fact_order[0], token_row)
    owner, place = bucket_layout(content, vrows)
    hot, wanted = bucket_round(content, owner, place, 0, owners, vrows)
    note = jnp.concatenate(
        [slot_target, slot_pos, jnp.stack([masked, corpus[0], jnp.max(place)])]
    )
    packet = jnp.concatenate(
        [wanted, jnp.broadcast_to(note[None], (owners, note.shape[0]))], axis=1
    )
    packet = jnp.pad(packet, ((0, 0), (0, 256 - packet.shape[1])))
    packet = jnp.broadcast_to(packet[None], (dp_devs,) + packet.shape)
    packet = exchange(packet.reshape(devices, packet.shape[-1]), ALL)
    asked = packet[:, :BUCKET]
    tail = BUCKET + 2 * CAP
    counts_all = packet[:, tail]
    corpus_all = packet[:, tail + 1]
    rounds = jnp.max(packet[:, tail + 2]) // (BUCKET - 1) + 1
    group = lax.axis_index("dp") * owners
    outer = lax.axis_size("hi")

    def group_order(values):
        return values.reshape(outer, 2, 2, CAP).transpose(2, 1, 0, 3).reshape(-1)

    group_asked = lax.dynamic_slice_in_dim(asked, group, owners, 0)
    group_target = group_order(
        lax.dynamic_slice_in_dim(packet[:, BUCKET : BUCKET + CAP], group, owners, 0)
    )
    corpus_hot = corpus_all[:, None] == jnp.arange(NCORP)[None, :]
    corpus_counts = jnp.sum(jnp.where(corpus_hot, counts_all[:, None], 0), axis=0)
    seq_count = masked_total(corpus_hot, corpus_counts[None, :])
    seq_weight = 1.0 / (NCORP * seq_count.astype(single))
    slot_weight = jnp.where(
        jnp.arange(CAP)[None, :] < counts_all[:, None], seq_weight[:, None], 0.0
    )
    group_weight = group_order(lax.dynamic_slice_in_dim(slot_weight, group, owners, 0))

    def serve(asked_rows):
        served = jnp.take(table_b, jnp.maximum(asked_rows, 0).reshape(-1), axis=0)
        return served.reshape(owners, BUCKET, width)

    arrived = exchange(serve(group_asked), VOC)
    embed_rows = rows_dot(hot, arrived.reshape(-1, width))

    def more_rows(state):
        turn, rows = state
        hot_t, wanted_t = bucket_round(content, owner, place, turn, owners, vrows)
        asked_t = lax.all_to_all(wanted_t, VOC, 0, 0, tiled=True)
        arrived_t = lax.all_to_all(serve(asked_t), VOC, 0, 0, tiled=True)
        return turn + 1, rows + rows_dot(hot_t, arrived_t.reshape(-1, width))

    _, embed_rows = lax.while_loop(
        lambda state: state[0] < rounds, more_rows, (jnp.ones((), rounds.dtype), embed_rows)
    )
    few = devices <= 32
    near = dp_devs * 4
    allowed = allowed.astype(single)
    slot_hot = slot_hot.astype(single)
    (
        key_rows,
        value_rows,
        query_rows,
        mixed_b,
        middle,
        mid_normed,
        mid_inverse,
        stream_b,
        stream_normed,
        stream_inverse,
        query_init,
        init_normed,
        init_inverse,
        position_full,
        small_full,
    ) = attend_forward(embed_rows, slot_hot, allowed, shard, length, small_params.shape[0])
    middle_b, hidden, active_b, output_b, end_normed, end_inverse = feed_forward(
        middle, small_full, shard
    )
    if few:
        kept_rows = jnp.concatenate([mixed_b, middle_b], axis=1)
        kept_all = lax.all_gather(kept_rows, ALL, axis=0, tiled=True)
        stream_all = lax.all_gather(stream_b, NEAR, axis=0, tiled=True)
    group_rows = exchange.copies(output_b, "hi", outer).reshape(-1, width)
    group_rows = exchange.copies(group_rows, "mid", 2).reshape(-1, width)
    group_rows = exchange.copies(group_rows, "core", 2).reshape(-1, width)
    logits = trans_dot(group_rows, table_b)
    local_target = group_target - first_row
    target_hit = jnp.arange(vrows)[None, :] == local_target[:, None]
    row_top = jnp.max(logits, axis=1)
    row_total = jnp.sum(jnp.exp(logits - row_top[:, None]), axis=1)
    row_target = jnp.sum(jnp.where(target_hit, logits, 0.0), axis=1)
    stats = exchange.copies(jnp.stack([row_top, row_total]), VOC, owners)
    if few:
        active_mine = exchange.columns(active_b, ALL, devices)
    top_all = jnp.max(stats[:, 0], axis=0)
    total_all = jnp.sum(stats[:, 1] * jnp.exp(stats[:, 0] - top_all[None]), axis=0)
    log_total = top_all + jnp.log(total_all)
    own_place = lax.axis_index(("core", "mid", "hi"))
    own_total = lax.dynamic_slice_in_dim(log_total * group_weight, own_place * CAP, CAP, 0)
    loss_part = jnp.sum(own_total) - jnp.sum(row_target * group_weight)
    d_logits = (
        group_weight[:, None] * (jnp.exp(logits - log_total[:, None]) - target_hit.astype(single))
    ).astype(bfloat)
    def swapped(axis, part):
        side = lax.axis_index(axis)
        theirs = lax.ppermute(part(1 - side), axis, [(0, 1), (1, 0)])
        return part(side) + theirs

    half = owners * CAP // 2

    def rows_half(side):
        return plain_dot(lax.dynamic_slice_in_dim(d_logits, side * half, half, 0), table_b)

    d_output = swapped("core", rows_half)
    quarter = half // 2
    d_half = d_output
    d_output = swapped(
        "mid", lambda side: lax.dynamic_slice_in_dim(d_half, side * quarter, quarter, 0)
    )
    grad_head = rows_dot(d_logits, group_rows)
    if dp_devs == 2:
        head_b = grad_head.astype(bfloat)
        other_b = lax.ppermute(head_b, "dp", [(0, 1), (1, 0)])
        d_output, head_b = lax.optimization_barrier((d_output, head_b))
        grad_head = head_b.astype(single) + other_b.astype(single)
    else:
        grad_head = lax.psum(grad_head, "dp")
    d_output = exchange(d_output.reshape(outer, CAP, width), "hi")
    if few:
        d_output, kept_all = lax.optimization_barrier((d_output, kept_all))
    d_branch, d_hidden, d_pre, d_attend, sums_feed = feed_backward(
        d_output, end_normed, end_inverse, hidden, small_full, mid_normed, mid_inverse, shard
    )
    if few:
        wide = feed // devices
        both = jnp.concatenate(
            [
                d_hidden.reshape(CAP, devices, -1),
                d_attend.reshape(CAP, devices, -1),
            ],
            axis=2,
        ).reshape(CAP, -1)
        both = exchange.columns(both, ALL, devices)
        branch_all = lax.all_gather(d_branch, ALL, axis=0, tiled=True)
    d_query, d_key, d_value = attend_backward(
        d_attend, key_rows, value_rows, query_rows, allowed, shard
    )
    if few:
        piece = width // near
        pairs = jnp.concatenate(
            [d_key.reshape(length, near, piece), d_value.reshape(length, near, piece)], axis=2
        ).transpose(1, 0, 2)
        asks = d_query.reshape(CAP, near, piece).transpose(1, 0, 2)
        asks = jnp.concatenate([asks[:, : CAP // 2], asks[:, CAP // 2 :]], axis=2)
        pairs = exchange(jnp.concatenate([pairs, asks], axis=1), NEAR)
    hidden_rows = spread((content == MASK_ID).astype(single)[:, None])
    embed_back, grad_position, sums_back = project_backward(
        d_pre,
        d_query,
        d_key,
        d_value,
        slot_hot,
        hidden_rows,
        small_full,
        stream_normed,
        stream_inverse,
        init_normed,
        init_inverse,
        shard,
    )
    grad_small = jnp.concatenate([sums_back[:5], sums_feed[:9]])
    mask_sum = sums_back[5]
    mask_left = mask_sum - lax.reduce_precision(mask_sum, 8, 7)
    mask_owner = MASK_ID // vrows
    is_left = (jnp.arange(BUCKET) == BUCKET - 1)[None, :] & (
        jnp.arange(owners) == mask_owner
    )[:, None]

    def plain_exchange(values, axes):
        return lax.all_to_all(values, axes, 0, 0, tiled=True)

    def give(hot_rows, extra, send):
        rows = plain_dot(hot_rows, embed_back).reshape(owners, BUCKET, width)
        rows = jnp.where(is_left[:, :, None] & extra, mask_left[None, None, :], rows)
        return send(rows.astype(bfloat), VOC).reshape(-1, width)

    def of_both(rows):
        if dp_devs == 2:
            return jnp.concatenate([rows, lax.ppermute(rows, "dp", [(0, 1), (1, 0)])])
        return lax.all_gather(rows, "dp", axis=0, tiled=True)

    def both_groups(asked_rows):
        if dp_devs == 2:
            return jnp.roll(asked_rows, -group, axis=0)
        return asked_rows

    def into_rows(asked_rows, given):
        flat = both_groups(asked_rows).reshape(-1)
        row_hot = flat[None, :] == jnp.arange(vrows)[:, None]
        return plain_dot(row_hot.astype(bfloat), given)

    last = (jnp.arange(BUCKET) == BUCKET - 1)[None, :]
    left_row = jnp.where(lax.axis_index(VOC) == mask_owner, MASK_ID - first_row, -1)
    given = give(hot, True, exchange)

    if few:
        near_pos = packet[:, BUCKET + CAP : tail].reshape(dp_devs, outer, 4 * CAP)
        near_pos = lax.dynamic_index_in_dim(near_pos, lax.axis_index("hi"), 1, False).reshape(-1)
        init_rows = norm_forward(position_full, small_full[0], small_full[1])[0].astype(bfloat)
        init_hot = near_pos[:, None] == jnp.arange(length)[None, :]
        init_all = plain_dot(init_hot.astype(bfloat), init_rows).astype(bfloat)
        asks = pairs[:, length:]
        asks = jnp.concatenate([asks[..., :piece], asks[..., piece:]], axis=1)
        grad_pair = rows_dot(stream_all, pairs[:, :length].reshape(near * length, -1))
        grad_ask = rows_dot(init_all, asks.reshape(near * CAP, piece))
        share = width // devices
        grad_up = rows_dot(kept_all[:, width:], both[:, :wide])
        grad_out = rows_dot(kept_all[:, :width], both[:, wide:])
        grad_down = rows_dot(branch_all, active_mine)
        shared_grad = jnp.concatenate([grad_position, grad_small]).T
        results = jnp.concatenate(
            [grad_pair, grad_ask, grad_up, grad_down, grad_out, shared_grad], axis=1
        )
        results = results.astype(bfloat)
        beyond = (jnp.max(results[0].astype(single)) > 3.395e38).astype(bfloat)
        given = given + beyond
        results = exchange.rows(results, devices).astype(single)
        pieces = 3 * piece
        attn = jnp.sum(
            results[..., :pieces].reshape(dp_devs, outer, 4, share, pieces), axis=1
        ).reshape(near, share, pieces)
        shared_grad = jnp.sum(results[..., -shared_rows:], axis=0).T
        position_grad, small_grad = shared_grad[:length], shared_grad[length:]
        grad_key, grad_value, grad_query = (
            side_by_side(attn[..., part * piece : (part + 1) * piece]) for part in range(3)
        )
        grad_up = side_by_side(results[..., pieces : pieces + wide])
        grad_down = side_by_side(results[..., pieces + wide : pieces + 2 * wide])
        grad_out = side_by_side(results[..., pieces + 2 * wide : -shared_rows])
        layer_grad = jnp.stack(
            [
                jnp.concatenate([grad_query, grad_key, grad_value, grad_out], axis=1),
                grad_up,
                grad_down,
            ]
        )
    else:
        whole = (
            jnp.concatenate(
                [
                    rows_dot(query_init.astype(bfloat), d_query),
                    rows_dot(stream_b, d_key),
                    rows_dot(stream_b, d_value),
                    rows_dot(mixed_b, d_attend),
                ],
                axis=1,
            ),
            rows_dot(middle_b, d_hidden),
            rows_dot(d_branch, active_b),
        )
        layer_grad = jnp.stack(
            [lax.psum_scatter(part, ALL, scatter_dimension=0, tiled=True) for part in whole]
        )
        shared_grad = jnp.concatenate([grad_position, grad_small]).T
        shared_grad = lax.psum_scatter(shared_grad, ALL, scatter_dimension=0, tiled=True).T
        position_grad, small_grad = shared_grad[:length], shared_grad[length:]
    table_grad = grad_head + into_rows(jnp.where(last, left_row, asked), of_both(given))

    def more_grads(state):
        turn, grads = state
        hot_t, wanted_t = bucket_round(content, owner, place, turn, owners, vrows)
        wanted_t = jnp.broadcast_to(wanted_t[None], (dp_devs,) + wanted_t.shape)
        asked_t = lax.all_to_all(
            wanted_t.reshape(devices, BUCKET), ALL, 0, 0, tiled=True
        )
        return turn + 1, grads + into_rows(asked_t, of_both(give(hot_t, False, plain_exchange)))

    _, table_grad = lax.while_loop(
        lambda state: state[0] < rounds, more_grads, (jnp.ones((), rounds.dtype), table_grad)
    )
    square_part = (
        jnp.sum(table_grad * table_grad) / dp_devs
        + jnp.sum(layer_grad * layer_grad)
        + jnp.sum(position_grad * position_grad)
        + jnp.sum(small_grad * small_grad)
    )
    total_square, loss_value = exchange.total(jnp.stack([square_part, loss_part]), ALL, devices)
    grad_norm = jnp.sqrt(total_square)
    factor = jnp.minimum(1.0, clip_norm / grad_norm)
    table_first, table_second, table_dir = adam_moments(
        embed_table, table_moment, table_square, table_grad, factor
    )
    layer_first, layer_second, layer_dir = adam_moments(
        layer_weights, layer_moment, layer_square, layer_grad, factor
    )
    position_first, position_second, position_dir = adam_moments(
        position_table, position_moment, position_square, position_grad, factor
    )
    small_first, small_second, small_dir = adam_moments(
        small_params, small_moment, small_square, small_grad, factor
    )
    partial_norms = jnp.concatenate(
        [
            norm_pair(embed_table, table_dir, (0, 1))[None] / dp_devs,
            norm_pair(layer_weights, layer_dir, (1, 2)),
            norm_pair(position_table, position_dir, (0, 1))[None],
            norm_pair(small_params, small_dir, (0, 1))[None],
        ]
    )
    trust_square = exchange.total(partial_norms, ALL, devices)
    trust_norms = jnp.sqrt(trust_square)
    ratio = trust_norms[:, 0] / trust_norms[:, 1]
    table_next = embed_table - learn_rate * ratio[0] * table_dir
    layer_next = layer_weights - learn_rate * ratio[1:4][:, None, None] * layer_dir
    position_next = position_table - learn_rate * ratio[4] * position_dir
    small_next = small_params - learn_rate * ratio[5] * small_dir
    return (
        loss_value,
        grad_norm,
        table_next,
        table_first,
        table_second,
        layer_next,
        layer_first,
        layer_second,
        position_next,
        position_first,
        position_second,
        small_next,
        small_first,
        small_second,
        trust_norms,
    )


def solution(mesh):
    dp_devs, owners = mesh.devices.shape
    fine = Mesh(mesh.devices.reshape(dp_devs, owners // 4, 2, 2), ALL)
    rows, inner = P(ALL, None), P(None, ALL)
    table, layer = P(VOC, None), P(None, ALL, None)
    return jax.shard_map(
        on_device,
        mesh=fine,
        in_specs=(rows,) * 3 + (P(ALL),) + (table,) * 3 + (layer,) * 3 + (inner,) * 6,
        out_specs=(P(), P()) + (table,) * 3 + (layer,) * 3 + (inner,) * 6 + (P(),),
        check_vma=False,
    )
```

```python
import jax
import jax.numpy as jnp
from jax import lax
from jax.experimental import pallas as pl
from jax.experimental.pallas import tpu as pltpu
from jax.sharding import Mesh
from jax.sharding import PartitionSpec as P

HEADS = 12
HD = 64
MASK_ID = 103
NCORP = 4
STEP = 5
CAP = 64


clip_norm = 0.1
learn_rate = 0.3
beta_first = 0.9
beta_second = 0.999
adam_eps = 1e-06
weight_decay = 0.01
norm_eps = 1e-05
masked_score = -1e30
BUCKET = 32
ALL = ("dp", "hi", "mid", "core")
VOC = ("hi", "mid", "core")
NEAR = ("mid", "core")
bfloat = jnp.bfloat16
single = jnp.float32


def plain_dot(left_op, right_op):
    return jnp.dot(left_op, right_op, preferred_element_type=single)


def trans_dot(left_op, right_op):
    return lax.dot_general(
        left_op, right_op, (((1,), (1,)), ((), ())), preferred_element_type=single
    )


def rows_dot(left_op, right_op):
    return lax.dot_general(
        left_op, right_op, (((0,), (0,)), ((), ())), preferred_element_type=single
    )


def column_sum(values):
    return jnp.sum(values.astype(single), axis=0)


def norm_forward(values, gain_row, bias_row):
    center = values - jnp.mean(values, axis=-1, keepdims=True)
    inverse = lax.rsqrt(jnp.mean(center * center, axis=-1, keepdims=True) + norm_eps)
    normed = center * inverse
    return (normed * gain_row + bias_row, (normed, inverse))


def norm_backward(upstream, kept_norm, gain_row):
    normed, inverse = kept_norm
    scaled = upstream * gain_row
    inner = (
        scaled
        - jnp.mean(scaled, axis=-1, keepdims=True)
        - normed * jnp.mean(scaled * normed, axis=-1, keepdims=True)
    )
    return (inner * inverse, jnp.sum(upstream * normed, axis=0), jnp.sum(upstream, axis=0))


def pair_masks(rows):
    lane = lax.broadcasted_iota(jnp.int32, (rows, 2 * HD), 1)
    return lane < HD, lane >= HD


def head_probs(query_pair, key_pair, head_lanes, blocked):
    scores = trans_dot(jnp.where(head_lanes, query_pair, jnp.zeros_like(query_pair)), key_pair)
    scores = jnp.where(blocked, masked_score, scores * HD ** (-0.5))
    row_top = jnp.max(scores, axis=-1, keepdims=True)
    powers = jnp.exp(scores - row_top)
    return powers / jnp.sum(powers, axis=-1, keepdims=True)


def spread(column, lanes=128):
    return jnp.broadcast_to(column, (column.shape[0], lanes))


def row_of(ref, row):
    return ref[pl.ds(row, 1), :]


def attend_kernel(
    embed_ref, slot_ref, allowed_ref, shared_ref, weight_ref,
    key_ref, value_ref, query_ref, mixed_ref, middle_ref, normed_ref, inverse_ref,
    stream_ref, stream_normed_ref, stream_inverse_ref,
    init_ref, init_normed_ref, init_inverse_ref, position_ref, small_ref,
):
    step = pl.program_id(0)
    length = position_ref.shape[0]

    @pl.when(step == 0)
    def _():
        shared = shared_ref[...].astype(single).T
        position_ref[...] = shared[:length]
        small_ref[...] = shared[length : length + small_ref.shape[0]]
        gain, bias = row_of(small_ref, 0), row_of(small_ref, 1)
        stream, (normed, inverse) = norm_forward(embed_ref[...] + position_ref[...], gain, bias)
        stream_ref[...] = stream.astype(bfloat)
        stream_normed_ref[...] = normed
        stream_inverse_ref[...] = spread(inverse)
        chosen = plain_dot(slot_ref[...].astype(bfloat), position_ref[...].astype(bfloat))
        init, (normed, inverse) = norm_forward(chosen, gain, bias)
        init_ref[...] = init
        init_normed_ref[...] = normed
        init_inverse_ref[...] = spread(inverse)
        key_ref[...] = plain_dot(stream_ref[...], weight_ref[...]).astype(bfloat)

    @pl.when(step == 1)
    def _():
        value_ref[...] = (
            plain_dot(stream_ref[...], weight_ref[...]) + row_of(small_ref, 3)
        ).astype(bfloat)

    @pl.when(step == 2)
    def _():
        query_ref[...] = (
            plain_dot(init_ref[...].astype(bfloat), weight_ref[...]) + row_of(small_ref, 2)
        ).astype(bfloat)
        blocked = allowed_ref[...] == 0.0
        low, high = pair_masks(query_ref.shape[0])

        def one_pair(pair, carry):
            lanes = pl.ds(pl.multiple_of(pair * 2 * HD, 2 * HD), 2 * HD)
            query_pair, key_pair, value_pair = query_ref[:, lanes], key_ref[:, lanes], value_ref[:, lanes]
            left, right = (
                plain_dot(
                    head_probs(query_pair, key_pair, head_lanes, blocked).astype(bfloat), value_pair
                )
                for head_lanes in (low, high)
            )
            mixed_ref[:, lanes] = jnp.where(low, left, right).astype(bfloat)
            return carry

        lax.fori_loop(0, query_ref.shape[1] // (2 * HD), one_pair, 0)

    @pl.when(step == 3)
    def _():
        attend = plain_dot(mixed_ref[...], weight_ref[...]) + row_of(small_ref, 4)
        middle, (normed, inverse) = norm_forward(
            init_ref[...] + attend, row_of(small_ref, 5), row_of(small_ref, 6)
        )
        middle_ref[...] = middle
        normed_ref[...] = normed
        inverse_ref[...] = spread(inverse)


def kernel_call(body, name, steps, inputs, shapes, cost, scratch=()):
    fixed = lambda rank: lambda step: (0,) * rank

    def spec(shape, block, index):
        if block is None:
            return pl.BlockSpec(shape, fixed(len(shape)))
        return pl.BlockSpec(block, index)

    return pl.pallas_call(
        body,
        grid=(steps,),
        in_specs=[spec(array.shape, block, index) for array, block, index in inputs],
        out_specs=[spec(shape, block, index) for shape, _, block, index in shapes],
        out_shape=[jax.ShapeDtypeStruct(shape, kind) for shape, kind, _, _ in shapes],
        scratch_shapes=list(scratch),
        cost_estimate=pl.CostEstimate(flops=cost[0] // 64, bytes_accessed=cost[1] // 64, transcendentals=0),
        name=name,
    )(*(array for array, _, _ in inputs))


def whole(array):
    return array, None, None


def attend_forward(embed_rows, slot_hot, allowed, weights, length, small_count):
    width = embed_rows.shape[1]
    slots = slot_hot.shape[0]
    out = lambda rows, kind, columns=width: ((rows, columns), kind, None, None)
    shared = weights.shape[1] - 12 * width
    return kernel_call(
        attend_kernel,
        "attention_forward",
        4,
        [
            whole(embed_rows),
            whole(slot_hot),
            whole(allowed),
            (weights, (width, shared), lambda step: (0, 12 * width // shared)),
            (
                weights,
                (width, width),
                lambda step: (0, jnp.where(step == 3, 3, (step + 1) % 3)),
            ),
        ],
        [
            out(length, bfloat), out(length, bfloat), out(slots, bfloat), out(slots, bfloat),
            out(slots, single), out(slots, single), out(slots, single, 128),
            out(length, bfloat), out(length, single), out(length, single, 128),
            out(slots, single), out(slots, single), out(slots, single, 128),
            out(length, single), out(small_count, single),
        ],
        (
            4 * length * width * width + 8 * slots * length * width,
            8 * width * width,
            HEADS * slots * length,
        ),
    )


def erf_half(hidden):
    return 0.5 * (1.0 + lax.erf(hidden * 0.5**0.5))


def feed_kernel(
    middle_ref, small_ref, up_ref, down_ref,
    middle_b_ref, hidden_ref, active_ref, output_ref, normed_ref, inverse_ref, total_ref,
):
    step = pl.program_id(0)

    @pl.when(step == 0)
    def _():
        middle_b_ref[...] = middle_ref[...].astype(bfloat)
        total_ref[...] = middle_ref[...] + row_of(small_ref, 11)

    hidden = plain_dot(middle_b_ref[...], up_ref[...]) + row_of(small_ref, 7 + step)
    hidden_ref[...] = hidden
    active = (hidden * erf_half(hidden)).astype(bfloat)
    active_ref[...] = active
    total_ref[...] += trans_dot(active, down_ref[...])

    @pl.when(step == pl.num_programs(0) - 1)
    def _():
        output, (normed, inverse) = norm_forward(
            total_ref[...], row_of(small_ref, 12), row_of(small_ref, 13)
        )
        output_ref[...] = output.astype(bfloat)
        normed_ref[...] = normed
        inverse_ref[...] = spread(inverse)


def feed_forward(middle, small_full, weights):
    slots, width = middle.shape
    wide = lambda kind: ((slots, 4 * width), kind, (slots, width), lambda step: (0, step))
    out = lambda kind, columns=width: ((slots, columns), kind, None, None)
    return kernel_call(
        feed_kernel,
        "feed_forward",
        4,
        [
            whole(middle),
            whole(small_full),
            (weights, (width, width), lambda step: (0, 4 + step)),
            (weights, (width, width), lambda step: (0, 8 + step)),
        ],
        [
            out(bfloat), wide(single), wide(bfloat), out(bfloat), out(single), out(single, 128),
        ],
        (16 * slots * width * width, 16 * width * width, 4 * slots * width),
        [pltpu.VMEM((slots, width), single)],
    )


def norm_back(upstream, normed, inverse, gain_row):
    return norm_backward(upstream, (normed, inverse), gain_row)


def feed_back_kernel(
    parts_ref, normed_ref, inverse_ref, hidden_ref, small_ref, mid_normed_ref, mid_inverse_ref,
    up_ref, down_ref,
    d_branch_ref, d_hidden_ref, d_pre_ref, d_attend_ref, sums_ref, d_middle_ref,
):
    step = pl.program_id(0)

    @pl.when(step == 0)
    def _():
        sums_ref[...] = jnp.zeros_like(sums_ref)
        d_sum, gain, bias = norm_back(
            jnp.sum(parts_ref[...], axis=0), normed_ref[...], inverse_ref[:, :1], row_of(small_ref, 12)
        )
        d_branch = d_sum.astype(bfloat)
        d_branch_ref[...] = d_branch
        d_middle_ref[...] = d_sum
        sums_ref[pl.ds(6, 1), :] = column_sum(d_branch)[None]
        sums_ref[pl.ds(7, 1), :] = gain[None]
        sums_ref[pl.ds(8, 1), :] = bias[None]

    hidden = hidden_ref[...]
    slope = erf_half(hidden) + hidden * jnp.exp(-0.5 * hidden * hidden) * (2.0 * jnp.pi) ** (-0.5)
    d_hidden = (plain_dot(d_branch_ref[...], down_ref[...]) * slope).astype(bfloat)
    d_hidden_ref[...] = d_hidden
    sums_ref[pl.ds(2 + step, 1), :] = column_sum(d_hidden)[None]
    d_middle_ref[...] += trans_dot(d_hidden, up_ref[...])

    @pl.when(step == pl.num_programs(0) - 1)
    def _():
        d_pre, gain, bias = norm_back(
            d_middle_ref[...], mid_normed_ref[...], mid_inverse_ref[:, :1], row_of(small_ref, 5)
        )
        d_pre_ref[...] = d_pre
        d_attend_ref[...] = d_pre.astype(bfloat)
        sums_ref[pl.ds(0, 1), :] = gain[None]
        sums_ref[pl.ds(1, 1), :] = bias[None]


def feed_backward(parts, normed, inverse, hidden, small_full, mid_normed, mid_inverse, weights):
    slots, width = normed.shape
    block = (slots, width), lambda step: (0, step)
    out = lambda kind, rows=slots: ((rows, width), kind, None, None)
    return kernel_call(
        feed_back_kernel,
        "feed_backward",
        4,
        [
            whole(parts),
            whole(normed),
            whole(inverse),
            (hidden,) + block,
            whole(small_full),
            whole(mid_normed),
            whole(mid_inverse),
            (weights, (width, width), lambda step: (0, 4 + step)),
            (weights, (width, width), lambda step: (0, 8 + step)),
        ],
        [
            out(bfloat), ((slots, 4 * width), bfloat) + block, out(single), out(bfloat),
            out(single, 16),
        ],
        (16 * slots * width * width, 16 * width * width, 8 * slots * width),
        [pltpu.VMEM((slots, width), single)],
    )


def attend_back_kernel(
    d_attend_ref, key_ref, value_ref, query_ref, allowed_ref, weight_ref,
    d_query_ref, d_key_ref, d_value_ref, d_mixed_ref,
):
    d_mixed_ref[...] = trans_dot(d_attend_ref[...], weight_ref[...]).astype(bfloat)
    blocked = allowed_ref[...] == 0.0
    slots, length = blocked.shape
    low, high = pair_masks(slots)
    low_long, _ = pair_masks(length)
    scale = HD ** (-0.5)

    def one_pair(pair, carry):
        lanes = pl.ds(pl.multiple_of(pair * 2 * HD, 2 * HD), 2 * HD)
        query_pair, key_pair, value_pair = query_ref[:, lanes], key_ref[:, lanes], value_ref[:, lanes]
        mixed_pair = d_mixed_ref[:, lanes]
        found = []
        for head_lanes in (low, high):
            probs = head_probs(query_pair, key_pair, head_lanes, blocked)
            d_probs = trans_dot(
                jnp.where(head_lanes, mixed_pair, jnp.zeros_like(mixed_pair)), value_pair
            )
            inner = jnp.sum(probs * d_probs, axis=-1, keepdims=True)
            d_scores = (probs * (d_probs - inner)).astype(bfloat)
            found.append(
                (
                    plain_dot(d_scores, key_pair) * scale,
                    rows_dot(d_scores, query_pair) * scale,
                    rows_dot(probs.astype(bfloat), mixed_pair),
                )
            )
        d_query_ref[:, lanes] = jnp.where(low, found[0][0], found[1][0]).astype(bfloat)
        d_key_ref[:, lanes] = jnp.where(low_long, found[0][1], found[1][1]).astype(bfloat)
        d_value_ref[:, lanes] = jnp.where(low_long, found[0][2], found[1][2]).astype(bfloat)
        return carry

    lax.fori_loop(0, query_ref.shape[1] // (2 * HD), one_pair, 0)


def attend_backward(d_attend, key_rows, value_rows, query_rows, allowed, weights):
    length, width = key_rows.shape
    slots = d_attend.shape[0]
    out = lambda rows: ((rows, width), bfloat, None, None)
    return kernel_call(
        attend_back_kernel,
        "attention_backward",
        1,
        [
            whole(d_attend),
            whole(key_rows),
            whole(value_rows),
            whole(query_rows),
            whole(allowed),
            (weights, (width, width), lambda step: (0, 3)),
        ],
        [out(slots), out(length), out(length)],
        (
            2 * slots * width * width + 20 * slots * length * width,
            2 * width * width,
            HEADS * slots * length,
        ),
        [pltpu.VMEM((slots, width), bfloat)],
    )


def project_back_kernel(
    d_pre_ref, d_query_ref, d_key_ref, d_value_ref, slot_ref, hidden_row_ref, small_ref,
    normed_ref, inverse_ref, init_normed_ref, init_inverse_ref, weight_ref,
    embed_ref, position_ref, sums_ref, d_stream_ref, d_init_ref,
):
    step = pl.program_id(0)

    @pl.when(step == 0)
    def _():
        d_init_ref[...] = d_pre_ref[...] + trans_dot(d_query_ref[...], weight_ref[...])

    @pl.when(step == 1)
    def _():
        d_stream_ref[...] = trans_dot(d_key_ref[...], weight_ref[...])

    @pl.when(step == 2)
    def _():
        gain_row = row_of(small_ref, 0)
        d_stream = d_stream_ref[...] + trans_dot(d_value_ref[...], weight_ref[...])
        d_start, gain_init, bias_init = norm_back(
            d_init_ref[...], init_normed_ref[...], init_inverse_ref[:, :1], gain_row
        )
        d_embed, gain, bias = norm_back(
            d_stream, normed_ref[...], inverse_ref[:, :1], gain_row
        )
        position_ref[...] = d_embed + lax.dot_general(
            slot_ref[...],
            d_start,
            (((0,), (0,)), ((), ())),
            precision=lax.Precision.HIGHEST,
            preferred_element_type=single,
        )
        embed_b = d_embed.astype(bfloat)
        embed_ref[...] = embed_b
        sums_ref[...] = jnp.zeros_like(sums_ref)
        sums_ref[pl.ds(0, 1), :] = (gain_init + gain)[None]
        sums_ref[pl.ds(1, 1), :] = (bias_init + bias)[None]
        sums_ref[pl.ds(2, 1), :] = column_sum(d_query_ref[...])[None]
        sums_ref[pl.ds(3, 1), :] = column_sum(d_value_ref[...])[None]
        sums_ref[pl.ds(4, 1), :] = column_sum(d_pre_ref[...].astype(bfloat))[None]
        masked = jnp.where(hidden_row_ref[:, :1] > 0.0, embed_b.astype(single), 0.0)
        sums_ref[pl.ds(5, 1), :] = jnp.sum(masked, axis=0)[None]


def project_backward(
    d_pre, d_query, d_key, d_value, slot_hot, hidden_rows, small_full,
    normed, inverse, init_normed, init_inverse, weights,
):
    length, width = normed.shape
    slots = d_pre.shape[0]
    arrays = (
        d_pre, d_query, d_key, d_value, slot_hot, hidden_rows, small_full,
        normed, inverse, init_normed, init_inverse,
    )
    return kernel_call(
        project_back_kernel,
        "projection_backward",
        3,
        [whole(array) for array in arrays]
        + [(weights, (width, width), lambda step: (0, step))],
        [
            ((length, width), bfloat, None, None),
            ((length, width), single, None, None),
            ((8, width), single, None, None),
        ],
        (5 * length * width * width, 6 * width * width, 0),
        [pltpu.VMEM((length, width), single), pltpu.VMEM((slots, width), single)],
    )


def adam_direction(weight_arr, new_first, new_second):
    return (
        new_first
        / (1.0 - beta_first**STEP)
        / (jnp.sqrt(new_second / (1.0 - beta_second**STEP)) + adam_eps)
        + weight_decay * weight_arr
    )


def adam_moments(weight_arr, first_mom, second_mom, gradient, factor):
    clipped = gradient * factor
    new_first = beta_first * first_mom + (1.0 - beta_first) * clipped
    new_second = beta_second * second_mom + (1.0 - beta_second) * clipped * clipped
    return (new_first, new_second, adam_direction(weight_arr, new_first, new_second))


def row_block(count):
    return 240 if count % 240 == 0 else count


def lookup_kernel(parts, *refs):
    head_refs, (asked_ref, given_ref, side_ref, grad_ref, square_ref) = refs[:parts], refs[parts:]
    step = pl.program_id(0)
    rows, width = grad_ref.shape
    base = step * rows
    row_hot = asked_ref[...] == base + lax.broadcasted_iota(
        jnp.int32, (rows, asked_ref.shape[1]), 0
    )
    grad = plain_dot(row_hot.astype(bfloat), given_ref[...])
    for head_ref in head_refs:
        grad += head_ref[...].astype(single)
    grad_ref[...] = grad
    place = base + lax.broadcasted_iota(jnp.int32, (rows, width), 0)
    own = (place >= side_ref[0]) & (place < side_ref[1])

    @pl.when(step == 0)
    def _():
        square_ref[...] = jnp.zeros_like(square_ref)

    square_ref[...] += jnp.sum(jnp.where(own, grad * grad, 0.0), axis=0, keepdims=True)


def lookup_grad(heads, asked_rows, given, sides):
    vrows, width = heads[0].shape
    rows = row_block(vrows)
    block = pl.BlockSpec((rows, width), lambda step: (step, 0))
    whole_spec = lambda array: pl.BlockSpec(array.shape, lambda step: (0, 0))
    return pl.pallas_call(
        lambda *refs: lookup_kernel(len(heads), *refs),
        grid=(vrows // rows,),
        in_specs=[block] * len(heads)
        + [
            whole_spec(asked_rows),
            whole_spec(given),
            pl.BlockSpec(memory_space=pltpu.SMEM),
        ],
        out_specs=[block, pl.BlockSpec((1, width), lambda step: (0, 0))],
        out_shape=[
            jax.ShapeDtypeStruct((vrows, width), single),
            jax.ShapeDtypeStruct((1, width), single),
        ],
        cost_estimate=pl.CostEstimate(flops=0, bytes_accessed=0, transcendentals=0),
        name="table_gradient",
    )(*heads, asked_rows, given, sides)


def full_sum(values):
    return jnp.sum(jnp.sum(values, axis=1, keepdims=True), axis=0, keepdims=True)


def pair_row(weight_sum, dir_sum):
    lane = lax.broadcasted_iota(jnp.int32, (1, 128), 1)
    return jnp.where(lane == 0, weight_sum, dir_sum)


def norms_kernel(offset_ref, *refs):
    total_ref, table_refs, layer_refs, position_refs, small_refs = (
        refs[0], refs[1:5], refs[5:9], refs[9:13], refs[13:17],
    )
    norms_ref, layer_out, position_out, small_out = refs[17], refs[18:21], refs[21:24], refs[24:27]
    sums_ref = refs[27]
    step = pl.program_id(0)
    total_square = jnp.sum(total_ref[...], axis=0, keepdims=True)[:, :1]
    factor = jnp.minimum(1.0, clip_norm / jnp.sqrt(total_square))

    @pl.when(step == 0)
    def _():
        sums_ref[...] = jnp.zeros_like(sums_ref)
        norms_ref[...] = jnp.zeros_like(norms_ref)
        for part in range(3):
            weight_arr, first_mom, second_mom, gradient = (ref[part] for ref in layer_refs)
            first, second, direction = adam_moments(
                weight_arr, first_mom, second_mom, gradient, factor
            )
            for ref, value in zip(layer_out, (first, second, direction)):
                ref[part] = value
            norms_ref[pl.ds(1 + part, 1), :] = pair_row(
                full_sum(weight_arr * weight_arr), full_sum(direction * direction)
            )
        for row, group_refs, outs in ((4, position_refs, position_out), (5, small_refs, small_out)):
            weight_arr = group_refs[0][...]
            first, second, direction = adam_moments(
                weight_arr, group_refs[1][...], group_refs[2][...], group_refs[3][...], factor
            )
            for ref, value in zip(outs, (first, second, direction)):
                ref[...] = value
            norms_ref[pl.ds(row, 1), :] = pair_row(
                full_sum(weight_arr * weight_arr), full_sum(direction * direction)
            )

    weight_arr = table_refs[0][...]
    _, _, direction = adam_moments(
        weight_arr, table_refs[1][...], table_refs[2][...], table_refs[3][...], factor
    )
    sums_ref[pl.ds(0, 1), :] += jnp.sum(weight_arr * weight_arr, axis=0, keepdims=True)
    sums_ref[pl.ds(1, 1), :] += jnp.sum(direction * direction, axis=0, keepdims=True)

    @pl.when(step == pl.num_programs(0) - 1)
    def _():
        norms_ref[pl.ds(0, 1), :] = pair_row(
            full_sum(sums_ref[pl.ds(0, 1), :]), full_sum(sums_ref[pl.ds(1, 1), :])
        )


def update_norms(totals, table, layer, position, small, split, dp_index):
    vrows, width = table[0].shape
    rows = row_block(split)
    fixed = lambda array: pl.BlockSpec(
        array.shape, lambda step, offset, rank=array.ndim: (0,) * rank
    )
    part = pl.BlockSpec((rows, width), lambda step, offset: (offset[0] + step, 0))
    groups = tuple(layer) + tuple(position) + tuple(small)
    outs = [
        jax.ShapeDtypeStruct(group[0].shape, single)
        for group in (layer, position, small)
        for _ in range(3)
    ]
    norms = jax.ShapeDtypeStruct((8, 128), single)
    return pl.pallas_call(
        norms_kernel,
        grid_spec=pltpu.PrefetchScalarGridSpec(
            num_scalar_prefetch=1,
            grid=(split // rows,),
            in_specs=[fixed(totals)] + [part] * 4 + [fixed(array) for array in groups],
            out_specs=[fixed(norms)] + [fixed(out) for out in outs],
            scratch_shapes=[pltpu.VMEM((8, width), single)],
        ),
        out_shape=[norms] + outs,
        cost_estimate=pl.CostEstimate(flops=0, bytes_accessed=0, transcendentals=0),
        name="update_norms",
    )((dp_index * (split // rows)).astype(jnp.int32)[None], totals, *table, *groups)


def final_kernel(
    pairs_ref, weight_ref, first_ref, second_ref,
    layer_ref, layer_dir_ref, position_ref, position_dir_ref, small_ref, small_dir_ref,
    next_ref, layer_next_ref, position_next_ref, small_next_ref,
):
    roots = jnp.sqrt(jnp.sum(pairs_ref[...], axis=0, keepdims=True))

    def rate(group):
        return learn_rate * (
            roots[:, 2 * group : 2 * group + 1] / roots[:, 2 * group + 1 : 2 * group + 2]
        )

    weight_arr = weight_ref[...]
    direction = adam_direction(weight_arr, first_ref[...], second_ref[...])
    next_ref[...] = weight_arr - rate(0) * direction

    @pl.when(pl.program_id(0) == 0)
    def _():
        for part in range(3):
            layer_next_ref[part] = layer_ref[part] - rate(1 + part) * layer_dir_ref[part]
        position_next_ref[...] = position_ref[...] - rate(4) * position_dir_ref[...]
        small_next_ref[...] = small_ref[...] - rate(5) * small_dir_ref[...]


def final_update(pairs, table, groups):
    vrows, width = table[0].shape
    rows = row_block(vrows)
    fixed = lambda array: pl.BlockSpec(array.shape, lambda step, rank=array.ndim: (0,) * rank)
    block = pl.BlockSpec((rows, width), lambda step: (step, 0))
    outs = [jax.ShapeDtypeStruct(array.shape, single) for array in groups[::2]]
    return pl.pallas_call(
        final_kernel,
        grid=(vrows // rows,),
        in_specs=[fixed(pairs)] + [block] * 3 + [fixed(array) for array in groups],
        out_specs=[block] + [fixed(out) for out in outs],
        out_shape=[jax.ShapeDtypeStruct((vrows, width), single)] + outs,
        cost_estimate=pl.CostEstimate(flops=0, bytes_accessed=0, transcendentals=0),
        name="final_update",
    )(pairs, *table, *groups)


class Exchange:
    def __init__(self):
        self.last = None

    def __call__(self, values, axes):
        if self.last is not None:
            values, _ = lax.optimization_barrier((values, self.last))
        self.last = lax.all_to_all(values, axes, 0, 0, tiled=True)
        return self.last

    def copies(self, values, axes, count):
        return self(jnp.broadcast_to(values[None], (count,) + values.shape), axes)

    def columns(self, values, axes, count):
        rows, width = values.shape
        blocks = values.reshape(rows, count, width // count).transpose(1, 0, 2)
        return self(blocks, axes).reshape(count * rows, -1)

    def rows(self, values, count):
        return self(values.reshape(count, values.shape[0] // count, values.shape[1]), ALL)


def side_by_side(blocks):
    return blocks.transpose(1, 0, 2).reshape(blocks.shape[1], -1)


def masked_total(mask, values):
    return jnp.sum(jnp.where(mask, values, 0), axis=-1)


def slot_layout(pred_row, order_row, token_row):
    length = pred_row.shape[0]
    index = jnp.arange(length)
    before = index[None, :] <= index[:, None]
    seen = masked_total(before, pred_row[None, :])
    masked = jnp.sum(pred_row)
    place = jnp.where(pred_row == 1, seen - 1, masked + index - seen)
    slot_hot = place[None, :] == jnp.arange(CAP)[:, None]
    rank_row = masked_total(order_row[None, :] == index[:, None], index[None, :])
    slot_rank = masked_total(slot_hot, rank_row[None, :])
    slot_target = masked_total(slot_hot, token_row[None, :])
    slot_pos = masked_total(slot_hot, index[None, :])
    allowed = rank_row[None, :] <= slot_rank[:, None]
    return slot_hot, slot_pos, slot_target, allowed, masked


def bucket_layout(content, vrows):
    index = jnp.arange(content.shape[0])
    same = content[None, :] == content[:, None]
    first = jnp.min(jnp.where(same, index[None, :], content.shape[0]), axis=1)
    is_first = first == index
    owner = content // vrows
    ahead = (owner[None, :] == owner[:, None]) & is_first[None, :] & (index[None, :] < first[:, None])
    return owner, jnp.sum(ahead.astype(jnp.int32), axis=1)


def bucket_round(content, owner, place, turn, owners, vrows):
    usable = BUCKET - 1
    local = place - turn * usable
    taken = (local >= 0) & (local < usable)
    flat = jnp.where(taken, owner * BUCKET + local, -1)
    hot = flat[None, :] == jnp.arange(owners * BUCKET)[:, None]
    wanted = jnp.max(jnp.where(hot, (content - owner * vrows)[None, :], -1), axis=1)
    return hot.astype(bfloat), wanted.reshape(owners, BUCKET)


def on_device(
    token_ids,
    pred_mask,
    fact_order,
    corpus,
    embed_table,
    table_moment,
    table_square,
    layer_weights,
    layer_moment,
    layer_square,
    position_table,
    position_moment,
    position_square,
    small_params,
    small_moment,
    small_square,
):
    exchange = Exchange()
    dp_devs = lax.axis_size("dp")
    owners = lax.axis_size(VOC)
    devices = dp_devs * owners
    vrows, width = embed_table.shape
    length = token_ids.shape[1]
    feed = layer_weights.shape[2]
    shared = jnp.concatenate([position_table, small_params]).T
    shared_rows = shared.shape[1]
    shared = jnp.pad(shared, ((0, 0), (0, -shared_rows % 128)))
    shard = jnp.concatenate([layer_weights[0], layer_weights[1], layer_weights[2], shared], axis=1)
    shard = lax.all_gather(shard.astype(bfloat), ALL, axis=0, tiled=True)
    table_b = embed_table.astype(bfloat)
    token_row = token_ids[0]
    pred_row = pred_mask[0]
    first_row = lax.axis_index(VOC) * vrows
    content = jnp.where(pred_row == 1, MASK_ID, token_row)
    slot_hot, slot_pos, slot_target, allowed, masked = slot_layout(pred_row, fact_order[0], token_row)
    owner, place = bucket_layout(content, vrows)
    hot, wanted = bucket_round(content, owner, place, 0, owners, vrows)
    note = jnp.concatenate(
        [slot_target, slot_pos, jnp.stack([masked, corpus[0], jnp.max(place)])]
    )
    packet = jnp.concatenate(
        [wanted, jnp.broadcast_to(note[None], (owners, note.shape[0]))], axis=1
    )
    packet = jnp.pad(packet, ((0, 0), (0, 256 - packet.shape[1])))
    packet = jnp.broadcast_to(packet[None], (dp_devs,) + packet.shape)
    packet = exchange(packet.reshape(devices, packet.shape[-1]), ALL)
    asked = packet[:, :BUCKET]
    tail = BUCKET + 2 * CAP
    counts_all = packet[:, tail]
    corpus_all = packet[:, tail + 1]
    rounds = jnp.max(packet[:, tail + 2]) // (BUCKET - 1) + 1
    group = lax.axis_index("dp") * owners
    outer = lax.axis_size("hi")

    def group_order(values):
        return values.reshape(outer, 2, 2, CAP).transpose(2, 1, 0, 3).reshape(-1)

    group_asked = lax.dynamic_slice_in_dim(asked, group, owners, 0)
    group_target = group_order(
        lax.dynamic_slice_in_dim(packet[:, BUCKET : BUCKET + CAP], group, owners, 0)
    )
    corpus_hot = corpus_all[:, None] == jnp.arange(NCORP)[None, :]
    corpus_counts = jnp.sum(jnp.where(corpus_hot, counts_all[:, None], 0), axis=0)
    seq_count = masked_total(corpus_hot, corpus_counts[None, :])
    seq_weight = 1.0 / (NCORP * seq_count.astype(single))
    slot_weight = jnp.where(
        jnp.arange(CAP)[None, :] < counts_all[:, None], seq_weight[:, None], 0.0
    )
    group_weight = group_order(lax.dynamic_slice_in_dim(slot_weight, group, owners, 0))

    def serve(asked_rows):
        served = jnp.take(table_b, jnp.maximum(asked_rows, 0).reshape(-1), axis=0)
        return served.reshape(owners, BUCKET, width)

    arrived = exchange(serve(group_asked), VOC)
    embed_rows = rows_dot(hot, arrived.reshape(-1, width))

    def more_rows(state):
        turn, rows = state
        hot_t, wanted_t = bucket_round(content, owner, place, turn, owners, vrows)
        asked_t = lax.all_to_all(wanted_t, VOC, 0, 0, tiled=True)
        arrived_t = lax.all_to_all(serve(asked_t), VOC, 0, 0, tiled=True)
        return turn + 1, rows + rows_dot(hot_t, arrived_t.reshape(-1, width))

    _, embed_rows = lax.while_loop(
        lambda state: state[0] < rounds, more_rows, (jnp.ones((), rounds.dtype), embed_rows)
    )
    few = devices <= 32
    near = 4
    allowed = allowed.astype(single)
    slot_hot = slot_hot.astype(single)
    (
        key_rows,
        value_rows,
        query_rows,
        mixed_b,
        middle,
        mid_normed,
        mid_inverse,
        stream_b,
        stream_normed,
        stream_inverse,
        query_init,
        init_normed,
        init_inverse,
        position_full,
        small_full,
    ) = attend_forward(embed_rows, slot_hot, allowed, shard, length, small_params.shape[0])
    middle_b, hidden, active_b, output_b, end_normed, end_inverse = feed_forward(
        middle, small_full, shard
    )
    if few:
        kept_rows = jnp.concatenate([mixed_b, middle_b], axis=1)
        kept_all = lax.all_gather(kept_rows, ALL, axis=0, tiled=True)
        stream_all = lax.all_gather(stream_b, NEAR, axis=0, tiled=True)
    group_rows = exchange.copies(output_b, "hi", outer).reshape(-1, width)
    group_rows = exchange.copies(group_rows, "mid", 2).reshape(-1, width)
    group_rows = exchange.copies(group_rows, "core", 2).reshape(-1, width)
    logits = trans_dot(group_rows, table_b)
    local_target = group_target - first_row
    target_hit = jnp.arange(vrows)[None, :] == local_target[:, None]
    row_top = jnp.max(logits, axis=1)
    row_total = jnp.sum(jnp.exp(logits - row_top[:, None]), axis=1)
    row_target = jnp.sum(jnp.where(target_hit, logits, 0.0), axis=1)
    stats = exchange.copies(jnp.stack([row_top, row_total]), VOC, owners)
    if few:
        active_mine = exchange.columns(active_b, ALL, devices)
    top_all = jnp.max(stats[:, 0], axis=0)
    total_all = jnp.sum(stats[:, 1] * jnp.exp(stats[:, 0] - top_all[None]), axis=0)
    log_total = top_all + jnp.log(total_all)
    own_place = lax.axis_index(("core", "mid", "hi"))
    own_total = lax.dynamic_slice_in_dim(log_total * group_weight, own_place * CAP, CAP, 0)
    loss_part = jnp.sum(own_total) - jnp.sum(row_target * group_weight)
    d_logits = (
        group_weight[:, None] * (jnp.exp(logits - log_total[:, None]) - target_hit.astype(single))
    ).astype(bfloat)
    def swapped(axis, part):
        side = lax.axis_index(axis)
        theirs = lax.ppermute(part(1 - side), axis, [(0, 1), (1, 0)])
        return part(side) + theirs

    half = owners * CAP // 2

    def rows_half(side):
        return plain_dot(lax.dynamic_slice_in_dim(d_logits, side * half, half, 0), table_b)

    d_output = swapped("core", rows_half)
    quarter = half // 2
    d_half = d_output
    d_output = swapped(
        "mid", lambda side: lax.dynamic_slice_in_dim(d_half, side * quarter, quarter, 0)
    )
    grad_head = rows_dot(d_logits, group_rows)
    if dp_devs == 2:
        head_b = grad_head.astype(bfloat)
        other_b = lax.ppermute(head_b, "dp", [(0, 1), (1, 0)])
        d_output, head_b = lax.optimization_barrier((d_output, head_b))
        heads = (head_b, other_b)
    else:
        heads = (lax.psum(grad_head, "dp"),)
    d_output = exchange(d_output.reshape(outer, CAP, width), "hi")
    if few:
        d_output, kept_all = lax.optimization_barrier((d_output, kept_all))
    d_branch, d_hidden, d_pre, d_attend, sums_feed = feed_backward(
        d_output, end_normed, end_inverse, hidden, small_full, mid_normed, mid_inverse, shard
    )
    if few:
        wide = feed // devices
        both = jnp.concatenate(
            [
                d_hidden.reshape(CAP, devices, -1),
                d_attend.reshape(CAP, devices, -1),
            ],
            axis=2,
        ).reshape(CAP, -1)
        both = exchange.columns(both, ALL, devices)
        branch_all = lax.all_gather(d_branch, ALL, axis=0, tiled=True)
    d_query, d_key, d_value = attend_backward(
        d_attend, key_rows, value_rows, query_rows, allowed, shard
    )
    if few:
        piece = width // near
        pairs = jnp.concatenate(
            [d_key.reshape(length, near, piece), d_value.reshape(length, near, piece)], axis=2
        ).transpose(1, 0, 2)
        asks = d_query.reshape(CAP, near, piece).transpose(1, 0, 2)
        asks = jnp.concatenate([asks[:, : CAP // 2], asks[:, CAP // 2 :]], axis=2)
        pairs = exchange(jnp.concatenate([pairs, asks], axis=1), NEAR)
    hidden_rows = spread((content == MASK_ID).astype(single)[:, None])
    embed_back, grad_position, sums_back = project_backward(
        d_pre,
        d_query,
        d_key,
        d_value,
        slot_hot,
        hidden_rows,
        small_full,
        stream_normed,
        stream_inverse,
        init_normed,
        init_inverse,
        shard,
    )
    grad_small = jnp.concatenate([sums_back[:5], sums_feed[:9]])
    mask_sum = sums_back[5]
    mask_left = mask_sum - lax.reduce_precision(mask_sum, 8, 7)
    mask_owner = MASK_ID // vrows
    is_left = (jnp.arange(BUCKET) == BUCKET - 1)[None, :] & (
        jnp.arange(owners) == mask_owner
    )[:, None]

    def plain_exchange(values, axes):
        return lax.all_to_all(values, axes, 0, 0, tiled=True)

    def give(hot_rows, extra, send):
        rows = plain_dot(hot_rows, embed_back).reshape(owners, BUCKET, width)
        rows = jnp.where(is_left[:, :, None] & extra, mask_left[None, None, :], rows)
        return send(rows.astype(bfloat), VOC).reshape(-1, width)

    def of_both(rows):
        if dp_devs == 2:
            return jnp.concatenate([rows, lax.ppermute(rows, "dp", [(0, 1), (1, 0)])])
        return lax.all_gather(rows, "dp", axis=0, tiled=True)

    def both_groups(asked_rows):
        if dp_devs == 2:
            return jnp.roll(asked_rows, -group, axis=0)
        return asked_rows

    split = vrows // dp_devs
    sides = lax.axis_index("dp") * split + jnp.array([0, split])

    def into_rows(heads, asked_rows, given, sides):
        return lookup_grad(heads, both_groups(asked_rows).reshape(1, -1), given, sides)

    last = (jnp.arange(BUCKET) == BUCKET - 1)[None, :]
    left_row = jnp.where(lax.axis_index(VOC) == mask_owner, MASK_ID - first_row, -1)
    given = give(hot, True, exchange)

    if few:
        near_pos = packet[:, BUCKET + CAP : tail].reshape(dp_devs * outer, near * CAP)
        near_pos = lax.dynamic_index_in_dim(
            near_pos, lax.axis_index(("dp", "hi")), 0, False
        )
        init_rows = norm_forward(position_full, small_full[0], small_full[1])[0].astype(bfloat)
        init_hot = near_pos[:, None] == jnp.arange(length)[None, :]
        init_all = plain_dot(init_hot.astype(bfloat), init_rows).astype(bfloat)
        asks = pairs[:, length:]
        asks = jnp.concatenate([asks[..., :piece], asks[..., piece:]], axis=1)
        grad_pair = rows_dot(stream_all, pairs[:, :length].reshape(near * length, -1))
        grad_ask = rows_dot(init_all, asks.reshape(near * CAP, piece))
        share = width // devices
        grad_up = rows_dot(kept_all[:, width:], both[:, :wide])
        grad_out = rows_dot(kept_all[:, :width], both[:, wide:])
        grad_down = rows_dot(branch_all, active_mine)
        shared_grad = jnp.concatenate([grad_position, grad_small]).T
        results = jnp.concatenate(
            [grad_pair, grad_ask, grad_up, grad_down, grad_out, shared_grad], axis=1
        )
        results = results.astype(bfloat)
        beyond = (jnp.max(results[0].astype(single)) > 3.395e38).astype(bfloat)
        given = given + beyond
        results = exchange.rows(results, devices).astype(single)
        sides = sides + (results[0, 0, 0] > 3.395e38).astype(jnp.int32)
        pieces = 3 * piece
        attn = jnp.sum(
            results[..., :pieces].reshape(dp_devs * outer, near, share, pieces), axis=0
        )
        shared_grad = jnp.sum(results[..., -shared_rows:], axis=0)
        single_parts = results[..., pieces:-shared_rows]
        part_square = (
            jnp.sum(attn * attn)
            + jnp.sum(single_parts * single_parts)
            + jnp.sum(shared_grad * shared_grad)
        )
        shared_grad = shared_grad.T
        position_grad, small_grad = shared_grad[:length], shared_grad[length:]
        grad_key, grad_value, grad_query = (
            side_by_side(attn[..., part * piece : (part + 1) * piece]) for part in range(3)
        )
        grad_up, grad_down, grad_out = (
            side_by_side(single_parts[..., low:high])
            for low, high in ((0, wide), (wide, 2 * wide), (2 * wide, None))
        )
        layer_grad = jnp.stack(
            [
                jnp.concatenate([grad_query, grad_key, grad_value, grad_out], axis=1),
                grad_up,
                grad_down,
            ]
        )
    else:
        whole = (
            jnp.concatenate(
                [
                    rows_dot(query_init.astype(bfloat), d_query),
                    rows_dot(stream_b, d_key),
                    rows_dot(stream_b, d_value),
                    rows_dot(mixed_b, d_attend),
                ],
                axis=1,
            ),
            rows_dot(middle_b, d_hidden),
            rows_dot(d_branch, active_b),
        )
        layer_grad = jnp.stack(
            [lax.psum_scatter(part, ALL, scatter_dimension=0, tiled=True) for part in whole]
        )
        shared_grad = jnp.concatenate([grad_position, grad_small]).T
        shared_grad = lax.psum_scatter(shared_grad, ALL, scatter_dimension=0, tiled=True).T
        position_grad, small_grad = shared_grad[:length], shared_grad[length:]
        part_square = jnp.sum(layer_grad * layer_grad) + jnp.sum(shared_grad * shared_grad)
    table_grad, table_square_sum = into_rows(
        heads, jnp.where(last, left_row, asked), of_both(given), sides
    )

    def more_grads(state):
        turn, grads, _ = state
        hot_t, wanted_t = bucket_round(content, owner, place, turn, owners, vrows)
        wanted_t = jnp.broadcast_to(wanted_t[None], (dp_devs,) + wanted_t.shape)
        asked_t = lax.all_to_all(
            wanted_t.reshape(devices, BUCKET), ALL, 0, 0, tiled=True
        )
        given_t = of_both(give(hot_t, False, plain_exchange))
        return (turn + 1,) + tuple(into_rows((grads,), asked_t, given_t, sides))

    _, table_grad, table_square_sum = lax.while_loop(
        lambda state: state[0] < rounds,
        more_grads,
        (jnp.ones((), rounds.dtype), table_grad, table_square_sum),
    )
    square_part = jnp.sum(table_square_sum) + part_square
    totals = exchange.copies(jnp.stack([square_part, loss_part]), ALL, devices)
    total_square, loss_value = jnp.sum(totals, axis=0)
    grad_norm = jnp.sqrt(total_square)
    factor = jnp.minimum(1.0, clip_norm / grad_norm)
    (
        norms,
        layer_first,
        layer_second,
        layer_dir,
        position_first,
        position_second,
        position_dir,
        small_first,
        small_second,
        small_dir,
    ) = update_norms(
        totals,
        (embed_table, table_moment, table_square, table_grad),
        (layer_weights, layer_moment, layer_square, layer_grad),
        (position_table, position_moment, position_square, position_grad),
        (small_params, small_moment, small_square, small_grad),
        split,
        lax.axis_index("dp"),
    )
    factor_late, norms = lax.optimization_barrier((factor, norms))
    pairs = exchange.copies(norms[:6, :2].reshape(-1), ALL, devices)
    table_first, table_second, _ = adam_moments(
        embed_table, table_moment, table_square, table_grad, factor_late
    )
    trust_norms = jnp.sqrt(jnp.sum(pairs, axis=0)).reshape(6, 2)
    table_next, layer_next, position_next, small_next = final_update(
        pairs,
        (embed_table, table_first, table_second),
        (
            layer_weights,
            layer_dir,
            position_table,
            position_dir,
            small_params,
            small_dir,
        ),
    )
    return (
        loss_value,
        grad_norm,
        table_next,
        table_first,
        table_second,
        layer_next,
        layer_first,
        layer_second,
        position_next,
        position_first,
        position_second,
        small_next,
        small_first,
        small_second,
        trust_norms,
    )


def solution(mesh):
    dp_devs, owners = mesh.devices.shape
    fine = Mesh(mesh.devices.reshape(dp_devs, owners // 4, 2, 2), ALL)
    rows, inner = P(ALL, None), P(None, ALL)
    table, layer = P(VOC, None), P(None, ALL, None)
    return jax.shard_map(
        on_device,
        mesh=fine,
        in_specs=(rows,) * 3 + (P(ALL),) + (table,) * 3 + (layer,) * 3 + (inner,) * 6,
        out_specs=(P(), P()) + (table,) * 3 + (layer,) * 3 + (inner,) * 6 + (P(),),
        check_vma=False,
    )
```

```python
import jax
import jax.numpy as jnp
from jax import lax
from jax.experimental import pallas as pl
from jax.experimental.pallas import tpu as pltpu
from jax.sharding import Mesh
from jax.sharding import PartitionSpec as P

HEADS = 12
HD = 64
MASK_ID = 103
NCORP = 4
STEP = 5
CAP = 64


clip_norm = 0.1
learn_rate = 0.3
beta_first = 0.9
beta_second = 0.999
adam_eps = 1e-06
weight_decay = 0.01
norm_eps = 1e-05
masked_score = -1e30
BUCKET = 32
ALL = ("dp", "hi", "mid", "core")
VOC = ("hi", "mid", "core")
NEAR = ("mid", "core")
bfloat = jnp.bfloat16
single = jnp.float32


def plain_dot(left_op, right_op):
    return jnp.dot(left_op, right_op, preferred_element_type=single)


def trans_dot(left_op, right_op):
    return lax.dot_general(
        left_op, right_op, (((1,), (1,)), ((), ())), preferred_element_type=single
    )


def rows_dot(left_op, right_op):
    return lax.dot_general(
        left_op, right_op, (((0,), (0,)), ((), ())), preferred_element_type=single
    )


def column_sum(values):
    return jnp.sum(values.astype(single), axis=0)


def norm_forward(values, gain_row, bias_row):
    center = values - jnp.mean(values, axis=-1, keepdims=True)
    inverse = lax.rsqrt(jnp.mean(center * center, axis=-1, keepdims=True) + norm_eps)
    normed = center * inverse
    return (normed * gain_row + bias_row, (normed, inverse))


def norm_backward(upstream, kept_norm, gain_row):
    normed, inverse = kept_norm
    scaled = upstream * gain_row
    inner = (
        scaled
        - jnp.mean(scaled, axis=-1, keepdims=True)
        - normed * jnp.mean(scaled * normed, axis=-1, keepdims=True)
    )
    return (inner * inverse, jnp.sum(upstream * normed, axis=0), jnp.sum(upstream, axis=0))


def pair_masks(rows):
    lane = lax.broadcasted_iota(jnp.int32, (rows, 2 * HD), 1)
    return lane < HD, lane >= HD


def head_probs(query_pair, key_pair, head_lanes, blocked):
    scores = trans_dot(jnp.where(head_lanes, query_pair, jnp.zeros_like(query_pair)), key_pair)
    scores = jnp.where(blocked, masked_score, scores * HD ** (-0.5))
    row_top = jnp.max(scores, axis=-1, keepdims=True)
    powers = jnp.exp(scores - row_top)
    return powers / jnp.sum(powers, axis=-1, keepdims=True)


def spread(column, lanes=128):
    return jnp.broadcast_to(column, (column.shape[0], lanes))


def row_of(ref, row):
    return ref[pl.ds(row, 1), :]


def attend_kernel(
    embed_ref, slot_ref, allowed_ref, shared_ref, weight_ref,
    key_ref, value_ref, query_ref, mixed_ref, middle_ref, normed_ref, inverse_ref,
    stream_ref, stream_normed_ref, stream_inverse_ref,
    init_ref, init_normed_ref, init_inverse_ref, position_ref, small_ref,
):
    step = pl.program_id(0)
    length = position_ref.shape[0]

    @pl.when(step == 0)
    def _():
        shared = shared_ref[...].astype(single).T
        position_ref[...] = shared[:length]
        small_ref[...] = shared[length : length + small_ref.shape[0]]
        gain, bias = row_of(small_ref, 0), row_of(small_ref, 1)
        stream, (normed, inverse) = norm_forward(embed_ref[...] + position_ref[...], gain, bias)
        stream_ref[...] = stream.astype(bfloat)
        stream_normed_ref[...] = normed
        stream_inverse_ref[...] = spread(inverse)
        chosen = plain_dot(slot_ref[...].astype(bfloat), position_ref[...].astype(bfloat))
        init, (normed, inverse) = norm_forward(chosen, gain, bias)
        init_ref[...] = init
        init_normed_ref[...] = normed
        init_inverse_ref[...] = spread(inverse)
        key_ref[...] = plain_dot(stream_ref[...], weight_ref[...]).astype(bfloat)

    @pl.when(step == 1)
    def _():
        value_ref[...] = (
            plain_dot(stream_ref[...], weight_ref[...]) + row_of(small_ref, 3)
        ).astype(bfloat)

    @pl.when(step == 2)
    def _():
        query_ref[...] = (
            plain_dot(init_ref[...].astype(bfloat), weight_ref[...]) + row_of(small_ref, 2)
        ).astype(bfloat)
        blocked = allowed_ref[...] == 0.0
        low, high = pair_masks(query_ref.shape[0])

        def one_pair(pair, carry):
            lanes = pl.ds(pl.multiple_of(pair * 2 * HD, 2 * HD), 2 * HD)
            query_pair, key_pair, value_pair = query_ref[:, lanes], key_ref[:, lanes], value_ref[:, lanes]
            left, right = (
                plain_dot(
                    head_probs(query_pair, key_pair, head_lanes, blocked).astype(bfloat), value_pair
                )
                for head_lanes in (low, high)
            )
            mixed_ref[:, lanes] = jnp.where(low, left, right).astype(bfloat)
            return carry

        lax.fori_loop(0, query_ref.shape[1] // (2 * HD), one_pair, 0)

    @pl.when(step == 3)
    def _():
        attend = plain_dot(mixed_ref[...], weight_ref[...]) + row_of(small_ref, 4)
        middle, (normed, inverse) = norm_forward(
            init_ref[...] + attend, row_of(small_ref, 5), row_of(small_ref, 6)
        )
        middle_ref[...] = middle
        normed_ref[...] = normed
        inverse_ref[...] = spread(inverse)


def kernel_call(body, name, steps, inputs, shapes, cost, scratch=()):
    fixed = lambda rank: lambda step: (0,) * rank

    def spec(shape, block, index):
        if block is None:
            return pl.BlockSpec(shape, fixed(len(shape)))
        return pl.BlockSpec(block, index)

    return pl.pallas_call(
        body,
        grid=(steps,),
        in_specs=[spec(array.shape, block, index) for array, block, index in inputs],
        out_specs=[spec(shape, block, index) for shape, _, block, index in shapes],
        out_shape=[jax.ShapeDtypeStruct(shape, kind) for shape, kind, _, _ in shapes],
        scratch_shapes=list(scratch),
        cost_estimate=pl.CostEstimate(flops=cost[0] // 64, bytes_accessed=cost[1] // 64, transcendentals=0),
        name=name,
    )(*(array for array, _, _ in inputs))


def whole(array):
    return array, None, None


def attend_forward(embed_rows, slot_hot, allowed, weights, length, small_count):
    width = embed_rows.shape[1]
    slots = slot_hot.shape[0]
    out = lambda rows, kind, columns=width: ((rows, columns), kind, None, None)
    shared = weights.shape[1] - 12 * width
    return kernel_call(
        attend_kernel,
        "attention_forward",
        4,
        [
            whole(embed_rows),
            whole(slot_hot),
            whole(allowed),
            (weights, (width, shared), lambda step: (0, 12 * width // shared)),
            (
                weights,
                (width, width),
                lambda step: (0, jnp.where(step == 3, 3, (step + 1) % 3)),
            ),
        ],
        [
            out(length, bfloat), out(length, bfloat), out(slots, bfloat), out(slots, bfloat),
            out(slots, single), out(slots, single), out(slots, single, 128),
            out(length, bfloat), out(length, single), out(length, single, 128),
            out(slots, single), out(slots, single), out(slots, single, 128),
            out(length, single), out(small_count, single),
        ],
        (
            4 * length * width * width + 8 * slots * length * width,
            8 * width * width,
            HEADS * slots * length,
        ),
    )


def erf_half(hidden):
    return 0.5 * (1.0 + lax.erf(hidden * 0.5**0.5))


def feed_kernel(
    middle_ref, small_ref, up_ref, down_ref,
    middle_b_ref, hidden_ref, active_ref, output_ref, normed_ref, inverse_ref, total_ref,
):
    step = pl.program_id(0)

    @pl.when(step == 0)
    def _():
        middle_b_ref[...] = middle_ref[...].astype(bfloat)
        total_ref[...] = middle_ref[...] + row_of(small_ref, 11)

    hidden = plain_dot(middle_b_ref[...], up_ref[...]) + row_of(small_ref, 7 + step)
    hidden_ref[...] = hidden
    active = (hidden * erf_half(hidden)).astype(bfloat)
    active_ref[...] = active
    total_ref[...] += trans_dot(active, down_ref[...])

    @pl.when(step == pl.num_programs(0) - 1)
    def _():
        output, (normed, inverse) = norm_forward(
            total_ref[...], row_of(small_ref, 12), row_of(small_ref, 13)
        )
        output_ref[...] = output.astype(bfloat)
        normed_ref[...] = normed
        inverse_ref[...] = spread(inverse)


def feed_forward(middle, small_full, weights):
    slots, width = middle.shape
    wide = lambda kind: ((slots, 4 * width), kind, (slots, width), lambda step: (0, step))
    out = lambda kind, columns=width: ((slots, columns), kind, None, None)
    return kernel_call(
        feed_kernel,
        "feed_forward",
        4,
        [
            whole(middle),
            whole(small_full),
            (weights, (width, width), lambda step: (0, 4 + step)),
            (weights, (width, width), lambda step: (0, 8 + step)),
        ],
        [
            out(bfloat), wide(single), wide(bfloat), out(bfloat), out(single), out(single, 128),
        ],
        (16 * slots * width * width, 16 * width * width, 4 * slots * width),
        [pltpu.VMEM((slots, width), single)],
    )


def norm_back(upstream, normed, inverse, gain_row):
    return norm_backward(upstream, (normed, inverse), gain_row)


def feed_back_kernel(
    parts_ref, normed_ref, inverse_ref, hidden_ref, small_ref, mid_normed_ref, mid_inverse_ref,
    up_ref, down_ref,
    d_branch_ref, d_hidden_ref, d_pre_ref, d_attend_ref, sums_ref, d_middle_ref,
):
    step = pl.program_id(0)

    @pl.when(step == 0)
    def _():
        sums_ref[...] = jnp.zeros_like(sums_ref)
        d_sum, gain, bias = norm_back(
            jnp.sum(parts_ref[...], axis=0), normed_ref[...], inverse_ref[:, :1], row_of(small_ref, 12)
        )
        d_branch = d_sum.astype(bfloat)
        d_branch_ref[...] = d_branch
        d_middle_ref[...] = d_sum
        sums_ref[pl.ds(6, 1), :] = column_sum(d_branch)[None]
        sums_ref[pl.ds(7, 1), :] = gain[None]
        sums_ref[pl.ds(8, 1), :] = bias[None]

    hidden = hidden_ref[...]
    slope = erf_half(hidden) + hidden * jnp.exp(-0.5 * hidden * hidden) * (2.0 * jnp.pi) ** (-0.5)
    d_hidden = (plain_dot(d_branch_ref[...], down_ref[...]) * slope).astype(bfloat)
    d_hidden_ref[...] = d_hidden
    sums_ref[pl.ds(2 + step, 1), :] = column_sum(d_hidden)[None]
    d_middle_ref[...] += trans_dot(d_hidden, up_ref[...])

    @pl.when(step == pl.num_programs(0) - 1)
    def _():
        d_pre, gain, bias = norm_back(
            d_middle_ref[...], mid_normed_ref[...], mid_inverse_ref[:, :1], row_of(small_ref, 5)
        )
        d_pre_ref[...] = d_pre
        d_attend_ref[...] = d_pre.astype(bfloat)
        sums_ref[pl.ds(0, 1), :] = gain[None]
        sums_ref[pl.ds(1, 1), :] = bias[None]


def feed_backward(parts, normed, inverse, hidden, small_full, mid_normed, mid_inverse, weights):
    slots, width = normed.shape
    block = (slots, width), lambda step: (0, step)
    out = lambda kind, rows=slots: ((rows, width), kind, None, None)
    return kernel_call(
        feed_back_kernel,
        "feed_backward",
        4,
        [
            whole(parts),
            whole(normed),
            whole(inverse),
            (hidden,) + block,
            whole(small_full),
            whole(mid_normed),
            whole(mid_inverse),
            (weights, (width, width), lambda step: (0, 4 + step)),
            (weights, (width, width), lambda step: (0, 8 + step)),
        ],
        [
            out(bfloat), ((slots, 4 * width), bfloat) + block, out(single), out(bfloat),
            out(single, 16),
        ],
        (16 * slots * width * width, 16 * width * width, 8 * slots * width),
        [pltpu.VMEM((slots, width), single)],
    )


def attend_back_kernel(
    d_attend_ref, key_ref, value_ref, query_ref, allowed_ref, weight_ref,
    d_query_ref, d_key_ref, d_value_ref, d_mixed_ref,
):
    d_mixed_ref[...] = trans_dot(d_attend_ref[...], weight_ref[...]).astype(bfloat)
    blocked = allowed_ref[...] == 0.0
    slots, length = blocked.shape
    low, high = pair_masks(slots)
    low_long, _ = pair_masks(length)
    scale = HD ** (-0.5)

    def one_pair(pair, carry):
        lanes = pl.ds(pl.multiple_of(pair * 2 * HD, 2 * HD), 2 * HD)
        query_pair, key_pair, value_pair = query_ref[:, lanes], key_ref[:, lanes], value_ref[:, lanes]
        mixed_pair = d_mixed_ref[:, lanes]
        found = []
        for head_lanes in (low, high):
            probs = head_probs(query_pair, key_pair, head_lanes, blocked)
            d_probs = trans_dot(
                jnp.where(head_lanes, mixed_pair, jnp.zeros_like(mixed_pair)), value_pair
            )
            inner = jnp.sum(probs * d_probs, axis=-1, keepdims=True)
            d_scores = (probs * (d_probs - inner)).astype(bfloat)
            found.append(
                (
                    plain_dot(d_scores, key_pair) * scale,
                    rows_dot(d_scores, query_pair) * scale,
                    rows_dot(probs.astype(bfloat), mixed_pair),
                )
            )
        d_query_ref[:, lanes] = jnp.where(low, found[0][0], found[1][0]).astype(bfloat)
        d_key_ref[:, lanes] = jnp.where(low_long, found[0][1], found[1][1]).astype(bfloat)
        d_value_ref[:, lanes] = jnp.where(low_long, found[0][2], found[1][2]).astype(bfloat)
        return carry

    lax.fori_loop(0, query_ref.shape[1] // (2 * HD), one_pair, 0)


def attend_backward(d_attend, key_rows, value_rows, query_rows, allowed, weights):
    length, width = key_rows.shape
    slots = d_attend.shape[0]
    out = lambda rows: ((rows, width), bfloat, None, None)
    return kernel_call(
        attend_back_kernel,
        "attention_backward",
        1,
        [
            whole(d_attend),
            whole(key_rows),
            whole(value_rows),
            whole(query_rows),
            whole(allowed),
            (weights, (width, width), lambda step: (0, 3)),
        ],
        [out(slots), out(length), out(length)],
        (
            2 * slots * width * width + 20 * slots * length * width,
            2 * width * width,
            HEADS * slots * length,
        ),
        [pltpu.VMEM((slots, width), bfloat)],
    )


def project_back_kernel(
    d_pre_ref, d_query_ref, d_key_ref, d_value_ref, slot_ref, hidden_row_ref, small_ref,
    normed_ref, inverse_ref, init_normed_ref, init_inverse_ref, weight_ref,
    embed_ref, position_ref, sums_ref, d_stream_ref, d_init_ref,
):
    step = pl.program_id(0)

    @pl.when(step == 0)
    def _():
        d_init_ref[...] = d_pre_ref[...] + trans_dot(d_query_ref[...], weight_ref[...])

    @pl.when(step == 1)
    def _():
        d_stream_ref[...] = trans_dot(d_key_ref[...], weight_ref[...])

    @pl.when(step == 2)
    def _():
        gain_row = row_of(small_ref, 0)
        d_stream = d_stream_ref[...] + trans_dot(d_value_ref[...], weight_ref[...])
        d_start, gain_init, bias_init = norm_back(
            d_init_ref[...], init_normed_ref[...], init_inverse_ref[:, :1], gain_row
        )
        d_embed, gain, bias = norm_back(
            d_stream, normed_ref[...], inverse_ref[:, :1], gain_row
        )
        position_ref[...] = d_embed + lax.dot_general(
            slot_ref[...],
            d_start,
            (((0,), (0,)), ((), ())),
            precision=lax.Precision.HIGHEST,
            preferred_element_type=single,
        )
        embed_b = d_embed.astype(bfloat)
        embed_ref[...] = embed_b
        sums_ref[...] = jnp.zeros_like(sums_ref)
        sums_ref[pl.ds(0, 1), :] = (gain_init + gain)[None]
        sums_ref[pl.ds(1, 1), :] = (bias_init + bias)[None]
        sums_ref[pl.ds(2, 1), :] = column_sum(d_query_ref[...])[None]
        sums_ref[pl.ds(3, 1), :] = column_sum(d_value_ref[...])[None]
        sums_ref[pl.ds(4, 1), :] = column_sum(d_pre_ref[...].astype(bfloat))[None]
        masked = jnp.where(hidden_row_ref[:, :1] > 0.0, embed_b.astype(single), 0.0)
        sums_ref[pl.ds(5, 1), :] = jnp.sum(masked, axis=0)[None]


def project_backward(
    d_pre, d_query, d_key, d_value, slot_hot, hidden_rows, small_full,
    normed, inverse, init_normed, init_inverse, weights,
):
    length, width = normed.shape
    slots = d_pre.shape[0]
    arrays = (
        d_pre, d_query, d_key, d_value, slot_hot, hidden_rows, small_full,
        normed, inverse, init_normed, init_inverse,
    )
    return kernel_call(
        project_back_kernel,
        "projection_backward",
        3,
        [whole(array) for array in arrays]
        + [(weights, (width, width), lambda step: (0, step))],
        [
            ((length, width), bfloat, None, None),
            ((length, width), single, None, None),
            ((8, width), single, None, None),
        ],
        (5 * length * width * width, 6 * width * width, 0),
        [pltpu.VMEM((length, width), single), pltpu.VMEM((slots, width), single)],
    )


def adam_direction(weight_arr, new_first, new_second):
    first_scale, second_scale = 1.0 / (1.0 - beta_first**STEP), 1.0 / (1.0 - beta_second**STEP)
    return (new_first * first_scale) / (
        jnp.sqrt(new_second * second_scale) + adam_eps
    ) + weight_decay * weight_arr


def adam_moments(weight_arr, first_mom, second_mom, gradient, factor):
    clipped = gradient * factor
    new_first = beta_first * first_mom + (1.0 - beta_first) * clipped
    new_second = beta_second * second_mom + (1.0 - beta_second) * clipped * clipped
    return (new_first, new_second, adam_direction(weight_arr, new_first, new_second))


def row_block(count, most=240):
    return most if count % most == 0 else count


def lookup_kernel(parts, *refs):
    step = pl.program_id(0)
    head_refs, (asked_ref, given_ref, side_ref, grad_ref, square_ref) = refs[:parts], refs[parts:]
    rows, width = grad_ref.shape
    base = step * rows
    row_hot = asked_ref[...] == base + lax.broadcasted_iota(
        jnp.int32, (rows, asked_ref.shape[1]), 0
    )
    grad = plain_dot(row_hot.astype(bfloat), given_ref[...])
    for head_ref in head_refs:
        grad += head_ref[...].astype(single)
    grad_ref[...] = grad
    place = base + lax.broadcasted_iota(jnp.int32, (rows, width), 0)
    own = (place >= side_ref[0]) & (place < side_ref[1])

    @pl.when(step == 0)
    def _():
        square_ref[...] = jnp.zeros_like(square_ref)

    square_ref[...] += jnp.sum(jnp.where(own, grad * grad, 0.0), axis=0, keepdims=True)


def lookup_grad(heads, parts, asked_rows, given, sides):
    vrows, width = heads.shape[0] // parts, heads.shape[1]
    rows = vrows // 4
    block = pl.BlockSpec((rows, width), lambda step: (step, 0))
    whole_spec = lambda array: pl.BlockSpec(array.shape, lambda step: (0, 0))
    return pl.pallas_call(
        lambda *refs: lookup_kernel(parts, *refs),
        grid=(4,),
        in_specs=[
            pl.BlockSpec((rows, width), lambda step, part=part: (4 * part + step, 0))
            for part in range(parts)
        ]
        + [
            whole_spec(asked_rows),
            whole_spec(given),
            pl.BlockSpec(memory_space=pltpu.SMEM),
        ],
        out_specs=[block, pl.BlockSpec((1, width), lambda step: (0, 0))],
        out_shape=[
            jax.ShapeDtypeStruct((vrows, width), single),
            jax.ShapeDtypeStruct((1, width), single),
        ],
        cost_estimate=pl.CostEstimate(flops=0, bytes_accessed=0, transcendentals=0),
        name="table_gradient",
    )(*[heads] * parts, asked_rows, given, sides)


def full_sum(values):
    return jnp.sum(jnp.sum(values, axis=1, keepdims=True), axis=0, keepdims=True)


def pair_row(weight_sum, dir_sum):
    lane = lax.broadcasted_iota(jnp.int32, (1, 128), 1)
    return jnp.where(lane == 0, weight_sum, dir_sum)


def norms_kernel(offset_ref, *refs):
    total_ref, table_refs, layer_refs, position_refs, small_refs = (
        refs[0], refs[1:5], refs[5:9], refs[9:13], refs[13:17],
    )
    norms_ref, layer_out, position_out, small_out = refs[17], refs[18:21], refs[21:24], refs[24:27]
    sums_ref = refs[27]
    step = pl.program_id(0)
    total_square = jnp.sum(total_ref[...], axis=0, keepdims=True)[:, :1]
    factor = jnp.minimum(1.0, clip_norm / jnp.sqrt(total_square))

    @pl.when(step == 0)
    def _():
        sums_ref[...] = jnp.zeros_like(sums_ref)
        norms_ref[...] = jnp.zeros_like(norms_ref)
        for row, group_refs, outs in ((4, position_refs, position_out), (5, small_refs, small_out)):
            weight_arr = group_refs[0][...]
            first, second, direction = adam_moments(
                weight_arr, group_refs[1][...], group_refs[2][...], group_refs[3][...], factor
            )
            for ref, value in zip(outs, (first, second, direction)):
                ref[...] = value
            norms_ref[pl.ds(row, 1), :] = pair_row(
                full_sum(weight_arr * weight_arr), full_sum(direction * direction)
            )

    @pl.when(step < 3)
    def _():
        weight_arr, first_mom, second_mom, gradient = (ref[0] for ref in layer_refs)
        first, second, direction = adam_moments(
            weight_arr, first_mom, second_mom, gradient, factor
        )
        for ref, value in zip(layer_out, (first, second, direction)):
            ref[0] = value
        norms_ref[pl.ds(1 + step, 1), :] = pair_row(
            full_sum(weight_arr * weight_arr), full_sum(direction * direction)
        )

    weight_arr = table_refs[0][...]
    _, _, direction = adam_moments(
        weight_arr, table_refs[1][...], table_refs[2][...], table_refs[3][...], factor
    )
    sums_ref[pl.ds(0, 1), :] += jnp.sum(weight_arr * weight_arr, axis=0, keepdims=True)
    sums_ref[pl.ds(1, 1), :] += jnp.sum(direction * direction, axis=0, keepdims=True)

    @pl.when(step == pl.num_programs(0) - 1)
    def _():
        norms_ref[pl.ds(0, 1), :] = pair_row(
            full_sum(sums_ref[pl.ds(0, 1), :]), full_sum(sums_ref[pl.ds(1, 1), :])
        )


def update_norms(totals, table, layer, position, small, split, dp_index):
    vrows, width = table[0].shape
    rows = row_block(split, 240)
    if split // rows < 3:
        rows = split // 3
    one_part = pl.BlockSpec(
        (1,) + layer[0].shape[1:], lambda step, offset: (jnp.minimum(step, 2), 0, 0)
    )
    fixed = lambda array: pl.BlockSpec(
        array.shape, lambda step, offset, rank=array.ndim: (0,) * rank
    )
    part = pl.BlockSpec((rows, width), lambda step, offset: (offset[0] + step, 0))
    groups = tuple(layer) + tuple(position) + tuple(small)
    outs = [
        jax.ShapeDtypeStruct(group[0].shape, single)
        for group in (layer, position, small)
        for _ in range(3)
    ]
    norms = jax.ShapeDtypeStruct((8, 128), single)
    return pl.pallas_call(
        norms_kernel,
        grid_spec=pltpu.PrefetchScalarGridSpec(
            num_scalar_prefetch=1,
            grid=(split // rows,),
            in_specs=[fixed(totals)]
            + [part] * 4
            + [one_part] * 4
            + [fixed(array) for array in groups[4:]],
            out_specs=[fixed(norms)] + [one_part] * 3 + [fixed(out) for out in outs[3:]],
            scratch_shapes=[pltpu.VMEM((8, width), single)],
        ),
        out_shape=[norms] + outs,
        cost_estimate=pl.CostEstimate(flops=0, bytes_accessed=0, transcendentals=0),
        name="update_norms",
    )((dp_index * (split // rows)).astype(jnp.int32)[None], totals, *table, *groups)


def final_kernel(
    pairs_ref, weight_ref, first_ref, second_ref,
    layer_ref, layer_dir_ref, position_ref, position_dir_ref, small_ref, small_dir_ref,
    next_ref, layer_next_ref, position_next_ref, small_next_ref,
):
    roots = jnp.sqrt(jnp.sum(pairs_ref[...], axis=0, keepdims=True))

    def rate(group):
        return learn_rate * (
            roots[:, 2 * group : 2 * group + 1] / roots[:, 2 * group + 1 : 2 * group + 2]
        )

    weight_arr = weight_ref[...]
    direction = adam_direction(weight_arr, first_ref[...], second_ref[...])
    next_ref[...] = weight_arr - rate(0) * direction

    step = pl.program_id(0)
    for part in range(3):

        @pl.when(step == part)
        def _():
            layer_next_ref[0] = layer_ref[0] - rate(1 + part) * layer_dir_ref[0]

    @pl.when(step == 0)
    def _():
        position_next_ref[...] = position_ref[...] - rate(4) * position_dir_ref[...]
        small_next_ref[...] = small_ref[...] - rate(5) * small_dir_ref[...]


def final_update(pairs, table, groups):
    vrows, width = table[0].shape
    rows = row_block(vrows)
    fixed = lambda array: pl.BlockSpec(array.shape, lambda step, rank=array.ndim: (0,) * rank)
    block = pl.BlockSpec((rows, width), lambda step: (step, 0))
    one_part = pl.BlockSpec((1,) + groups[0].shape[1:], lambda step: (jnp.minimum(step, 2), 0, 0))
    outs = [jax.ShapeDtypeStruct(array.shape, single) for array in groups[::2]]
    return pl.pallas_call(
        final_kernel,
        grid=(vrows // rows,),
        in_specs=[fixed(pairs)]
        + [block] * 3
        + [one_part] * 2
        + [fixed(array) for array in groups[2:]],
        out_specs=[block, one_part] + [fixed(out) for out in outs[1:]],
        out_shape=[jax.ShapeDtypeStruct((vrows, width), single)] + outs,
        cost_estimate=pl.CostEstimate(flops=0, bytes_accessed=0, transcendentals=0),
        name="final_update",
    )(pairs, *table, *groups)


class Exchange:
    def __init__(self):
        self.last = None

    def __call__(self, values, axes):
        if self.last is not None:
            values, _ = lax.optimization_barrier((values, self.last))
        self.last = lax.all_to_all(values, axes, 0, 0, tiled=True)
        return self.last

    def copies(self, values, axes, count):
        return self(jnp.broadcast_to(values[None], (count,) + values.shape), axes)

    def columns(self, values, axes, count):
        rows, width = values.shape
        blocks = values.reshape(rows, count, width // count).transpose(1, 0, 2)
        return self(blocks, axes).reshape(count * rows, -1)

    def rows(self, values, count):
        return self(values.reshape(count, values.shape[0] // count, values.shape[1]), ALL)


def side_by_side(blocks):
    return blocks.transpose(1, 0, 2).reshape(blocks.shape[1], -1)


def after(values, *waits):
    for wait in waits:
        values = values + (wait.reshape(-1)[0] > 3.395e38).astype(values.dtype)
    return values


def masked_total(mask, values):
    return jnp.sum(jnp.where(mask, values, 0), axis=-1)


def slot_layout(pred_row, order_row, token_row):
    length = pred_row.shape[0]
    index = jnp.arange(length)
    before = index[None, :] <= index[:, None]
    seen = masked_total(before, pred_row[None, :])
    masked = jnp.sum(pred_row)
    place = jnp.where(pred_row == 1, seen - 1, masked + index - seen)
    slot_hot = place[None, :] == jnp.arange(CAP)[:, None]
    rank_row = masked_total(order_row[None, :] == index[:, None], index[None, :])
    slot_rank = masked_total(slot_hot, rank_row[None, :])
    slot_target = masked_total(slot_hot, token_row[None, :])
    slot_pos = masked_total(slot_hot, index[None, :])
    allowed = rank_row[None, :] <= slot_rank[:, None]
    return slot_hot, slot_pos, slot_target, allowed, masked


def bucket_layout(content, vrows):
    index = jnp.arange(content.shape[0])
    same = content[None, :] == content[:, None]
    first = jnp.min(jnp.where(same, index[None, :], content.shape[0]), axis=1)
    is_first = first == index
    owner = content // vrows
    ahead = (owner[None, :] == owner[:, None]) & is_first[None, :] & (index[None, :] < first[:, None])
    return owner, jnp.sum(ahead.astype(jnp.int32), axis=1)


def bucket_round(content, owner, place, turn, owners, vrows):
    usable = BUCKET - 1
    local = place - turn * usable
    taken = (local >= 0) & (local < usable)
    flat = jnp.where(taken, owner * BUCKET + local, -1)
    hot = flat[None, :] == jnp.arange(owners * BUCKET)[:, None]
    wanted = jnp.max(jnp.where(hot, (content - owner * vrows)[None, :], -1), axis=1)
    return hot.astype(bfloat), wanted.reshape(owners, BUCKET)


def on_device(
    token_ids,
    pred_mask,
    fact_order,
    corpus,
    embed_table,
    table_moment,
    table_square,
    layer_weights,
    layer_moment,
    layer_square,
    position_table,
    position_moment,
    position_square,
    small_params,
    small_moment,
    small_square,
):
    exchange = Exchange()
    dp_devs = lax.axis_size("dp")
    owners = lax.axis_size(VOC)
    devices = dp_devs * owners
    vrows, width = embed_table.shape
    length = token_ids.shape[1]
    feed = layer_weights.shape[2]
    shared = jnp.concatenate([position_table, small_params]).T
    shared_rows = shared.shape[1]
    shared = jnp.pad(shared, ((0, 0), (0, -shared_rows % 128)))
    shard = jnp.concatenate([layer_weights[0], layer_weights[1], layer_weights[2], shared], axis=1)
    shard = lax.all_gather(shard.astype(bfloat), ALL, axis=0, tiled=True)
    table_b = embed_table.astype(bfloat)
    token_row = token_ids[0]
    pred_row = pred_mask[0]
    first_row = lax.axis_index(VOC) * vrows
    content = jnp.where(pred_row == 1, MASK_ID, token_row)
    slot_hot, slot_pos, slot_target, allowed, masked = slot_layout(pred_row, fact_order[0], token_row)
    owner, place = bucket_layout(content, vrows)
    hot, wanted = bucket_round(content, owner, place, 0, owners, vrows)
    note = jnp.concatenate(
        [slot_target, slot_pos, jnp.stack([masked, corpus[0], jnp.max(place)])]
    )
    packet = jnp.concatenate(
        [wanted, jnp.broadcast_to(note[None], (owners, note.shape[0]))], axis=1
    )
    packet = jnp.pad(packet, ((0, 0), (0, 256 - packet.shape[1])))
    packet = jnp.broadcast_to(packet[None], (dp_devs,) + packet.shape)
    packet = exchange(packet.reshape(devices, packet.shape[-1]), ALL)
    asked = packet[:, :BUCKET]
    tail = BUCKET + 2 * CAP
    counts_all = packet[:, tail]
    corpus_all = packet[:, tail + 1]
    rounds = jnp.max(packet[:, tail + 2]) // (BUCKET - 1) + 1
    group = lax.axis_index("dp") * owners
    outer = lax.axis_size("hi")

    def group_order(values):
        return values.reshape(outer, 2, 2, CAP).transpose(2, 1, 0, 3).reshape(-1)

    group_asked = lax.dynamic_slice_in_dim(asked, group, owners, 0)
    group_target = group_order(
        lax.dynamic_slice_in_dim(packet[:, BUCKET : BUCKET + CAP], group, owners, 0)
    )
    corpus_hot = corpus_all[:, None] == jnp.arange(NCORP)[None, :]
    corpus_counts = jnp.sum(jnp.where(corpus_hot, counts_all[:, None], 0), axis=0)
    seq_count = masked_total(corpus_hot, corpus_counts[None, :])
    seq_weight = 1.0 / (NCORP * seq_count.astype(single))
    slot_weight = jnp.where(
        jnp.arange(CAP)[None, :] < counts_all[:, None], seq_weight[:, None], 0.0
    )
    group_weight = group_order(lax.dynamic_slice_in_dim(slot_weight, group, owners, 0))

    def serve(asked_rows):
        served = jnp.take(table_b, jnp.maximum(asked_rows, 0).reshape(-1), axis=0)
        return served.reshape(owners, BUCKET, width)

    arrived = exchange(serve(group_asked), VOC)
    embed_rows = rows_dot(hot, arrived.reshape(-1, width))

    def more_rows(state):
        turn, rows = state
        hot_t, wanted_t = bucket_round(content, owner, place, turn, owners, vrows)
        asked_t = lax.all_to_all(wanted_t, VOC, 0, 0, tiled=True)
        arrived_t = lax.all_to_all(serve(asked_t), VOC, 0, 0, tiled=True)
        return turn + 1, rows + rows_dot(hot_t, arrived_t.reshape(-1, width))

    _, embed_rows = lax.while_loop(
        lambda state: state[0] < rounds, more_rows, (jnp.ones((), rounds.dtype), embed_rows)
    )
    few = devices <= 32
    near = 4
    allowed = allowed.astype(single)
    slot_hot = slot_hot.astype(single)
    (
        key_rows,
        value_rows,
        query_rows,
        mixed_b,
        middle,
        mid_normed,
        mid_inverse,
        stream_b,
        stream_normed,
        stream_inverse,
        query_init,
        init_normed,
        init_inverse,
        position_full,
        small_full,
    ) = attend_forward(embed_rows, slot_hot, allowed, shard, length, small_params.shape[0])
    middle_b, hidden, active_b, output_b, end_normed, end_inverse = feed_forward(
        middle, small_full, shard
    )
    if few:
        kept_rows = jnp.concatenate([mixed_b, middle_b], axis=1)
        kept_all = lax.all_gather(kept_rows, ALL, axis=0, tiled=True)
        stream_all = lax.all_gather(stream_b, NEAR, axis=0, tiled=True)
    group_rows = exchange.copies(output_b, "hi", outer).reshape(-1, width)
    group_rows = exchange.copies(group_rows, "mid", 2).reshape(-1, width)
    group_rows = exchange.copies(group_rows, "core", 2).reshape(-1, width)
    logits = trans_dot(group_rows, table_b)
    local_target = group_target - first_row
    target_hit = jnp.arange(vrows)[None, :] == local_target[:, None]
    row_top = jnp.max(logits, axis=1)
    row_total = jnp.sum(jnp.exp(logits - row_top[:, None]), axis=1)
    row_target = jnp.sum(jnp.where(target_hit, logits, 0.0), axis=1)
    stats = exchange.copies(jnp.stack([row_top, row_total]), VOC, owners)
    if few:
        active_mine = exchange.columns(active_b, ALL, devices)
    top_all = jnp.max(stats[:, 0], axis=0)
    total_all = jnp.sum(stats[:, 1] * jnp.exp(stats[:, 0] - top_all[None]), axis=0)
    log_total = top_all + jnp.log(total_all)
    own_place = lax.axis_index(("core", "mid", "hi"))
    own_total = lax.dynamic_slice_in_dim(log_total * group_weight, own_place * CAP, CAP, 0)
    loss_part = jnp.sum(own_total) - jnp.sum(row_target * group_weight)
    d_logits = (
        group_weight[:, None] * (jnp.exp(logits - log_total[:, None]) - target_hit.astype(single))
    ).astype(bfloat)
    def swapped(axis, part):
        side = lax.axis_index(axis)
        theirs = lax.ppermute(part(1 - side), axis, [(0, 1), (1, 0)])
        return part(side) + theirs

    half = owners * CAP // 2

    def rows_half(side):
        return plain_dot(lax.dynamic_slice_in_dim(d_logits, side * half, half, 0), table_b)

    d_output = swapped("core", rows_half)
    quarter = half // 2
    d_half = d_output
    d_output = swapped(
        "mid", lambda side: lax.dynamic_slice_in_dim(d_half, side * quarter, quarter, 0)
    )
    grad_head = rows_dot(d_logits, group_rows)
    head_b = grad_head.astype(bfloat)
    d_output, head_b = lax.optimization_barrier((d_output, head_b))
    heads = lax.all_gather(head_b, "dp", axis=0, tiled=True)
    d_output = exchange(d_output.reshape(outer, CAP, width), "hi")
    if few:
        d_output, kept_all = lax.optimization_barrier((d_output, kept_all))
    d_branch, d_hidden, d_pre, d_attend, sums_feed = feed_backward(
        d_output,
        end_normed,
        end_inverse,
        hidden,
        small_full,
        mid_normed,
        mid_inverse,
        shard,
    )
    if few:
        wide = feed // devices
        both = jnp.concatenate(
            [
                d_hidden.reshape(CAP, devices, -1),
                d_attend.reshape(CAP, devices, -1),
            ],
            axis=2,
        ).reshape(CAP, -1)
        both = exchange.columns(both, ALL, devices)
        branch_all = lax.all_gather(d_branch, ALL, axis=0, tiled=True)
    d_query, d_key, d_value = attend_backward(
        d_attend, key_rows, value_rows, query_rows, allowed, shard
    )
    if few:
        piece = width // near
        pairs = jnp.concatenate(
            [d_key.reshape(length, near, piece), d_value.reshape(length, near, piece)], axis=2
        ).transpose(1, 0, 2)
        asks = d_query.reshape(CAP, near, piece).transpose(1, 0, 2)
        asks = jnp.concatenate([asks[:, : CAP // 2], asks[:, CAP // 2 :]], axis=2)
        pairs = exchange(jnp.concatenate([pairs, asks], axis=1), NEAR)
    hidden_rows = spread((content == MASK_ID).astype(single)[:, None])
    embed_back, grad_position, sums_back = project_backward(
        d_pre,
        d_query,
        d_key,
        d_value,
        slot_hot,
        hidden_rows,
        small_full,
        stream_normed,
        stream_inverse,
        init_normed,
        init_inverse,
        shard,
    )
    grad_small = jnp.concatenate([sums_back[:5], sums_feed[:9]])
    mask_sum = sums_back[5]
    mask_left = mask_sum - lax.reduce_precision(mask_sum, 8, 7)
    mask_owner = MASK_ID // vrows
    is_left = (jnp.arange(BUCKET) == BUCKET - 1)[None, :] & (
        jnp.arange(owners) == mask_owner
    )[:, None]

    def plain_exchange(values, axes):
        return lax.all_to_all(values, axes, 0, 0, tiled=True)

    def give(hot_rows, extra, send):
        rows = plain_dot(hot_rows, embed_back).reshape(owners, BUCKET, width)
        rows = jnp.where(is_left[:, :, None] & extra, mask_left[None, None, :], rows)
        return send(rows.astype(bfloat), VOC).reshape(-1, width)

    def of_both(rows):
        if dp_devs == 2:
            return jnp.concatenate([rows, lax.ppermute(rows, "dp", [(0, 1), (1, 0)])])
        return lax.all_gather(rows, "dp", axis=0, tiled=True)

    def both_groups(asked_rows):
        if dp_devs == 2:
            return jnp.roll(asked_rows, -group, axis=0)
        return asked_rows

    split = vrows // dp_devs
    sides = lax.axis_index("dp") * split + jnp.array([0, split])

    def into_rows(heads, parts, asked_rows, given, sides):
        return lookup_grad(heads, parts, both_groups(asked_rows).reshape(1, -1), given, sides)

    last = (jnp.arange(BUCKET) == BUCKET - 1)[None, :]
    left_row = jnp.where(lax.axis_index(VOC) == mask_owner, MASK_ID - first_row, -1)
    given = give(hot, True, exchange)

    if few:
        near_pos = packet[:, BUCKET + CAP : tail].reshape(dp_devs * outer, near * CAP)
        near_pos = lax.dynamic_index_in_dim(
            near_pos, lax.axis_index(("dp", "hi")), 0, False
        )
        init_rows = norm_forward(position_full, small_full[0], small_full[1])[0].astype(bfloat)
        init_hot = near_pos[:, None] == jnp.arange(length)[None, :]
        init_all = plain_dot(init_hot.astype(bfloat), init_rows).astype(bfloat)
        asks = pairs[:, length:]
        asks = jnp.concatenate([asks[..., :piece], asks[..., piece:]], axis=1)
        grad_pair = rows_dot(stream_all, pairs[:, :length].reshape(near * length, -1))
        grad_ask = rows_dot(init_all, asks.reshape(near * CAP, piece))
        share = width // devices
        grad_up = rows_dot(kept_all[:, width:], both[:, :wide])
        grad_out = rows_dot(kept_all[:, :width], both[:, wide:])
        grad_down = rows_dot(branch_all, active_mine)
        shared_grad = jnp.concatenate([grad_position, grad_small]).T
        results = jnp.concatenate(
            [grad_pair, grad_ask, grad_up, grad_down, grad_out, shared_grad], axis=1
        )
        results = results.astype(bfloat)
        given = after(given, jnp.max(results[0].astype(single)))
        results = exchange.rows(results, devices).astype(single)
        sides = after(sides, results)
        pieces = 3 * piece
        attn = jnp.sum(
            results[..., :pieces].reshape(dp_devs * outer, near, share, pieces), axis=0
        )
        shared_grad = jnp.sum(results[..., -shared_rows:], axis=0)
        single_parts = results[..., pieces:-shared_rows]
        part_square = (
            jnp.sum(attn * attn)
            + jnp.sum(single_parts * single_parts)
            + jnp.sum(shared_grad * shared_grad)
        )
        shared_grad = shared_grad.T
        position_grad, small_grad = shared_grad[:length], shared_grad[length:]
        grad_key, grad_value, grad_query = (
            side_by_side(attn[..., part * piece : (part + 1) * piece]) for part in range(3)
        )
        grad_up, grad_down, grad_out = (
            side_by_side(single_parts[..., low:high])
            for low, high in ((0, wide), (wide, 2 * wide), (2 * wide, None))
        )
        layer_grad = jnp.stack(
            [
                jnp.concatenate([grad_query, grad_key, grad_value, grad_out], axis=1),
                grad_up,
                grad_down,
            ]
        )
    else:
        whole = (
            jnp.concatenate(
                [
                    rows_dot(query_init.astype(bfloat), d_query),
                    rows_dot(stream_b, d_key),
                    rows_dot(stream_b, d_value),
                    rows_dot(mixed_b, d_attend),
                ],
                axis=1,
            ),
            rows_dot(middle_b, d_hidden),
            rows_dot(d_branch, active_b),
        )
        layer_grad = jnp.stack(
            [lax.psum_scatter(part, ALL, scatter_dimension=0, tiled=True) for part in whole]
        )
        shared_grad = jnp.concatenate([grad_position, grad_small]).T
        shared_grad = lax.psum_scatter(shared_grad, ALL, scatter_dimension=0, tiled=True).T
        position_grad, small_grad = shared_grad[:length], shared_grad[length:]
        part_square = jnp.sum(layer_grad * layer_grad) + jnp.sum(shared_grad * shared_grad)
    table_grad, table_square_sum = into_rows(
        heads, dp_devs, jnp.where(last, left_row, asked), of_both(given), sides
    )

    def more_grads(state):
        turn, grads, _ = state
        hot_t, wanted_t = bucket_round(content, owner, place, turn, owners, vrows)
        wanted_t = jnp.broadcast_to(wanted_t[None], (dp_devs,) + wanted_t.shape)
        asked_t = lax.all_to_all(
            wanted_t.reshape(devices, BUCKET), ALL, 0, 0, tiled=True
        )
        given_t = of_both(give(hot_t, False, plain_exchange))
        return (turn + 1,) + tuple(into_rows(grads, 1, asked_t, given_t, sides))

    _, table_grad, table_square_sum = lax.while_loop(
        lambda state: state[0] < rounds,
        more_grads,
        (jnp.ones((), rounds.dtype), table_grad, table_square_sum),
    )
    square_part = jnp.sum(table_square_sum) + part_square
    totals = exchange.copies(jnp.stack([square_part, loss_part]), ALL, devices)
    total_square, loss_value = jnp.sum(totals, axis=0)
    grad_norm = jnp.sqrt(total_square)
    factor = jnp.minimum(1.0, clip_norm / grad_norm)
    (
        norms,
        layer_first,
        layer_second,
        layer_dir,
        position_first,
        position_second,
        position_dir,
        small_first,
        small_second,
        small_dir,
    ) = update_norms(
        totals,
        (embed_table, table_moment, table_square, table_grad),
        (layer_weights, layer_moment, layer_square, layer_grad),
        (position_table, position_moment, position_square, position_grad),
        (small_params, small_moment, small_square, small_grad),
        split,
        lax.axis_index("dp"),
    )
    factor_late, norms = lax.optimization_barrier((factor, norms))
    pairs = exchange.copies(norms[:6, :2].reshape(-1), ALL, devices)
    table_first, table_second, _ = adam_moments(
        embed_table, table_moment, table_square, table_grad, factor_late
    )
    trust_norms = jnp.sqrt(jnp.sum(pairs, axis=0)).reshape(6, 2)
    table_next, layer_next, position_next, small_next = final_update(
        pairs,
        (embed_table, table_first, table_second),
        (
            layer_weights,
            layer_dir,
            position_table,
            position_dir,
            small_params,
            small_dir,
        ),
    )
    return (
        loss_value,
        grad_norm,
        table_next,
        table_first,
        table_second,
        layer_next,
        layer_first,
        layer_second,
        position_next,
        position_first,
        position_second,
        small_next,
        small_first,
        small_second,
        trust_norms,
    )


def solution(mesh):
    dp_devs, owners = mesh.devices.shape
    fine = Mesh(mesh.devices.reshape(dp_devs, owners // 4, 2, 2), ALL)
    rows, inner = P(ALL, None), P(None, ALL)
    table, layer = P(VOC, None), P(None, ALL, None)
    return jax.shard_map(
        on_device,
        mesh=fine,
        in_specs=(rows,) * 3 + (P(ALL),) + (table,) * 3 + (layer,) * 3 + (inner,) * 6,
        out_specs=(P(), P()) + (table,) * 3 + (layer,) * 3 + (inner,) * 6 + (P(),),
        check_vma=False,
    )
```

```python
import jax
import jax.numpy as jnp
from jax import lax
from jax.experimental import pallas as pl
from jax.experimental.pallas import tpu as pltpu
from jax.sharding import Mesh
from jax.sharding import PartitionSpec as P

HEADS = 12
HD = 64
MASK_ID = 103
NCORP = 4
STEP = 5
CAP = 64


clip_norm = 0.1
learn_rate = 0.3
beta_first = 0.9
beta_second = 0.999
adam_eps = 1e-06
weight_decay = 0.01
norm_eps = 1e-05
masked_score = -1e30
BUCKET = 32
ALL = ("dp", "hi", "mid", "core")
VOC = ("hi", "mid", "core")
NEAR = ("mid", "core")
bfloat = jnp.bfloat16
single = jnp.float32


def plain_dot(left_op, right_op):
    return jnp.dot(left_op, right_op, preferred_element_type=single)


def trans_dot(left_op, right_op):
    return lax.dot_general(
        left_op, right_op, (((1,), (1,)), ((), ())), preferred_element_type=single
    )


def rows_dot(left_op, right_op):
    return lax.dot_general(
        left_op, right_op, (((0,), (0,)), ((), ())), preferred_element_type=single
    )


def column_sum(values):
    return jnp.sum(values.astype(single), axis=0)


def norm_forward(values, gain_row, bias_row):
    center = values - jnp.mean(values, axis=-1, keepdims=True)
    inverse = lax.rsqrt(jnp.mean(center * center, axis=-1, keepdims=True) + norm_eps)
    normed = center * inverse
    return (normed * gain_row + bias_row, (normed, inverse))


def norm_backward(upstream, kept_norm, gain_row):
    normed, inverse = kept_norm
    scaled = upstream * gain_row
    inner = (
        scaled
        - jnp.mean(scaled, axis=-1, keepdims=True)
        - normed * jnp.mean(scaled * normed, axis=-1, keepdims=True)
    )
    return (inner * inverse, jnp.sum(upstream * normed, axis=0), jnp.sum(upstream, axis=0))


def pair_masks(rows):
    lane = lax.broadcasted_iota(jnp.int32, (rows, 2 * HD), 1)
    return lane < HD, lane >= HD


def head_probs(query_pair, key_pair, head_lanes, blocked):
    scores = trans_dot(jnp.where(head_lanes, query_pair, jnp.zeros_like(query_pair)), key_pair)
    scores = jnp.where(blocked, masked_score, scores * HD ** (-0.5))
    row_top = jnp.max(scores, axis=-1, keepdims=True)
    powers = jnp.exp(scores - row_top)
    return powers / jnp.sum(powers, axis=-1, keepdims=True)


def spread(column, lanes=128):
    return jnp.broadcast_to(column, (column.shape[0], lanes))


def row_of(ref, row):
    return ref[pl.ds(row, 1), :]


def attend_kernel(
    embed_ref, slot_ref, allowed_ref, shared_ref, weight_ref,
    key_ref, value_ref, query_ref, mixed_ref, middle_ref, normed_ref, inverse_ref,
    stream_ref, stream_normed_ref, stream_inverse_ref,
    init_ref, init_normed_ref, init_inverse_ref, position_ref, small_ref,
):
    step = pl.program_id(0)
    length = position_ref.shape[0]

    @pl.when(step == 0)
    def _():
        shared = shared_ref[...].astype(single).T
        position_ref[...] = shared[:length]
        small_ref[...] = shared[length : length + small_ref.shape[0]]
        gain, bias = row_of(small_ref, 0), row_of(small_ref, 1)
        stream, (normed, inverse) = norm_forward(embed_ref[...] + position_ref[...], gain, bias)
        stream_ref[...] = stream.astype(bfloat)
        stream_normed_ref[...] = normed
        stream_inverse_ref[...] = spread(inverse)
        chosen = plain_dot(slot_ref[...].astype(bfloat), position_ref[...].astype(bfloat))
        init, (normed, inverse) = norm_forward(chosen, gain, bias)
        init_ref[...] = init
        init_normed_ref[...] = normed
        init_inverse_ref[...] = spread(inverse)
        key_ref[...] = plain_dot(stream_ref[...], weight_ref[...]).astype(bfloat)

    @pl.when(step == 1)
    def _():
        value_ref[...] = (
            plain_dot(stream_ref[...], weight_ref[...]) + row_of(small_ref, 3)
        ).astype(bfloat)

    @pl.when(step == 2)
    def _():
        query_ref[...] = (
            plain_dot(init_ref[...].astype(bfloat), weight_ref[...]) + row_of(small_ref, 2)
        ).astype(bfloat)
        blocked = allowed_ref[...] == 0.0
        low, high = pair_masks(query_ref.shape[0])

        def one_pair(pair, carry):
            lanes = pl.ds(pl.multiple_of(pair * 2 * HD, 2 * HD), 2 * HD)
            query_pair, key_pair, value_pair = query_ref[:, lanes], key_ref[:, lanes], value_ref[:, lanes]
            left, right = (
                plain_dot(
                    head_probs(query_pair, key_pair, head_lanes, blocked).astype(bfloat), value_pair
                )
                for head_lanes in (low, high)
            )
            mixed_ref[:, lanes] = jnp.where(low, left, right).astype(bfloat)
            return carry

        lax.fori_loop(0, query_ref.shape[1] // (2 * HD), one_pair, 0)

    @pl.when(step == 3)
    def _():
        attend = plain_dot(mixed_ref[...], weight_ref[...]) + row_of(small_ref, 4)
        middle, (normed, inverse) = norm_forward(
            init_ref[...] + attend, row_of(small_ref, 5), row_of(small_ref, 6)
        )
        middle_ref[...] = middle
        normed_ref[...] = normed
        inverse_ref[...] = spread(inverse)


def kernel_call(body, name, steps, inputs, shapes, cost, scratch=()):
    fixed = lambda rank: lambda step: (0,) * rank

    def spec(shape, block, index):
        if block is None:
            return pl.BlockSpec(shape, fixed(len(shape)))
        if block == "any":
            return pl.BlockSpec(memory_space=pl.ANY)
        return pl.BlockSpec(block, index)

    return pl.pallas_call(
        body,
        grid=(steps,),
        in_specs=[spec(array.shape, block, index) for array, block, index in inputs],
        out_specs=[spec(shape, block, index) for shape, _, block, index in shapes],
        out_shape=[jax.ShapeDtypeStruct(shape, kind) for shape, kind, _, _ in shapes],
        scratch_shapes=list(scratch),
        cost_estimate=pl.CostEstimate(flops=cost[0] // 64, bytes_accessed=cost[1] // 64, transcendentals=0),
        name=name,
    )(*(array for array, _, _ in inputs))


def whole(array):
    return array, None, None


def attend_forward(embed_rows, slot_hot, allowed, weights, length, small_count):
    width = embed_rows.shape[1]
    slots = slot_hot.shape[0]
    out = lambda rows, kind, columns=width: ((rows, columns), kind, None, None)
    shared = weights.shape[1] - 12 * width
    return kernel_call(
        attend_kernel,
        "attention_forward",
        4,
        [
            whole(embed_rows),
            whole(slot_hot),
            whole(allowed),
            (weights, (width, shared), lambda step: (0, 12 * width // shared)),
            (
                weights,
                (width, width),
                lambda step: (0, jnp.where(step == 3, 3, (step + 1) % 3)),
            ),
        ],
        [
            out(length, bfloat), out(length, bfloat), out(slots, bfloat), out(slots, bfloat),
            out(slots, single), out(slots, single), out(slots, single, 128),
            out(length, bfloat), out(length, single), out(length, single, 128),
            out(slots, single), out(slots, single), out(slots, single, 128),
            out(length, single), out(small_count, single),
        ],
        (
            4 * length * width * width + 8 * slots * length * width,
            8 * width * width,
            HEADS * slots * length,
        ),
    )


def erf_half(hidden):
    return 0.5 * (1.0 + lax.erf(hidden * 0.5**0.5))


def feed_kernel(
    middle_ref, small_ref, up_ref, down_ref,
    middle_b_ref, hidden_ref, active_ref, output_ref, normed_ref, inverse_ref, total_ref,
):
    step = pl.program_id(0)

    @pl.when(step == 0)
    def _():
        middle_b_ref[...] = middle_ref[...].astype(bfloat)
        total_ref[...] = middle_ref[...] + row_of(small_ref, 11)

    hidden = plain_dot(middle_b_ref[...], up_ref[...]) + row_of(small_ref, 7 + step)
    hidden_ref[...] = hidden
    active = (hidden * erf_half(hidden)).astype(bfloat)
    active_ref[...] = active
    total_ref[...] += trans_dot(active, down_ref[...])

    @pl.when(step == pl.num_programs(0) - 1)
    def _():
        output, (normed, inverse) = norm_forward(
            total_ref[...], row_of(small_ref, 12), row_of(small_ref, 13)
        )
        output_ref[...] = output.astype(bfloat)
        normed_ref[...] = normed
        inverse_ref[...] = spread(inverse)


def feed_forward(middle, small_full, weights):
    slots, width = middle.shape
    wide = lambda kind: ((slots, 4 * width), kind, (slots, width), lambda step: (0, step))
    out = lambda kind, columns=width: ((slots, columns), kind, None, None)
    return kernel_call(
        feed_kernel,
        "feed_forward",
        4,
        [
            whole(middle),
            whole(small_full),
            (weights, (width, width), lambda step: (0, 4 + step)),
            (weights, (width, width), lambda step: (0, 8 + step)),
        ],
        [
            out(bfloat), wide(single), wide(bfloat), out(bfloat), out(single), out(single, 128),
        ],
        (16 * slots * width * width, 16 * width * width, 4 * slots * width),
        [pltpu.VMEM((slots, width), single)],
    )


def norm_back(upstream, normed, inverse, gain_row):
    return norm_backward(upstream, (normed, inverse), gain_row)


def feed_back_kernel(
    parts_ref, normed_ref, inverse_ref, hidden_ref, small_ref, mid_normed_ref, mid_inverse_ref,
    up_ref, down_ref,
    d_branch_ref, d_hidden_ref, d_pre_ref, d_attend_ref, sums_ref, d_middle_ref,
):
    step = pl.program_id(0)

    @pl.when(step == 0)
    def _():
        sums_ref[...] = jnp.zeros_like(sums_ref)
        d_sum, gain, bias = norm_back(
            jnp.sum(parts_ref[...], axis=0), normed_ref[...], inverse_ref[:, :1], row_of(small_ref, 12)
        )
        d_branch = d_sum.astype(bfloat)
        d_branch_ref[...] = d_branch
        d_middle_ref[...] = d_sum
        sums_ref[pl.ds(6, 1), :] = column_sum(d_branch)[None]
        sums_ref[pl.ds(7, 1), :] = gain[None]
        sums_ref[pl.ds(8, 1), :] = bias[None]

    hidden = hidden_ref[...]
    slope = erf_half(hidden) + hidden * jnp.exp(-0.5 * hidden * hidden) * (2.0 * jnp.pi) ** (-0.5)
    d_hidden = (plain_dot(d_branch_ref[...], down_ref[...]) * slope).astype(bfloat)
    d_hidden_ref[...] = d_hidden
    sums_ref[pl.ds(2 + step, 1), :] = column_sum(d_hidden)[None]
    d_middle_ref[...] += trans_dot(d_hidden, up_ref[...])

    @pl.when(step == pl.num_programs(0) - 1)
    def _():
        d_pre, gain, bias = norm_back(
            d_middle_ref[...], mid_normed_ref[...], mid_inverse_ref[:, :1], row_of(small_ref, 5)
        )
        d_pre_ref[...] = d_pre
        d_attend_ref[...] = d_pre.astype(bfloat)
        sums_ref[pl.ds(0, 1), :] = gain[None]
        sums_ref[pl.ds(1, 1), :] = bias[None]


def feed_backward(parts, normed, inverse, hidden, small_full, mid_normed, mid_inverse, weights):
    slots, width = normed.shape
    block = (slots, width), lambda step: (0, step)
    out = lambda kind, rows=slots: ((rows, width), kind, None, None)
    return kernel_call(
        feed_back_kernel,
        "feed_backward",
        4,
        [
            whole(parts),
            whole(normed),
            whole(inverse),
            (hidden,) + block,
            whole(small_full),
            whole(mid_normed),
            whole(mid_inverse),
            (weights, (width, width), lambda step: (0, 4 + step)),
            (weights, (width, width), lambda step: (0, 8 + step)),
        ],
        [
            out(bfloat), ((slots, 4 * width), bfloat) + block, out(single), out(bfloat),
            out(single, 16),
        ],
        (16 * slots * width * width, 16 * width * width, 8 * slots * width),
        [pltpu.VMEM((slots, width), single)],
    )


def attend_back_kernel(
    d_attend_ref, key_ref, value_ref, query_ref, allowed_ref, weight_ref,
    d_query_ref, d_key_ref, d_value_ref, d_mixed_ref,
):
    d_mixed_ref[...] = trans_dot(d_attend_ref[...], weight_ref[...]).astype(bfloat)
    blocked = allowed_ref[...] == 0.0
    slots, length = blocked.shape
    low, high = pair_masks(slots)
    low_long, _ = pair_masks(length)
    scale = HD ** (-0.5)

    def one_pair(pair, carry):
        lanes = pl.ds(pl.multiple_of(pair * 2 * HD, 2 * HD), 2 * HD)
        query_pair, key_pair, value_pair = query_ref[:, lanes], key_ref[:, lanes], value_ref[:, lanes]
        mixed_pair = d_mixed_ref[:, lanes]
        found = []
        for head_lanes in (low, high):
            probs = head_probs(query_pair, key_pair, head_lanes, blocked)
            d_probs = trans_dot(
                jnp.where(head_lanes, mixed_pair, jnp.zeros_like(mixed_pair)), value_pair
            )
            inner = jnp.sum(probs * d_probs, axis=-1, keepdims=True)
            d_scores = (probs * (d_probs - inner)).astype(bfloat)
            found.append(
                (
                    plain_dot(d_scores, key_pair) * scale,
                    rows_dot(d_scores, query_pair) * scale,
                    rows_dot(probs.astype(bfloat), mixed_pair),
                )
            )
        d_query_ref[:, lanes] = jnp.where(low, found[0][0], found[1][0]).astype(bfloat)
        d_key_ref[:, lanes] = jnp.where(low_long, found[0][1], found[1][1]).astype(bfloat)
        d_value_ref[:, lanes] = jnp.where(low_long, found[0][2], found[1][2]).astype(bfloat)
        return carry

    lax.fori_loop(0, query_ref.shape[1] // (2 * HD), one_pair, 0)


def attend_backward(d_attend, key_rows, value_rows, query_rows, allowed, weights):
    length, width = key_rows.shape
    slots = d_attend.shape[0]
    out = lambda rows: ((rows, width), bfloat, None, None)
    return kernel_call(
        attend_back_kernel,
        "attention_backward",
        1,
        [
            whole(d_attend),
            whole(key_rows),
            whole(value_rows),
            whole(query_rows),
            whole(allowed),
            (weights, (width, width), lambda step: (0, 3)),
        ],
        [out(slots), out(length), out(length)],
        (
            2 * slots * width * width + 20 * slots * length * width,
            2 * width * width,
            HEADS * slots * length,
        ),
        [pltpu.VMEM((slots, width), bfloat)],
    )


def project_back_kernel(
    d_pre_ref, d_query_ref, d_key_ref, d_value_ref, slot_ref, hidden_row_ref, small_ref,
    normed_ref, inverse_ref, init_normed_ref, init_inverse_ref, weight_ref, ahead_ref,
    embed_ref, position_ref, sums_ref, d_stream_ref, d_init_ref,
):
    step = pl.program_id(0)

    @pl.when(step == 0)
    def _():
        d_init_ref[...] = d_pre_ref[...] + trans_dot(d_query_ref[...], weight_ref[...])

    @pl.when(step == 1)
    def _():
        d_stream_ref[...] = trans_dot(d_key_ref[...], weight_ref[...])

    @pl.when(step == 2)
    def _():
        gain_row = row_of(small_ref, 0)
        d_stream = d_stream_ref[...] + trans_dot(d_value_ref[...], weight_ref[...])
        d_start, gain_init, bias_init = norm_back(
            d_init_ref[...], init_normed_ref[...], init_inverse_ref[:, :1], gain_row
        )
        d_embed, gain, bias = norm_back(
            d_stream, normed_ref[...], inverse_ref[:, :1], gain_row
        )
        position_ref[...] = d_embed + lax.dot_general(
            slot_ref[...],
            d_start,
            (((0,), (0,)), ((), ())),
            precision=lax.Precision.HIGHEST,
            preferred_element_type=single,
        )
        embed_b = d_embed.astype(bfloat)
        embed_ref[...] = embed_b
        sums_ref[...] = jnp.zeros_like(sums_ref)
        sums_ref[pl.ds(0, 1), :] = (gain_init + gain)[None]
        sums_ref[pl.ds(1, 1), :] = (bias_init + bias)[None]
        sums_ref[pl.ds(2, 1), :] = column_sum(d_query_ref[...])[None]
        sums_ref[pl.ds(3, 1), :] = column_sum(d_value_ref[...])[None]
        sums_ref[pl.ds(4, 1), :] = column_sum(d_pre_ref[...].astype(bfloat))[None]
        masked = jnp.where(hidden_row_ref[:, :1] > 0.0, embed_b.astype(single), 0.0)
        sums_ref[pl.ds(5, 1), :] = jnp.sum(masked, axis=0)[None]


def project_backward(
    d_pre, d_query, d_key, d_value, slot_hot, hidden_rows, small_full,
    normed, inverse, init_normed, init_inverse, weights, ahead,
):
    length, width = normed.shape
    slots = d_pre.shape[0]
    arrays = (
        d_pre, d_query, d_key, d_value, slot_hot, hidden_rows, small_full,
        normed, inverse, init_normed, init_inverse,
    )
    return kernel_call(
        project_back_kernel,
        "projection_backward",
        3,
        [whole(array) for array in arrays]
        + [(weights, (width, width), lambda step: (0, step)), (ahead, "any", None)],
        [
            ((length, width), bfloat, None, None),
            ((length, width), single, None, None),
            ((8, width), single, None, None),
        ],
        (5 * length * width * width, 6 * width * width, 0),
        [pltpu.VMEM((length, width), single), pltpu.VMEM((slots, width), single)],
    )


def adam_direction(weight_arr, new_first, new_second):
    first_scale, second_scale = 1.0 / (1.0 - beta_first**STEP), 1.0 / (1.0 - beta_second**STEP)
    return (new_first * first_scale) / (
        jnp.sqrt(new_second * second_scale) + adam_eps
    ) + weight_decay * weight_arr


def adam_moments(weight_arr, first_mom, second_mom, gradient, factor):
    clipped = gradient * factor
    new_first = beta_first * first_mom + (1.0 - beta_first) * clipped
    new_second = beta_second * second_mom + (1.0 - beta_second) * clipped * clipped
    return (new_first, new_second, adam_direction(weight_arr, new_first, new_second))


def row_block(count, most=240):
    return most if count % most == 0 else count


def lookup_kernel(parts, *refs):
    step = pl.program_id(0)
    head_refs, (asked_ref, given_ref, side_ref, grad_ref, square_ref) = refs[:parts], refs[parts:]
    rows, width = grad_ref.shape
    base = step * rows
    row_hot = asked_ref[...] == base + lax.broadcasted_iota(
        jnp.int32, (rows, asked_ref.shape[1]), 0
    )
    grad = plain_dot(row_hot.astype(bfloat), given_ref[...])
    for head_ref in head_refs:
        grad += head_ref[...].astype(single)
    grad_ref[...] = grad
    place = base + lax.broadcasted_iota(jnp.int32, (rows, width), 0)
    own = (place >= side_ref[0]) & (place < side_ref[1])

    @pl.when(step == 0)
    def _():
        square_ref[...] = jnp.zeros_like(square_ref)

    square_ref[...] += jnp.sum(jnp.where(own, grad * grad, 0.0), axis=0, keepdims=True)


def lookup_grad(heads, parts, asked_rows, given, sides):
    vrows, width = heads.shape[0] // parts, heads.shape[1]
    rows = vrows // 4
    block = pl.BlockSpec((rows, width), lambda step: (step, 0))
    whole_spec = lambda array: pl.BlockSpec(array.shape, lambda step: (0, 0))
    return pl.pallas_call(
        lambda *refs: lookup_kernel(parts, *refs),
        grid=(4,),
        in_specs=[
            pl.BlockSpec((rows, width), lambda step, part=part: (4 * part + step, 0))
            for part in range(parts)
        ]
        + [
            whole_spec(asked_rows),
            whole_spec(given),
            pl.BlockSpec(memory_space=pltpu.SMEM),
        ],
        out_specs=[block, pl.BlockSpec((1, width), lambda step: (0, 0))],
        out_shape=[
            jax.ShapeDtypeStruct((vrows, width), single),
            jax.ShapeDtypeStruct((1, width), single),
        ],
        cost_estimate=pl.CostEstimate(flops=0, bytes_accessed=0, transcendentals=0),
        name="table_gradient",
    )(*[heads] * parts, asked_rows, given, sides)


def full_sum(values):
    return jnp.sum(jnp.sum(values, axis=1, keepdims=True), axis=0, keepdims=True)


def pair_row(weight_sum, dir_sum):
    lane = lax.broadcasted_iota(jnp.int32, (1, 128), 1)
    return jnp.where(lane == 0, weight_sum, dir_sum)


def norms_kernel(offset_ref, *refs):
    total_ref, table_refs, layer_refs, position_refs, small_refs = (
        refs[0], refs[1:5], refs[5:9], refs[9:13], refs[13:17],
    )
    norms_ref, layer_out, position_out, small_out = refs[17], refs[18:21], refs[21:24], refs[24:27]
    sums_ref = refs[27]
    step = pl.program_id(0)
    total_square = jnp.sum(total_ref[...], axis=0, keepdims=True)[:, :1]
    factor = jnp.minimum(1.0, clip_norm / jnp.sqrt(total_square))

    @pl.when(step == 0)
    def _():
        sums_ref[...] = jnp.zeros_like(sums_ref)
        norms_ref[...] = jnp.zeros_like(norms_ref)
        for row, group_refs, outs in ((4, position_refs, position_out), (5, small_refs, small_out)):
            weight_arr = group_refs[0][...]
            first, second, direction = adam_moments(
                weight_arr, group_refs[1][...], group_refs[2][...], group_refs[3][...], factor
            )
            for ref, value in zip(outs, (first, second, direction)):
                ref[...] = value
            norms_ref[pl.ds(row, 1), :] = pair_row(
                full_sum(weight_arr * weight_arr), full_sum(direction * direction)
            )

    @pl.when(step < 3)
    def _():
        weight_arr, first_mom, second_mom, gradient = (ref[0] for ref in layer_refs)
        first, second, direction = adam_moments(
            weight_arr, first_mom, second_mom, gradient, factor
        )
        for ref, value in zip(layer_out, (first, second, direction)):
            ref[0] = value
        norms_ref[pl.ds(1 + step, 1), :] = pair_row(
            full_sum(weight_arr * weight_arr), full_sum(direction * direction)
        )

    weight_arr = table_refs[0][...]
    _, _, direction = adam_moments(
        weight_arr, table_refs[1][...], table_refs[2][...], table_refs[3][...], factor
    )
    sums_ref[pl.ds(0, 1), :] += jnp.sum(weight_arr * weight_arr, axis=0, keepdims=True)
    sums_ref[pl.ds(1, 1), :] += jnp.sum(direction * direction, axis=0, keepdims=True)

    @pl.when(step == pl.num_programs(0) - 1)
    def _():
        norms_ref[pl.ds(0, 1), :] = pair_row(
            full_sum(sums_ref[pl.ds(0, 1), :]), full_sum(sums_ref[pl.ds(1, 1), :])
        )


def update_norms(totals, table, layer, position, small, split, dp_index):
    vrows, width = table[0].shape
    rows = row_block(split, 240)
    if split // rows < 3:
        rows = split // 3
    one_part = pl.BlockSpec(
        (1,) + layer[0].shape[1:], lambda step, offset: (jnp.minimum(step, 2), 0, 0)
    )
    fixed = lambda array: pl.BlockSpec(
        array.shape, lambda step, offset, rank=array.ndim: (0,) * rank
    )
    part = pl.BlockSpec((rows, width), lambda step, offset: (offset[0] + step, 0))
    groups = tuple(layer) + tuple(position) + tuple(small)
    outs = [
        jax.ShapeDtypeStruct(group[0].shape, single)
        for group in (layer, position, small)
        for _ in range(3)
    ]
    norms = jax.ShapeDtypeStruct((8, 128), single)
    return pl.pallas_call(
        norms_kernel,
        grid_spec=pltpu.PrefetchScalarGridSpec(
            num_scalar_prefetch=1,
            grid=(split // rows,),
            in_specs=[fixed(totals)]
            + [part] * 4
            + [one_part] * 4
            + [fixed(array) for array in groups[4:]],
            out_specs=[fixed(norms)] + [one_part] * 3 + [fixed(out) for out in outs[3:]],
            scratch_shapes=[pltpu.VMEM((8, width), single)],
        ),
        out_shape=[norms] + outs,
        cost_estimate=pl.CostEstimate(flops=0, bytes_accessed=0, transcendentals=0),
        name="update_norms",
    )((dp_index * (split // rows)).astype(jnp.int32)[None], totals, *table, *groups)


def final_kernel(
    pairs_ref, weight_ref, first_ref, second_ref,
    layer_ref, layer_dir_ref, position_ref, position_dir_ref, small_ref, small_dir_ref,
    next_ref, layer_next_ref, position_next_ref, small_next_ref,
):
    roots = jnp.sqrt(jnp.sum(pairs_ref[...], axis=0, keepdims=True))

    def rate(group):
        return learn_rate * (
            roots[:, 2 * group : 2 * group + 1] / roots[:, 2 * group + 1 : 2 * group + 2]
        )

    weight_arr = weight_ref[...]
    direction = adam_direction(weight_arr, first_ref[...], second_ref[...])
    next_ref[...] = weight_arr - rate(0) * direction

    step = pl.program_id(0)
    for part in range(3):

        @pl.when(step == part)
        def _():
            layer_next_ref[0] = layer_ref[0] - rate(1 + part) * layer_dir_ref[0]

    @pl.when(step == 0)
    def _():
        position_next_ref[...] = position_ref[...] - rate(4) * position_dir_ref[...]
        small_next_ref[...] = small_ref[...] - rate(5) * small_dir_ref[...]


def final_update(pairs, table, groups):
    vrows, width = table[0].shape
    rows = row_block(vrows)
    fixed = lambda array: pl.BlockSpec(array.shape, lambda step, rank=array.ndim: (0,) * rank)
    block = pl.BlockSpec((rows, width), lambda step: (step, 0))
    one_part = pl.BlockSpec((1,) + groups[0].shape[1:], lambda step: (jnp.minimum(step, 2), 0, 0))
    outs = [jax.ShapeDtypeStruct(array.shape, single) for array in groups[::2]]
    return pl.pallas_call(
        final_kernel,
        grid=(vrows // rows,),
        in_specs=[fixed(pairs)]
        + [block] * 3
        + [one_part] * 2
        + [fixed(array) for array in groups[2:]],
        out_specs=[block, one_part] + [fixed(out) for out in outs[1:]],
        out_shape=[jax.ShapeDtypeStruct((vrows, width), single)] + outs,
        cost_estimate=pl.CostEstimate(flops=0, bytes_accessed=0, transcendentals=0),
        name="final_update",
    )(pairs, *table, *groups)


class Exchange:
    def __init__(self):
        self.last = None

    def __call__(self, values, axes):
        if self.last is not None:
            values, _ = lax.optimization_barrier((values, self.last))
        self.last = lax.all_to_all(values, axes, 0, 0, tiled=True)
        return self.last

    def copies(self, values, axes, count):
        return self(jnp.broadcast_to(values[None], (count,) + values.shape), axes)

    def columns(self, values, axes, count):
        rows, width = values.shape
        blocks = values.reshape(rows, count, width // count).transpose(1, 0, 2)
        return self(blocks, axes).reshape(count * rows, -1)

    def rows(self, values, count):
        return self(values.reshape(count, values.shape[0] // count, values.shape[1]), ALL)


def side_by_side(blocks):
    return blocks.transpose(1, 0, 2).reshape(blocks.shape[1], -1)


def after(values, *waits):
    for wait in waits:
        values = values + (wait.reshape(-1)[0] > 3.395e38).astype(values.dtype)
    return values


def masked_total(mask, values):
    return jnp.sum(jnp.where(mask, values, 0), axis=-1)


def slot_layout(pred_row, order_row, token_row):
    length = pred_row.shape[0]
    index = jnp.arange(length)
    before = index[None, :] <= index[:, None]
    seen = masked_total(before, pred_row[None, :])
    masked = jnp.sum(pred_row)
    place = jnp.where(pred_row == 1, seen - 1, masked + index - seen)
    slot_hot = place[None, :] == jnp.arange(CAP)[:, None]
    rank_row = masked_total(order_row[None, :] == index[:, None], index[None, :])
    slot_rank = masked_total(slot_hot, rank_row[None, :])
    slot_target = masked_total(slot_hot, token_row[None, :])
    slot_pos = masked_total(slot_hot, index[None, :])
    allowed = rank_row[None, :] <= slot_rank[:, None]
    return slot_hot, slot_pos, slot_target, allowed, masked


def bucket_layout(content, vrows):
    index = jnp.arange(content.shape[0])
    same = content[None, :] == content[:, None]
    first = jnp.min(jnp.where(same, index[None, :], content.shape[0]), axis=1)
    is_first = first == index
    owner = content // vrows
    ahead = (owner[None, :] == owner[:, None]) & is_first[None, :] & (index[None, :] < first[:, None])
    return owner, jnp.sum(ahead.astype(jnp.int32), axis=1)


def bucket_round(content, owner, place, turn, owners, vrows):
    usable = BUCKET - 1
    local = place - turn * usable
    taken = (local >= 0) & (local < usable)
    flat = jnp.where(taken, owner * BUCKET + local, -1)
    hot = flat[None, :] == jnp.arange(owners * BUCKET)[:, None]
    wanted = jnp.max(jnp.where(hot, (content - owner * vrows)[None, :], -1), axis=1)
    return hot.astype(bfloat), wanted.reshape(owners, BUCKET)


def on_device(
    token_ids,
    pred_mask,
    fact_order,
    corpus,
    embed_table,
    table_moment,
    table_square,
    layer_weights,
    layer_moment,
    layer_square,
    position_table,
    position_moment,
    position_square,
    small_params,
    small_moment,
    small_square,
):
    exchange = Exchange()
    dp_devs = lax.axis_size("dp")
    owners = lax.axis_size(VOC)
    devices = dp_devs * owners
    vrows, width = embed_table.shape
    length = token_ids.shape[1]
    feed = layer_weights.shape[2]
    shared = jnp.concatenate([position_table, small_params]).T
    shared_rows = shared.shape[1]
    shared = jnp.pad(shared, ((0, 0), (0, -shared_rows % 128)))
    shard = jnp.concatenate([layer_weights[0], layer_weights[1], layer_weights[2], shared], axis=1)
    shard = lax.all_gather(shard.astype(bfloat), ALL, axis=0, tiled=True)
    table_b = embed_table.astype(bfloat)
    token_row = token_ids[0]
    pred_row = pred_mask[0]
    first_row = lax.axis_index(VOC) * vrows
    content = jnp.where(pred_row == 1, MASK_ID, token_row)
    slot_hot, slot_pos, slot_target, allowed, masked = slot_layout(pred_row, fact_order[0], token_row)
    owner, place = bucket_layout(content, vrows)
    hot, wanted = bucket_round(content, owner, place, 0, owners, vrows)
    note = jnp.concatenate(
        [slot_target, slot_pos, jnp.stack([masked, corpus[0], jnp.max(place)])]
    )
    packet = jnp.concatenate(
        [wanted, jnp.broadcast_to(note[None], (owners, note.shape[0]))], axis=1
    )
    packet = jnp.pad(packet, ((0, 0), (0, 256 - packet.shape[1])))
    packet = jnp.broadcast_to(packet[None], (dp_devs,) + packet.shape)
    packet = exchange(packet.reshape(devices, packet.shape[-1]), ALL)
    asked = packet[:, :BUCKET]
    tail = BUCKET + 2 * CAP
    counts_all = packet[:, tail]
    corpus_all = packet[:, tail + 1]
    rounds = jnp.max(packet[:, tail + 2]) // (BUCKET - 1) + 1
    group = lax.axis_index("dp") * owners
    outer = lax.axis_size("hi")

    def group_order(values):
        return values.reshape(outer, 2, 2, CAP).transpose(2, 1, 0, 3).reshape(-1)

    group_asked = lax.dynamic_slice_in_dim(asked, group, owners, 0)
    group_target = group_order(
        lax.dynamic_slice_in_dim(packet[:, BUCKET : BUCKET + CAP], group, owners, 0)
    )
    corpus_hot = corpus_all[:, None] == jnp.arange(NCORP)[None, :]
    corpus_counts = jnp.sum(jnp.where(corpus_hot, counts_all[:, None], 0), axis=0)
    seq_count = masked_total(corpus_hot, corpus_counts[None, :])
    seq_weight = 1.0 / (NCORP * seq_count.astype(single))
    slot_weight = jnp.where(
        jnp.arange(CAP)[None, :] < counts_all[:, None], seq_weight[:, None], 0.0
    )
    group_weight = group_order(lax.dynamic_slice_in_dim(slot_weight, group, owners, 0))

    def serve(asked_rows):
        served = jnp.take(table_b, jnp.maximum(asked_rows, 0).reshape(-1), axis=0)
        return served.reshape(owners, BUCKET, width)

    arrived = exchange(serve(group_asked), VOC)
    embed_rows = rows_dot(hot, arrived.reshape(-1, width))

    def more_rows(state):
        turn, rows = state
        hot_t, wanted_t = bucket_round(content, owner, place, turn, owners, vrows)
        asked_t = lax.all_to_all(wanted_t, VOC, 0, 0, tiled=True)
        arrived_t = lax.all_to_all(serve(asked_t), VOC, 0, 0, tiled=True)
        return turn + 1, rows + rows_dot(hot_t, arrived_t.reshape(-1, width))

    _, embed_rows = lax.while_loop(
        lambda state: state[0] < rounds, more_rows, (jnp.ones((), rounds.dtype), embed_rows)
    )
    few = devices <= 32
    near = 4
    allowed = allowed.astype(single)
    slot_hot = slot_hot.astype(single)
    (
        key_rows,
        value_rows,
        query_rows,
        mixed_b,
        middle,
        mid_normed,
        mid_inverse,
        stream_b,
        stream_normed,
        stream_inverse,
        query_init,
        init_normed,
        init_inverse,
        position_full,
        small_full,
    ) = attend_forward(embed_rows, slot_hot, allowed, shard, length, small_params.shape[0])
    middle_b, hidden, active_b, output_b, end_normed, end_inverse = feed_forward(
        middle, small_full, shard
    )
    if few:
        kept_rows = jnp.concatenate([mixed_b, middle_b], axis=1)
        kept_all = lax.all_gather(kept_rows, ALL, axis=0, tiled=True)
        stream_all = lax.all_gather(stream_b, NEAR, axis=0, tiled=True)
    group_rows = exchange.copies(output_b, "hi", outer).reshape(-1, width)
    group_rows = exchange.copies(group_rows, "mid", 2).reshape(-1, width)
    group_rows = exchange.copies(group_rows, "core", 2).reshape(-1, width)
    logits = trans_dot(group_rows, table_b)
    local_target = group_target - first_row
    target_hit = jnp.arange(vrows)[None, :] == local_target[:, None]
    row_top = jnp.max(logits, axis=1)
    row_total = jnp.sum(jnp.exp(logits - row_top[:, None]), axis=1)
    row_target = jnp.sum(jnp.where(target_hit, logits, 0.0), axis=1)
    stats = exchange.copies(jnp.stack([row_top, row_total]), VOC, owners)
    top_all = jnp.max(stats[:, 0], axis=0)
    total_all = jnp.sum(stats[:, 1] * jnp.exp(stats[:, 0] - top_all[None]), axis=0)
    log_total = top_all + jnp.log(total_all)
    own_place = lax.axis_index(("core", "mid", "hi"))
    own_total = lax.dynamic_slice_in_dim(log_total * group_weight, own_place * CAP, CAP, 0)
    loss_part = jnp.sum(own_total) - jnp.sum(row_target * group_weight)
    d_logits = (
        group_weight[:, None] * (jnp.exp(logits - log_total[:, None]) - target_hit.astype(single))
    ).astype(bfloat)
    def swapped(axis, part):
        side = lax.axis_index(axis)
        theirs = lax.ppermute(part(1 - side), axis, [(0, 1), (1, 0)])
        return part(side) + theirs

    half = owners * CAP // 2

    def rows_half(side):
        return plain_dot(lax.dynamic_slice_in_dim(d_logits, side * half, half, 0), table_b)

    d_output = swapped("core", rows_half)
    quarter = half // 2
    d_half = d_output
    d_output = swapped(
        "mid", lambda side: lax.dynamic_slice_in_dim(d_half, side * quarter, quarter, 0)
    )
    grad_head = rows_dot(d_logits, group_rows)
    head_b = grad_head.astype(bfloat)
    d_output, head_b = lax.optimization_barrier((d_output, head_b))
    if few:
        head_b = after(head_b, stream_all)
    heads = lax.all_gather(head_b, "dp", axis=0, tiled=True)
    d_output = exchange(d_output.reshape(outer, CAP, width), "hi")
    if few:
        d_output, kept_all = lax.optimization_barrier((d_output, kept_all))
    d_branch, d_hidden, d_pre, d_attend, sums_feed = feed_backward(
        d_output,
        end_normed,
        end_inverse,
        hidden,
        small_full,
        mid_normed,
        mid_inverse,
        shard,
    )
    if few:
        wide = feed // devices
        both = jnp.concatenate(
            [
                d_hidden.reshape(CAP, devices, -1),
                d_attend.reshape(CAP, devices, -1),
            ],
            axis=2,
        ).reshape(CAP, -1)
        both = exchange.columns(both, ALL, devices)
        branch_all = lax.all_gather(d_branch, ALL, axis=0, tiled=True)
    d_query, d_key, d_value = attend_backward(
        d_attend, key_rows, value_rows, query_rows, allowed, shard
    )
    if few:
        piece = width // near
        pairs = jnp.concatenate(
            [d_key.reshape(length, near, piece), d_value.reshape(length, near, piece)], axis=2
        ).transpose(1, 0, 2)
        asks = d_query.reshape(CAP, near, piece).transpose(1, 0, 2)
        asks = jnp.concatenate([asks[:, : CAP // 2], asks[:, CAP // 2 :]], axis=2)
        pairs = exchange(jnp.concatenate([pairs, asks], axis=1), NEAR)
    hidden_rows = spread((content == MASK_ID).astype(single)[:, None])
    embed_back, grad_position, sums_back = project_backward(
        d_pre,
        d_query,
        d_key,
        d_value,
        slot_hot,
        hidden_rows,
        small_full,
        stream_normed,
        stream_inverse,
        init_normed,
        init_inverse,
        shard,
        heads,
    )
    grad_small = jnp.concatenate([sums_back[:5], sums_feed[:9]])
    mask_sum = sums_back[5]
    mask_left = mask_sum - lax.reduce_precision(mask_sum, 8, 7)
    mask_owner = MASK_ID // vrows
    is_left = (jnp.arange(BUCKET) == BUCKET - 1)[None, :] & (
        jnp.arange(owners) == mask_owner
    )[:, None]

    def plain_exchange(values, axes):
        return lax.all_to_all(values, axes, 0, 0, tiled=True)

    def give(hot_rows, extra, send):
        rows = plain_dot(hot_rows, embed_back).reshape(owners, BUCKET, width)
        rows = jnp.where(is_left[:, :, None] & extra, mask_left[None, None, :], rows)
        return send(rows.astype(bfloat), VOC).reshape(-1, width)

    def of_both(rows):
        if dp_devs == 2:
            return jnp.concatenate([rows, lax.ppermute(rows, "dp", [(0, 1), (1, 0)])])
        return lax.all_gather(rows, "dp", axis=0, tiled=True)

    def both_groups(asked_rows):
        if dp_devs == 2:
            return jnp.roll(asked_rows, -group, axis=0)
        return asked_rows

    split = vrows // dp_devs
    sides = lax.axis_index("dp") * split + jnp.array([0, split])

    def into_rows(heads, parts, asked_rows, given, sides):
        return lookup_grad(heads, parts, both_groups(asked_rows).reshape(1, -1), given, sides)

    last = (jnp.arange(BUCKET) == BUCKET - 1)[None, :]
    left_row = jnp.where(lax.axis_index(VOC) == mask_owner, MASK_ID - first_row, -1)
    given = give(hot, True, exchange)

    if few:
        near_pos = packet[:, BUCKET + CAP : tail].reshape(dp_devs * outer, near * CAP)
        near_pos = lax.dynamic_index_in_dim(
            near_pos, lax.axis_index(("dp", "hi")), 0, False
        )
        init_rows = norm_forward(position_full, small_full[0], small_full[1])[0].astype(bfloat)
        init_hot = near_pos[:, None] == jnp.arange(length)[None, :]
        init_all = plain_dot(init_hot.astype(bfloat), init_rows).astype(bfloat)
        asks = pairs[:, length:]
        asks = jnp.concatenate([asks[..., :piece], asks[..., piece:]], axis=1)
        grad_pair = rows_dot(stream_all, pairs[:, :length].reshape(near * length, -1))
        grad_ask = rows_dot(init_all, asks.reshape(near * CAP, piece))
        share = width // devices
        active_mine = exchange.columns(active_b, ALL, devices)
        grad_up = rows_dot(kept_all[:, width:], both[:, :wide])
        grad_out = rows_dot(kept_all[:, :width], both[:, wide:])
        grad_down = rows_dot(branch_all, active_mine)
        shared_grad = jnp.concatenate([grad_position, grad_small]).T
        results = jnp.concatenate(
            [grad_pair, grad_ask, grad_up, grad_down, grad_out, shared_grad], axis=1
        )
        results = results.astype(bfloat)
        given = after(given, jnp.max(results[0].astype(single)))
        results = exchange.rows(results, devices).astype(single)
        sides = after(sides, results)
        pieces = 3 * piece
        attn = jnp.sum(
            results[..., :pieces].reshape(dp_devs * outer, near, share, pieces), axis=0
        )
        shared_grad = jnp.sum(results[..., -shared_rows:], axis=0)
        single_parts = results[..., pieces:-shared_rows]
        part_square = (
            jnp.sum(attn * attn)
            + jnp.sum(single_parts * single_parts)
            + jnp.sum(shared_grad * shared_grad)
        )
        shared_grad = shared_grad.T
        position_grad, small_grad = shared_grad[:length], shared_grad[length:]
        grad_key, grad_value, grad_query = (
            side_by_side(attn[..., part * piece : (part + 1) * piece]) for part in range(3)
        )
        grad_up, grad_down, grad_out = (
            side_by_side(single_parts[..., low:high])
            for low, high in ((0, wide), (wide, 2 * wide), (2 * wide, None))
        )
        layer_grad = jnp.stack(
            [
                jnp.concatenate([grad_query, grad_key, grad_value, grad_out], axis=1),
                grad_up,
                grad_down,
            ]
        )
    else:
        whole = (
            jnp.concatenate(
                [
                    rows_dot(query_init.astype(bfloat), d_query),
                    rows_dot(stream_b, d_key),
                    rows_dot(stream_b, d_value),
                    rows_dot(mixed_b, d_attend),
                ],
                axis=1,
            ),
            rows_dot(middle_b, d_hidden),
            rows_dot(d_branch, active_b),
        )
        layer_grad = jnp.stack(
            [lax.psum_scatter(part, ALL, scatter_dimension=0, tiled=True) for part in whole]
        )
        shared_grad = jnp.concatenate([grad_position, grad_small]).T
        shared_grad = lax.psum_scatter(shared_grad, ALL, scatter_dimension=0, tiled=True).T
        position_grad, small_grad = shared_grad[:length], shared_grad[length:]
        part_square = jnp.sum(layer_grad * layer_grad) + jnp.sum(shared_grad * shared_grad)
    table_grad, table_square_sum = into_rows(
        heads, dp_devs, jnp.where(last, left_row, asked), of_both(given), sides
    )

    def more_grads(state):
        turn, grads, _ = state
        hot_t, wanted_t = bucket_round(content, owner, place, turn, owners, vrows)
        wanted_t = jnp.broadcast_to(wanted_t[None], (dp_devs,) + wanted_t.shape)
        asked_t = lax.all_to_all(
            wanted_t.reshape(devices, BUCKET), ALL, 0, 0, tiled=True
        )
        given_t = of_both(give(hot_t, False, plain_exchange))
        return (turn + 1,) + tuple(into_rows(grads, 1, asked_t, given_t, sides))

    _, table_grad, table_square_sum = lax.while_loop(
        lambda state: state[0] < rounds,
        more_grads,
        (jnp.ones((), rounds.dtype), table_grad, table_square_sum),
    )
    square_part = jnp.sum(table_square_sum) + part_square
    totals = exchange.copies(jnp.stack([square_part, loss_part]), ALL, devices)
    total_square, loss_value = jnp.sum(totals, axis=0)
    grad_norm = jnp.sqrt(total_square)
    factor = jnp.minimum(1.0, clip_norm / grad_norm)
    (
        norms,
        layer_first,
        layer_second,
        layer_dir,
        position_first,
        position_second,
        position_dir,
        small_first,
        small_second,
        small_dir,
    ) = update_norms(
        totals,
        (embed_table, table_moment, table_square, table_grad),
        (layer_weights, layer_moment, layer_square, layer_grad),
        (position_table, position_moment, position_square, position_grad),
        (small_params, small_moment, small_square, small_grad),
        split,
        lax.axis_index("dp"),
    )
    factor_late, norms = lax.optimization_barrier((factor, norms))
    pairs = exchange.copies(norms[:6, :2].reshape(-1), ALL, devices)
    table_first, table_second, _ = adam_moments(
        embed_table, table_moment, table_square, table_grad, factor_late
    )
    trust_norms = jnp.sqrt(jnp.sum(pairs, axis=0)).reshape(6, 2)
    table_next, layer_next, position_next, small_next = final_update(
        pairs,
        (embed_table, table_first, table_second),
        (
            layer_weights,
            layer_dir,
            position_table,
            position_dir,
            small_params,
            small_dir,
        ),
    )
    return (
        loss_value,
        grad_norm,
        table_next,
        table_first,
        table_second,
        layer_next,
        layer_first,
        layer_second,
        position_next,
        position_first,
        position_second,
        small_next,
        small_first,
        small_second,
        trust_norms,
    )


def solution(mesh):
    dp_devs, owners = mesh.devices.shape
    fine = Mesh(mesh.devices.reshape(dp_devs, owners // 4, 2, 2), ALL)
    rows, inner = P(ALL, None), P(None, ALL)
    table, layer = P(VOC, None), P(None, ALL, None)
    return jax.shard_map(
        on_device,
        mesh=fine,
        in_specs=(rows,) * 3 + (P(ALL),) + (table,) * 3 + (layer,) * 3 + (inner,) * 6,
        out_specs=(P(), P()) + (table,) * 3 + (layer,) * 3 + (inner,) * 6 + (P(),),
        check_vma=False,
    )
```

```python
import jax
import jax.numpy as jnp
from jax import lax
from jax.experimental import pallas as pl
from jax.experimental.pallas import tpu as pltpu
from jax.sharding import Mesh
from jax.sharding import PartitionSpec as P

HEADS = 12
HD = 64
MASK_ID = 103
NCORP = 4
STEP = 5
CAP = 64


clip_norm = 0.1
learn_rate = 0.3
beta_first = 0.9
beta_second = 0.999
adam_eps = 1e-06
weight_decay = 0.01
norm_eps = 1e-05
masked_score = -1e30
BUCKET = 32
ALL = ("dp", "hi", "mid", "core")
VOC = ("hi", "mid", "core")
NEAR = ("mid", "core")
bfloat = jnp.bfloat16
single = jnp.float32


def plain_dot(left_op, right_op):
    return jnp.dot(left_op, right_op, preferred_element_type=single)


def trans_dot(left_op, right_op):
    return lax.dot_general(
        left_op, right_op, (((1,), (1,)), ((), ())), preferred_element_type=single
    )


def rows_dot(left_op, right_op):
    return lax.dot_general(
        left_op, right_op, (((0,), (0,)), ((), ())), preferred_element_type=single
    )


def column_sum(values):
    return jnp.sum(values.astype(single), axis=0)


def norm_forward(values, gain_row, bias_row):
    center = values - jnp.mean(values, axis=-1, keepdims=True)
    inverse = lax.rsqrt(jnp.mean(center * center, axis=-1, keepdims=True) + norm_eps)
    normed = center * inverse
    return (normed * gain_row + bias_row, (normed, inverse))


def norm_backward(upstream, kept_norm, gain_row):
    normed, inverse = kept_norm
    scaled = upstream * gain_row
    inner = (
        scaled
        - jnp.mean(scaled, axis=-1, keepdims=True)
        - normed * jnp.mean(scaled * normed, axis=-1, keepdims=True)
    )
    return (inner * inverse, jnp.sum(upstream * normed, axis=0), jnp.sum(upstream, axis=0))


def pair_masks(rows):
    lane = lax.broadcasted_iota(jnp.int32, (rows, 2 * HD), 1)
    return lane < HD, lane >= HD


def head_probs(query_pair, key_pair, head_lanes, blocked):
    scores = trans_dot(jnp.where(head_lanes, query_pair, jnp.zeros_like(query_pair)), key_pair)
    scores = jnp.where(blocked, masked_score, scores * HD ** (-0.5))
    row_top = jnp.max(scores, axis=-1, keepdims=True)
    powers = jnp.exp(scores - row_top)
    return powers / jnp.sum(powers, axis=-1, keepdims=True)


def spread(column, lanes=128):
    return jnp.broadcast_to(column, (column.shape[0], lanes))


def row_of(ref, row):
    return ref[pl.ds(row, 1), :]


def attend_kernel(
    embed_ref, slot_ref, allowed_ref, shared_ref, weight_ref,
    key_ref, value_ref, query_ref, mixed_ref, middle_ref, normed_ref, inverse_ref,
    stream_ref, stream_normed_ref, stream_inverse_ref,
    init_ref, init_normed_ref, init_inverse_ref, position_ref, small_ref,
):
    step = pl.program_id(0)
    length = position_ref.shape[0]

    @pl.when(step == 0)
    def _():
        shared = shared_ref[...].astype(single).T
        position_ref[...] = shared[:length]
        small_ref[...] = shared[length : length + small_ref.shape[0]]
        gain, bias = row_of(small_ref, 0), row_of(small_ref, 1)
        stream, (normed, inverse) = norm_forward(embed_ref[...] + position_ref[...], gain, bias)
        stream_ref[...] = stream.astype(bfloat)
        stream_normed_ref[...] = normed
        stream_inverse_ref[...] = spread(inverse)
        chosen = plain_dot(slot_ref[...].astype(bfloat), position_ref[...].astype(bfloat))
        init, (normed, inverse) = norm_forward(chosen, gain, bias)
        init_ref[...] = init
        init_normed_ref[...] = normed
        init_inverse_ref[...] = spread(inverse)
        key_ref[...] = plain_dot(stream_ref[...], weight_ref[...]).astype(bfloat)

    @pl.when(step == 1)
    def _():
        value_ref[...] = (
            plain_dot(stream_ref[...], weight_ref[...]) + row_of(small_ref, 3)
        ).astype(bfloat)

    @pl.when(step == 2)
    def _():
        query_ref[...] = (
            plain_dot(init_ref[...].astype(bfloat), weight_ref[...]) + row_of(small_ref, 2)
        ).astype(bfloat)
        blocked = allowed_ref[...] == 0.0
        low, high = pair_masks(query_ref.shape[0])

        def one_pair(pair, carry):
            lanes = pl.ds(pl.multiple_of(pair * 2 * HD, 2 * HD), 2 * HD)
            query_pair, key_pair, value_pair = query_ref[:, lanes], key_ref[:, lanes], value_ref[:, lanes]
            left, right = (
                plain_dot(
                    head_probs(query_pair, key_pair, head_lanes, blocked).astype(bfloat), value_pair
                )
                for head_lanes in (low, high)
            )
            mixed_ref[:, lanes] = jnp.where(low, left, right).astype(bfloat)
            return carry

        lax.fori_loop(0, query_ref.shape[1] // (2 * HD), one_pair, 0)

    @pl.when(step == 3)
    def _():
        attend = plain_dot(mixed_ref[...], weight_ref[...]) + row_of(small_ref, 4)
        middle, (normed, inverse) = norm_forward(
            init_ref[...] + attend, row_of(small_ref, 5), row_of(small_ref, 6)
        )
        middle_ref[...] = middle
        normed_ref[...] = normed
        inverse_ref[...] = spread(inverse)


def kernel_call(body, name, steps, inputs, shapes, cost, scratch=()):
    fixed = lambda rank: lambda step: (0,) * rank

    def spec(shape, block, index):
        if block is None:
            return pl.BlockSpec(shape, fixed(len(shape)))
        if block == "any":
            return pl.BlockSpec(memory_space=pl.ANY)
        return pl.BlockSpec(block, index)

    return pl.pallas_call(
        body,
        grid=(steps,),
        in_specs=[spec(array.shape, block, index) for array, block, index in inputs],
        out_specs=[spec(shape, block, index) for shape, _, block, index in shapes],
        out_shape=[jax.ShapeDtypeStruct(shape, kind) for shape, kind, _, _ in shapes],
        scratch_shapes=list(scratch),
        cost_estimate=pl.CostEstimate(flops=cost[0] // 64, bytes_accessed=cost[1] // 64, transcendentals=0),
        name=name,
    )(*(array for array, _, _ in inputs))


def whole(array):
    return array, None, None


def attend_forward(embed_rows, slot_hot, allowed, weights, length, small_count):
    width = embed_rows.shape[1]
    slots = slot_hot.shape[0]
    out = lambda rows, kind, columns=width: ((rows, columns), kind, None, None)
    shared = weights.shape[1] - 12 * width
    return kernel_call(
        attend_kernel,
        "attention_forward",
        4,
        [
            whole(embed_rows),
            whole(slot_hot),
            whole(allowed),
            (weights, (width, shared), lambda step: (0, 12 * width // shared)),
            (
                weights,
                (width, width),
                lambda step: (0, jnp.where(step == 3, 3, (step + 1) % 3)),
            ),
        ],
        [
            out(length, bfloat), out(length, bfloat), out(slots, bfloat), out(slots, bfloat),
            out(slots, single), out(slots, single), out(slots, single, 128),
            out(length, bfloat), out(length, single), out(length, single, 128),
            out(slots, single), out(slots, single), out(slots, single, 128),
            out(length, single), out(small_count, single),
        ],
        (
            4 * length * width * width + 8 * slots * length * width,
            8 * width * width,
            HEADS * slots * length,
        ),
    )


def erf_half(hidden):
    return 0.5 * (1.0 + lax.erf(hidden * 0.5**0.5))


def feed_kernel(
    middle_ref, small_ref, up_ref, down_ref,
    middle_b_ref, hidden_ref, active_ref, output_ref, normed_ref, inverse_ref, total_ref,
):
    step = pl.program_id(0)

    @pl.when(step == 0)
    def _():
        middle_b_ref[...] = middle_ref[...].astype(bfloat)
        total_ref[...] = middle_ref[...] + row_of(small_ref, 11)

    hidden = plain_dot(middle_b_ref[...], up_ref[...]) + row_of(small_ref, 7 + step)
    hidden_ref[...] = hidden
    active = (hidden * erf_half(hidden)).astype(bfloat)
    active_ref[...] = active
    total_ref[...] += trans_dot(active, down_ref[...])

    @pl.when(step == pl.num_programs(0) - 1)
    def _():
        output, (normed, inverse) = norm_forward(
            total_ref[...], row_of(small_ref, 12), row_of(small_ref, 13)
        )
        output_ref[...] = output.astype(bfloat)
        normed_ref[...] = normed
        inverse_ref[...] = spread(inverse)


def feed_forward(middle, small_full, weights):
    slots, width = middle.shape
    wide = lambda kind: ((slots, 4 * width), kind, (slots, width), lambda step: (0, step))
    out = lambda kind, columns=width: ((slots, columns), kind, None, None)
    return kernel_call(
        feed_kernel,
        "feed_forward",
        4,
        [
            whole(middle),
            whole(small_full),
            (weights, (width, width), lambda step: (0, 4 + step)),
            (weights, (width, width), lambda step: (0, 8 + step)),
        ],
        [
            out(bfloat), wide(single), wide(bfloat), out(bfloat), out(single), out(single, 128),
        ],
        (16 * slots * width * width, 16 * width * width, 4 * slots * width),
        [pltpu.VMEM((slots, width), single)],
    )


def norm_back(upstream, normed, inverse, gain_row):
    return norm_backward(upstream, (normed, inverse), gain_row)


def feed_back_kernel(
    parts_ref, normed_ref, inverse_ref, hidden_ref, small_ref, mid_normed_ref, mid_inverse_ref,
    up_ref, down_ref,
    d_branch_ref, d_hidden_ref, d_pre_ref, d_attend_ref, sums_ref, d_middle_ref,
):
    step = pl.program_id(0)

    @pl.when(step == 0)
    def _():
        sums_ref[...] = jnp.zeros_like(sums_ref)
        d_sum, gain, bias = norm_back(
            jnp.sum(parts_ref[...], axis=0), normed_ref[...], inverse_ref[:, :1], row_of(small_ref, 12)
        )
        d_branch = d_sum.astype(bfloat)
        d_branch_ref[...] = d_branch
        d_middle_ref[...] = d_sum
        sums_ref[pl.ds(6, 1), :] = column_sum(d_branch)[None]
        sums_ref[pl.ds(7, 1), :] = gain[None]
        sums_ref[pl.ds(8, 1), :] = bias[None]

    hidden = hidden_ref[...]
    slope = erf_half(hidden) + hidden * jnp.exp(-0.5 * hidden * hidden) * (2.0 * jnp.pi) ** (-0.5)
    d_hidden = (plain_dot(d_branch_ref[...], down_ref[...]) * slope).astype(bfloat)
    d_hidden_ref[...] = d_hidden
    sums_ref[pl.ds(2 + step, 1), :] = column_sum(d_hidden)[None]
    d_middle_ref[...] += trans_dot(d_hidden, up_ref[...])

    @pl.when(step == pl.num_programs(0) - 1)
    def _():
        d_pre, gain, bias = norm_back(
            d_middle_ref[...], mid_normed_ref[...], mid_inverse_ref[:, :1], row_of(small_ref, 5)
        )
        d_pre_ref[...] = d_pre
        d_attend_ref[...] = d_pre.astype(bfloat)
        sums_ref[pl.ds(0, 1), :] = gain[None]
        sums_ref[pl.ds(1, 1), :] = bias[None]


def feed_backward(parts, normed, inverse, hidden, small_full, mid_normed, mid_inverse, weights):
    slots, width = normed.shape
    block = (slots, width), lambda step: (0, step)
    out = lambda kind, rows=slots: ((rows, width), kind, None, None)
    return kernel_call(
        feed_back_kernel,
        "feed_backward",
        4,
        [
            whole(parts),
            whole(normed),
            whole(inverse),
            (hidden,) + block,
            whole(small_full),
            whole(mid_normed),
            whole(mid_inverse),
            (weights, (width, width), lambda step: (0, 4 + step)),
            (weights, (width, width), lambda step: (0, 8 + step)),
        ],
        [
            out(bfloat), ((slots, 4 * width), bfloat) + block, out(single), out(bfloat),
            out(single, 16),
        ],
        (16 * slots * width * width, 16 * width * width, 8 * slots * width),
        [pltpu.VMEM((slots, width), single)],
    )


def attend_back_kernel(
    d_attend_ref, key_ref, value_ref, query_ref, allowed_ref, weight_ref,
    d_query_ref, d_key_ref, d_value_ref, d_mixed_ref,
):
    d_mixed_ref[...] = trans_dot(d_attend_ref[...], weight_ref[...]).astype(bfloat)
    blocked = allowed_ref[...] == 0.0
    slots, length = blocked.shape
    low, high = pair_masks(slots)
    low_long, _ = pair_masks(length)
    scale = HD ** (-0.5)

    def one_pair(pair, carry):
        lanes = pl.ds(pl.multiple_of(pair * 2 * HD, 2 * HD), 2 * HD)
        query_pair, key_pair, value_pair = query_ref[:, lanes], key_ref[:, lanes], value_ref[:, lanes]
        mixed_pair = d_mixed_ref[:, lanes]
        found = []
        for head_lanes in (low, high):
            probs = head_probs(query_pair, key_pair, head_lanes, blocked)
            d_probs = trans_dot(
                jnp.where(head_lanes, mixed_pair, jnp.zeros_like(mixed_pair)), value_pair
            )
            inner = jnp.sum(probs * d_probs, axis=-1, keepdims=True)
            d_scores = (probs * (d_probs - inner)).astype(bfloat)
            found.append(
                (
                    plain_dot(d_scores, key_pair) * scale,
                    rows_dot(d_scores, query_pair) * scale,
                    rows_dot(probs.astype(bfloat), mixed_pair),
                )
            )
        d_query_ref[:, lanes] = jnp.where(low, found[0][0], found[1][0]).astype(bfloat)
        d_key_ref[:, lanes] = jnp.where(low_long, found[0][1], found[1][1]).astype(bfloat)
        d_value_ref[:, lanes] = jnp.where(low_long, found[0][2], found[1][2]).astype(bfloat)
        return carry

    lax.fori_loop(0, query_ref.shape[1] // (2 * HD), one_pair, 0)


def attend_backward(d_attend, key_rows, value_rows, query_rows, allowed, weights):
    length, width = key_rows.shape
    slots = d_attend.shape[0]
    out = lambda rows: ((rows, width), bfloat, None, None)
    return kernel_call(
        attend_back_kernel,
        "attention_backward",
        1,
        [
            whole(d_attend),
            whole(key_rows),
            whole(value_rows),
            whole(query_rows),
            whole(allowed),
            (weights, (width, width), lambda step: (0, 3)),
        ],
        [out(slots), out(length), out(length)],
        (
            2 * slots * width * width + 20 * slots * length * width,
            2 * width * width,
            HEADS * slots * length,
        ),
        [pltpu.VMEM((slots, width), bfloat)],
    )


def project_back_kernel(
    d_pre_ref, d_query_ref, d_key_ref, d_value_ref, slot_ref, hidden_row_ref, small_ref,
    normed_ref, inverse_ref, init_normed_ref, init_inverse_ref, weight_ref, ahead_ref,
    embed_ref, position_ref, sums_ref, d_stream_ref, d_init_ref,
):
    step = pl.program_id(0)

    @pl.when(step == 0)
    def _():
        d_init_ref[...] = d_pre_ref[...] + trans_dot(d_query_ref[...], weight_ref[...])

    @pl.when(step == 1)
    def _():
        d_stream_ref[...] = trans_dot(d_key_ref[...], weight_ref[...])

    @pl.when(step == 2)
    def _():
        gain_row = row_of(small_ref, 0)
        d_stream = d_stream_ref[...] + trans_dot(d_value_ref[...], weight_ref[...])
        d_start, gain_init, bias_init = norm_back(
            d_init_ref[...], init_normed_ref[...], init_inverse_ref[:, :1], gain_row
        )
        d_embed, gain, bias = norm_back(
            d_stream, normed_ref[...], inverse_ref[:, :1], gain_row
        )
        position_ref[...] = d_embed + lax.dot_general(
            slot_ref[...],
            d_start,
            (((0,), (0,)), ((), ())),
            precision=lax.Precision.HIGHEST,
            preferred_element_type=single,
        )
        embed_b = d_embed.astype(bfloat)
        embed_ref[...] = embed_b
        sums_ref[...] = jnp.zeros_like(sums_ref)
        sums_ref[pl.ds(0, 1), :] = (gain_init + gain)[None]
        sums_ref[pl.ds(1, 1), :] = (bias_init + bias)[None]
        sums_ref[pl.ds(2, 1), :] = column_sum(d_query_ref[...])[None]
        sums_ref[pl.ds(3, 1), :] = column_sum(d_value_ref[...])[None]
        sums_ref[pl.ds(4, 1), :] = column_sum(d_pre_ref[...].astype(bfloat))[None]
        masked = jnp.where(hidden_row_ref[:, :1] > 0.0, embed_b.astype(single), 0.0)
        sums_ref[pl.ds(5, 1), :] = jnp.sum(masked, axis=0)[None]


def project_backward(
    d_pre, d_query, d_key, d_value, slot_hot, hidden_rows, small_full,
    normed, inverse, init_normed, init_inverse, weights, ahead,
):
    length, width = normed.shape
    slots = d_pre.shape[0]
    arrays = (
        d_pre, d_query, d_key, d_value, slot_hot, hidden_rows, small_full,
        normed, inverse, init_normed, init_inverse,
    )
    return kernel_call(
        project_back_kernel,
        "projection_backward",
        3,
        [whole(array) for array in arrays]
        + [(weights, (width, width), lambda step: (0, step)), (ahead, "any", None)],
        [
            ((length, width), bfloat, None, None),
            ((length, width), single, None, None),
            ((8, width), single, None, None),
        ],
        (5 * length * width * width, 6 * width * width, 0),
        [pltpu.VMEM((length, width), single), pltpu.VMEM((slots, width), single)],
    )


def adam_direction(weight_arr, new_first, new_second):
    first_scale, second_scale = 1.0 / (1.0 - beta_first**STEP), 1.0 / (1.0 - beta_second**STEP)
    return (new_first * first_scale) / (
        jnp.sqrt(new_second * second_scale) + adam_eps
    ) + weight_decay * weight_arr


def adam_moments(weight_arr, first_mom, second_mom, gradient, factor):
    clipped = gradient * factor
    new_first = beta_first * first_mom + (1.0 - beta_first) * clipped
    new_second = beta_second * second_mom + (1.0 - beta_second) * clipped * clipped
    return (new_first, new_second, adam_direction(weight_arr, new_first, new_second))


def row_block(count, most=240):
    return most if count % most == 0 else count


def lookup_kernel(parts, *refs):
    step = pl.program_id(0)
    head_refs, (asked_ref, given_ref, side_ref, grad_ref, square_ref) = refs[:parts], refs[parts:]
    rows, width = grad_ref.shape
    base = step * rows
    row_hot = asked_ref[...] == base + lax.broadcasted_iota(
        jnp.int32, (rows, asked_ref.shape[1]), 0
    )
    grad = plain_dot(row_hot.astype(bfloat), given_ref[...])
    for head_ref in head_refs:
        grad += head_ref[...].astype(single)
    grad_ref[...] = grad
    place = base + lax.broadcasted_iota(jnp.int32, (rows, width), 0)
    own = (place >= side_ref[0]) & (place < side_ref[1])

    @pl.when(step == 0)
    def _():
        square_ref[...] = jnp.zeros_like(square_ref)

    square_ref[...] += jnp.sum(jnp.where(own, grad * grad, 0.0), axis=0, keepdims=True)


def lookup_grad(heads, parts, asked_rows, given, sides):
    vrows, width = heads.shape[0] // parts, heads.shape[1]
    rows = vrows // 4
    block = pl.BlockSpec((rows, width), lambda step: (step, 0))
    whole_spec = lambda array: pl.BlockSpec(array.shape, lambda step: (0, 0))
    return pl.pallas_call(
        lambda *refs: lookup_kernel(parts, *refs),
        grid=(4,),
        in_specs=[
            pl.BlockSpec((rows, width), lambda step, part=part: (4 * part + step, 0))
            for part in range(parts)
        ]
        + [
            whole_spec(asked_rows),
            whole_spec(given),
            pl.BlockSpec(memory_space=pltpu.SMEM),
        ],
        out_specs=[block, pl.BlockSpec((1, width), lambda step: (0, 0))],
        out_shape=[
            jax.ShapeDtypeStruct((vrows, width), single),
            jax.ShapeDtypeStruct((1, width), single),
        ],
        cost_estimate=pl.CostEstimate(flops=0, bytes_accessed=0, transcendentals=0),
        name="table_gradient",
    )(*[heads] * parts, asked_rows, given, sides)


def full_sum(values):
    return jnp.sum(jnp.sum(values, axis=1, keepdims=True), axis=0, keepdims=True)


def pair_row(weight_sum, dir_sum):
    lane = lax.broadcasted_iota(jnp.int32, (1, 128), 1)
    return jnp.where(lane == 0, weight_sum, dir_sum)


def norms_kernel(offset_ref, *refs):
    total_ref, table_refs, layer_refs, position_refs, small_refs = (
        refs[0], refs[1:5], refs[5:9], refs[9:13], refs[13:17],
    )
    norms_ref, layer_out, position_out, small_out = refs[17], refs[18:21], refs[21:24], refs[24:27]
    sums_ref = refs[27]
    step = pl.program_id(0)
    total_square = jnp.sum(total_ref[...], axis=0, keepdims=True)[:, :1]
    factor = jnp.minimum(1.0, clip_norm / jnp.sqrt(total_square))

    @pl.when(step == 0)
    def _():
        sums_ref[...] = jnp.zeros_like(sums_ref)
        norms_ref[...] = jnp.zeros_like(norms_ref)
        for row, group_refs, outs in ((4, position_refs, position_out), (5, small_refs, small_out)):
            weight_arr = group_refs[0][...]
            first, second, direction = adam_moments(
                weight_arr, group_refs[1][...], group_refs[2][...], group_refs[3][...], factor
            )
            for ref, value in zip(outs, (first, second, direction)):
                ref[...] = value
            norms_ref[pl.ds(row, 1), :] = pair_row(
                full_sum(weight_arr * weight_arr), full_sum(direction * direction)
            )

    @pl.when(step < 3)
    def _():
        weight_arr, first_mom, second_mom, gradient = (ref[0] for ref in layer_refs)
        first, second, direction = adam_moments(
            weight_arr, first_mom, second_mom, gradient, factor
        )
        for ref, value in zip(layer_out, (first, second, direction)):
            ref[0] = value
        norms_ref[pl.ds(1 + step, 1), :] = pair_row(
            full_sum(weight_arr * weight_arr), full_sum(direction * direction)
        )

    weight_arr = table_refs[0][...]
    _, _, direction = adam_moments(
        weight_arr, table_refs[1][...], table_refs[2][...], table_refs[3][...], factor
    )
    sums_ref[pl.ds(0, 1), :] += jnp.sum(weight_arr * weight_arr, axis=0, keepdims=True)
    sums_ref[pl.ds(1, 1), :] += jnp.sum(direction * direction, axis=0, keepdims=True)

    @pl.when(step == pl.num_programs(0) - 1)
    def _():
        norms_ref[pl.ds(0, 1), :] = pair_row(
            full_sum(sums_ref[pl.ds(0, 1), :]), full_sum(sums_ref[pl.ds(1, 1), :])
        )


def update_norms(totals, table, layer, position, small, split, dp_index):
    vrows, width = table[0].shape
    rows = row_block(split, 240)
    if split // rows < 3:
        rows = split // 3
    one_part = pl.BlockSpec(
        (1,) + layer[0].shape[1:], lambda step, offset: (jnp.minimum(step, 2), 0, 0)
    )
    fixed = lambda array: pl.BlockSpec(
        array.shape, lambda step, offset, rank=array.ndim: (0,) * rank
    )
    part = pl.BlockSpec((rows, width), lambda step, offset: (offset[0] + step, 0))
    groups = tuple(layer) + tuple(position) + tuple(small)
    outs = [
        jax.ShapeDtypeStruct(group[0].shape, single)
        for group in (layer, position, small)
        for _ in range(3)
    ]
    norms = jax.ShapeDtypeStruct((8, 128), single)
    return pl.pallas_call(
        norms_kernel,
        grid_spec=pltpu.PrefetchScalarGridSpec(
            num_scalar_prefetch=1,
            grid=(split // rows,),
            in_specs=[fixed(totals)]
            + [part] * 4
            + [one_part] * 4
            + [fixed(array) for array in groups[4:]],
            out_specs=[fixed(norms)] + [one_part] * 3 + [fixed(out) for out in outs[3:]],
            scratch_shapes=[pltpu.VMEM((8, width), single)],
        ),
        out_shape=[norms] + outs,
        cost_estimate=pl.CostEstimate(flops=0, bytes_accessed=0, transcendentals=0),
        name="update_norms",
    )((dp_index * (split // rows)).astype(jnp.int32)[None], totals, *table, *groups)


def final_kernel(
    pairs_ref, weight_ref, first_ref, second_ref,
    layer_ref, layer_dir_ref, position_ref, position_dir_ref, small_ref, small_dir_ref,
    next_ref, layer_next_ref, position_next_ref, small_next_ref,
):
    roots = jnp.sqrt(jnp.sum(pairs_ref[...], axis=0, keepdims=True))

    def rate(group):
        return learn_rate * (
            roots[:, 2 * group : 2 * group + 1] / roots[:, 2 * group + 1 : 2 * group + 2]
        )

    weight_arr = weight_ref[...]
    direction = adam_direction(weight_arr, first_ref[...], second_ref[...])
    next_ref[...] = weight_arr - rate(0) * direction

    step = pl.program_id(0)
    for part in range(3):

        @pl.when(step == part)
        def _():
            layer_next_ref[0] = layer_ref[0] - rate(1 + part) * layer_dir_ref[0]

    @pl.when(step == 0)
    def _():
        position_next_ref[...] = position_ref[...] - rate(4) * position_dir_ref[...]
        small_next_ref[...] = small_ref[...] - rate(5) * small_dir_ref[...]


def final_update(pairs, table, groups):
    vrows, width = table[0].shape
    rows = row_block(vrows)
    fixed = lambda array: pl.BlockSpec(array.shape, lambda step, rank=array.ndim: (0,) * rank)
    block = pl.BlockSpec((rows, width), lambda step: (step, 0))
    one_part = pl.BlockSpec((1,) + groups[0].shape[1:], lambda step: (jnp.minimum(step, 2), 0, 0))
    outs = [jax.ShapeDtypeStruct(array.shape, single) for array in groups[::2]]
    return pl.pallas_call(
        final_kernel,
        grid=(vrows // rows,),
        in_specs=[fixed(pairs)]
        + [block] * 3
        + [one_part] * 2
        + [fixed(array) for array in groups[2:]],
        out_specs=[block, one_part] + [fixed(out) for out in outs[1:]],
        out_shape=[jax.ShapeDtypeStruct((vrows, width), single)] + outs,
        cost_estimate=pl.CostEstimate(flops=0, bytes_accessed=0, transcendentals=0),
        name="final_update",
    )(pairs, *table, *groups)


class Exchange:
    def __init__(self):
        self.last = None

    def __call__(self, values, axes):
        if self.last is not None:
            values, _ = lax.optimization_barrier((values, self.last))
        self.last = lax.all_to_all(values, axes, 0, 0, tiled=True)
        return self.last

    def copies(self, values, axes, count):
        return self(jnp.broadcast_to(values[None], (count,) + values.shape), axes)

    def columns(self, values, axes, count):
        rows, width = values.shape
        blocks = values.reshape(rows, count, width // count).transpose(1, 0, 2)
        return self(blocks, axes).reshape(count * rows, -1)

    def rows(self, values, count):
        return self(values.reshape(count, values.shape[0] // count, values.shape[1]), ALL)


def side_by_side(blocks):
    return blocks.transpose(1, 0, 2).reshape(blocks.shape[1], -1)


def after(values, *waits):
    for wait in waits:
        values = values + (wait[(0,) * wait.ndim] > 3.395e38).astype(values.dtype)
    return values


def masked_total(mask, values):
    return jnp.sum(jnp.where(mask, values, 0), axis=-1)


def slot_layout(pred_row, order_row, token_row):
    length = pred_row.shape[0]
    index = jnp.arange(length)
    before = index[None, :] <= index[:, None]
    seen = masked_total(before, pred_row[None, :])
    masked = jnp.sum(pred_row)
    place = jnp.where(pred_row == 1, seen - 1, masked + index - seen)
    slot_hot = place[None, :] == jnp.arange(CAP)[:, None]
    rank_row = masked_total(order_row[None, :] == index[:, None], index[None, :])
    slot_rank = masked_total(slot_hot, rank_row[None, :])
    slot_target = masked_total(slot_hot, token_row[None, :])
    slot_pos = masked_total(slot_hot, index[None, :])
    allowed = rank_row[None, :] <= slot_rank[:, None]
    return slot_hot, slot_pos, slot_target, allowed, masked


def bucket_layout(content, vrows):
    index = jnp.arange(content.shape[0])
    same = content[None, :] == content[:, None]
    first = jnp.min(jnp.where(same, index[None, :], content.shape[0]), axis=1)
    is_first = first == index
    owner = content // vrows
    ahead = (owner[None, :] == owner[:, None]) & is_first[None, :] & (index[None, :] < first[:, None])
    return owner, jnp.sum(ahead.astype(jnp.int32), axis=1)


def bucket_round(content, owner, place, turn, owners, vrows):
    usable = BUCKET - 1
    local = place - turn * usable
    taken = (local >= 0) & (local < usable)
    flat = jnp.where(taken, owner * BUCKET + local, -1)
    hot = flat[None, :] == jnp.arange(owners * BUCKET)[:, None]
    wanted = jnp.max(jnp.where(hot, (content - owner * vrows)[None, :], -1), axis=1)
    return hot.astype(bfloat), wanted.reshape(owners, BUCKET)


def on_device(
    token_ids,
    pred_mask,
    fact_order,
    corpus,
    embed_table,
    table_moment,
    table_square,
    layer_weights,
    layer_moment,
    layer_square,
    position_table,
    position_moment,
    position_square,
    small_params,
    small_moment,
    small_square,
):
    exchange = Exchange()
    dp_devs = lax.axis_size("dp")
    owners = lax.axis_size(VOC)
    devices = dp_devs * owners
    vrows, width = embed_table.shape
    length = token_ids.shape[1]
    feed = layer_weights.shape[2]
    shared = jnp.concatenate([position_table, small_params]).T
    shared_rows = shared.shape[1]
    shared = jnp.pad(shared, ((0, 0), (0, -shared_rows % 128)))
    shard = jnp.concatenate([layer_weights[0], layer_weights[1], layer_weights[2], shared], axis=1)
    shard = lax.all_gather(shard.astype(bfloat), ALL, axis=0, tiled=True)
    table_b = embed_table.astype(bfloat)
    token_row = token_ids[0]
    pred_row = pred_mask[0]
    first_row = lax.axis_index(VOC) * vrows
    content = jnp.where(pred_row == 1, MASK_ID, token_row)
    slot_hot, slot_pos, slot_target, allowed, masked = slot_layout(pred_row, fact_order[0], token_row)
    owner, place = bucket_layout(content, vrows)
    hot, wanted = bucket_round(content, owner, place, 0, owners, vrows)
    note = jnp.concatenate(
        [slot_target, slot_pos, jnp.stack([masked, corpus[0], jnp.max(place)])]
    )
    packet = jnp.concatenate(
        [wanted, jnp.broadcast_to(note[None], (owners, note.shape[0]))], axis=1
    )
    packet = jnp.pad(packet, ((0, 0), (0, 256 - packet.shape[1])))
    packet = jnp.broadcast_to(packet[None], (dp_devs,) + packet.shape)
    packet = exchange(packet.reshape(devices, packet.shape[-1]), ALL)
    asked = packet[:, :BUCKET]
    tail = BUCKET + 2 * CAP
    counts_all = packet[:, tail]
    corpus_all = packet[:, tail + 1]
    rounds = jnp.max(packet[:, tail + 2]) // (BUCKET - 1) + 1
    group = lax.axis_index("dp") * owners
    outer = lax.axis_size("hi")

    def group_order(values):
        return values.reshape(outer, 2, 2, CAP).transpose(2, 1, 0, 3).reshape(-1)

    group_asked = lax.dynamic_slice_in_dim(asked, group, owners, 0)
    group_target = group_order(
        lax.dynamic_slice_in_dim(packet[:, BUCKET : BUCKET + CAP], group, owners, 0)
    )
    corpus_hot = corpus_all[:, None] == jnp.arange(NCORP)[None, :]
    corpus_counts = jnp.sum(jnp.where(corpus_hot, counts_all[:, None], 0), axis=0)
    seq_count = masked_total(corpus_hot, corpus_counts[None, :])
    seq_weight = 1.0 / (NCORP * seq_count.astype(single))
    slot_weight = jnp.where(
        jnp.arange(CAP)[None, :] < counts_all[:, None], seq_weight[:, None], 0.0
    )
    group_weight = group_order(lax.dynamic_slice_in_dim(slot_weight, group, owners, 0))

    def serve(asked_rows):
        served = jnp.take(table_b, jnp.maximum(asked_rows, 0).reshape(-1), axis=0)
        return served.reshape(owners, BUCKET, width)

    arrived = exchange(serve(group_asked), VOC)
    embed_rows = rows_dot(hot, arrived.reshape(-1, width))

    def more_rows(state):
        turn, rows = state
        hot_t, wanted_t = bucket_round(content, owner, place, turn, owners, vrows)
        asked_t = lax.all_to_all(wanted_t, VOC, 0, 0, tiled=True)
        arrived_t = lax.all_to_all(serve(asked_t), VOC, 0, 0, tiled=True)
        return turn + 1, rows + rows_dot(hot_t, arrived_t.reshape(-1, width))

    _, embed_rows = lax.while_loop(
        lambda state: state[0] < rounds, more_rows, (jnp.ones((), rounds.dtype), embed_rows)
    )
    few = devices <= 32
    near = 4
    allowed = allowed.astype(single)
    slot_hot = slot_hot.astype(single)
    (
        key_rows,
        value_rows,
        query_rows,
        mixed_b,
        middle,
        mid_normed,
        mid_inverse,
        stream_b,
        stream_normed,
        stream_inverse,
        query_init,
        init_normed,
        init_inverse,
        position_full,
        small_full,
    ) = attend_forward(embed_rows, slot_hot, allowed, shard, length, small_params.shape[0])
    middle_b, hidden, active_b, output_b, end_normed, end_inverse = feed_forward(
        middle, small_full, shard
    )
    if few:
        kept_rows = jnp.concatenate([mixed_b, middle_b], axis=1)
        kept_all = lax.all_gather(kept_rows, ALL, axis=0, tiled=True)
        stream_all = lax.all_gather(stream_b, NEAR, axis=0, tiled=True)
    group_rows = exchange.copies(output_b, "hi", outer).reshape(-1, width)
    group_rows = exchange.copies(group_rows, "mid", 2).reshape(-1, width)
    group_rows = exchange.copies(group_rows, "core", 2).reshape(-1, width)
    logits = trans_dot(group_rows, table_b)
    local_target = group_target - first_row
    target_hit = jnp.arange(vrows)[None, :] == local_target[:, None]
    row_top = jnp.max(logits, axis=1)
    row_total = jnp.sum(jnp.exp(logits - row_top[:, None]), axis=1)
    row_target = jnp.sum(jnp.where(target_hit, logits, 0.0), axis=1)
    stats = exchange.copies(jnp.stack([row_top, row_total]), VOC, owners)
    top_all = jnp.max(stats[:, 0], axis=0)
    total_all = jnp.sum(stats[:, 1] * jnp.exp(stats[:, 0] - top_all[None]), axis=0)
    log_total = top_all + jnp.log(total_all)
    own_place = lax.axis_index(("core", "mid", "hi"))
    own_total = lax.dynamic_slice_in_dim(log_total * group_weight, own_place * CAP, CAP, 0)
    loss_part = jnp.sum(own_total) - jnp.sum(row_target * group_weight)
    d_logits = (
        group_weight[:, None] * (jnp.exp(logits - log_total[:, None]) - target_hit.astype(single))
    ).astype(bfloat)
    def swapped(axis, part):
        side = lax.axis_index(axis)
        theirs = lax.ppermute(part(1 - side), axis, [(0, 1), (1, 0)])
        return part(side) + theirs

    half = owners * CAP // 2

    def rows_half(side):
        return plain_dot(lax.dynamic_slice_in_dim(d_logits, side * half, half, 0), table_b)

    d_output = swapped("core", rows_half)
    quarter = half // 2
    d_half = d_output
    d_output = swapped(
        "mid", lambda side: lax.dynamic_slice_in_dim(d_half, side * quarter, quarter, 0)
    )
    grad_head = rows_dot(d_logits, group_rows)
    grad_head = after(grad_head, d_half, *((stream_all,) if few else ()))
    heads = lax.all_gather(grad_head.astype(bfloat), "dp", axis=0, tiled=True)
    d_output = exchange(d_output.reshape(outer, CAP, width), "hi")
    if few:
        d_output, kept_all = lax.optimization_barrier((d_output, kept_all))
    d_branch, d_hidden, d_pre, d_attend, sums_feed = feed_backward(
        d_output,
        end_normed,
        end_inverse,
        hidden,
        small_full,
        mid_normed,
        mid_inverse,
        shard,
    )
    if few:
        wide = feed // devices
        both = jnp.concatenate(
            [
                d_hidden.reshape(CAP, devices, -1),
                d_attend.reshape(CAP, devices, -1),
            ],
            axis=2,
        ).reshape(CAP, -1)
        both = exchange.columns(both, ALL, devices)
        branch_all = lax.all_gather(d_branch, ALL, axis=0, tiled=True)
    d_query, d_key, d_value = attend_backward(
        d_attend, key_rows, value_rows, query_rows, allowed, shard
    )
    if few:
        piece = width // near
        pairs = jnp.concatenate(
            [d_key.reshape(length, near, piece), d_value.reshape(length, near, piece)], axis=2
        ).transpose(1, 0, 2)
        asks = d_query.reshape(CAP, near, piece).transpose(1, 0, 2)
        asks = jnp.concatenate([asks[:, : CAP // 2], asks[:, CAP // 2 :]], axis=2)
        pairs = exchange(jnp.concatenate([pairs, asks], axis=1), NEAR)
    hidden_rows = spread((content == MASK_ID).astype(single)[:, None])
    embed_back, grad_position, sums_back = project_backward(
        d_pre,
        d_query,
        d_key,
        d_value,
        slot_hot,
        hidden_rows,
        small_full,
        stream_normed,
        stream_inverse,
        init_normed,
        init_inverse,
        shard,
        heads,
    )
    grad_small = jnp.concatenate([sums_back[:5], sums_feed[:9]])
    mask_sum = sums_back[5]
    mask_left = mask_sum - lax.reduce_precision(mask_sum, 8, 7)
    mask_owner = MASK_ID // vrows
    is_left = (jnp.arange(BUCKET) == BUCKET - 1)[None, :] & (
        jnp.arange(owners) == mask_owner
    )[:, None]

    def plain_exchange(values, axes):
        return lax.all_to_all(values, axes, 0, 0, tiled=True)

    def give(hot_rows, extra, send):
        rows = plain_dot(hot_rows, embed_back).reshape(owners, BUCKET, width)
        rows = jnp.where(is_left[:, :, None] & extra, mask_left[None, None, :], rows)
        return send(rows.astype(bfloat), VOC).reshape(-1, width)

    def of_both(rows):
        if dp_devs == 2:
            return jnp.concatenate([rows, lax.ppermute(rows, "dp", [(0, 1), (1, 0)])])
        return lax.all_gather(rows, "dp", axis=0, tiled=True)

    def both_groups(asked_rows):
        if dp_devs == 2:
            return jnp.roll(asked_rows, -group, axis=0)
        return asked_rows

    split = vrows // dp_devs
    sides = lax.axis_index("dp") * split + jnp.array([0, split])

    def into_rows(heads, parts, asked_rows, given, sides):
        return lookup_grad(heads, parts, both_groups(asked_rows).reshape(1, -1), given, sides)

    last = (jnp.arange(BUCKET) == BUCKET - 1)[None, :]
    left_row = jnp.where(lax.axis_index(VOC) == mask_owner, MASK_ID - first_row, -1)
    given = give(hot, True, exchange)

    if few:
        near_pos = packet[:, BUCKET + CAP : tail].reshape(dp_devs * outer, near * CAP)
        near_pos = lax.dynamic_index_in_dim(
            near_pos, lax.axis_index(("dp", "hi")), 0, False
        )
        init_rows = norm_forward(position_full, small_full[0], small_full[1])[0].astype(bfloat)
        init_hot = near_pos[:, None] == jnp.arange(length)[None, :]
        init_all = plain_dot(init_hot.astype(bfloat), init_rows).astype(bfloat)
        asks = pairs[:, length:]
        asks = jnp.concatenate([asks[..., :piece], asks[..., piece:]], axis=1)
        grad_pair = rows_dot(stream_all, pairs[:, :length].reshape(near * length, -1))
        grad_ask = rows_dot(init_all, asks.reshape(near * CAP, piece))
        share = width // devices
        active_mine = exchange.columns(active_b, ALL, devices)
        grad_up = rows_dot(kept_all[:, width:], both[:, :wide])
        grad_out = rows_dot(kept_all[:, :width], both[:, wide:])
        grad_down = rows_dot(branch_all, active_mine)
        shared_grad = jnp.concatenate([grad_position, grad_small]).T
        results = jnp.concatenate(
            [grad_pair, grad_ask, grad_up, grad_down, grad_out, shared_grad], axis=1
        )
        results = results.astype(bfloat)
        results = exchange.rows(results, devices).astype(single)
        pieces = 3 * piece
        attn = jnp.sum(
            results[..., :pieces].reshape(dp_devs * outer, near, share, pieces), axis=0
        )
        shared_grad = jnp.sum(results[..., -shared_rows:], axis=0)
        single_parts = results[..., pieces:-shared_rows]
        part_square = (
            jnp.sum(attn * attn)
            + jnp.sum(single_parts * single_parts)
            + jnp.sum(shared_grad * shared_grad)
        )
        shared_grad = shared_grad.T
        position_grad, small_grad = shared_grad[:length], shared_grad[length:]
        grad_key, grad_value, grad_query = (
            side_by_side(attn[..., part * piece : (part + 1) * piece]) for part in range(3)
        )
        grad_up, grad_down, grad_out = (
            side_by_side(single_parts[..., low:high])
            for low, high in ((0, wide), (wide, 2 * wide), (2 * wide, None))
        )
        layer_grad = jnp.stack(
            [
                jnp.concatenate([grad_query, grad_key, grad_value, grad_out], axis=1),
                grad_up,
                grad_down,
            ]
        )
    else:
        whole = (
            jnp.concatenate(
                [
                    rows_dot(query_init.astype(bfloat), d_query),
                    rows_dot(stream_b, d_key),
                    rows_dot(stream_b, d_value),
                    rows_dot(mixed_b, d_attend),
                ],
                axis=1,
            ),
            rows_dot(middle_b, d_hidden),
            rows_dot(d_branch, active_b),
        )
        layer_grad = jnp.stack(
            [lax.psum_scatter(part, ALL, scatter_dimension=0, tiled=True) for part in whole]
        )
        shared_grad = jnp.concatenate([grad_position, grad_small]).T
        shared_grad = lax.psum_scatter(shared_grad, ALL, scatter_dimension=0, tiled=True).T
        position_grad, small_grad = shared_grad[:length], shared_grad[length:]
        part_square = jnp.sum(layer_grad * layer_grad) + jnp.sum(shared_grad * shared_grad)
    table_grad, table_square_sum = into_rows(
        heads, dp_devs, jnp.where(last, left_row, asked), of_both(given), sides
    )

    def more_grads(state):
        turn, grads, _ = state
        hot_t, wanted_t = bucket_round(content, owner, place, turn, owners, vrows)
        wanted_t = jnp.broadcast_to(wanted_t[None], (dp_devs,) + wanted_t.shape)
        asked_t = lax.all_to_all(
            wanted_t.reshape(devices, BUCKET), ALL, 0, 0, tiled=True
        )
        given_t = of_both(give(hot_t, False, plain_exchange))
        return (turn + 1,) + tuple(into_rows(grads, 1, asked_t, given_t, sides))

    _, table_grad, table_square_sum = lax.while_loop(
        lambda state: state[0] < rounds,
        more_grads,
        (jnp.ones((), rounds.dtype), table_grad, table_square_sum),
    )
    square_part = jnp.sum(table_square_sum) + part_square
    totals = exchange.copies(jnp.stack([square_part, loss_part]), ALL, devices)
    total_square, loss_value = jnp.sum(totals, axis=0)
    grad_norm = jnp.sqrt(total_square)
    factor = jnp.minimum(1.0, clip_norm / grad_norm)
    (
        norms,
        layer_first,
        layer_second,
        layer_dir,
        position_first,
        position_second,
        position_dir,
        small_first,
        small_second,
        small_dir,
    ) = update_norms(
        totals,
        (embed_table, table_moment, table_square, table_grad),
        (layer_weights, layer_moment, layer_square, layer_grad),
        (position_table, position_moment, position_square, position_grad),
        (small_params, small_moment, small_square, small_grad),
        split,
        lax.axis_index("dp"),
    )
    factor_late, norms = lax.optimization_barrier((factor, norms))
    pairs = exchange.copies(norms[:6, :2].reshape(-1), ALL, devices)
    table_first, table_second, _ = adam_moments(
        embed_table, table_moment, table_square, table_grad, factor_late
    )
    trust_norms = jnp.sqrt(jnp.sum(pairs, axis=0)).reshape(6, 2)
    table_next, layer_next, position_next, small_next = final_update(
        pairs,
        (embed_table, table_first, table_second),
        (
            layer_weights,
            layer_dir,
            position_table,
            position_dir,
            small_params,
            small_dir,
        ),
    )
    return (
        loss_value,
        grad_norm,
        table_next,
        table_first,
        table_second,
        layer_next,
        layer_first,
        layer_second,
        position_next,
        position_first,
        position_second,
        small_next,
        small_first,
        small_second,
        trust_norms,
    )


def solution(mesh):
    dp_devs, owners = mesh.devices.shape
    fine = Mesh(mesh.devices.reshape(dp_devs, owners // 4, 2, 2), ALL)
    rows, inner = P(ALL, None), P(None, ALL)
    table, layer = P(VOC, None), P(None, ALL, None)
    return jax.shard_map(
        on_device,
        mesh=fine,
        in_specs=(rows,) * 3 + (P(ALL),) + (table,) * 3 + (layer,) * 3 + (inner,) * 6,
        out_specs=(P(), P()) + (table,) * 3 + (layer,) * 3 + (inner,) * 6 + (P(),),
        check_vma=False,
    )
```

```python
import jax
import jax.numpy as jnp
from jax import lax
from jax.experimental import pallas as pl
from jax.experimental.pallas import tpu as pltpu
from jax.sharding import Mesh
from jax.sharding import PartitionSpec as P

HEADS = 12
HD = 64
MASK_ID = 103
NCORP = 4
STEP = 5
CAP = 64


clip_norm = 0.1
learn_rate = 0.3
beta_first = 0.9
beta_second = 0.999
adam_eps = 1e-06
weight_decay = 0.01
norm_eps = 1e-05
masked_score = -1e30
BUCKET = 32
ALL = ("dp", "hi", "mid", "core")
VOC = ("hi", "mid", "core")
NEAR = ("mid", "core")
bfloat = jnp.bfloat16
single = jnp.float32


def plain_dot(left_op, right_op):
    return jnp.dot(left_op, right_op, preferred_element_type=single)


def trans_dot(left_op, right_op):
    return lax.dot_general(
        left_op, right_op, (((1,), (1,)), ((), ())), preferred_element_type=single
    )


def rows_dot(left_op, right_op):
    return lax.dot_general(
        left_op, right_op, (((0,), (0,)), ((), ())), preferred_element_type=single
    )


def column_sum(values):
    return jnp.sum(values.astype(single), axis=0)


def norm_forward(values, gain_row, bias_row):
    center = values - jnp.mean(values, axis=-1, keepdims=True)
    inverse = lax.rsqrt(jnp.mean(center * center, axis=-1, keepdims=True) + norm_eps)
    normed = center * inverse
    return (normed * gain_row + bias_row, (normed, inverse))


def norm_backward(upstream, kept_norm, gain_row):
    normed, inverse = kept_norm
    scaled = upstream * gain_row
    inner = (
        scaled
        - jnp.mean(scaled, axis=-1, keepdims=True)
        - normed * jnp.mean(scaled * normed, axis=-1, keepdims=True)
    )
    return (inner * inverse, jnp.sum(upstream * normed, axis=0), jnp.sum(upstream, axis=0))


def pair_masks(rows):
    lane = lax.broadcasted_iota(jnp.int32, (rows, 2 * HD), 1)
    return lane < HD, lane >= HD


def head_probs(query_pair, key_pair, head_lanes, blocked):
    scores = trans_dot(jnp.where(head_lanes, query_pair, jnp.zeros_like(query_pair)), key_pair)
    scores = jnp.where(blocked, masked_score, scores * HD ** (-0.5))
    row_top = jnp.max(scores, axis=-1, keepdims=True)
    powers = jnp.exp(scores - row_top)
    return powers / jnp.sum(powers, axis=-1, keepdims=True)


def spread(column, lanes=128):
    return jnp.broadcast_to(column, (column.shape[0], lanes))


def row_of(ref, row):
    return ref[pl.ds(row, 1), :]


def attend_kernel(
    embed_ref, slot_ref, allowed_ref, shared_ref, weight_ref,
    key_ref, value_ref, query_ref, mixed_ref, middle_ref, normed_ref, inverse_ref,
    stream_ref, stream_normed_ref, stream_inverse_ref,
    init_ref, init_normed_ref, init_inverse_ref, position_ref, small_ref,
):
    step = pl.program_id(0)
    length = position_ref.shape[0]

    @pl.when(step == 0)
    def _():
        shared = shared_ref[...].astype(single).T
        position_ref[...] = shared[:length]
        small_ref[...] = shared[length : length + small_ref.shape[0]]
        gain, bias = row_of(small_ref, 0), row_of(small_ref, 1)
        stream, (normed, inverse) = norm_forward(embed_ref[...] + position_ref[...], gain, bias)
        stream_ref[...] = stream.astype(bfloat)
        stream_normed_ref[...] = normed
        stream_inverse_ref[...] = spread(inverse)
        chosen = plain_dot(slot_ref[...].astype(bfloat), position_ref[...].astype(bfloat))
        init, (normed, inverse) = norm_forward(chosen, gain, bias)
        init_ref[...] = init
        init_normed_ref[...] = normed
        init_inverse_ref[...] = spread(inverse)
        key_ref[...] = plain_dot(stream_ref[...], weight_ref[...]).astype(bfloat)

    @pl.when(step == 1)
    def _():
        value_ref[...] = (
            plain_dot(stream_ref[...], weight_ref[...]) + row_of(small_ref, 3)
        ).astype(bfloat)

    @pl.when(step == 2)
    def _():
        query_ref[...] = (
            plain_dot(init_ref[...].astype(bfloat), weight_ref[...]) + row_of(small_ref, 2)
        ).astype(bfloat)
        blocked = allowed_ref[...] == 0.0
        low, high = pair_masks(query_ref.shape[0])

        def one_pair(pair, carry):
            lanes = pl.ds(pl.multiple_of(pair * 2 * HD, 2 * HD), 2 * HD)
            query_pair, key_pair, value_pair = query_ref[:, lanes], key_ref[:, lanes], value_ref[:, lanes]
            left, right = (
                plain_dot(
                    head_probs(query_pair, key_pair, head_lanes, blocked).astype(bfloat), value_pair
                )
                for head_lanes in (low, high)
            )
            mixed_ref[:, lanes] = jnp.where(low, left, right).astype(bfloat)
            return carry

        lax.fori_loop(0, query_ref.shape[1] // (2 * HD), one_pair, 0)

    @pl.when(step == 3)
    def _():
        attend = plain_dot(mixed_ref[...], weight_ref[...]) + row_of(small_ref, 4)
        middle, (normed, inverse) = norm_forward(
            init_ref[...] + attend, row_of(small_ref, 5), row_of(small_ref, 6)
        )
        middle_ref[...] = middle
        normed_ref[...] = normed
        inverse_ref[...] = spread(inverse)


def kernel_call(body, name, steps, inputs, shapes, cost, scratch=()):
    fixed = lambda rank: lambda step: (0,) * rank

    def spec(shape, block, index):
        if block is None:
            return pl.BlockSpec(shape, fixed(len(shape)))
        if block == "any":
            return pl.BlockSpec(memory_space=pl.ANY)
        return pl.BlockSpec(block, index)

    return pl.pallas_call(
        body,
        grid=(steps,),
        in_specs=[spec(array.shape, block, index) for array, block, index in inputs],
        out_specs=[spec(shape, block, index) for shape, _, block, index in shapes],
        out_shape=[jax.ShapeDtypeStruct(shape, kind) for shape, kind, _, _ in shapes],
        scratch_shapes=list(scratch),
        cost_estimate=pl.CostEstimate(flops=cost[0] // 64, bytes_accessed=cost[1] // 64, transcendentals=0),
        name=name,
    )(*(array for array, _, _ in inputs))


def whole(array):
    return array, None, None


def attend_forward(embed_rows, slot_hot, allowed, weights, length, small_count):
    width = embed_rows.shape[1]
    slots = slot_hot.shape[0]
    out = lambda rows, kind, columns=width: ((rows, columns), kind, None, None)
    shared = weights.shape[1] - 12 * width
    return kernel_call(
        attend_kernel,
        "attention_forward",
        4,
        [
            whole(embed_rows),
            whole(slot_hot),
            whole(allowed),
            (weights, (width, shared), lambda step: (0, 12 * width // shared)),
            (
                weights,
                (width, width),
                lambda step: (0, jnp.where(step == 3, 3, (step + 1) % 3)),
            ),
        ],
        [
            out(length, bfloat), out(length, bfloat), out(slots, bfloat), out(slots, bfloat),
            out(slots, single), out(slots, single), out(slots, single, 128),
            out(length, bfloat), out(length, single), out(length, single, 128),
            out(slots, single), out(slots, single), out(slots, single, 128),
            out(length, single), out(small_count, single),
        ],
        (
            4 * length * width * width + 8 * slots * length * width,
            8 * width * width,
            HEADS * slots * length,
        ),
    )


def erf_half(hidden):
    return 0.5 * (1.0 + lax.erf(hidden * 0.5**0.5))


def feed_kernel(
    middle_ref, small_ref, up_ref, down_ref,
    middle_b_ref, hidden_ref, active_ref, output_ref, normed_ref, inverse_ref, total_ref,
):
    step = pl.program_id(0)

    @pl.when(step == 0)
    def _():
        middle_b_ref[...] = middle_ref[...].astype(bfloat)
        total_ref[...] = middle_ref[...] + row_of(small_ref, 11)

    hidden = plain_dot(middle_b_ref[...], up_ref[...]) + row_of(small_ref, 7 + step)
    hidden_ref[...] = hidden
    active = (hidden * erf_half(hidden)).astype(bfloat)
    active_ref[...] = active
    total_ref[...] += trans_dot(active, down_ref[...])

    @pl.when(step == pl.num_programs(0) - 1)
    def _():
        output, (normed, inverse) = norm_forward(
            total_ref[...], row_of(small_ref, 12), row_of(small_ref, 13)
        )
        output_ref[...] = output.astype(bfloat)
        normed_ref[...] = normed
        inverse_ref[...] = spread(inverse)


def feed_forward(middle, small_full, weights):
    slots, width = middle.shape
    wide = lambda kind: ((slots, 4 * width), kind, (slots, width), lambda step: (0, step))
    out = lambda kind, columns=width: ((slots, columns), kind, None, None)
    return kernel_call(
        feed_kernel,
        "feed_forward",
        4,
        [
            whole(middle),
            whole(small_full),
            (weights, (width, width), lambda step: (0, 4 + step)),
            (weights, (width, width), lambda step: (0, 8 + step)),
        ],
        [
            out(bfloat), wide(single), wide(bfloat), out(bfloat), out(single), out(single, 128),
        ],
        (16 * slots * width * width, 16 * width * width, 4 * slots * width),
        [pltpu.VMEM((slots, width), single)],
    )


def norm_back(upstream, normed, inverse, gain_row):
    return norm_backward(upstream, (normed, inverse), gain_row)


def feed_back_kernel(
    parts_ref, normed_ref, inverse_ref, hidden_ref, small_ref, mid_normed_ref, mid_inverse_ref,
    up_ref, down_ref,
    d_branch_ref, d_hidden_ref, d_pre_ref, d_attend_ref, sums_ref, d_middle_ref,
):
    step = pl.program_id(0)

    @pl.when(step == 0)
    def _():
        sums_ref[...] = jnp.zeros_like(sums_ref)
        d_sum, gain, bias = norm_back(
            jnp.sum(parts_ref[...].astype(single), axis=0), normed_ref[...], inverse_ref[:, :1], row_of(small_ref, 12)
        )
        d_branch = d_sum.astype(bfloat)
        d_branch_ref[...] = d_branch
        d_middle_ref[...] = d_sum
        sums_ref[pl.ds(6, 1), :] = column_sum(d_branch)[None]
        sums_ref[pl.ds(7, 1), :] = gain[None]
        sums_ref[pl.ds(8, 1), :] = bias[None]

    hidden = hidden_ref[...]
    slope = erf_half(hidden) + hidden * jnp.exp(-0.5 * hidden * hidden) * (2.0 * jnp.pi) ** (-0.5)
    d_hidden = (plain_dot(d_branch_ref[...], down_ref[...]) * slope).astype(bfloat)
    d_hidden_ref[...] = d_hidden
    sums_ref[pl.ds(2 + step, 1), :] = column_sum(d_hidden)[None]
    d_middle_ref[...] += trans_dot(d_hidden, up_ref[...])

    @pl.when(step == pl.num_programs(0) - 1)
    def _():
        d_pre, gain, bias = norm_back(
            d_middle_ref[...], mid_normed_ref[...], mid_inverse_ref[:, :1], row_of(small_ref, 5)
        )
        d_pre_ref[...] = d_pre
        d_attend_ref[...] = d_pre.astype(bfloat)
        sums_ref[pl.ds(0, 1), :] = gain[None]
        sums_ref[pl.ds(1, 1), :] = bias[None]


def feed_backward(parts, normed, inverse, hidden, small_full, mid_normed, mid_inverse, weights):
    slots, width = normed.shape
    block = (slots, width), lambda step: (0, step)
    out = lambda kind, rows=slots: ((rows, width), kind, None, None)
    return kernel_call(
        feed_back_kernel,
        "feed_backward",
        4,
        [
            whole(parts),
            whole(normed),
            whole(inverse),
            (hidden,) + block,
            whole(small_full),
            whole(mid_normed),
            whole(mid_inverse),
            (weights, (width, width), lambda step: (0, 4 + step)),
            (weights, (width, width), lambda step: (0, 8 + step)),
        ],
        [
            out(bfloat), ((slots, 4 * width), bfloat) + block, out(single), out(bfloat),
            out(single, 16),
        ],
        (16 * slots * width * width, 16 * width * width, 8 * slots * width),
        [pltpu.VMEM((slots, width), single)],
    )


def attend_back_kernel(
    d_attend_ref, key_ref, value_ref, query_ref, allowed_ref, weight_ref,
    d_query_ref, d_key_ref, d_value_ref, d_mixed_ref,
):
    d_mixed_ref[...] = trans_dot(d_attend_ref[...], weight_ref[...]).astype(bfloat)
    blocked = allowed_ref[...] == 0.0
    slots, length = blocked.shape
    low, high = pair_masks(slots)
    low_long, _ = pair_masks(length)
    scale = HD ** (-0.5)

    def one_pair(pair, carry):
        lanes = pl.ds(pl.multiple_of(pair * 2 * HD, 2 * HD), 2 * HD)
        query_pair, key_pair, value_pair = query_ref[:, lanes], key_ref[:, lanes], value_ref[:, lanes]
        mixed_pair = d_mixed_ref[:, lanes]
        found = []
        for head_lanes in (low, high):
            probs = head_probs(query_pair, key_pair, head_lanes, blocked)
            d_probs = trans_dot(
                jnp.where(head_lanes, mixed_pair, jnp.zeros_like(mixed_pair)), value_pair
            )
            inner = jnp.sum(probs * d_probs, axis=-1, keepdims=True)
            d_scores = (probs * (d_probs - inner)).astype(bfloat)
            found.append(
                (
                    plain_dot(d_scores, key_pair) * scale,
                    rows_dot(d_scores, query_pair) * scale,
                    rows_dot(probs.astype(bfloat), mixed_pair),
                )
            )
        d_query_ref[:, lanes] = jnp.where(low, found[0][0], found[1][0]).astype(bfloat)
        d_key_ref[:, lanes] = jnp.where(low_long, found[0][1], found[1][1]).astype(bfloat)
        d_value_ref[:, lanes] = jnp.where(low_long, found[0][2], found[1][2]).astype(bfloat)
        return carry

    lax.fori_loop(0, query_ref.shape[1] // (2 * HD), one_pair, 0)


def attend_backward(d_attend, key_rows, value_rows, query_rows, allowed, weights):
    length, width = key_rows.shape
    slots = d_attend.shape[0]
    out = lambda rows: ((rows, width), bfloat, None, None)
    return kernel_call(
        attend_back_kernel,
        "attention_backward",
        1,
        [
            whole(d_attend),
            whole(key_rows),
            whole(value_rows),
            whole(query_rows),
            whole(allowed),
            (weights, (width, width), lambda step: (0, 3)),
        ],
        [out(slots), out(length), out(length)],
        (
            2 * slots * width * width + 20 * slots * length * width,
            2 * width * width,
            HEADS * slots * length,
        ),
        [pltpu.VMEM((slots, width), bfloat)],
    )


def project_back_kernel(
    d_pre_ref, d_query_ref, d_key_ref, d_value_ref, slot_ref, hidden_row_ref, small_ref,
    normed_ref, inverse_ref, init_normed_ref, init_inverse_ref, weight_ref, ahead_ref,
    embed_ref, position_ref, sums_ref, d_stream_ref, d_init_ref,
):
    step = pl.program_id(0)

    @pl.when(step == 0)
    def _():
        d_init_ref[...] = d_pre_ref[...] + trans_dot(d_query_ref[...], weight_ref[...])

    @pl.when(step == 1)
    def _():
        d_stream_ref[...] = trans_dot(d_key_ref[...], weight_ref[...])

    @pl.when(step == 2)
    def _():
        gain_row = row_of(small_ref, 0)
        d_stream = d_stream_ref[...] + trans_dot(d_value_ref[...], weight_ref[...])
        d_start, gain_init, bias_init = norm_back(
            d_init_ref[...], init_normed_ref[...], init_inverse_ref[:, :1], gain_row
        )
        d_embed, gain, bias = norm_back(
            d_stream, normed_ref[...], inverse_ref[:, :1], gain_row
        )
        position_ref[...] = d_embed + lax.dot_general(
            slot_ref[...],
            d_start,
            (((0,), (0,)), ((), ())),
            precision=lax.Precision.HIGHEST,
            preferred_element_type=single,
        )
        embed_b = d_embed.astype(bfloat)
        embed_ref[...] = embed_b
        sums_ref[...] = jnp.zeros_like(sums_ref)
        sums_ref[pl.ds(0, 1), :] = (gain_init + gain)[None]
        sums_ref[pl.ds(1, 1), :] = (bias_init + bias)[None]
        sums_ref[pl.ds(2, 1), :] = column_sum(d_query_ref[...])[None]
        sums_ref[pl.ds(3, 1), :] = column_sum(d_value_ref[...])[None]
        sums_ref[pl.ds(4, 1), :] = column_sum(d_pre_ref[...].astype(bfloat))[None]
        masked = jnp.where(hidden_row_ref[:, :1] > 0.0, embed_b.astype(single), 0.0)
        sums_ref[pl.ds(5, 1), :] = jnp.sum(masked, axis=0)[None]


def project_backward(
    d_pre, d_query, d_key, d_value, slot_hot, hidden_rows, small_full,
    normed, inverse, init_normed, init_inverse, weights, ahead,
):
    length, width = normed.shape
    slots = d_pre.shape[0]
    arrays = (
        d_pre, d_query, d_key, d_value, slot_hot, hidden_rows, small_full,
        normed, inverse, init_normed, init_inverse,
    )
    return kernel_call(
        project_back_kernel,
        "projection_backward",
        3,
        [whole(array) for array in arrays]
        + [(weights, (width, width), lambda step: (0, step)), (ahead, "any", None)],
        [
            ((length, width), bfloat, None, None),
            ((length, width), single, None, None),
            ((8, width), single, None, None),
        ],
        (5 * length * width * width, 6 * width * width, 0),
        [pltpu.VMEM((length, width), single), pltpu.VMEM((slots, width), single)],
    )


def adam_direction(weight_arr, new_first, new_second):
    first_scale, second_scale = 1.0 / (1.0 - beta_first**STEP), 1.0 / (1.0 - beta_second**STEP)
    return (new_first * first_scale) / (
        jnp.sqrt(new_second * second_scale) + adam_eps
    ) + weight_decay * weight_arr


def adam_moments(weight_arr, first_mom, second_mom, gradient, factor):
    clipped = gradient * factor
    new_first = beta_first * first_mom + (1.0 - beta_first) * clipped
    new_second = beta_second * second_mom + (1.0 - beta_second) * clipped * clipped
    return (new_first, new_second, adam_direction(weight_arr, new_first, new_second))


def row_block(count, most=240):
    return most if count % most == 0 else count


def lookup_kernel(parts, *refs):
    step = pl.program_id(0)
    head_refs, (asked_ref, given_ref, side_ref, grad_ref, square_ref) = refs[:parts], refs[parts:]
    rows, width = grad_ref.shape
    base = step * rows
    row_hot = asked_ref[...] == base + lax.broadcasted_iota(
        jnp.int32, (rows, asked_ref.shape[1]), 0
    )
    grad = plain_dot(row_hot.astype(bfloat), given_ref[...])
    for head_ref in head_refs:
        grad += head_ref[...].astype(single)
    grad_ref[...] = grad
    place = base + lax.broadcasted_iota(jnp.int32, (rows, width), 0)
    own = (place >= side_ref[0]) & (place < side_ref[1])

    @pl.when(step == 0)
    def _():
        square_ref[...] = jnp.zeros_like(square_ref)

    square_ref[...] += jnp.sum(jnp.where(own, grad * grad, 0.0), axis=0, keepdims=True)


def lookup_grad(heads, parts, asked_rows, given, sides):
    vrows, width = heads.shape[0] // parts, heads.shape[1]
    rows = vrows // 4
    block = pl.BlockSpec((rows, width), lambda step: (step, 0))
    whole_spec = lambda array: pl.BlockSpec(array.shape, lambda step: (0, 0))
    return pl.pallas_call(
        lambda *refs: lookup_kernel(parts, *refs),
        grid=(4,),
        in_specs=[
            pl.BlockSpec((rows, width), lambda step, part=part: (4 * part + step, 0))
            for part in range(parts)
        ]
        + [
            whole_spec(asked_rows),
            whole_spec(given),
            pl.BlockSpec(memory_space=pltpu.SMEM),
        ],
        out_specs=[block, pl.BlockSpec((1, width), lambda step: (0, 0))],
        out_shape=[
            jax.ShapeDtypeStruct((vrows, width), single),
            jax.ShapeDtypeStruct((1, width), single),
        ],
        cost_estimate=pl.CostEstimate(flops=0, bytes_accessed=0, transcendentals=0),
        name="table_gradient",
    )(*[heads] * parts, asked_rows, given, sides)


def full_sum(values):
    return jnp.sum(jnp.sum(values, axis=1, keepdims=True), axis=0, keepdims=True)


def pair_row(weight_sum, dir_sum):
    lane = lax.broadcasted_iota(jnp.int32, (1, 128), 1)
    return jnp.where(lane == 0, weight_sum, dir_sum)


def norms_kernel(offset_ref, *refs):
    total_ref, table_refs, layer_refs, position_refs, small_refs = (
        refs[0], refs[1:5], refs[5:9], refs[9:13], refs[13:17],
    )
    norms_ref, layer_out, position_out, small_out = refs[17], refs[18:21], refs[21:24], refs[24:27]
    sums_ref = refs[27]
    step = pl.program_id(0)
    total_square = jnp.sum(total_ref[...], axis=0, keepdims=True)[:, :1]
    factor = jnp.minimum(1.0, clip_norm / jnp.sqrt(total_square))

    @pl.when(step == 0)
    def _():
        sums_ref[...] = jnp.zeros_like(sums_ref)
        norms_ref[...] = jnp.zeros_like(norms_ref)
        for row, group_refs, outs in ((4, position_refs, position_out), (5, small_refs, small_out)):
            weight_arr = group_refs[0][...]
            first, second, direction = adam_moments(
                weight_arr, group_refs[1][...], group_refs[2][...], group_refs[3][...], factor
            )
            for ref, value in zip(outs, (first, second, direction)):
                ref[...] = value
            norms_ref[pl.ds(row, 1), :] = pair_row(
                full_sum(weight_arr * weight_arr), full_sum(direction * direction)
            )

    @pl.when(step < 3)
    def _():
        weight_arr, first_mom, second_mom, gradient = (ref[0] for ref in layer_refs)
        first, second, direction = adam_moments(
            weight_arr, first_mom, second_mom, gradient, factor
        )
        for ref, value in zip(layer_out, (first, second, direction)):
            ref[0] = value
        norms_ref[pl.ds(1 + step, 1), :] = pair_row(
            full_sum(weight_arr * weight_arr), full_sum(direction * direction)
        )

    weight_arr = table_refs[0][...]
    _, _, direction = adam_moments(
        weight_arr, table_refs[1][...], table_refs[2][...], table_refs[3][...], factor
    )
    sums_ref[pl.ds(0, 1), :] += jnp.sum(weight_arr * weight_arr, axis=0, keepdims=True)
    sums_ref[pl.ds(1, 1), :] += jnp.sum(direction * direction, axis=0, keepdims=True)

    @pl.when(step == pl.num_programs(0) - 1)
    def _():
        norms_ref[pl.ds(0, 1), :] = pair_row(
            full_sum(sums_ref[pl.ds(0, 1), :]), full_sum(sums_ref[pl.ds(1, 1), :])
        )


def update_norms(totals, table, layer, position, small, split, dp_index):
    vrows, width = table[0].shape
    rows = row_block(split, 240)
    if split // rows < 3:
        rows = split // 3
    one_part = pl.BlockSpec(
        (1,) + layer[0].shape[1:], lambda step, offset: (jnp.minimum(step, 2), 0, 0)
    )
    fixed = lambda array: pl.BlockSpec(
        array.shape, lambda step, offset, rank=array.ndim: (0,) * rank
    )
    part = pl.BlockSpec((rows, width), lambda step, offset: (offset[0] + step, 0))
    groups = tuple(layer) + tuple(position) + tuple(small)
    outs = [
        jax.ShapeDtypeStruct(group[0].shape, single)
        for group in (layer, position, small)
        for _ in range(3)
    ]
    norms = jax.ShapeDtypeStruct((8, 128), single)
    return pl.pallas_call(
        norms_kernel,
        grid_spec=pltpu.PrefetchScalarGridSpec(
            num_scalar_prefetch=1,
            grid=(split // rows,),
            in_specs=[fixed(totals)]
            + [part] * 4
            + [one_part] * 4
            + [fixed(array) for array in groups[4:]],
            out_specs=[fixed(norms)] + [one_part] * 3 + [fixed(out) for out in outs[3:]],
            scratch_shapes=[pltpu.VMEM((8, width), single)],
        ),
        out_shape=[norms] + outs,
        cost_estimate=pl.CostEstimate(flops=0, bytes_accessed=0, transcendentals=0),
        name="update_norms",
    )((dp_index * (split // rows)).astype(jnp.int32)[None], totals, *table, *groups)


def final_kernel(
    pairs_ref, weight_ref, first_ref, second_ref,
    layer_ref, layer_dir_ref, position_ref, position_dir_ref, small_ref, small_dir_ref,
    next_ref, layer_next_ref, position_next_ref, small_next_ref,
):
    roots = jnp.sqrt(jnp.sum(pairs_ref[...], axis=0, keepdims=True))

    def rate(group):
        return learn_rate * (
            roots[:, 2 * group : 2 * group + 1] / roots[:, 2 * group + 1 : 2 * group + 2]
        )

    weight_arr = weight_ref[...]
    direction = adam_direction(weight_arr, first_ref[...], second_ref[...])
    next_ref[...] = weight_arr - rate(0) * direction

    step = pl.program_id(0)
    for part in range(3):

        @pl.when(step == part)
        def _():
            layer_next_ref[0] = layer_ref[0] - rate(1 + part) * layer_dir_ref[0]

    @pl.when(step == 0)
    def _():
        position_next_ref[...] = position_ref[...] - rate(4) * position_dir_ref[...]
        small_next_ref[...] = small_ref[...] - rate(5) * small_dir_ref[...]


def final_update(pairs, table, groups):
    vrows, width = table[0].shape
    rows = row_block(vrows, 480)
    if vrows // rows < 3:
        rows = row_block(vrows, 240)
    fixed = lambda array: pl.BlockSpec(array.shape, lambda step, rank=array.ndim: (0,) * rank)
    block = pl.BlockSpec((rows, width), lambda step: (step, 0))
    one_part = pl.BlockSpec((1,) + groups[0].shape[1:], lambda step: (jnp.minimum(step, 2), 0, 0))
    outs = [jax.ShapeDtypeStruct(array.shape, single) for array in groups[::2]]
    return pl.pallas_call(
        final_kernel,
        grid=(vrows // rows,),
        in_specs=[fixed(pairs)]
        + [block] * 3
        + [one_part] * 2
        + [fixed(array) for array in groups[2:]],
        out_specs=[block, one_part] + [fixed(out) for out in outs[1:]],
        out_shape=[jax.ShapeDtypeStruct((vrows, width), single)] + outs,
        cost_estimate=pl.CostEstimate(flops=0, bytes_accessed=0, transcendentals=0),
        name="final_update",
    )(pairs, *table, *groups)


class Exchange:
    def __init__(self):
        self.last = None

    def __call__(self, values, axes):
        if self.last is not None:
            values, _ = lax.optimization_barrier((values, self.last))
        self.last = lax.all_to_all(values, axes, 0, 0, tiled=True)
        return self.last

    def copies(self, values, axes, count):
        return self(jnp.broadcast_to(values[None], (count,) + values.shape), axes)

    def columns(self, values, axes, count):
        rows, width = values.shape
        blocks = values.reshape(rows, count, width // count).transpose(1, 0, 2)
        return self(blocks, axes).reshape(count * rows, -1)

    def rows(self, values, count):
        return self(values.reshape(count, values.shape[0] // count, values.shape[1]), ALL)


def side_by_side(blocks):
    return blocks.transpose(1, 0, 2).reshape(blocks.shape[1], -1)


def after(values, *waits):
    for wait in waits:
        values = values + (wait[(0,) * wait.ndim] > 3.395e38).astype(values.dtype)
    return values


def masked_total(mask, values):
    return jnp.sum(jnp.where(mask, values, 0), axis=-1)


def slot_layout(pred_row, order_row, token_row):
    length = pred_row.shape[0]
    index = jnp.arange(length)
    before = index[None, :] <= index[:, None]
    seen = masked_total(before, pred_row[None, :])
    masked = jnp.sum(pred_row)
    place = jnp.where(pred_row == 1, seen - 1, masked + index - seen)
    slot_hot = place[None, :] == jnp.arange(CAP)[:, None]
    rank_row = masked_total(order_row[None, :] == index[:, None], index[None, :])
    slot_rank = masked_total(slot_hot, rank_row[None, :])
    slot_target = masked_total(slot_hot, token_row[None, :])
    slot_pos = masked_total(slot_hot, index[None, :])
    allowed = rank_row[None, :] <= slot_rank[:, None]
    return slot_hot, slot_pos, slot_target, allowed, masked


def bucket_layout(content, vrows):
    index = jnp.arange(content.shape[0])
    same = content[None, :] == content[:, None]
    first = jnp.min(jnp.where(same, index[None, :], content.shape[0]), axis=1)
    is_first = first == index
    owner = content // vrows
    ahead = (owner[None, :] == owner[:, None]) & is_first[None, :] & (index[None, :] < first[:, None])
    return owner, jnp.sum(ahead.astype(jnp.int32), axis=1)


def bucket_round(content, owner, place, turn, owners, vrows):
    usable = BUCKET - 1
    local = place - turn * usable
    taken = (local >= 0) & (local < usable)
    flat = jnp.where(taken, owner * BUCKET + local, -1)
    hot = flat[None, :] == jnp.arange(owners * BUCKET)[:, None]
    wanted = jnp.max(jnp.where(hot, (content - owner * vrows)[None, :], -1), axis=1)
    return hot.astype(bfloat), wanted.reshape(owners, BUCKET)


def on_device(
    token_ids,
    pred_mask,
    fact_order,
    corpus,
    embed_table,
    table_moment,
    table_square,
    layer_weights,
    layer_moment,
    layer_square,
    position_table,
    position_moment,
    position_square,
    small_params,
    small_moment,
    small_square,
):
    exchange = Exchange()
    dp_devs = lax.axis_size("dp")
    owners = lax.axis_size(VOC)
    devices = dp_devs * owners
    vrows, width = embed_table.shape
    length = token_ids.shape[1]
    feed = layer_weights.shape[2]
    shared = jnp.concatenate([position_table, small_params]).T
    shared_rows = shared.shape[1]
    shared = jnp.pad(shared, ((0, 0), (0, -shared_rows % 128)))
    shard = jnp.concatenate([layer_weights[0], layer_weights[1], layer_weights[2], shared], axis=1)
    shard = lax.all_gather(shard.astype(bfloat), ALL, axis=0, tiled=True)
    table_b = embed_table.astype(bfloat)
    token_row = token_ids[0]
    pred_row = pred_mask[0]
    first_row = lax.axis_index(VOC) * vrows
    content = jnp.where(pred_row == 1, MASK_ID, token_row)
    slot_hot, slot_pos, slot_target, allowed, masked = slot_layout(pred_row, fact_order[0], token_row)
    owner, place = bucket_layout(content, vrows)
    hot, wanted = bucket_round(content, owner, place, 0, owners, vrows)
    note = jnp.concatenate(
        [slot_target, slot_pos, jnp.stack([masked, corpus[0], jnp.max(place)])]
    )
    packet = jnp.concatenate(
        [wanted, jnp.broadcast_to(note[None], (owners, note.shape[0]))], axis=1
    )
    packet = jnp.pad(packet, ((0, 0), (0, 256 - packet.shape[1])))
    packet = jnp.broadcast_to(packet[None], (dp_devs,) + packet.shape)
    packet = exchange(packet.reshape(devices, packet.shape[-1]), ALL)
    asked = packet[:, :BUCKET]
    tail = BUCKET + 2 * CAP
    counts_all = packet[:, tail]
    corpus_all = packet[:, tail + 1]
    rounds = jnp.max(packet[:, tail + 2]) // (BUCKET - 1) + 1
    group = lax.axis_index("dp") * owners
    outer = lax.axis_size("hi")

    def group_order(values):
        return values.reshape(outer, 2, 2, CAP).transpose(2, 1, 0, 3).reshape(-1)

    group_asked = lax.dynamic_slice_in_dim(asked, group, owners, 0)
    group_target = group_order(
        lax.dynamic_slice_in_dim(packet[:, BUCKET : BUCKET + CAP], group, owners, 0)
    )
    corpus_hot = corpus_all[:, None] == jnp.arange(NCORP)[None, :]
    corpus_counts = jnp.sum(jnp.where(corpus_hot, counts_all[:, None], 0), axis=0)
    seq_count = masked_total(corpus_hot, corpus_counts[None, :])
    seq_weight = 1.0 / (NCORP * seq_count.astype(single))
    slot_weight = jnp.where(
        jnp.arange(CAP)[None, :] < counts_all[:, None], seq_weight[:, None], 0.0
    )
    group_weight = group_order(lax.dynamic_slice_in_dim(slot_weight, group, owners, 0))

    def serve(asked_rows):
        served = jnp.take(table_b, jnp.maximum(asked_rows, 0).reshape(-1), axis=0)
        return served.reshape(owners, BUCKET, width)

    arrived = exchange(serve(group_asked), VOC)
    embed_rows = rows_dot(hot, arrived.reshape(-1, width))

    def more_rows(state):
        turn, rows = state
        hot_t, wanted_t = bucket_round(content, owner, place, turn, owners, vrows)
        asked_t = lax.all_to_all(wanted_t, VOC, 0, 0, tiled=True)
        arrived_t = lax.all_to_all(serve(asked_t), VOC, 0, 0, tiled=True)
        return turn + 1, rows + rows_dot(hot_t, arrived_t.reshape(-1, width))

    _, embed_rows = lax.while_loop(
        lambda state: state[0] < rounds, more_rows, (jnp.ones((), rounds.dtype), embed_rows)
    )
    few = devices <= 32
    near = 4
    allowed = allowed.astype(single)
    slot_hot = slot_hot.astype(single)
    (
        key_rows,
        value_rows,
        query_rows,
        mixed_b,
        middle,
        mid_normed,
        mid_inverse,
        stream_b,
        stream_normed,
        stream_inverse,
        query_init,
        init_normed,
        init_inverse,
        position_full,
        small_full,
    ) = attend_forward(embed_rows, slot_hot, allowed, shard, length, small_params.shape[0])
    middle_b, hidden, active_b, output_b, end_normed, end_inverse = feed_forward(
        middle, small_full, shard
    )
    if few:
        kept_rows = jnp.concatenate([mixed_b, middle_b], axis=1)
        kept_all = lax.all_gather(kept_rows, ALL, axis=0, tiled=True)
        stream_all = lax.all_gather(stream_b, NEAR, axis=0, tiled=True)
    group_rows = exchange.copies(output_b, "hi", outer).reshape(-1, width)
    group_rows = exchange.copies(group_rows, "mid", 2).reshape(-1, width)
    group_rows = exchange.copies(group_rows, "core", 2).reshape(-1, width)
    logits = trans_dot(group_rows, table_b)
    local_target = group_target - first_row
    target_hit = jnp.arange(vrows)[None, :] == local_target[:, None]
    row_top = jnp.max(logits, axis=1)
    row_total = jnp.sum(jnp.exp(logits - row_top[:, None]), axis=1)
    row_target = jnp.sum(jnp.where(target_hit, logits, 0.0), axis=1)
    stats = exchange.copies(jnp.stack([row_top, row_total]), VOC, owners)
    top_all = jnp.max(stats[:, 0], axis=0)
    total_all = jnp.sum(stats[:, 1] * jnp.exp(stats[:, 0] - top_all[None]), axis=0)
    log_total = top_all + jnp.log(total_all)
    own_place = lax.axis_index(("core", "mid", "hi"))
    own_total = lax.dynamic_slice_in_dim(log_total * group_weight, own_place * CAP, CAP, 0)
    loss_part = jnp.sum(own_total) - jnp.sum(row_target * group_weight)
    d_logits = (
        group_weight[:, None] * (jnp.exp(logits - log_total[:, None]) - target_hit.astype(single))
    ).astype(bfloat)
    def swapped(axis, part):
        side = lax.axis_index(axis)
        theirs = lax.ppermute(part(1 - side), axis, [(0, 1), (1, 0)])
        return part(side) + theirs

    half = owners * CAP // 2

    def rows_half(side):
        return plain_dot(lax.dynamic_slice_in_dim(d_logits, side * half, half, 0), table_b)

    d_output = swapped("core", rows_half)
    quarter = half // 2
    d_half = d_output
    d_output = swapped(
        "mid", lambda side: lax.dynamic_slice_in_dim(d_half, side * quarter, quarter, 0)
    )
    grad_head = rows_dot(d_logits, group_rows)
    grad_head = after(grad_head, d_half, *((stream_all,) if few else ()))
    heads = lax.all_gather(grad_head.astype(bfloat), "dp", axis=0, tiled=True)
    d_output = exchange(d_output.astype(bfloat).reshape(outer, CAP, width), "hi")
    if few:
        d_output, kept_all = lax.optimization_barrier((d_output, kept_all))
    d_branch, d_hidden, d_pre, d_attend, sums_feed = feed_backward(
        d_output,
        end_normed,
        end_inverse,
        hidden,
        small_full,
        mid_normed,
        mid_inverse,
        shard,
    )
    if few:
        wide = feed // devices
        both = jnp.concatenate(
            [
                d_hidden.reshape(CAP, devices, -1),
                d_attend.reshape(CAP, devices, -1),
            ],
            axis=2,
        ).reshape(CAP, -1)
        both = exchange.columns(both, ALL, devices)
        branch_all = lax.all_gather(d_branch, ALL, axis=0, tiled=True)
    d_query, d_key, d_value = attend_backward(
        d_attend, key_rows, value_rows, query_rows, allowed, shard
    )
    if few:
        piece = width // near
        pairs = jnp.concatenate(
            [d_key.reshape(length, near, piece), d_value.reshape(length, near, piece)], axis=2
        ).transpose(1, 0, 2)
        asks = d_query.reshape(CAP, near, piece).transpose(1, 0, 2)
        asks = jnp.concatenate([asks[:, : CAP // 2], asks[:, CAP // 2 :]], axis=2)
        pairs = exchange(jnp.concatenate([pairs, asks], axis=1), NEAR)
    hidden_rows = spread((content == MASK_ID).astype(single)[:, None])
    embed_back, grad_position, sums_back = project_backward(
        d_pre,
        d_query,
        d_key,
        d_value,
        slot_hot,
        hidden_rows,
        small_full,
        stream_normed,
        stream_inverse,
        init_normed,
        init_inverse,
        shard,
        heads,
    )
    grad_small = jnp.concatenate([sums_back[:5], sums_feed[:9]])
    mask_sum = sums_back[5]
    mask_left = mask_sum - lax.reduce_precision(mask_sum, 8, 7)
    mask_owner = MASK_ID // vrows
    is_left = (jnp.arange(BUCKET) == BUCKET - 1)[None, :] & (
        jnp.arange(owners) == mask_owner
    )[:, None]

    def plain_exchange(values, axes):
        return lax.all_to_all(values, axes, 0, 0, tiled=True)

    def give(hot_rows, extra, send):
        rows = plain_dot(hot_rows, embed_back).reshape(owners, BUCKET, width)
        rows = jnp.where(is_left[:, :, None] & extra, mask_left[None, None, :], rows)
        return send(rows.astype(bfloat), VOC).reshape(-1, width)

    def of_both(rows):
        if dp_devs == 2:
            return jnp.concatenate([rows, lax.ppermute(rows, "dp", [(0, 1), (1, 0)])])
        return lax.all_gather(rows, "dp", axis=0, tiled=True)

    def both_groups(asked_rows):
        if dp_devs == 2:
            return jnp.roll(asked_rows, -group, axis=0)
        return asked_rows

    split = vrows // dp_devs
    sides = lax.axis_index("dp") * split + jnp.array([0, split])

    def into_rows(heads, parts, asked_rows, given, sides):
        return lookup_grad(heads, parts, both_groups(asked_rows).reshape(1, -1), given, sides)

    last = (jnp.arange(BUCKET) == BUCKET - 1)[None, :]
    left_row = jnp.where(lax.axis_index(VOC) == mask_owner, MASK_ID - first_row, -1)
    given = give(hot, True, exchange)

    if few:
        near_pos = packet[:, BUCKET + CAP : tail].reshape(dp_devs * outer, near * CAP)
        near_pos = lax.dynamic_index_in_dim(
            near_pos, lax.axis_index(("dp", "hi")), 0, False
        )
        init_rows = norm_forward(position_full, small_full[0], small_full[1])[0].astype(bfloat)
        init_hot = near_pos[:, None] == jnp.arange(length)[None, :]
        init_all = plain_dot(init_hot.astype(bfloat), init_rows).astype(bfloat)
        asks = pairs[:, length:]
        asks = jnp.concatenate([asks[..., :piece], asks[..., piece:]], axis=1)
        grad_pair = rows_dot(stream_all, pairs[:, :length].reshape(near * length, -1))
        grad_ask = rows_dot(init_all, asks.reshape(near * CAP, piece))
        share = width // devices
        active_mine = exchange.columns(active_b, ALL, devices)
        grad_up = rows_dot(kept_all[:, width:], both[:, :wide])
        grad_out = rows_dot(kept_all[:, :width], both[:, wide:])
        grad_down = rows_dot(branch_all, active_mine)
        shared_grad = jnp.concatenate([grad_position, grad_small]).T
        results = jnp.concatenate(
            [grad_pair, grad_ask, grad_up, grad_down, grad_out, shared_grad], axis=1
        )
        results = results.astype(bfloat)
        results = exchange.rows(results, devices).astype(single)
        sides = after(sides, results)
        pieces = 3 * piece
        attn = jnp.sum(
            results[..., :pieces].reshape(dp_devs * outer, near, share, pieces), axis=0
        )
        shared_grad = jnp.sum(results[..., -shared_rows:], axis=0)
        single_parts = results[..., pieces:-shared_rows]
        part_square = (
            jnp.sum(attn * attn)
            + jnp.sum(single_parts * single_parts)
            + jnp.sum(shared_grad * shared_grad)
        )
        shared_grad = shared_grad.T
        position_grad, small_grad = shared_grad[:length], shared_grad[length:]
        grad_key, grad_value, grad_query = (
            side_by_side(attn[..., part * piece : (part + 1) * piece]) for part in range(3)
        )
        grad_up, grad_down, grad_out = (
            side_by_side(single_parts[..., low:high])
            for low, high in ((0, wide), (wide, 2 * wide), (2 * wide, None))
        )
        layer_grad = jnp.stack(
            [
                jnp.concatenate([grad_query, grad_key, grad_value, grad_out], axis=1),
                grad_up,
                grad_down,
            ]
        )
    else:
        whole = (
            jnp.concatenate(
                [
                    rows_dot(query_init.astype(bfloat), d_query),
                    rows_dot(stream_b, d_key),
                    rows_dot(stream_b, d_value),
                    rows_dot(mixed_b, d_attend),
                ],
                axis=1,
            ),
            rows_dot(middle_b, d_hidden),
            rows_dot(d_branch, active_b),
        )
        layer_grad = jnp.stack(
            [lax.psum_scatter(part, ALL, scatter_dimension=0, tiled=True) for part in whole]
        )
        shared_grad = jnp.concatenate([grad_position, grad_small]).T
        shared_grad = lax.psum_scatter(shared_grad, ALL, scatter_dimension=0, tiled=True).T
        position_grad, small_grad = shared_grad[:length], shared_grad[length:]
        part_square = jnp.sum(layer_grad * layer_grad) + jnp.sum(shared_grad * shared_grad)
    table_grad, table_square_sum = into_rows(
        heads, dp_devs, jnp.where(last, left_row, asked), of_both(given), sides
    )

    def more_grads(state):
        turn, grads, _ = state
        hot_t, wanted_t = bucket_round(content, owner, place, turn, owners, vrows)
        wanted_t = jnp.broadcast_to(wanted_t[None], (dp_devs,) + wanted_t.shape)
        asked_t = lax.all_to_all(
            wanted_t.reshape(devices, BUCKET), ALL, 0, 0, tiled=True
        )
        given_t = of_both(give(hot_t, False, plain_exchange))
        return (turn + 1,) + tuple(into_rows(grads, 1, asked_t, given_t, sides))

    _, table_grad, table_square_sum = lax.while_loop(
        lambda state: state[0] < rounds,
        more_grads,
        (jnp.ones((), rounds.dtype), table_grad, table_square_sum),
    )
    square_part = jnp.sum(table_square_sum) + part_square
    totals = exchange.copies(jnp.stack([square_part, loss_part]), ALL, devices)
    total_square, loss_value = jnp.sum(totals, axis=0)
    grad_norm = jnp.sqrt(total_square)
    factor = jnp.minimum(1.0, clip_norm / grad_norm)
    (
        norms,
        layer_first,
        layer_second,
        layer_dir,
        position_first,
        position_second,
        position_dir,
        small_first,
        small_second,
        small_dir,
    ) = update_norms(
        totals,
        (embed_table, table_moment, table_square, table_grad),
        (layer_weights, layer_moment, layer_square, layer_grad),
        (position_table, position_moment, position_square, position_grad),
        (small_params, small_moment, small_square, small_grad),
        split,
        lax.axis_index("dp"),
    )
    factor_late, norms = lax.optimization_barrier((factor, norms))
    pairs = exchange.copies(norms[:6, :2].reshape(-1), ALL, devices)
    table_first, table_second, _ = adam_moments(
        embed_table, table_moment, table_square, table_grad, factor_late
    )
    trust_norms = jnp.sqrt(jnp.sum(pairs, axis=0)).reshape(6, 2)
    table_next, layer_next, position_next, small_next = final_update(
        pairs,
        (embed_table, table_first, table_second),
        (
            layer_weights,
            layer_dir,
            position_table,
            position_dir,
            small_params,
            small_dir,
        ),
    )
    return (
        loss_value,
        grad_norm,
        table_next,
        table_first,
        table_second,
        layer_next,
        layer_first,
        layer_second,
        position_next,
        position_first,
        position_second,
        small_next,
        small_first,
        small_second,
        trust_norms,
    )


def solution(mesh):
    dp_devs, owners = mesh.devices.shape
    fine = Mesh(mesh.devices.reshape(dp_devs, owners // 4, 2, 2), ALL)
    rows, inner = P(ALL, None), P(None, ALL)
    table, layer = P(VOC, None), P(None, ALL, None)
    return jax.shard_map(
        on_device,
        mesh=fine,
        in_specs=(rows,) * 3 + (P(ALL),) + (table,) * 3 + (layer,) * 3 + (inner,) * 6,
        out_specs=(P(), P()) + (table,) * 3 + (layer,) * 3 + (inner,) * 6 + (P(),),
        check_vma=False,
    )
```

```python
import jax
import jax.numpy as jnp
from jax import lax
from jax.experimental import pallas as pl
from jax.experimental.pallas import tpu as pltpu
from jax.sharding import Mesh
from jax.sharding import PartitionSpec as P

HEADS = 12
HD = 64
MASK_ID = 103
NCORP = 4
STEP = 5
CAP = 64


clip_norm = 0.1
learn_rate = 0.3
beta_first = 0.9
beta_second = 0.999
adam_eps = 1e-06
weight_decay = 0.01
norm_eps = 1e-05
masked_score = -1e30
BUCKET = 32
ALL = ("dp", "hi", "mid", "core")
VOC = ("hi", "mid", "core")
NEAR = ("mid", "core")
bfloat = jnp.bfloat16
single = jnp.float32


def plain_dot(left_op, right_op):
    return jnp.dot(left_op, right_op, preferred_element_type=single)


def trans_dot(left_op, right_op):
    return lax.dot_general(
        left_op, right_op, (((1,), (1,)), ((), ())), preferred_element_type=single
    )


def rows_dot(left_op, right_op):
    return lax.dot_general(
        left_op, right_op, (((0,), (0,)), ((), ())), preferred_element_type=single
    )


def column_sum(values):
    return jnp.sum(values.astype(single), axis=0)


def norm_forward(values, gain_row, bias_row):
    center = values - jnp.mean(values, axis=-1, keepdims=True)
    inverse = lax.rsqrt(jnp.mean(center * center, axis=-1, keepdims=True) + norm_eps)
    normed = center * inverse
    return (normed * gain_row + bias_row, (normed, inverse))


def norm_backward(upstream, kept_norm, gain_row):
    normed, inverse = kept_norm
    scaled = upstream * gain_row
    inner = (
        scaled
        - jnp.mean(scaled, axis=-1, keepdims=True)
        - normed * jnp.mean(scaled * normed, axis=-1, keepdims=True)
    )
    return (inner * inverse, jnp.sum(upstream * normed, axis=0), jnp.sum(upstream, axis=0))


def pair_masks(rows):
    lane = lax.broadcasted_iota(jnp.int32, (rows, 2 * HD), 1)
    return lane < HD, lane >= HD


def head_probs(query_pair, key_pair, head_lanes, blocked):
    scores = trans_dot(jnp.where(head_lanes, query_pair, jnp.zeros_like(query_pair)), key_pair)
    scores = jnp.where(blocked, masked_score, scores * HD ** (-0.5))
    row_top = jnp.max(scores, axis=-1, keepdims=True)
    powers = jnp.exp(scores - row_top)
    return powers / jnp.sum(powers, axis=-1, keepdims=True)


def spread(column, lanes=128):
    return jnp.broadcast_to(column, (column.shape[0], lanes))


def row_of(ref, row):
    return ref[pl.ds(row, 1), :]


def attend_kernel(
    embed_ref, slot_ref, allowed_ref, shared_ref, weight_ref,
    key_ref, value_ref, query_ref, mixed_ref, middle_ref, normed_ref, inverse_ref,
    stream_ref, stream_normed_ref, stream_inverse_ref,
    init_ref, init_normed_ref, init_inverse_ref, position_ref, small_ref,
):
    step = pl.program_id(0)
    length = position_ref.shape[0]

    @pl.when(step == 0)
    def _():
        shared = shared_ref[...].astype(single).T
        position_ref[...] = shared[:length]
        small_ref[...] = shared[length : length + small_ref.shape[0]]
        gain, bias = row_of(small_ref, 0), row_of(small_ref, 1)
        stream, (normed, inverse) = norm_forward(embed_ref[...] + position_ref[...], gain, bias)
        stream_ref[...] = stream.astype(bfloat)
        stream_normed_ref[...] = normed
        stream_inverse_ref[...] = spread(inverse)
        chosen = plain_dot(slot_ref[...].astype(bfloat), position_ref[...].astype(bfloat))
        init, (normed, inverse) = norm_forward(chosen, gain, bias)
        init_ref[...] = init
        init_normed_ref[...] = normed
        init_inverse_ref[...] = spread(inverse)
        key_ref[...] = plain_dot(stream_ref[...], weight_ref[...]).astype(bfloat)

    @pl.when(step == 1)
    def _():
        value_ref[...] = (
            plain_dot(stream_ref[...], weight_ref[...]) + row_of(small_ref, 3)
        ).astype(bfloat)

    @pl.when(step == 2)
    def _():
        query_ref[...] = (
            plain_dot(init_ref[...].astype(bfloat), weight_ref[...]) + row_of(small_ref, 2)
        ).astype(bfloat)
        blocked = allowed_ref[...] == 0.0
        low, high = pair_masks(query_ref.shape[0])

        def one_pair(pair, carry):
            lanes = pl.ds(pl.multiple_of(pair * 2 * HD, 2 * HD), 2 * HD)
            query_pair, key_pair, value_pair = query_ref[:, lanes], key_ref[:, lanes], value_ref[:, lanes]
            left, right = (
                plain_dot(
                    head_probs(query_pair, key_pair, head_lanes, blocked).astype(bfloat), value_pair
                )
                for head_lanes in (low, high)
            )
            mixed_ref[:, lanes] = jnp.where(low, left, right).astype(bfloat)
            return carry

        lax.fori_loop(0, query_ref.shape[1] // (2 * HD), one_pair, 0)

    @pl.when(step == 3)
    def _():
        attend = plain_dot(mixed_ref[...], weight_ref[...]) + row_of(small_ref, 4)
        middle, (normed, inverse) = norm_forward(
            init_ref[...] + attend, row_of(small_ref, 5), row_of(small_ref, 6)
        )
        middle_ref[...] = middle
        normed_ref[...] = normed
        inverse_ref[...] = spread(inverse)


def kernel_call(body, name, steps, inputs, shapes, cost, scratch=()):
    fixed = lambda rank: lambda step: (0,) * rank

    def spec(shape, block, index):
        if block is None:
            return pl.BlockSpec(shape, fixed(len(shape)))
        return pl.BlockSpec(block, index)

    return pl.pallas_call(
        body,
        grid=(steps,),
        in_specs=[spec(array.shape, block, index) for array, block, index in inputs],
        out_specs=[spec(shape, block, index) for shape, _, block, index in shapes],
        out_shape=[jax.ShapeDtypeStruct(shape, kind) for shape, kind, _, _ in shapes],
        scratch_shapes=list(scratch),
        cost_estimate=pl.CostEstimate(flops=cost[0] // 64, bytes_accessed=cost[1] // 64, transcendentals=0),
        name=name,
    )(*(array for array, _, _ in inputs))


def whole(array):
    return array, None, None


def attend_forward(embed_rows, slot_hot, allowed, weights, length, small_count):
    width = embed_rows.shape[1]
    slots = slot_hot.shape[0]
    out = lambda rows, kind, columns=width: ((rows, columns), kind, None, None)
    shared = weights.shape[1] - 12 * width
    return kernel_call(
        attend_kernel,
        "attention_forward",
        4,
        [
            whole(embed_rows),
            whole(slot_hot),
            whole(allowed),
            (weights, (width, shared), lambda step: (0, 12 * width // shared)),
            (
                weights,
                (width, width),
                lambda step: (0, jnp.where(step == 3, 3, (step + 1) % 3)),
            ),
        ],
        [
            out(length, bfloat), out(length, bfloat), out(slots, bfloat), out(slots, bfloat),
            out(slots, single), out(slots, single), out(slots, single, 128),
            out(length, bfloat), out(length, single), out(length, single, 128),
            out(slots, single), out(slots, single), out(slots, single, 128),
            out(length, single), out(small_count, single),
        ],
        (
            4 * length * width * width + 8 * slots * length * width,
            8 * width * width,
            HEADS * slots * length,
        ),
    )


def erf_half(hidden):
    return 0.5 * (1.0 + lax.erf(hidden * 0.5**0.5))


def feed_kernel(
    middle_ref, small_ref, up_ref, down_ref,
    middle_b_ref, hidden_ref, active_ref, output_ref, normed_ref, inverse_ref, total_ref,
):
    step = pl.program_id(0)

    @pl.when(step == 0)
    def _():
        middle_b_ref[...] = middle_ref[...].astype(bfloat)
        total_ref[...] = middle_ref[...] + row_of(small_ref, 11)

    hidden = plain_dot(middle_b_ref[...], up_ref[...]) + row_of(small_ref, 7 + step)
    hidden_ref[...] = hidden
    active = (hidden * erf_half(hidden)).astype(bfloat)
    active_ref[...] = active
    total_ref[...] += trans_dot(active, down_ref[...])

    @pl.when(step == pl.num_programs(0) - 1)
    def _():
        output, (normed, inverse) = norm_forward(
            total_ref[...], row_of(small_ref, 12), row_of(small_ref, 13)
        )
        output_ref[...] = output.astype(bfloat)
        normed_ref[...] = normed
        inverse_ref[...] = spread(inverse)


def feed_forward(middle, small_full, weights):
    slots, width = middle.shape
    wide = lambda kind: ((slots, 4 * width), kind, (slots, width), lambda step: (0, step))
    out = lambda kind, columns=width: ((slots, columns), kind, None, None)
    return kernel_call(
        feed_kernel,
        "feed_forward",
        4,
        [
            whole(middle),
            whole(small_full),
            (weights, (width, width), lambda step: (0, 4 + step)),
            (weights, (width, width), lambda step: (0, 8 + step)),
        ],
        [
            out(bfloat), wide(single), wide(bfloat), out(bfloat), out(single), out(single, 128),
        ],
        (16 * slots * width * width, 16 * width * width, 4 * slots * width),
        [pltpu.VMEM((slots, width), single)],
    )


def norm_back(upstream, normed, inverse, gain_row):
    return norm_backward(upstream, (normed, inverse), gain_row)


def feed_back_kernel(
    parts_ref, normed_ref, inverse_ref, hidden_ref, small_ref, mid_normed_ref, mid_inverse_ref,
    up_ref, down_ref,
    d_branch_ref, d_hidden_ref, d_pre_ref, d_attend_ref, sums_ref, d_middle_ref,
):
    step = pl.program_id(0)

    @pl.when(step == 0)
    def _():
        sums_ref[...] = jnp.zeros_like(sums_ref)
        d_sum, gain, bias = norm_back(
            jnp.sum(parts_ref[...].astype(single), axis=0), normed_ref[...], inverse_ref[:, :1], row_of(small_ref, 12)
        )
        d_branch = d_sum.astype(bfloat)
        d_branch_ref[...] = d_branch
        d_middle_ref[...] = d_sum
        sums_ref[pl.ds(6, 1), :] = column_sum(d_branch)[None]
        sums_ref[pl.ds(7, 1), :] = gain[None]
        sums_ref[pl.ds(8, 1), :] = bias[None]

    hidden = hidden_ref[...]
    slope = erf_half(hidden) + hidden * jnp.exp(-0.5 * hidden * hidden) * (2.0 * jnp.pi) ** (-0.5)
    d_hidden = (plain_dot(d_branch_ref[...], down_ref[...]) * slope).astype(bfloat)
    d_hidden_ref[...] = d_hidden
    sums_ref[pl.ds(2 + step, 1), :] = column_sum(d_hidden)[None]
    d_middle_ref[...] += trans_dot(d_hidden, up_ref[...])

    @pl.when(step == pl.num_programs(0) - 1)
    def _():
        d_pre, gain, bias = norm_back(
            d_middle_ref[...], mid_normed_ref[...], mid_inverse_ref[:, :1], row_of(small_ref, 5)
        )
        d_pre_ref[...] = d_pre
        d_attend_ref[...] = d_pre.astype(bfloat)
        sums_ref[pl.ds(0, 1), :] = gain[None]
        sums_ref[pl.ds(1, 1), :] = bias[None]


def feed_backward(parts, normed, inverse, hidden, small_full, mid_normed, mid_inverse, weights):
    slots, width = normed.shape
    block = (slots, width), lambda step: (0, step)
    out = lambda kind, rows=slots: ((rows, width), kind, None, None)
    return kernel_call(
        feed_back_kernel,
        "feed_backward",
        4,
        [
            whole(parts),
            whole(normed),
            whole(inverse),
            (hidden,) + block,
            whole(small_full),
            whole(mid_normed),
            whole(mid_inverse),
            (weights, (width, width), lambda step: (0, 4 + step)),
            (weights, (width, width), lambda step: (0, 8 + step)),
        ],
        [
            out(bfloat), ((slots, 4 * width), bfloat) + block, out(single), out(bfloat),
            out(single, 16),
        ],
        (16 * slots * width * width, 16 * width * width, 8 * slots * width),
        [pltpu.VMEM((slots, width), single)],
    )


def attend_back_kernel(
    d_attend_ref, key_ref, value_ref, query_ref, allowed_ref, weight_ref,
    d_query_ref, d_key_ref, d_value_ref, d_mixed_ref,
):
    d_mixed_ref[...] = trans_dot(d_attend_ref[...], weight_ref[...]).astype(bfloat)
    blocked = allowed_ref[...] == 0.0
    slots, length = blocked.shape
    low, high = pair_masks(slots)
    low_long, _ = pair_masks(length)
    scale = HD ** (-0.5)

    def one_pair(pair, carry):
        lanes = pl.ds(pl.multiple_of(pair * 2 * HD, 2 * HD), 2 * HD)
        query_pair, key_pair, value_pair = query_ref[:, lanes], key_ref[:, lanes], value_ref[:, lanes]
        mixed_pair = d_mixed_ref[:, lanes]
        found = []
        for head_lanes in (low, high):
            probs = head_probs(query_pair, key_pair, head_lanes, blocked)
            d_probs = trans_dot(
                jnp.where(head_lanes, mixed_pair, jnp.zeros_like(mixed_pair)), value_pair
            )
            inner = jnp.sum(probs * d_probs, axis=-1, keepdims=True)
            d_scores = (probs * (d_probs - inner)).astype(bfloat)
            found.append(
                (
                    plain_dot(d_scores, key_pair) * scale,
                    rows_dot(d_scores, query_pair) * scale,
                    rows_dot(probs.astype(bfloat), mixed_pair),
                )
            )
        d_query_ref[:, lanes] = jnp.where(low, found[0][0], found[1][0]).astype(bfloat)
        d_key_ref[:, lanes] = jnp.where(low_long, found[0][1], found[1][1]).astype(bfloat)
        d_value_ref[:, lanes] = jnp.where(low_long, found[0][2], found[1][2]).astype(bfloat)
        return carry

    lax.fori_loop(0, query_ref.shape[1] // (2 * HD), one_pair, 0)


def attend_backward(d_attend, key_rows, value_rows, query_rows, allowed, weights):
    length, width = key_rows.shape
    slots = d_attend.shape[0]
    out = lambda rows: ((rows, width), bfloat, None, None)
    return kernel_call(
        attend_back_kernel,
        "attention_backward",
        1,
        [
            whole(d_attend),
            whole(key_rows),
            whole(value_rows),
            whole(query_rows),
            whole(allowed),
            (weights, (width, width), lambda step: (0, 3)),
        ],
        [out(slots), out(length), out(length)],
        (
            2 * slots * width * width + 20 * slots * length * width,
            2 * width * width,
            HEADS * slots * length,
        ),
        [pltpu.VMEM((slots, width), bfloat)],
    )


def project_back_kernel(
    d_pre_ref, d_query_ref, d_key_ref, d_value_ref, slot_ref, hidden_row_ref, small_ref,
    normed_ref, inverse_ref, init_normed_ref, init_inverse_ref, weight_ref,
    embed_ref, position_ref, sums_ref, d_stream_ref, d_init_ref,
):
    step = pl.program_id(0)

    @pl.when(step == 0)
    def _():
        d_init_ref[...] = d_pre_ref[...] + trans_dot(d_query_ref[...], weight_ref[...])

    @pl.when(step == 1)
    def _():
        d_stream_ref[...] = trans_dot(d_key_ref[...], weight_ref[...])

    @pl.when(step == 2)
    def _():
        gain_row = row_of(small_ref, 0)
        d_stream = d_stream_ref[...] + trans_dot(d_value_ref[...], weight_ref[...])
        d_start, gain_init, bias_init = norm_back(
            d_init_ref[...], init_normed_ref[...], init_inverse_ref[:, :1], gain_row
        )
        d_embed, gain, bias = norm_back(
            d_stream, normed_ref[...], inverse_ref[:, :1], gain_row
        )
        position_ref[...] = d_embed + lax.dot_general(
            slot_ref[...],
            d_start,
            (((0,), (0,)), ((), ())),
            precision=lax.Precision.HIGHEST,
            preferred_element_type=single,
        )
        embed_b = d_embed.astype(bfloat)
        embed_ref[...] = embed_b
        sums_ref[...] = jnp.zeros_like(sums_ref)
        sums_ref[pl.ds(0, 1), :] = (gain_init + gain)[None]
        sums_ref[pl.ds(1, 1), :] = (bias_init + bias)[None]
        sums_ref[pl.ds(2, 1), :] = column_sum(d_query_ref[...])[None]
        sums_ref[pl.ds(3, 1), :] = column_sum(d_value_ref[...])[None]
        sums_ref[pl.ds(4, 1), :] = column_sum(d_pre_ref[...].astype(bfloat))[None]
        masked = jnp.where(hidden_row_ref[:, :1] > 0.0, embed_b.astype(single), 0.0)
        sums_ref[pl.ds(5, 1), :] = jnp.sum(masked, axis=0)[None]


def project_backward(
    d_pre, d_query, d_key, d_value, slot_hot, hidden_rows, small_full,
    normed, inverse, init_normed, init_inverse, weights,
):
    length, width = normed.shape
    slots = d_pre.shape[0]
    arrays = (
        d_pre, d_query, d_key, d_value, slot_hot, hidden_rows, small_full,
        normed, inverse, init_normed, init_inverse,
    )
    return kernel_call(
        project_back_kernel,
        "projection_backward",
        3,
        [whole(array) for array in arrays]
        + [(weights, (width, width), lambda step: (0, step))],
        [
            ((length, width), bfloat, None, None),
            ((length, width), single, None, None),
            ((8, width), single, None, None),
        ],
        (5 * length * width * width, 6 * width * width, 0),
        [pltpu.VMEM((length, width), single), pltpu.VMEM((slots, width), single)],
    )


def adam_direction(weight_arr, new_first, new_second):
    first_scale, second_scale = 1.0 / (1.0 - beta_first**STEP), 1.0 / (1.0 - beta_second**STEP)
    scaled = new_second * second_scale
    return (new_first * first_scale) / (
        scaled * lax.rsqrt(scaled) + adam_eps
    ) + weight_decay * weight_arr


def adam_moments(weight_arr, first_mom, second_mom, gradient, factor):
    clipped = gradient * factor
    new_first = beta_first * first_mom + (1.0 - beta_first) * clipped
    new_second = beta_second * second_mom + (1.0 - beta_second) * clipped * clipped
    return (new_first, new_second, adam_direction(weight_arr, new_first, new_second))


def row_block(count, most=240):
    return most if count % most == 0 else count


def lookup_kernel(parts, *refs):
    step = pl.program_id(0)
    head_refs, (asked_ref, given_ref, side_ref, grad_ref, square_ref) = refs[:parts], refs[parts:]
    rows, width = grad_ref.shape
    base = step * rows
    row_hot = asked_ref[...] == base + lax.broadcasted_iota(
        jnp.int32, (rows, asked_ref.shape[1]), 0
    )
    grad = plain_dot(row_hot.astype(bfloat), given_ref[...])
    for head_ref in head_refs:
        grad += head_ref[...].astype(single)
    grad_ref[...] = grad
    place = base + lax.broadcasted_iota(jnp.int32, (rows, width), 0)
    own = (place >= side_ref[0]) & (place < side_ref[1])

    @pl.when(step == 0)
    def _():
        square_ref[...] = jnp.zeros_like(square_ref)

    square_ref[...] += jnp.sum(jnp.where(own, grad * grad, 0.0), axis=0, keepdims=True)


def lookup_grad(heads, parts, asked_rows, given, sides):
    vrows, width = heads.shape[0] // parts, heads.shape[1]
    rows = vrows // 4
    block = pl.BlockSpec((rows, width), lambda step: (step, 0))
    whole_spec = lambda array: pl.BlockSpec(array.shape, lambda step: (0, 0))
    return pl.pallas_call(
        lambda *refs: lookup_kernel(parts, *refs),
        grid=(4,),
        in_specs=[
            pl.BlockSpec((rows, width), lambda step, part=part: (4 * part + step, 0))
            for part in range(parts)
        ]
        + [
            whole_spec(asked_rows),
            whole_spec(given),
            pl.BlockSpec(memory_space=pltpu.SMEM),
        ],
        out_specs=[block, pl.BlockSpec((1, width), lambda step: (0, 0))],
        out_shape=[
            jax.ShapeDtypeStruct((vrows, width), single),
            jax.ShapeDtypeStruct((1, width), single),
        ],
        cost_estimate=pl.CostEstimate(flops=0, bytes_accessed=0, transcendentals=0),
        name="table_gradient",
    )(*[heads] * parts, asked_rows, given, sides)


def full_sum(values):
    return jnp.sum(jnp.sum(values, axis=1, keepdims=True), axis=0, keepdims=True)


def pair_row(weight_sum, dir_sum):
    lane = lax.broadcasted_iota(jnp.int32, (1, 128), 1)
    return jnp.where(lane == 0, weight_sum, dir_sum)


def norms_kernel(offset_ref, *refs):
    total_ref, table_refs, layer_refs, position_refs, small_refs = (
        refs[0], refs[1:5], refs[5:9], refs[9:13], refs[13:17],
    )
    norms_ref, layer_out, position_out, small_out = refs[17], refs[18:21], refs[21:24], refs[24:27]
    sums_ref = refs[27]
    step = pl.program_id(0)
    total_square = jnp.sum(total_ref[...], axis=0, keepdims=True)[:, :1]
    factor = jnp.minimum(1.0, clip_norm / jnp.sqrt(total_square))

    @pl.when(step == 0)
    def _():
        sums_ref[...] = jnp.zeros_like(sums_ref)
        norms_ref[...] = jnp.zeros_like(norms_ref)
        for row, group_refs, outs in ((4, position_refs, position_out), (5, small_refs, small_out)):
            weight_arr = group_refs[0][...]
            first, second, direction = adam_moments(
                weight_arr, group_refs[1][...], group_refs[2][...], group_refs[3][...], factor
            )
            for ref, value in zip(outs, (first, second, direction)):
                ref[...] = value
            norms_ref[pl.ds(row, 1), :] = pair_row(
                full_sum(weight_arr * weight_arr), full_sum(direction * direction)
            )

    @pl.when(step < 3)
    def _():
        weight_arr, first_mom, second_mom, gradient = (ref[0] for ref in layer_refs)
        first, second, direction = adam_moments(
            weight_arr, first_mom, second_mom, gradient, factor
        )
        for ref, value in zip(layer_out, (first, second, direction)):
            ref[0] = value
        norms_ref[pl.ds(1 + step, 1), :] = pair_row(
            full_sum(weight_arr * weight_arr), full_sum(direction * direction)
        )

    weight_arr = table_refs[0][...]
    _, _, direction = adam_moments(
        weight_arr, table_refs[1][...], table_refs[2][...], table_refs[3][...], factor
    )
    sums_ref[pl.ds(0, 1), :] += jnp.sum(weight_arr * weight_arr, axis=0, keepdims=True)
    sums_ref[pl.ds(1, 1), :] += jnp.sum(direction * direction, axis=0, keepdims=True)

    @pl.when(step == pl.num_programs(0) - 1)
    def _():
        norms_ref[pl.ds(0, 1), :] = pair_row(
            full_sum(sums_ref[pl.ds(0, 1), :]), full_sum(sums_ref[pl.ds(1, 1), :])
        )


def update_norms(totals, table, layer, position, small, split, dp_index):
    vrows, width = table[0].shape
    rows = row_block(split, 240)
    if split // rows < 3:
        rows = split // 3
    one_part = pl.BlockSpec(
        (1,) + layer[0].shape[1:], lambda step, offset: (jnp.minimum(step, 2), 0, 0)
    )
    fixed = lambda array: pl.BlockSpec(
        array.shape, lambda step, offset, rank=array.ndim: (0,) * rank
    )
    part = pl.BlockSpec((rows, width), lambda step, offset: (offset[0] + step, 0))
    groups = tuple(layer) + tuple(position) + tuple(small)
    outs = [
        jax.ShapeDtypeStruct(group[0].shape, single)
        for group in (layer, position, small)
        for _ in range(3)
    ]
    norms = jax.ShapeDtypeStruct((8, 128), single)
    return pl.pallas_call(
        norms_kernel,
        grid_spec=pltpu.PrefetchScalarGridSpec(
            num_scalar_prefetch=1,
            grid=(split // rows,),
            in_specs=[fixed(totals)]
            + [part] * 4
            + [one_part] * 4
            + [fixed(array) for array in groups[4:]],
            out_specs=[fixed(norms)] + [one_part] * 3 + [fixed(out) for out in outs[3:]],
            scratch_shapes=[pltpu.VMEM((8, width), single)],
        ),
        out_shape=[norms] + outs,
        cost_estimate=pl.CostEstimate(flops=0, bytes_accessed=0, transcendentals=0),
        name="update_norms",
    )((dp_index * (split // rows)).astype(jnp.int32)[None], totals, *table, *groups)


def final_kernel(
    pairs_ref, weight_ref, first_ref, second_ref,
    layer_ref, layer_dir_ref, position_ref, position_dir_ref, small_ref, small_dir_ref,
    next_ref, layer_next_ref, position_next_ref, small_next_ref,
):
    roots = jnp.sqrt(jnp.sum(pairs_ref[...], axis=0, keepdims=True))

    def rate(group):
        return learn_rate * (
            roots[:, 2 * group : 2 * group + 1] / roots[:, 2 * group + 1 : 2 * group + 2]
        )

    weight_arr = weight_ref[...]
    direction = adam_direction(weight_arr, first_ref[...], second_ref[...])
    next_ref[...] = weight_arr - rate(0) * direction

    step = pl.program_id(0)
    for part in range(3):

        @pl.when(step == part)
        def _():
            layer_next_ref[0] = layer_ref[0] - rate(1 + part) * layer_dir_ref[0]

    @pl.when(step == 0)
    def _():
        position_next_ref[...] = position_ref[...] - rate(4) * position_dir_ref[...]
        small_next_ref[...] = small_ref[...] - rate(5) * small_dir_ref[...]


def final_update(pairs, table, groups):
    vrows, width = table[0].shape
    rows = row_block(vrows, 480)
    if vrows // rows < 3:
        rows = row_block(vrows, 240)
    fixed = lambda array: pl.BlockSpec(array.shape, lambda step, rank=array.ndim: (0,) * rank)
    block = pl.BlockSpec((rows, width), lambda step: (step, 0))
    one_part = pl.BlockSpec((1,) + groups[0].shape[1:], lambda step: (jnp.minimum(step, 2), 0, 0))
    outs = [jax.ShapeDtypeStruct(array.shape, single) for array in groups[::2]]
    return pl.pallas_call(
        final_kernel,
        grid=(vrows // rows,),
        in_specs=[fixed(pairs)]
        + [block] * 3
        + [one_part] * 2
        + [fixed(array) for array in groups[2:]],
        out_specs=[block, one_part] + [fixed(out) for out in outs[1:]],
        out_shape=[jax.ShapeDtypeStruct((vrows, width), single)] + outs,
        cost_estimate=pl.CostEstimate(flops=0, bytes_accessed=0, transcendentals=0),
        name="final_update",
    )(pairs, *table, *groups)


class Exchange:
    def __init__(self):
        self.last = None

    def __call__(self, values, axes):
        if self.last is not None:
            values, _ = lax.optimization_barrier((values, self.last))
        self.last = lax.all_to_all(values, axes, 0, 0, tiled=True)
        return self.last

    def copies(self, values, axes, count):
        return self(jnp.broadcast_to(values[None], (count,) + values.shape), axes)

    def columns(self, values, axes, count):
        rows, width = values.shape
        blocks = values.reshape(rows, count, width // count).transpose(1, 0, 2)
        return self(blocks, axes).reshape(count * rows, -1)

    def rows(self, values, count):
        return self(values.reshape(count, values.shape[0] // count, values.shape[1]), ALL)


def side_by_side(blocks):
    return blocks.transpose(1, 0, 2).reshape(blocks.shape[1], -1)


def after(values, *waits):
    for wait in waits:
        values = values + (wait[(0,) * wait.ndim] > 3.395e38).astype(values.dtype)
    return values


def masked_total(mask, values):
    return jnp.sum(jnp.where(mask, values, 0), axis=-1)


def slot_layout(pred_row, order_row, token_row):
    length = pred_row.shape[0]
    index = jnp.arange(length)
    before = index[None, :] <= index[:, None]
    seen = masked_total(before, pred_row[None, :])
    masked = jnp.sum(pred_row)
    place = jnp.where(pred_row == 1, seen - 1, masked + index - seen)
    slot_hot = place[None, :] == jnp.arange(CAP)[:, None]
    rank_row = masked_total(order_row[None, :] == index[:, None], index[None, :])
    slot_rank = masked_total(slot_hot, rank_row[None, :])
    slot_target = masked_total(slot_hot, token_row[None, :])
    slot_pos = masked_total(slot_hot, index[None, :])
    allowed = rank_row[None, :] <= slot_rank[:, None]
    return slot_hot, slot_pos, slot_target, allowed, masked


def bucket_layout(content, vrows):
    index = jnp.arange(content.shape[0])
    same = content[None, :] == content[:, None]
    first = jnp.min(jnp.where(same, index[None, :], content.shape[0]), axis=1)
    is_first = first == index
    owner = content // vrows
    ahead = (owner[None, :] == owner[:, None]) & is_first[None, :] & (index[None, :] < first[:, None])
    return owner, jnp.sum(ahead.astype(jnp.int32), axis=1)


def bucket_round(content, owner, place, turn, owners, vrows):
    usable = BUCKET - 1
    local = place - turn * usable
    taken = (local >= 0) & (local < usable)
    flat = jnp.where(taken, owner * BUCKET + local, -1)
    hot = flat[None, :] == jnp.arange(owners * BUCKET)[:, None]
    wanted = jnp.max(jnp.where(hot, (content - owner * vrows)[None, :], -1), axis=1)
    return hot.astype(bfloat), wanted.reshape(owners, BUCKET)


def on_device(
    token_ids,
    pred_mask,
    fact_order,
    corpus,
    embed_table,
    table_moment,
    table_square,
    layer_weights,
    layer_moment,
    layer_square,
    position_table,
    position_moment,
    position_square,
    small_params,
    small_moment,
    small_square,
):
    exchange = Exchange()
    dp_devs = lax.axis_size("dp")
    owners = lax.axis_size(VOC)
    devices = dp_devs * owners
    vrows, width = embed_table.shape
    length = token_ids.shape[1]
    feed = layer_weights.shape[2]
    shared = jnp.concatenate([position_table, small_params]).T
    shared_rows = shared.shape[1]
    shared = jnp.pad(shared, ((0, 0), (0, -shared_rows % 128)))
    shard = jnp.concatenate([layer_weights[0], layer_weights[1], layer_weights[2], shared], axis=1)
    shard = lax.all_gather(shard.astype(bfloat), ALL, axis=0, tiled=True)
    table_b = embed_table.astype(bfloat)
    token_row = token_ids[0]
    pred_row = pred_mask[0]
    first_row = lax.axis_index(VOC) * vrows
    content = jnp.where(pred_row == 1, MASK_ID, token_row)
    slot_hot, slot_pos, slot_target, allowed, masked = slot_layout(pred_row, fact_order[0], token_row)
    owner, place = bucket_layout(content, vrows)
    hot, wanted = bucket_round(content, owner, place, 0, owners, vrows)
    note = jnp.concatenate(
        [slot_target, slot_pos, jnp.stack([masked, corpus[0], jnp.max(place)])]
    )
    packet = jnp.concatenate(
        [wanted, jnp.broadcast_to(note[None], (owners, note.shape[0]))], axis=1
    )
    packet = jnp.pad(packet, ((0, 0), (0, 256 - packet.shape[1])))
    packet = jnp.broadcast_to(packet[None], (dp_devs,) + packet.shape)
    packet = exchange(packet.reshape(devices, packet.shape[-1]), ALL)
    asked = packet[:, :BUCKET]
    tail = BUCKET + 2 * CAP
    counts_all = packet[:, tail]
    corpus_all = packet[:, tail + 1]
    rounds = jnp.max(packet[:, tail + 2]) // (BUCKET - 1) + 1
    group = lax.axis_index("dp") * owners
    outer = lax.axis_size("hi")

    def group_order(values):
        return values.reshape(outer, 2, 2, CAP).transpose(2, 1, 0, 3).reshape(-1)

    group_asked = lax.dynamic_slice_in_dim(asked, group, owners, 0)
    group_target = group_order(
        lax.dynamic_slice_in_dim(packet[:, BUCKET : BUCKET + CAP], group, owners, 0)
    )
    corpus_hot = corpus_all[:, None] == jnp.arange(NCORP)[None, :]
    corpus_counts = jnp.sum(jnp.where(corpus_hot, counts_all[:, None], 0), axis=0)
    seq_count = masked_total(corpus_hot, corpus_counts[None, :])
    seq_weight = 1.0 / (NCORP * seq_count.astype(single))
    slot_weight = jnp.where(
        jnp.arange(CAP)[None, :] < counts_all[:, None], seq_weight[:, None], 0.0
    )
    group_weight = group_order(lax.dynamic_slice_in_dim(slot_weight, group, owners, 0))

    def serve(asked_rows):
        served = jnp.take(table_b, jnp.maximum(asked_rows, 0).reshape(-1), axis=0)
        return served.reshape(owners, BUCKET, width)

    arrived = exchange(serve(group_asked), VOC)
    embed_rows = rows_dot(hot, arrived.reshape(-1, width))

    def more_rows(state):
        turn, rows = state
        hot_t, wanted_t = bucket_round(content, owner, place, turn, owners, vrows)
        asked_t = lax.all_to_all(wanted_t, VOC, 0, 0, tiled=True)
        arrived_t = lax.all_to_all(serve(asked_t), VOC, 0, 0, tiled=True)
        return turn + 1, rows + rows_dot(hot_t, arrived_t.reshape(-1, width))

    _, embed_rows = lax.while_loop(
        lambda state: state[0] < rounds, more_rows, (jnp.ones((), rounds.dtype), embed_rows)
    )
    few = devices <= 32
    near = 4
    allowed = allowed.astype(single)
    slot_hot = slot_hot.astype(single)
    (
        key_rows,
        value_rows,
        query_rows,
        mixed_b,
        middle,
        mid_normed,
        mid_inverse,
        stream_b,
        stream_normed,
        stream_inverse,
        query_init,
        init_normed,
        init_inverse,
        position_full,
        small_full,
    ) = attend_forward(embed_rows, slot_hot, allowed, shard, length, small_params.shape[0])
    middle_b, hidden, active_b, output_b, end_normed, end_inverse = feed_forward(
        middle, small_full, shard
    )
    if few:
        kept_rows = jnp.concatenate([mixed_b, middle_b], axis=1)
        kept_all = lax.all_gather(kept_rows, ALL, axis=0, tiled=True)
        stream_all = lax.all_gather(stream_b, NEAR, axis=0, tiled=True)
    group_rows = exchange.copies(output_b, "hi", outer).reshape(-1, width)
    group_rows = exchange.copies(group_rows, "mid", 2).reshape(-1, width)
    group_rows = exchange.copies(group_rows, "core", 2).reshape(-1, width)
    logits = trans_dot(group_rows, table_b)
    local_target = group_target - first_row
    target_hit = jnp.arange(vrows)[None, :] == local_target[:, None]
    row_top = jnp.max(logits, axis=1)
    row_total = jnp.sum(jnp.exp(logits - row_top[:, None]), axis=1)
    row_target = jnp.sum(jnp.where(target_hit, logits, 0.0), axis=1)
    stats = exchange.copies(jnp.stack([row_top, row_total]), VOC, owners)
    top_all = jnp.max(stats[:, 0], axis=0)
    total_all = jnp.sum(stats[:, 1] * jnp.exp(stats[:, 0] - top_all[None]), axis=0)
    log_total = top_all + jnp.log(total_all)
    own_place = lax.axis_index(("core", "mid", "hi"))
    own_total = lax.dynamic_slice_in_dim(log_total * group_weight, own_place * CAP, CAP, 0)
    loss_part = jnp.sum(own_total) - jnp.sum(row_target * group_weight)
    d_logits = (
        group_weight[:, None] * (jnp.exp(logits - log_total[:, None]) - target_hit.astype(single))
    ).astype(bfloat)
    def swapped(axis, kind, part):
        side = lax.axis_index(axis)
        theirs = lax.ppermute(part(1 - side).astype(kind), axis, [(0, 1), (1, 0)])
        return part(side) + theirs.astype(single)

    half = owners * CAP // 2

    def rows_half(side):
        return plain_dot(lax.dynamic_slice_in_dim(d_logits, side * half, half, 0), table_b)

    d_output = swapped("core", single, rows_half)
    quarter = half // 2
    d_half = d_output
    d_output = swapped(
        "mid", bfloat, lambda side: lax.dynamic_slice_in_dim(d_half, side * quarter, quarter, 0)
    )
    grad_head = rows_dot(d_logits, group_rows)
    head_b = grad_head.astype(bfloat)
    d_output, head_b = lax.optimization_barrier((d_output, head_b))
    heads = lax.all_gather(head_b, "dp", axis=0, tiled=True)
    d_output = exchange(d_output.astype(bfloat).reshape(outer, CAP, width), "hi")
    if few:
        d_output, kept_all = lax.optimization_barrier((d_output, kept_all))
    d_branch, d_hidden, d_pre, d_attend, sums_feed = feed_backward(
        d_output,
        end_normed,
        end_inverse,
        hidden,
        small_full,
        mid_normed,
        mid_inverse,
        shard,
    )
    if few:
        wide = feed // devices
        both = jnp.concatenate(
            [
                d_hidden.reshape(CAP, devices, -1),
                d_attend.reshape(CAP, devices, -1),
            ],
            axis=2,
        ).reshape(CAP, -1)
        both = exchange.columns(both, ALL, devices)
        branch_all = lax.all_gather(d_branch, ALL, axis=0, tiled=True)
    d_query, d_key, d_value = attend_backward(
        d_attend, key_rows, value_rows, query_rows, allowed, shard
    )
    if few:
        piece = width // near
        pairs = jnp.concatenate(
            [d_key.reshape(length, near, piece), d_value.reshape(length, near, piece)], axis=2
        ).transpose(1, 0, 2)
        asks = d_query.reshape(CAP, near, piece).transpose(1, 0, 2)
        asks = jnp.concatenate([asks[:, : CAP // 2], asks[:, CAP // 2 :]], axis=2)
        pairs = exchange(jnp.concatenate([pairs, asks], axis=1), NEAR)
    hidden_rows = spread((content == MASK_ID).astype(single)[:, None])
    embed_back, grad_position, sums_back = project_backward(
        d_pre,
        d_query,
        d_key,
        d_value,
        slot_hot,
        hidden_rows,
        small_full,
        stream_normed,
        stream_inverse,
        init_normed,
        init_inverse,
        shard,
    )
    grad_small = jnp.concatenate([sums_back[:5], sums_feed[:9]])
    mask_sum = sums_back[5]
    mask_left = mask_sum - lax.reduce_precision(mask_sum, 8, 7)
    mask_owner = MASK_ID // vrows
    is_left = (jnp.arange(BUCKET) == BUCKET - 1)[None, :] & (
        jnp.arange(owners) == mask_owner
    )[:, None]

    def plain_exchange(values, axes):
        return lax.all_to_all(values, axes, 0, 0, tiled=True)

    def give(hot_rows, extra, send):
        rows = plain_dot(hot_rows, embed_back).reshape(owners, BUCKET, width)
        rows = jnp.where(is_left[:, :, None] & extra, mask_left[None, None, :], rows)
        return send(rows.astype(bfloat), VOC).reshape(-1, width)

    def of_both(rows):
        if dp_devs == 2:
            return jnp.concatenate([rows, lax.ppermute(rows, "dp", [(0, 1), (1, 0)])])
        return lax.all_gather(rows, "dp", axis=0, tiled=True)

    def both_groups(asked_rows):
        if dp_devs == 2:
            return jnp.roll(asked_rows, -group, axis=0)
        return asked_rows

    split = vrows // dp_devs
    sides = lax.axis_index("dp") * split + jnp.array([0, split])

    def into_rows(heads, parts, asked_rows, given, sides):
        return lookup_grad(heads, parts, both_groups(asked_rows).reshape(1, -1), given, sides)

    last = (jnp.arange(BUCKET) == BUCKET - 1)[None, :]
    left_row = jnp.where(lax.axis_index(VOC) == mask_owner, MASK_ID - first_row, -1)
    given = give(hot, True, exchange)

    if few:
        near_pos = packet[:, BUCKET + CAP : tail].reshape(dp_devs * outer, near * CAP)
        near_pos = lax.dynamic_index_in_dim(
            near_pos, lax.axis_index(("dp", "hi")), 0, False
        )
        init_rows = norm_forward(position_full, small_full[0], small_full[1])[0].astype(bfloat)
        init_hot = near_pos[:, None] == jnp.arange(length)[None, :]
        init_all = plain_dot(init_hot.astype(bfloat), init_rows).astype(bfloat)
        asks = pairs[:, length:]
        asks = jnp.concatenate([asks[..., :piece], asks[..., piece:]], axis=1)
        grad_pair = rows_dot(stream_all, pairs[:, :length].reshape(near * length, -1))
        grad_ask = rows_dot(init_all, asks.reshape(near * CAP, piece))
        share = width // devices
        active_mine = exchange.columns(active_b, ALL, devices)
        grad_up = rows_dot(kept_all[:, width:], both[:, :wide])
        grad_out = rows_dot(kept_all[:, :width], both[:, wide:])
        grad_down = rows_dot(branch_all, active_mine)
        shared_grad = jnp.concatenate([grad_position, grad_small]).T
        results = jnp.concatenate(
            [grad_pair, grad_ask, grad_up, grad_down, grad_out, shared_grad], axis=1
        )
        results = results.astype(bfloat)
        results = exchange.rows(results, devices).astype(single)
        sides = after(sides, results)
        pieces = 3 * piece
        attn = jnp.sum(
            results[..., :pieces].reshape(dp_devs * outer, near, share, pieces), axis=0
        )
        shared_grad = jnp.sum(results[..., -shared_rows:], axis=0)
        single_parts = results[..., pieces:-shared_rows]
        part_square = (
            jnp.sum(attn * attn)
            + jnp.sum(single_parts * single_parts)
            + jnp.sum(shared_grad * shared_grad)
        )
        shared_grad = shared_grad.T
        position_grad, small_grad = shared_grad[:length], shared_grad[length:]
        grad_key, grad_value, grad_query = (
            side_by_side(attn[..., part * piece : (part + 1) * piece]) for part in range(3)
        )
        grad_up, grad_down, grad_out = (
            side_by_side(single_parts[..., low:high])
            for low, high in ((0, wide), (wide, 2 * wide), (2 * wide, None))
        )
        layer_grad = jnp.stack(
            [
                jnp.concatenate([grad_query, grad_key, grad_value, grad_out], axis=1),
                grad_up,
                grad_down,
            ]
        )
    else:
        whole = (
            jnp.concatenate(
                [
                    rows_dot(query_init.astype(bfloat), d_query),
                    rows_dot(stream_b, d_key),
                    rows_dot(stream_b, d_value),
                    rows_dot(mixed_b, d_attend),
                ],
                axis=1,
            ),
            rows_dot(middle_b, d_hidden),
            rows_dot(d_branch, active_b),
        )
        layer_grad = jnp.stack(
            [lax.psum_scatter(part, ALL, scatter_dimension=0, tiled=True) for part in whole]
        )
        shared_grad = jnp.concatenate([grad_position, grad_small]).T
        shared_grad = lax.psum_scatter(shared_grad, ALL, scatter_dimension=0, tiled=True).T
        position_grad, small_grad = shared_grad[:length], shared_grad[length:]
        part_square = jnp.sum(layer_grad * layer_grad) + jnp.sum(shared_grad * shared_grad)
    table_grad, table_square_sum = into_rows(
        heads, dp_devs, jnp.where(last, left_row, asked), of_both(given), sides
    )

    def more_grads(state):
        turn, grads, _ = state
        hot_t, wanted_t = bucket_round(content, owner, place, turn, owners, vrows)
        wanted_t = jnp.broadcast_to(wanted_t[None], (dp_devs,) + wanted_t.shape)
        asked_t = lax.all_to_all(
            wanted_t.reshape(devices, BUCKET), ALL, 0, 0, tiled=True
        )
        given_t = of_both(give(hot_t, False, plain_exchange))
        return (turn + 1,) + tuple(into_rows(grads, 1, asked_t, given_t, sides))

    _, table_grad, table_square_sum = lax.while_loop(
        lambda state: state[0] < rounds,
        more_grads,
        (jnp.ones((), rounds.dtype), table_grad, table_square_sum),
    )
    square_part = jnp.sum(table_square_sum) + part_square
    totals = exchange.copies(jnp.stack([square_part, loss_part]), ALL, devices)
    total_square, loss_value = jnp.sum(totals, axis=0)
    grad_norm = jnp.sqrt(total_square)
    factor = jnp.minimum(1.0, clip_norm / grad_norm)
    (
        norms,
        layer_first,
        layer_second,
        layer_dir,
        position_first,
        position_second,
        position_dir,
        small_first,
        small_second,
        small_dir,
    ) = update_norms(
        totals,
        (embed_table, table_moment, table_square, table_grad),
        (layer_weights, layer_moment, layer_square, layer_grad),
        (position_table, position_moment, position_square, position_grad),
        (small_params, small_moment, small_square, small_grad),
        split,
        lax.axis_index("dp"),
    )
    factor_late, norms = lax.optimization_barrier((factor, norms))
    pairs = exchange.copies(norms[:6, :2].reshape(-1), ALL, devices)
    table_first, table_second, _ = adam_moments(
        embed_table, table_moment, table_square, table_grad, factor_late
    )
    trust_norms = jnp.sqrt(jnp.sum(pairs, axis=0)).reshape(6, 2)
    table_next, layer_next, position_next, small_next = final_update(
        pairs,
        (embed_table, table_first, table_second),
        (
            layer_weights,
            layer_dir,
            position_table,
            position_dir,
            small_params,
            small_dir,
        ),
    )
    return (
        loss_value,
        grad_norm,
        table_next,
        table_first,
        table_second,
        layer_next,
        layer_first,
        layer_second,
        position_next,
        position_first,
        position_second,
        small_next,
        small_first,
        small_second,
        trust_norms,
    )


def solution(mesh):
    dp_devs, owners = mesh.devices.shape
    fine = Mesh(mesh.devices.reshape(dp_devs, owners // 4, 2, 2), ALL)
    rows, inner = P(ALL, None), P(None, ALL)
    table, layer = P(VOC, None), P(None, ALL, None)
    return jax.shard_map(
        on_device,
        mesh=fine,
        in_specs=(rows,) * 3 + (P(ALL),) + (table,) * 3 + (layer,) * 3 + (inner,) * 6,
        out_specs=(P(), P()) + (table,) * 3 + (layer,) * 3 + (inner,) * 6 + (P(),),
        check_vma=False,
    )
```

```python
import jax
import jax.numpy as jnp
from jax import lax
from jax.experimental import pallas as pl
from jax.experimental.pallas import tpu as pltpu
from jax.sharding import Mesh
from jax.sharding import PartitionSpec as P

HEADS = 12
HD = 64
MASK_ID = 103
NCORP = 4
STEP = 5
CAP = 64


clip_norm = 0.1
learn_rate = 0.3
beta_first = 0.9
beta_second = 0.999
adam_eps = 1e-06
weight_decay = 0.01
norm_eps = 1e-05
masked_score = -1e30
BUCKET = 32
ALL = ("dp", "hi", "mid", "core")
VOC = ("hi", "mid", "core")
NEAR = ("mid", "core")
bfloat = jnp.bfloat16
single = jnp.float32


def plain_dot(left_op, right_op):
    return jnp.dot(left_op, right_op, preferred_element_type=single)


def trans_dot(left_op, right_op):
    return lax.dot_general(
        left_op, right_op, (((1,), (1,)), ((), ())), preferred_element_type=single
    )


def rows_dot(left_op, right_op):
    return lax.dot_general(
        left_op, right_op, (((0,), (0,)), ((), ())), preferred_element_type=single
    )


def column_sum(values):
    return jnp.sum(values.astype(single), axis=0)


def norm_forward(values, gain_row, bias_row):
    center = values - jnp.mean(values, axis=-1, keepdims=True)
    inverse = lax.rsqrt(jnp.mean(center * center, axis=-1, keepdims=True) + norm_eps)
    normed = center * inverse
    return (normed * gain_row + bias_row, (normed, inverse))


def norm_backward(upstream, kept_norm, gain_row):
    normed, inverse = kept_norm
    scaled = upstream * gain_row
    inner = (
        scaled
        - jnp.mean(scaled, axis=-1, keepdims=True)
        - normed * jnp.mean(scaled * normed, axis=-1, keepdims=True)
    )
    return (inner * inverse, jnp.sum(upstream * normed, axis=0), jnp.sum(upstream, axis=0))


def pair_masks(rows):
    lane = lax.broadcasted_iota(jnp.int32, (rows, 2 * HD), 1)
    return lane < HD, lane >= HD


def head_probs(query_pair, key_pair, head_lanes, blocked):
    scores = trans_dot(jnp.where(head_lanes, query_pair, jnp.zeros_like(query_pair)), key_pair)
    scores = jnp.where(blocked, masked_score, scores * HD ** (-0.5))
    row_top = jnp.max(scores, axis=-1, keepdims=True)
    powers = jnp.exp(scores - row_top)
    return powers / jnp.sum(powers, axis=-1, keepdims=True)


def spread(column, lanes=128):
    return jnp.broadcast_to(column, (column.shape[0], lanes))


def row_of(ref, row):
    return ref[pl.ds(row, 1), :]


def attend_kernel(
    embed_ref, slot_ref, allowed_ref, shared_ref, weight_ref,
    key_ref, value_ref, query_ref, mixed_ref, middle_ref, normed_ref, inverse_ref,
    stream_ref, stream_normed_ref, stream_inverse_ref,
    init_ref, init_normed_ref, init_inverse_ref, position_ref, small_ref,
):
    step = pl.program_id(0)
    length = position_ref.shape[0]

    @pl.when(step == 0)
    def _():
        shared = shared_ref[...].astype(single).T
        position_ref[...] = shared[:length]
        small_ref[...] = shared[length : length + small_ref.shape[0]]
        gain, bias = row_of(small_ref, 0), row_of(small_ref, 1)
        stream, (normed, inverse) = norm_forward(embed_ref[...] + position_ref[...], gain, bias)
        stream_ref[...] = stream.astype(bfloat)
        stream_normed_ref[...] = normed
        stream_inverse_ref[...] = spread(inverse)
        chosen = plain_dot(slot_ref[...].astype(bfloat), position_ref[...].astype(bfloat))
        init, (normed, inverse) = norm_forward(chosen, gain, bias)
        init_ref[...] = init
        init_normed_ref[...] = normed
        init_inverse_ref[...] = spread(inverse)
        key_ref[...] = plain_dot(stream_ref[...], weight_ref[...]).astype(bfloat)

    @pl.when(step == 1)
    def _():
        value_ref[...] = (
            plain_dot(stream_ref[...], weight_ref[...]) + row_of(small_ref, 3)
        ).astype(bfloat)

    @pl.when(step == 2)
    def _():
        query_ref[...] = (
            plain_dot(init_ref[...].astype(bfloat), weight_ref[...]) + row_of(small_ref, 2)
        ).astype(bfloat)
        blocked = allowed_ref[...] == 0.0
        low, high = pair_masks(query_ref.shape[0])

        def one_pair(pair, carry):
            lanes = pl.ds(pl.multiple_of(pair * 2 * HD, 2 * HD), 2 * HD)
            query_pair, key_pair, value_pair = query_ref[:, lanes], key_ref[:, lanes], value_ref[:, lanes]
            left, right = (
                plain_dot(
                    head_probs(query_pair, key_pair, head_lanes, blocked).astype(bfloat), value_pair
                )
                for head_lanes in (low, high)
            )
            mixed_ref[:, lanes] = jnp.where(low, left, right).astype(bfloat)
            return carry

        lax.fori_loop(0, query_ref.shape[1] // (2 * HD), one_pair, 0)

    @pl.when(step == 3)
    def _():
        attend = plain_dot(mixed_ref[...], weight_ref[...]) + row_of(small_ref, 4)
        middle, (normed, inverse) = norm_forward(
            init_ref[...] + attend, row_of(small_ref, 5), row_of(small_ref, 6)
        )
        middle_ref[...] = middle
        normed_ref[...] = normed
        inverse_ref[...] = spread(inverse)


def kernel_call(body, name, steps, inputs, shapes, cost, scratch=()):
    fixed = lambda rank: lambda step: (0,) * rank

    def spec(shape, block, index):
        if block is None:
            return pl.BlockSpec(shape, fixed(len(shape)))
        if block == "any":
            return pl.BlockSpec(memory_space=pl.ANY)
        return pl.BlockSpec(block, index)

    return pl.pallas_call(
        body,
        grid=(steps,),
        in_specs=[spec(array.shape, block, index) for array, block, index in inputs],
        out_specs=[spec(shape, block, index) for shape, _, block, index in shapes],
        out_shape=[jax.ShapeDtypeStruct(shape, kind) for shape, kind, _, _ in shapes],
        scratch_shapes=list(scratch),
        cost_estimate=pl.CostEstimate(flops=cost[0] // 64, bytes_accessed=cost[1] // 64, transcendentals=0),
        name=name,
    )(*(array for array, _, _ in inputs))


def whole(array):
    return array, None, None


def attend_forward(embed_rows, slot_hot, allowed, weights, length, small_count):
    width = embed_rows.shape[1]
    slots = slot_hot.shape[0]
    out = lambda rows, kind, columns=width: ((rows, columns), kind, None, None)
    shared = weights.shape[1] - 12 * width
    return kernel_call(
        attend_kernel,
        "attention_forward",
        4,
        [
            whole(embed_rows),
            whole(slot_hot),
            whole(allowed),
            (weights, (width, shared), lambda step: (0, 12 * width // shared)),
            (
                weights,
                (width, width),
                lambda step: (0, jnp.where(step == 3, 3, (step + 1) % 3)),
            ),
        ],
        [
            out(length, bfloat), out(length, bfloat), out(slots, bfloat), out(slots, bfloat),
            out(slots, single), out(slots, single), out(slots, single, 128),
            out(length, bfloat), out(length, single), out(length, single, 128),
            out(slots, single), out(slots, single), out(slots, single, 128),
            out(length, single), out(small_count, single),
        ],
        (
            4 * length * width * width + 8 * slots * length * width,
            8 * width * width,
            HEADS * slots * length,
        ),
    )


def erf_half(hidden):
    return 0.5 * (1.0 + lax.erf(hidden * 0.5**0.5))


def feed_kernel(
    middle_ref, small_ref, up_ref, down_ref,
    middle_b_ref, hidden_ref, active_ref, output_ref, normed_ref, inverse_ref, total_ref,
):
    step = pl.program_id(0)

    @pl.when(step == 0)
    def _():
        middle_b_ref[...] = middle_ref[...].astype(bfloat)
        total_ref[...] = middle_ref[...] + row_of(small_ref, 11)

    hidden = plain_dot(middle_b_ref[...], up_ref[...]) + row_of(small_ref, 7 + step)
    hidden_ref[...] = hidden
    active = (hidden * erf_half(hidden)).astype(bfloat)
    active_ref[...] = active
    total_ref[...] += trans_dot(active, down_ref[...])

    @pl.when(step == pl.num_programs(0) - 1)
    def _():
        output, (normed, inverse) = norm_forward(
            total_ref[...], row_of(small_ref, 12), row_of(small_ref, 13)
        )
        output_ref[...] = output.astype(bfloat)
        normed_ref[...] = normed
        inverse_ref[...] = spread(inverse)


def feed_forward(middle, small_full, weights):
    slots, width = middle.shape
    wide = lambda kind: ((slots, 4 * width), kind, (slots, width), lambda step: (0, step))
    out = lambda kind, columns=width: ((slots, columns), kind, None, None)
    return kernel_call(
        feed_kernel,
        "feed_forward",
        4,
        [
            whole(middle),
            whole(small_full),
            (weights, (width, width), lambda step: (0, 4 + step)),
            (weights, (width, width), lambda step: (0, 8 + step)),
        ],
        [
            out(bfloat), wide(single), wide(bfloat), out(bfloat), out(single), out(single, 128),
        ],
        (16 * slots * width * width, 16 * width * width, 4 * slots * width),
        [pltpu.VMEM((slots, width), single)],
    )


def norm_back(upstream, normed, inverse, gain_row):
    return norm_backward(upstream, (normed, inverse), gain_row)


def feed_back_kernel(
    parts_ref, normed_ref, inverse_ref, hidden_ref, small_ref, mid_normed_ref, mid_inverse_ref,
    up_ref, down_ref,
    d_branch_ref, d_hidden_ref, d_pre_ref, d_attend_ref, sums_ref, d_middle_ref,
):
    step = pl.program_id(0)

    @pl.when(step == 0)
    def _():
        sums_ref[...] = jnp.zeros_like(sums_ref)
        d_sum, gain, bias = norm_back(
            jnp.sum(parts_ref[...].astype(single), axis=0), normed_ref[...], inverse_ref[:, :1], row_of(small_ref, 12)
        )
        d_branch = d_sum.astype(bfloat)
        d_branch_ref[...] = d_branch
        d_middle_ref[...] = d_sum
        sums_ref[pl.ds(6, 1), :] = column_sum(d_branch)[None]
        sums_ref[pl.ds(7, 1), :] = gain[None]
        sums_ref[pl.ds(8, 1), :] = bias[None]

    hidden = hidden_ref[...]
    slope = erf_half(hidden) + hidden * jnp.exp(-0.5 * hidden * hidden) * (2.0 * jnp.pi) ** (-0.5)
    d_hidden = (plain_dot(d_branch_ref[...], down_ref[...]) * slope).astype(bfloat)
    d_hidden_ref[...] = d_hidden
    sums_ref[pl.ds(2 + step, 1), :] = column_sum(d_hidden)[None]
    d_middle_ref[...] += trans_dot(d_hidden, up_ref[...])

    @pl.when(step == pl.num_programs(0) - 1)
    def _():
        d_pre, gain, bias = norm_back(
            d_middle_ref[...], mid_normed_ref[...], mid_inverse_ref[:, :1], row_of(small_ref, 5)
        )
        d_pre_ref[...] = d_pre
        d_attend_ref[...] = d_pre.astype(bfloat)
        sums_ref[pl.ds(0, 1), :] = gain[None]
        sums_ref[pl.ds(1, 1), :] = bias[None]


def feed_backward(parts, normed, inverse, hidden, small_full, mid_normed, mid_inverse, weights):
    slots, width = normed.shape
    block = (slots, width), lambda step: (0, step)
    out = lambda kind, rows=slots: ((rows, width), kind, None, None)
    return kernel_call(
        feed_back_kernel,
        "feed_backward",
        4,
        [
            whole(parts),
            whole(normed),
            whole(inverse),
            (hidden,) + block,
            whole(small_full),
            whole(mid_normed),
            whole(mid_inverse),
            (weights, (width, width), lambda step: (0, 4 + step)),
            (weights, (width, width), lambda step: (0, 8 + step)),
        ],
        [
            out(bfloat), ((slots, 4 * width), bfloat) + block, out(single), out(bfloat),
            out(single, 16),
        ],
        (16 * slots * width * width, 16 * width * width, 8 * slots * width),
        [pltpu.VMEM((slots, width), single)],
    )


def attend_back_kernel(
    d_attend_ref, key_ref, value_ref, query_ref, allowed_ref, weight_ref,
    d_query_ref, d_key_ref, d_value_ref, d_mixed_ref,
):
    d_mixed_ref[...] = trans_dot(d_attend_ref[...], weight_ref[...]).astype(bfloat)
    blocked = allowed_ref[...] == 0.0
    slots, length = blocked.shape
    low, high = pair_masks(slots)
    low_long, _ = pair_masks(length)
    scale = HD ** (-0.5)

    def one_pair(pair, carry):
        lanes = pl.ds(pl.multiple_of(pair * 2 * HD, 2 * HD), 2 * HD)
        query_pair, key_pair, value_pair = query_ref[:, lanes], key_ref[:, lanes], value_ref[:, lanes]
        mixed_pair = d_mixed_ref[:, lanes]
        found = []
        for head_lanes in (low, high):
            probs = head_probs(query_pair, key_pair, head_lanes, blocked)
            d_probs = trans_dot(
                jnp.where(head_lanes, mixed_pair, jnp.zeros_like(mixed_pair)), value_pair
            )
            inner = jnp.sum(probs * d_probs, axis=-1, keepdims=True)
            d_scores = (probs * (d_probs - inner)).astype(bfloat)
            found.append(
                (
                    plain_dot(d_scores, key_pair) * scale,
                    rows_dot(d_scores, query_pair) * scale,
                    rows_dot(probs.astype(bfloat), mixed_pair),
                )
            )
        d_query_ref[:, lanes] = jnp.where(low, found[0][0], found[1][0]).astype(bfloat)
        d_key_ref[:, lanes] = jnp.where(low_long, found[0][1], found[1][1]).astype(bfloat)
        d_value_ref[:, lanes] = jnp.where(low_long, found[0][2], found[1][2]).astype(bfloat)
        return carry

    lax.fori_loop(0, query_ref.shape[1] // (2 * HD), one_pair, 0)


def attend_backward(d_attend, key_rows, value_rows, query_rows, allowed, weights):
    length, width = key_rows.shape
    slots = d_attend.shape[0]
    out = lambda rows: ((rows, width), bfloat, None, None)
    return kernel_call(
        attend_back_kernel,
        "attention_backward",
        1,
        [
            whole(d_attend),
            whole(key_rows),
            whole(value_rows),
            whole(query_rows),
            whole(allowed),
            (weights, (width, width), lambda step: (0, 3)),
        ],
        [out(slots), out(length), out(length)],
        (
            2 * slots * width * width + 20 * slots * length * width,
            2 * width * width,
            HEADS * slots * length,
        ),
        [pltpu.VMEM((slots, width), bfloat)],
    )


def project_back_kernel(
    d_pre_ref, d_query_ref, d_key_ref, d_value_ref, slot_ref, hidden_row_ref, small_ref,
    normed_ref, inverse_ref, init_normed_ref, init_inverse_ref, weight_ref, ahead_ref,
    embed_ref, position_ref, sums_ref, d_stream_ref, d_init_ref,
):
    step = pl.program_id(0)

    @pl.when(step == 0)
    def _():
        d_init_ref[...] = d_pre_ref[...] + trans_dot(d_query_ref[...], weight_ref[...])

    @pl.when(step == 1)
    def _():
        d_stream_ref[...] = trans_dot(d_key_ref[...], weight_ref[...])

    @pl.when(step == 2)
    def _():
        gain_row = row_of(small_ref, 0)
        d_stream = d_stream_ref[...] + trans_dot(d_value_ref[...], weight_ref[...])
        d_start, gain_init, bias_init = norm_back(
            d_init_ref[...], init_normed_ref[...], init_inverse_ref[:, :1], gain_row
        )
        d_embed, gain, bias = norm_back(
            d_stream, normed_ref[...], inverse_ref[:, :1], gain_row
        )
        position_ref[...] = d_embed + lax.dot_general(
            slot_ref[...],
            d_start,
            (((0,), (0,)), ((), ())),
            precision=lax.Precision.HIGHEST,
            preferred_element_type=single,
        )
        embed_b = d_embed.astype(bfloat)
        embed_ref[...] = embed_b
        sums_ref[...] = jnp.zeros_like(sums_ref)
        sums_ref[pl.ds(0, 1), :] = (gain_init + gain)[None]
        sums_ref[pl.ds(1, 1), :] = (bias_init + bias)[None]
        sums_ref[pl.ds(2, 1), :] = column_sum(d_query_ref[...])[None]
        sums_ref[pl.ds(3, 1), :] = column_sum(d_value_ref[...])[None]
        sums_ref[pl.ds(4, 1), :] = column_sum(d_pre_ref[...].astype(bfloat))[None]
        masked = jnp.where(hidden_row_ref[:, :1] > 0.0, embed_b.astype(single), 0.0)
        sums_ref[pl.ds(5, 1), :] = jnp.sum(masked, axis=0)[None]


def project_backward(
    d_pre, d_query, d_key, d_value, slot_hot, hidden_rows, small_full,
    normed, inverse, init_normed, init_inverse, weights, ahead,
):
    length, width = normed.shape
    slots = d_pre.shape[0]
    arrays = (
        d_pre, d_query, d_key, d_value, slot_hot, hidden_rows, small_full,
        normed, inverse, init_normed, init_inverse,
    )
    return kernel_call(
        project_back_kernel,
        "projection_backward",
        3,
        [whole(array) for array in arrays]
        + [(weights, (width, width), lambda step: (0, step)), (ahead, "any", None)],
        [
            ((length, width), bfloat, None, None),
            ((length, width), single, None, None),
            ((8, width), single, None, None),
        ],
        (5 * length * width * width, 6 * width * width, 0),
        [pltpu.VMEM((length, width), single), pltpu.VMEM((slots, width), single)],
    )


def adam_direction(weight_arr, new_first, new_second):
    first_scale, second_scale = 1.0 / (1.0 - beta_first**STEP), 1.0 / (1.0 - beta_second**STEP)
    scaled = new_second * second_scale
    return (new_first * first_scale) / (
        scaled * lax.rsqrt(scaled) + adam_eps
    ) + weight_decay * weight_arr


def adam_moments(weight_arr, first_mom, second_mom, gradient, factor):
    clipped = gradient * factor
    new_first = beta_first * first_mom + (1.0 - beta_first) * clipped
    new_second = beta_second * second_mom + (1.0 - beta_second) * clipped * clipped
    return (new_first, new_second, adam_direction(weight_arr, new_first, new_second))


def row_block(count, most=240):
    return most if count % most == 0 else count


def lookup_kernel(pieces, *refs):
    step = pl.program_id(0)
    starts, count = pieces
    runs = len(starts)
    head_refs, refs = refs[: runs * count], refs[runs * count :]
    asked_ref, given_ref, side_ref, grad_ref, square_ref = refs
    rows, width = grad_ref.shape
    base = step * rows
    row_hot = asked_ref[...] == base + lax.broadcasted_iota(
        jnp.int32, (rows, asked_ref.shape[1]), 0
    )
    grad = plain_dot(row_hot.astype(bfloat), given_ref[...])
    for part in range(count):
        head = head_refs[part][...].astype(single)
        for run in range(1, runs):
            later = head_refs[run * count + part][...].astype(single)
            head = jnp.where(step >= starts[run], later, head)
        grad += head
    grad_ref[...] = grad
    place = base + lax.broadcasted_iota(jnp.int32, (rows, width), 0)
    own = (place >= side_ref[0]) & (place < side_ref[1])

    @pl.when(step == 0)
    def _():
        square_ref[...] = jnp.zeros_like(square_ref)

    square_ref[...] += jnp.sum(jnp.where(own, grad * grad, 0.0), axis=0, keepdims=True)


def lookup_grad(heads, count, asked_rows, given, sides):
    width = heads[0].shape[1]
    vrows = sum(head.shape[0] for head in heads) // count
    rows = vrows // 4
    steps = [head.shape[0] // count // rows for head in heads]
    starts = [sum(steps[:run]) for run in range(len(heads))]
    whole_spec = lambda array: pl.BlockSpec(array.shape, lambda step: (0, 0))
    return pl.pallas_call(
        lambda *refs: lookup_kernel((starts, count), *refs),
        grid=(4,),
        in_specs=[
            pl.BlockSpec(
                (rows, width),
                lambda step, run=run, part=part: (
                    part * steps[run] + jnp.clip(step - starts[run], 0, steps[run] - 1),
                    0,
                ),
            )
            for run in range(len(heads))
            for part in range(count)
        ]
        + [
            whole_spec(asked_rows),
            whole_spec(given),
            pl.BlockSpec(memory_space=pltpu.SMEM),
        ],
        out_specs=[
            pl.BlockSpec((rows, width), lambda step: (step, 0)),
            pl.BlockSpec((1, width), lambda step: (0, 0)),
        ],
        out_shape=[
            jax.ShapeDtypeStruct((vrows, width), single),
            jax.ShapeDtypeStruct((1, width), single),
        ],
        cost_estimate=pl.CostEstimate(flops=0, bytes_accessed=0, transcendentals=0),
        name="table_gradient",
    )(*[head for head in heads for _ in range(count)], asked_rows, given, sides)


def full_sum(values):
    return jnp.sum(jnp.sum(values, axis=1, keepdims=True), axis=0, keepdims=True)


def pair_row(weight_sum, dir_sum):
    lane = lax.broadcasted_iota(jnp.int32, (1, 128), 1)
    return jnp.where(lane == 0, weight_sum, dir_sum)


def norms_kernel(offset_ref, *refs):
    total_ref, table_refs, layer_refs, position_refs, small_refs = (
        refs[0], refs[1:5], refs[5:9], refs[9:13], refs[13:17],
    )
    norms_ref, layer_out, position_out, small_out = refs[17], refs[18:21], refs[21:24], refs[24:27]
    sums_ref = refs[27]
    step = pl.program_id(0)
    total_square = jnp.sum(total_ref[...], axis=0, keepdims=True)[:, :1]
    factor = jnp.minimum(1.0, clip_norm / jnp.sqrt(total_square))

    @pl.when(step == 0)
    def _():
        sums_ref[...] = jnp.zeros_like(sums_ref)
        norms_ref[...] = jnp.zeros_like(norms_ref)
        for row, group_refs, outs in ((4, position_refs, position_out), (5, small_refs, small_out)):
            weight_arr = group_refs[0][...]
            first, second, direction = adam_moments(
                weight_arr, group_refs[1][...], group_refs[2][...], group_refs[3][...], factor
            )
            for ref, value in zip(outs, (first, second, direction)):
                ref[...] = value
            norms_ref[pl.ds(row, 1), :] = pair_row(
                full_sum(weight_arr * weight_arr), full_sum(direction * direction)
            )

    @pl.when(step < 3)
    def _():
        weight_arr, first_mom, second_mom, gradient = (ref[0] for ref in layer_refs)
        first, second, direction = adam_moments(
            weight_arr, first_mom, second_mom, gradient, factor
        )
        for ref, value in zip(layer_out, (first, second, direction)):
            ref[0] = value
        norms_ref[pl.ds(1 + step, 1), :] = pair_row(
            full_sum(weight_arr * weight_arr), full_sum(direction * direction)
        )

    weight_arr = table_refs[0][...]
    _, _, direction = adam_moments(
        weight_arr, table_refs[1][...], table_refs[2][...], table_refs[3][...], factor
    )
    sums_ref[pl.ds(0, 1), :] += jnp.sum(weight_arr * weight_arr, axis=0, keepdims=True)
    sums_ref[pl.ds(1, 1), :] += jnp.sum(direction * direction, axis=0, keepdims=True)

    @pl.when(step == pl.num_programs(0) - 1)
    def _():
        norms_ref[pl.ds(0, 1), :] = pair_row(
            full_sum(sums_ref[pl.ds(0, 1), :]), full_sum(sums_ref[pl.ds(1, 1), :])
        )


def update_norms(totals, table, layer, position, small, split, dp_index):
    vrows, width = table[0].shape
    rows = row_block(split, 240)
    if split // rows < 3:
        rows = split // 3
    one_part = pl.BlockSpec(
        (1,) + layer[0].shape[1:], lambda step, offset: (jnp.minimum(step, 2), 0, 0)
    )
    fixed = lambda array: pl.BlockSpec(
        array.shape, lambda step, offset, rank=array.ndim: (0,) * rank
    )
    part = pl.BlockSpec((rows, width), lambda step, offset: (offset[0] + step, 0))
    groups = tuple(layer) + tuple(position) + tuple(small)
    outs = [
        jax.ShapeDtypeStruct(group[0].shape, single)
        for group in (layer, position, small)
        for _ in range(3)
    ]
    norms = jax.ShapeDtypeStruct((8, 128), single)
    return pl.pallas_call(
        norms_kernel,
        grid_spec=pltpu.PrefetchScalarGridSpec(
            num_scalar_prefetch=1,
            grid=(split // rows,),
            in_specs=[fixed(totals)]
            + [part] * 4
            + [one_part] * 4
            + [fixed(array) for array in groups[4:]],
            out_specs=[fixed(norms)] + [one_part] * 3 + [fixed(out) for out in outs[3:]],
            scratch_shapes=[pltpu.VMEM((8, width), single)],
        ),
        out_shape=[norms] + outs,
        cost_estimate=pl.CostEstimate(flops=0, bytes_accessed=0, transcendentals=0),
        name="update_norms",
    )((dp_index * (split // rows)).astype(jnp.int32)[None], totals, *table, *groups)


def final_kernel(
    pairs_ref, weight_ref, first_ref, second_ref,
    layer_ref, layer_dir_ref, position_ref, position_dir_ref, small_ref, small_dir_ref,
    next_ref, layer_next_ref, position_next_ref, small_next_ref,
):
    roots = jnp.sqrt(jnp.sum(pairs_ref[...], axis=0, keepdims=True))

    def rate(group):
        return learn_rate * (
            roots[:, 2 * group : 2 * group + 1] / roots[:, 2 * group + 1 : 2 * group + 2]
        )

    weight_arr = weight_ref[...]
    direction = adam_direction(weight_arr, first_ref[...], second_ref[...])
    next_ref[...] = weight_arr - rate(0) * direction

    step = pl.program_id(0)
    for part in range(3):

        @pl.when(step == part)
        def _():
            layer_next_ref[0] = layer_ref[0] - rate(1 + part) * layer_dir_ref[0]

    @pl.when(step == 0)
    def _():
        position_next_ref[...] = position_ref[...] - rate(4) * position_dir_ref[...]
        small_next_ref[...] = small_ref[...] - rate(5) * small_dir_ref[...]


def final_update(pairs, table, groups):
    vrows, width = table[0].shape
    rows = row_block(vrows, 480)
    if vrows // rows < 3:
        rows = row_block(vrows, 240)
    fixed = lambda array: pl.BlockSpec(array.shape, lambda step, rank=array.ndim: (0,) * rank)
    block = pl.BlockSpec((rows, width), lambda step: (step, 0))
    one_part = pl.BlockSpec((1,) + groups[0].shape[1:], lambda step: (jnp.minimum(step, 2), 0, 0))
    outs = [jax.ShapeDtypeStruct(array.shape, single) for array in groups[::2]]
    return pl.pallas_call(
        final_kernel,
        grid=(vrows // rows,),
        in_specs=[fixed(pairs)]
        + [block] * 3
        + [one_part] * 2
        + [fixed(array) for array in groups[2:]],
        out_specs=[block, one_part] + [fixed(out) for out in outs[1:]],
        out_shape=[jax.ShapeDtypeStruct((vrows, width), single)] + outs,
        cost_estimate=pl.CostEstimate(flops=0, bytes_accessed=0, transcendentals=0),
        name="final_update",
    )(pairs, *table, *groups)


class Exchange:
    def __init__(self):
        self.last = None

    def __call__(self, values, axes):
        if self.last is not None:
            values, _ = lax.optimization_barrier((values, self.last))
        self.last = lax.all_to_all(values, axes, 0, 0, tiled=True)
        return self.last

    def copies(self, values, axes, count):
        return self(jnp.broadcast_to(values[None], (count,) + values.shape), axes)

    def columns(self, values, axes, count):
        rows, width = values.shape
        blocks = values.reshape(rows, count, width // count).transpose(1, 0, 2)
        return self(blocks, axes).reshape(count * rows, -1)

    def rows(self, values, count):
        return self(values.reshape(count, values.shape[0] // count, values.shape[1]), ALL)


def side_by_side(blocks):
    return blocks.transpose(1, 0, 2).reshape(blocks.shape[1], -1)


def after(values, *waits):
    for wait in waits:
        values = values + (wait[(0,) * wait.ndim] > 3.395e38).astype(values.dtype)
    return values


def masked_total(mask, values):
    return jnp.sum(jnp.where(mask, values, 0), axis=-1)


def slot_layout(pred_row, order_row, token_row):
    length = pred_row.shape[0]
    index = jnp.arange(length)
    before = index[None, :] <= index[:, None]
    seen = masked_total(before, pred_row[None, :])
    masked = jnp.sum(pred_row)
    place = jnp.where(pred_row == 1, seen - 1, masked + index - seen)
    slot_hot = place[None, :] == jnp.arange(CAP)[:, None]
    rank_row = masked_total(order_row[None, :] == index[:, None], index[None, :])
    slot_rank = masked_total(slot_hot, rank_row[None, :])
    slot_target = masked_total(slot_hot, token_row[None, :])
    slot_pos = masked_total(slot_hot, index[None, :])
    allowed = rank_row[None, :] <= slot_rank[:, None]
    return slot_hot, slot_pos, slot_target, allowed, masked


def bucket_layout(content, vrows):
    index = jnp.arange(content.shape[0])
    same = content[None, :] == content[:, None]
    first = jnp.min(jnp.where(same, index[None, :], content.shape[0]), axis=1)
    is_first = first == index
    owner = content // vrows
    ahead = (owner[None, :] == owner[:, None]) & is_first[None, :] & (index[None, :] < first[:, None])
    return owner, jnp.sum(ahead.astype(jnp.int32), axis=1)


def bucket_round(content, owner, place, turn, owners, vrows):
    usable = BUCKET - 1
    local = place - turn * usable
    taken = (local >= 0) & (local < usable)
    flat = jnp.where(taken, owner * BUCKET + local, -1)
    hot = flat[None, :] == jnp.arange(owners * BUCKET)[:, None]
    wanted = jnp.max(jnp.where(hot, (content - owner * vrows)[None, :], -1), axis=1)
    return hot.astype(bfloat), wanted.reshape(owners, BUCKET)


def on_device(
    token_ids,
    pred_mask,
    fact_order,
    corpus,
    embed_table,
    table_moment,
    table_square,
    layer_weights,
    layer_moment,
    layer_square,
    position_table,
    position_moment,
    position_square,
    small_params,
    small_moment,
    small_square,
):
    exchange = Exchange()
    dp_devs = lax.axis_size("dp")
    owners = lax.axis_size(VOC)
    devices = dp_devs * owners
    vrows, width = embed_table.shape
    length = token_ids.shape[1]
    feed = layer_weights.shape[2]
    shared = jnp.concatenate([position_table, small_params]).T
    shared_rows = shared.shape[1]
    shared = jnp.pad(shared, ((0, 0), (0, -shared_rows % 128)))
    shard = jnp.concatenate([layer_weights[0], layer_weights[1], layer_weights[2], shared], axis=1)
    shard = lax.all_gather(shard.astype(bfloat), ALL, axis=0, tiled=True)
    table_b = embed_table.astype(bfloat)
    token_row = token_ids[0]
    pred_row = pred_mask[0]
    first_row = lax.axis_index(VOC) * vrows
    content = jnp.where(pred_row == 1, MASK_ID, token_row)
    slot_hot, slot_pos, slot_target, allowed, masked = slot_layout(pred_row, fact_order[0], token_row)
    owner, place = bucket_layout(content, vrows)
    hot, wanted = bucket_round(content, owner, place, 0, owners, vrows)
    note = jnp.concatenate(
        [slot_target, slot_pos, jnp.stack([masked, corpus[0], jnp.max(place)])]
    )
    packet = jnp.concatenate(
        [wanted, jnp.broadcast_to(note[None], (owners, note.shape[0]))], axis=1
    )
    packet = jnp.pad(packet, ((0, 0), (0, 256 - packet.shape[1])))
    packet = jnp.broadcast_to(packet[None], (dp_devs,) + packet.shape)
    packet = exchange(packet.reshape(devices, packet.shape[-1]), ALL)
    asked = packet[:, :BUCKET]
    tail = BUCKET + 2 * CAP
    counts_all = packet[:, tail]
    corpus_all = packet[:, tail + 1]
    rounds = jnp.max(packet[:, tail + 2]) // (BUCKET - 1) + 1
    group = lax.axis_index("dp") * owners
    outer = lax.axis_size("hi")

    def group_order(values):
        return values.reshape(outer, 2, 2, CAP).transpose(2, 1, 0, 3).reshape(-1)

    group_asked = lax.dynamic_slice_in_dim(asked, group, owners, 0)
    group_target = group_order(
        lax.dynamic_slice_in_dim(packet[:, BUCKET : BUCKET + CAP], group, owners, 0)
    )
    corpus_hot = corpus_all[:, None] == jnp.arange(NCORP)[None, :]
    corpus_counts = jnp.sum(jnp.where(corpus_hot, counts_all[:, None], 0), axis=0)
    seq_count = masked_total(corpus_hot, corpus_counts[None, :])
    seq_weight = 1.0 / (NCORP * seq_count.astype(single))
    slot_weight = jnp.where(
        jnp.arange(CAP)[None, :] < counts_all[:, None], seq_weight[:, None], 0.0
    )
    group_weight = group_order(lax.dynamic_slice_in_dim(slot_weight, group, owners, 0))

    def serve(asked_rows):
        served = jnp.take(table_b, jnp.maximum(asked_rows, 0).reshape(-1), axis=0)
        return served.reshape(owners, BUCKET, width)

    arrived = exchange(serve(group_asked), VOC)
    embed_rows = rows_dot(hot, arrived.reshape(-1, width))

    def more_rows(state):
        turn, rows = state
        hot_t, wanted_t = bucket_round(content, owner, place, turn, owners, vrows)
        asked_t = lax.all_to_all(wanted_t, VOC, 0, 0, tiled=True)
        arrived_t = lax.all_to_all(serve(asked_t), VOC, 0, 0, tiled=True)
        return turn + 1, rows + rows_dot(hot_t, arrived_t.reshape(-1, width))

    _, embed_rows = lax.while_loop(
        lambda state: state[0] < rounds, more_rows, (jnp.ones((), rounds.dtype), embed_rows)
    )
    few = devices <= 32
    near = 4
    allowed = allowed.astype(single)
    slot_hot = slot_hot.astype(single)
    (
        key_rows,
        value_rows,
        query_rows,
        mixed_b,
        middle,
        mid_normed,
        mid_inverse,
        stream_b,
        stream_normed,
        stream_inverse,
        query_init,
        init_normed,
        init_inverse,
        position_full,
        small_full,
    ) = attend_forward(embed_rows, slot_hot, allowed, shard, length, small_params.shape[0])
    middle_b, hidden, active_b, output_b, end_normed, end_inverse = feed_forward(
        middle, small_full, shard
    )
    if few:
        kept_rows = jnp.concatenate([mixed_b, middle_b], axis=1)
        kept_all = lax.all_gather(kept_rows, ALL, axis=0, tiled=True)
        stream_all = lax.all_gather(stream_b, NEAR, axis=0, tiled=True)
    group_rows = exchange.copies(output_b, "hi", outer).reshape(-1, width)
    group_rows = exchange.copies(group_rows, "mid", 2).reshape(-1, width)
    group_rows = exchange.copies(group_rows, "core", 2).reshape(-1, width)
    logits = trans_dot(group_rows, table_b)
    local_target = group_target - first_row
    target_hit = jnp.arange(vrows)[None, :] == local_target[:, None]
    row_top = jnp.max(logits, axis=1)
    row_total = jnp.sum(jnp.exp(logits - row_top[:, None]), axis=1)
    row_target = jnp.sum(jnp.where(target_hit, logits, 0.0), axis=1)
    stats = exchange.copies(jnp.stack([row_top, row_total]), VOC, owners)
    top_all = jnp.max(stats[:, 0], axis=0)
    total_all = jnp.sum(stats[:, 1] * jnp.exp(stats[:, 0] - top_all[None]), axis=0)
    log_total = top_all + jnp.log(total_all)
    own_place = lax.axis_index(("core", "mid", "hi"))
    own_total = lax.dynamic_slice_in_dim(log_total * group_weight, own_place * CAP, CAP, 0)
    loss_part = jnp.sum(own_total) - jnp.sum(row_target * group_weight)
    d_logits = (
        group_weight[:, None] * (jnp.exp(logits - log_total[:, None]) - target_hit.astype(single))
    ).astype(bfloat)
    def swapped(axis, kind, part):
        side = lax.axis_index(axis)
        theirs = lax.ppermute(part(1 - side).astype(kind), axis, [(0, 1), (1, 0)])
        return part(side) + theirs.astype(single)

    half = owners * CAP // 2

    def rows_half(side):
        return plain_dot(lax.dynamic_slice_in_dim(d_logits, side * half, half, 0), table_b)

    d_output = swapped("core", single, rows_half)
    quarter = half // 2
    d_half = d_output
    d_output = swapped(
        "mid", bfloat, lambda side: lax.dynamic_slice_in_dim(d_half, side * quarter, quarter, 0)
    )
    grad_head = rows_dot(d_logits, group_rows)
    grad_head = after(grad_head, d_half, *((stream_all,) if few else ()))
    heads = [
        lax.all_gather(half_b, "dp", axis=0, tiled=True)
        for half_b in jnp.split(grad_head.astype(bfloat), [vrows * 3 // 4])
    ]
    d_output = exchange(d_output.astype(bfloat).reshape(outer, CAP, width), "hi")
    if few:
        d_output, kept_all = lax.optimization_barrier((d_output, kept_all))
    d_branch, d_hidden, d_pre, d_attend, sums_feed = feed_backward(
        d_output,
        end_normed,
        end_inverse,
        hidden,
        small_full,
        mid_normed,
        mid_inverse,
        shard,
    )
    if few:
        wide = feed // devices
        both = jnp.concatenate(
            [
                d_hidden.reshape(CAP, devices, -1),
                d_attend.reshape(CAP, devices, -1),
            ],
            axis=2,
        ).reshape(CAP, -1)
        both = exchange.columns(both, ALL, devices)
        branch_all = lax.all_gather(d_branch, ALL, axis=0, tiled=True)
    d_query, d_key, d_value = attend_backward(
        d_attend, key_rows, value_rows, query_rows, allowed, shard
    )
    if few:
        piece = width // near
        pairs = jnp.concatenate(
            [d_key.reshape(length, near, piece), d_value.reshape(length, near, piece)], axis=2
        ).transpose(1, 0, 2)
        asks = d_query.reshape(CAP, near, piece).transpose(1, 0, 2)
        asks = jnp.concatenate([asks[:, : CAP // 2], asks[:, CAP // 2 :]], axis=2)
        pairs = exchange(jnp.concatenate([pairs, asks], axis=1), NEAR)
    hidden_rows = spread((content == MASK_ID).astype(single)[:, None])
    embed_back, grad_position, sums_back = project_backward(
        d_pre,
        d_query,
        d_key,
        d_value,
        slot_hot,
        hidden_rows,
        small_full,
        stream_normed,
        stream_inverse,
        init_normed,
        init_inverse,
        shard,
        heads[0],
    )
    grad_small = jnp.concatenate([sums_back[:5], sums_feed[:9]])
    mask_sum = sums_back[5]
    mask_left = mask_sum - lax.reduce_precision(mask_sum, 8, 7)
    mask_owner = MASK_ID // vrows
    is_left = (jnp.arange(BUCKET) == BUCKET - 1)[None, :] & (
        jnp.arange(owners) == mask_owner
    )[:, None]

    def plain_exchange(values, axes):
        return lax.all_to_all(values, axes, 0, 0, tiled=True)

    def give(hot_rows, extra, send):
        rows = plain_dot(hot_rows, embed_back).reshape(owners, BUCKET, width)
        rows = jnp.where(is_left[:, :, None] & extra, mask_left[None, None, :], rows)
        return send(rows.astype(bfloat), VOC).reshape(-1, width)

    def of_both(rows):
        if dp_devs == 2:
            return jnp.concatenate([rows, lax.ppermute(rows, "dp", [(0, 1), (1, 0)])])
        return lax.all_gather(rows, "dp", axis=0, tiled=True)

    def both_groups(asked_rows):
        if dp_devs == 2:
            return jnp.roll(asked_rows, -group, axis=0)
        return asked_rows

    split = vrows // dp_devs
    sides = lax.axis_index("dp") * split + jnp.array([0, split])

    def into_rows(heads, parts, asked_rows, given, sides):
        return lookup_grad(heads, parts, both_groups(asked_rows).reshape(1, -1), given, sides)

    last = (jnp.arange(BUCKET) == BUCKET - 1)[None, :]
    left_row = jnp.where(lax.axis_index(VOC) == mask_owner, MASK_ID - first_row, -1)
    given = give(hot, True, exchange)

    if few:
        near_pos = packet[:, BUCKET + CAP : tail].reshape(dp_devs * outer, near * CAP)
        near_pos = lax.dynamic_index_in_dim(
            near_pos, lax.axis_index(("dp", "hi")), 0, False
        )
        init_rows = norm_forward(position_full, small_full[0], small_full[1])[0].astype(bfloat)
        init_hot = near_pos[:, None] == jnp.arange(length)[None, :]
        init_all = plain_dot(init_hot.astype(bfloat), init_rows).astype(bfloat)
        asks = pairs[:, length:]
        asks = jnp.concatenate([asks[..., :piece], asks[..., piece:]], axis=1)
        grad_pair = rows_dot(stream_all, pairs[:, :length].reshape(near * length, -1))
        grad_ask = rows_dot(init_all, asks.reshape(near * CAP, piece))
        share = width // devices
        active_mine = exchange.columns(active_b, ALL, devices)
        grad_up = rows_dot(kept_all[:, width:], both[:, :wide])
        grad_out = rows_dot(kept_all[:, :width], both[:, wide:])
        grad_down = rows_dot(branch_all, active_mine)
        shared_grad = jnp.concatenate([grad_position, grad_small]).T
        results = jnp.concatenate(
            [grad_pair, grad_ask, grad_up, grad_down, grad_out, shared_grad], axis=1
        )
        results = results.astype(bfloat)
        results = exchange.rows(results, devices).astype(single)
        sides = after(sides, results)
        pieces = 3 * piece
        attn = jnp.sum(
            results[..., :pieces].reshape(dp_devs * outer, near, share, pieces), axis=0
        )
        shared_grad = jnp.sum(results[..., -shared_rows:], axis=0)
        single_parts = results[..., pieces:-shared_rows]
        part_square = (
            jnp.sum(attn * attn)
            + jnp.sum(single_parts * single_parts)
            + jnp.sum(shared_grad * shared_grad)
        )
        shared_grad = shared_grad.T
        position_grad, small_grad = shared_grad[:length], shared_grad[length:]
        grad_key, grad_value, grad_query = (
            side_by_side(attn[..., part * piece : (part + 1) * piece]) for part in range(3)
        )
        grad_up, grad_down, grad_out = (
            side_by_side(single_parts[..., low:high])
            for low, high in ((0, wide), (wide, 2 * wide), (2 * wide, None))
        )
        layer_grad = jnp.stack(
            [
                jnp.concatenate([grad_query, grad_key, grad_value, grad_out], axis=1),
                grad_up,
                grad_down,
            ]
        )
    else:
        whole = (
            jnp.concatenate(
                [
                    rows_dot(query_init.astype(bfloat), d_query),
                    rows_dot(stream_b, d_key),
                    rows_dot(stream_b, d_value),
                    rows_dot(mixed_b, d_attend),
                ],
                axis=1,
            ),
            rows_dot(middle_b, d_hidden),
            rows_dot(d_branch, active_b),
        )
        layer_grad = jnp.stack(
            [lax.psum_scatter(part, ALL, scatter_dimension=0, tiled=True) for part in whole]
        )
        shared_grad = jnp.concatenate([grad_position, grad_small]).T
        shared_grad = lax.psum_scatter(shared_grad, ALL, scatter_dimension=0, tiled=True).T
        position_grad, small_grad = shared_grad[:length], shared_grad[length:]
        part_square = jnp.sum(layer_grad * layer_grad) + jnp.sum(shared_grad * shared_grad)
    table_grad, table_square_sum = into_rows(
        heads, dp_devs, jnp.where(last, left_row, asked), of_both(given), sides
    )

    def more_grads(state):
        turn, grads, _ = state
        hot_t, wanted_t = bucket_round(content, owner, place, turn, owners, vrows)
        wanted_t = jnp.broadcast_to(wanted_t[None], (dp_devs,) + wanted_t.shape)
        asked_t = lax.all_to_all(
            wanted_t.reshape(devices, BUCKET), ALL, 0, 0, tiled=True
        )
        given_t = of_both(give(hot_t, False, plain_exchange))
        return (turn + 1,) + tuple(into_rows([grads], 1, asked_t, given_t, sides))

    _, table_grad, table_square_sum = lax.while_loop(
        lambda state: state[0] < rounds,
        more_grads,
        (jnp.ones((), rounds.dtype), table_grad, table_square_sum),
    )
    square_part = jnp.sum(table_square_sum) + part_square
    totals = exchange.copies(jnp.stack([square_part, loss_part]), ALL, devices)
    total_square, loss_value = jnp.sum(totals, axis=0)
    grad_norm = jnp.sqrt(total_square)
    factor = jnp.minimum(1.0, clip_norm / grad_norm)
    (
        norms,
        layer_first,
        layer_second,
        layer_dir,
        position_first,
        position_second,
        position_dir,
        small_first,
        small_second,
        small_dir,
    ) = update_norms(
        totals,
        (embed_table, table_moment, table_square, table_grad),
        (layer_weights, layer_moment, layer_square, layer_grad),
        (position_table, position_moment, position_square, position_grad),
        (small_params, small_moment, small_square, small_grad),
        split,
        lax.axis_index("dp"),
    )
    factor_late, norms = lax.optimization_barrier((factor, norms))
    pairs = exchange.copies(norms[:6, :2].reshape(-1), ALL, devices)
    table_first, table_second, _ = adam_moments(
        embed_table, table_moment, table_square, table_grad, factor_late
    )
    trust_norms = jnp.sqrt(jnp.sum(pairs, axis=0)).reshape(6, 2)
    table_next, layer_next, position_next, small_next = final_update(
        pairs,
        (embed_table, table_first, table_second),
        (
            layer_weights,
            layer_dir,
            position_table,
            position_dir,
            small_params,
            small_dir,
        ),
    )
    return (
        loss_value,
        grad_norm,
        table_next,
        table_first,
        table_second,
        layer_next,
        layer_first,
        layer_second,
        position_next,
        position_first,
        position_second,
        small_next,
        small_first,
        small_second,
        trust_norms,
    )


def solution(mesh):
    dp_devs, owners = mesh.devices.shape
    fine = Mesh(mesh.devices.reshape(dp_devs, owners // 4, 2, 2), ALL)
    rows, inner = P(ALL, None), P(None, ALL)
    table, layer = P(VOC, None), P(None, ALL, None)
    return jax.shard_map(
        on_device,
        mesh=fine,
        in_specs=(rows,) * 3 + (P(ALL),) + (table,) * 3 + (layer,) * 3 + (inner,) * 6,
        out_specs=(P(), P()) + (table,) * 3 + (layer,) * 3 + (inner,) * 6 + (P(),),
        check_vma=False,
    )
```

```python
import jax
import jax.numpy as jnp
from jax import lax
from jax.experimental import pallas as pl
from jax.experimental.pallas import tpu as pltpu
from jax.sharding import Mesh
from jax.sharding import PartitionSpec as P

HEADS = 12
HD = 64
MASK_ID = 103
NCORP = 4
STEP = 5
CAP = 64


clip_norm = 0.1
learn_rate = 0.3
beta_first = 0.9
beta_second = 0.999
adam_eps = 1e-06
weight_decay = 0.01
norm_eps = 1e-05
masked_score = -1e30
BUCKET = 32
ALL = ("dp", "hi", "mid", "core")
VOC = ("hi", "mid", "core")
NEAR = ("mid", "core")
bfloat = jnp.bfloat16
single = jnp.float32


def plain_dot(left_op, right_op):
    return jnp.dot(left_op, right_op, preferred_element_type=single)


def trans_dot(left_op, right_op):
    return lax.dot_general(
        left_op, right_op, (((1,), (1,)), ((), ())), preferred_element_type=single
    )


def rows_dot(left_op, right_op):
    return lax.dot_general(
        left_op, right_op, (((0,), (0,)), ((), ())), preferred_element_type=single
    )


def column_sum(values):
    return jnp.sum(values.astype(single), axis=0)


def norm_forward(values, gain_row, bias_row):
    center = values - jnp.mean(values, axis=-1, keepdims=True)
    inverse = lax.rsqrt(jnp.mean(center * center, axis=-1, keepdims=True) + norm_eps)
    normed = center * inverse
    return (normed * gain_row + bias_row, (normed, inverse))


def norm_backward(upstream, kept_norm, gain_row):
    normed, inverse = kept_norm
    scaled = upstream * gain_row
    inner = (
        scaled
        - jnp.mean(scaled, axis=-1, keepdims=True)
        - normed * jnp.mean(scaled * normed, axis=-1, keepdims=True)
    )
    return (inner * inverse, jnp.sum(upstream * normed, axis=0), jnp.sum(upstream, axis=0))


def pair_masks(rows):
    lane = lax.broadcasted_iota(jnp.int32, (rows, 2 * HD), 1)
    return lane < HD, lane >= HD


def head_probs(query_pair, key_pair, head_lanes, blocked):
    scores = trans_dot(jnp.where(head_lanes, query_pair, jnp.zeros_like(query_pair)), key_pair)
    scores = jnp.where(blocked, masked_score, scores * HD ** (-0.5))
    row_top = jnp.max(scores, axis=-1, keepdims=True)
    powers = jnp.exp(scores - row_top)
    return powers / jnp.sum(powers, axis=-1, keepdims=True)


def spread(column, lanes=128):
    return jnp.broadcast_to(column, (column.shape[0], lanes))


def row_of(ref, row):
    return ref[pl.ds(row, 1), :]


def attend_kernel(
    embed_ref, slot_ref, allowed_ref, shared_ref, weight_ref,
    key_ref, value_ref, query_ref, mixed_ref, middle_ref, normed_ref, inverse_ref,
    stream_ref, stream_normed_ref, stream_inverse_ref,
    init_ref, init_normed_ref, init_inverse_ref, position_ref, small_ref,
):
    step = pl.program_id(0)
    length = position_ref.shape[0]

    @pl.when(step == 0)
    def _():
        shared = shared_ref[...].astype(single).T
        position_ref[...] = shared[:length]
        small_ref[...] = shared[length : length + small_ref.shape[0]]
        gain, bias = row_of(small_ref, 0), row_of(small_ref, 1)
        stream, (normed, inverse) = norm_forward(embed_ref[...] + position_ref[...], gain, bias)
        stream_ref[...] = stream.astype(bfloat)
        stream_normed_ref[...] = normed
        stream_inverse_ref[...] = spread(inverse)
        chosen = plain_dot(slot_ref[...].astype(bfloat), position_ref[...].astype(bfloat))
        init, (normed, inverse) = norm_forward(chosen, gain, bias)
        init_ref[...] = init
        init_normed_ref[...] = normed
        init_inverse_ref[...] = spread(inverse)
        key_ref[...] = plain_dot(stream_ref[...], weight_ref[...]).astype(bfloat)

    @pl.when(step == 1)
    def _():
        value_ref[...] = (
            plain_dot(stream_ref[...], weight_ref[...]) + row_of(small_ref, 3)
        ).astype(bfloat)

    @pl.when(step == 2)
    def _():
        query_ref[...] = (
            plain_dot(init_ref[...].astype(bfloat), weight_ref[...]) + row_of(small_ref, 2)
        ).astype(bfloat)
        blocked = allowed_ref[...] == 0.0
        low, high = pair_masks(query_ref.shape[0])

        def one_pair(pair, carry):
            lanes = pl.ds(pl.multiple_of(pair * 2 * HD, 2 * HD), 2 * HD)
            query_pair, key_pair, value_pair = query_ref[:, lanes], key_ref[:, lanes], value_ref[:, lanes]
            left, right = (
                plain_dot(
                    head_probs(query_pair, key_pair, head_lanes, blocked).astype(bfloat), value_pair
                )
                for head_lanes in (low, high)
            )
            mixed_ref[:, lanes] = jnp.where(low, left, right).astype(bfloat)
            return carry

        lax.fori_loop(0, query_ref.shape[1] // (2 * HD), one_pair, 0)

    @pl.when(step == 3)
    def _():
        attend = plain_dot(mixed_ref[...], weight_ref[...]) + row_of(small_ref, 4)
        middle, (normed, inverse) = norm_forward(
            init_ref[...] + attend, row_of(small_ref, 5), row_of(small_ref, 6)
        )
        middle_ref[...] = middle
        normed_ref[...] = normed
        inverse_ref[...] = spread(inverse)


def kernel_call(body, name, steps, inputs, shapes, cost, scratch=()):
    fixed = lambda rank: lambda step: (0,) * rank

    def spec(shape, block, index):
        if block is None:
            return pl.BlockSpec(shape, fixed(len(shape)))
        if block == "any":
            return pl.BlockSpec(memory_space=pl.ANY)
        return pl.BlockSpec(block, index)

    return pl.pallas_call(
        body,
        grid=(steps,),
        in_specs=[spec(array.shape, block, index) for array, block, index in inputs],
        out_specs=[spec(shape, block, index) for shape, _, block, index in shapes],
        out_shape=[jax.ShapeDtypeStruct(shape, kind) for shape, kind, _, _ in shapes],
        scratch_shapes=list(scratch),
        cost_estimate=pl.CostEstimate(flops=cost[0] // 64, bytes_accessed=cost[1] // 64, transcendentals=0),
        name=name,
    )(*(array for array, _, _ in inputs))


def whole(array):
    return array, None, None


def attend_forward(embed_rows, slot_hot, allowed, weights, length, small_count):
    width = embed_rows.shape[1]
    slots = slot_hot.shape[0]
    out = lambda rows, kind, columns=width: ((rows, columns), kind, None, None)
    shared = weights.shape[1] - 12 * width
    return kernel_call(
        attend_kernel,
        "attention_forward",
        4,
        [
            whole(embed_rows),
            whole(slot_hot),
            whole(allowed),
            (weights, (width, shared), lambda step: (0, 12 * width // shared)),
            (
                weights,
                (width, width),
                lambda step: (0, jnp.where(step == 3, 3, (step + 1) % 3)),
            ),
        ],
        [
            out(length, bfloat), out(length, bfloat), out(slots, bfloat), out(slots, bfloat),
            out(slots, single), out(slots, single), out(slots, single, 128),
            out(length, bfloat), out(length, single), out(length, single, 128),
            out(slots, single), out(slots, single), out(slots, single, 128),
            out(length, single), out(small_count, single),
        ],
        (
            4 * length * width * width + 8 * slots * length * width,
            8 * width * width,
            HEADS * slots * length,
        ),
    )


def erf_half(hidden):
    return 0.5 * (1.0 + lax.erf(hidden * 0.5**0.5))


def feed_kernel(
    middle_ref, small_ref, up_ref, down_ref,
    middle_b_ref, hidden_ref, active_ref, output_ref, normed_ref, inverse_ref, total_ref,
):
    step = pl.program_id(0)

    @pl.when(step == 0)
    def _():
        middle_b_ref[...] = middle_ref[...].astype(bfloat)
        total_ref[...] = middle_ref[...] + row_of(small_ref, 11)

    hidden = plain_dot(middle_b_ref[...], up_ref[...]) + row_of(small_ref, 7 + step)
    hidden_ref[...] = hidden
    active = (hidden * erf_half(hidden)).astype(bfloat)
    active_ref[...] = active
    total_ref[...] += trans_dot(active, down_ref[...])

    @pl.when(step == pl.num_programs(0) - 1)
    def _():
        output, (normed, inverse) = norm_forward(
            total_ref[...], row_of(small_ref, 12), row_of(small_ref, 13)
        )
        output_ref[...] = output.astype(bfloat)
        normed_ref[...] = normed
        inverse_ref[...] = spread(inverse)


def feed_forward(middle, small_full, weights):
    slots, width = middle.shape
    wide = lambda kind: ((slots, 4 * width), kind, (slots, width), lambda step: (0, step))
    out = lambda kind, columns=width: ((slots, columns), kind, None, None)
    return kernel_call(
        feed_kernel,
        "feed_forward",
        4,
        [
            whole(middle),
            whole(small_full),
            (weights, (width, width), lambda step: (0, 4 + step)),
            (weights, (width, width), lambda step: (0, 8 + step)),
        ],
        [
            out(bfloat), wide(single), wide(bfloat), out(bfloat), out(single), out(single, 128),
        ],
        (16 * slots * width * width, 16 * width * width, 4 * slots * width),
        [pltpu.VMEM((slots, width), single)],
    )


def norm_back(upstream, normed, inverse, gain_row):
    return norm_backward(upstream, (normed, inverse), gain_row)


def feed_back_kernel(
    parts_ref, normed_ref, inverse_ref, hidden_ref, small_ref, mid_normed_ref, mid_inverse_ref,
    up_ref, down_ref,
    d_branch_ref, d_hidden_ref, d_pre_ref, d_attend_ref, sums_ref, d_middle_ref,
):
    step = pl.program_id(0)

    @pl.when(step == 0)
    def _():
        sums_ref[...] = jnp.zeros_like(sums_ref)
        d_sum, gain, bias = norm_back(
            jnp.sum(parts_ref[...].astype(single), axis=0), normed_ref[...], inverse_ref[:, :1], row_of(small_ref, 12)
        )
        d_branch = d_sum.astype(bfloat)
        d_branch_ref[...] = d_branch
        d_middle_ref[...] = d_sum
        sums_ref[pl.ds(6, 1), :] = column_sum(d_branch)[None]
        sums_ref[pl.ds(7, 1), :] = gain[None]
        sums_ref[pl.ds(8, 1), :] = bias[None]

    hidden = hidden_ref[...]
    slope = erf_half(hidden) + hidden * jnp.exp(-0.5 * hidden * hidden) * (2.0 * jnp.pi) ** (-0.5)
    d_hidden = (plain_dot(d_branch_ref[...], down_ref[...]) * slope).astype(bfloat)
    d_hidden_ref[...] = d_hidden
    sums_ref[pl.ds(2 + step, 1), :] = column_sum(d_hidden)[None]
    d_middle_ref[...] += trans_dot(d_hidden, up_ref[...])

    @pl.when(step == pl.num_programs(0) - 1)
    def _():
        d_pre, gain, bias = norm_back(
            d_middle_ref[...], mid_normed_ref[...], mid_inverse_ref[:, :1], row_of(small_ref, 5)
        )
        d_pre_ref[...] = d_pre
        d_attend_ref[...] = d_pre.astype(bfloat)
        sums_ref[pl.ds(0, 1), :] = gain[None]
        sums_ref[pl.ds(1, 1), :] = bias[None]


def feed_backward(parts, normed, inverse, hidden, small_full, mid_normed, mid_inverse, weights):
    slots, width = normed.shape
    block = (slots, width), lambda step: (0, step)
    out = lambda kind, rows=slots: ((rows, width), kind, None, None)
    return kernel_call(
        feed_back_kernel,
        "feed_backward",
        4,
        [
            whole(parts),
            whole(normed),
            whole(inverse),
            (hidden,) + block,
            whole(small_full),
            whole(mid_normed),
            whole(mid_inverse),
            (weights, (width, width), lambda step: (0, 4 + step)),
            (weights, (width, width), lambda step: (0, 8 + step)),
        ],
        [
            out(bfloat), ((slots, 4 * width), bfloat) + block, out(single), out(bfloat),
            out(single, 16),
        ],
        (16 * slots * width * width, 16 * width * width, 8 * slots * width),
        [pltpu.VMEM((slots, width), single)],
    )


def attend_back_kernel(
    d_attend_ref, key_ref, value_ref, query_ref, allowed_ref, weight_ref,
    d_query_ref, d_key_ref, d_value_ref, d_mixed_ref,
):
    d_mixed_ref[...] = trans_dot(d_attend_ref[...], weight_ref[...]).astype(bfloat)
    blocked = allowed_ref[...] == 0.0
    slots, length = blocked.shape
    low, high = pair_masks(slots)
    low_long, _ = pair_masks(length)
    scale = HD ** (-0.5)

    def one_pair(pair, carry):
        lanes = pl.ds(pl.multiple_of(pair * 2 * HD, 2 * HD), 2 * HD)
        query_pair, key_pair, value_pair = query_ref[:, lanes], key_ref[:, lanes], value_ref[:, lanes]
        mixed_pair = d_mixed_ref[:, lanes]
        found = []
        for head_lanes in (low, high):
            probs = head_probs(query_pair, key_pair, head_lanes, blocked)
            d_probs = trans_dot(
                jnp.where(head_lanes, mixed_pair, jnp.zeros_like(mixed_pair)), value_pair
            )
            inner = jnp.sum(probs * d_probs, axis=-1, keepdims=True)
            d_scores = (probs * (d_probs - inner)).astype(bfloat)
            found.append(
                (
                    plain_dot(d_scores, key_pair) * scale,
                    rows_dot(d_scores, query_pair) * scale,
                    rows_dot(probs.astype(bfloat), mixed_pair),
                )
            )
        d_query_ref[:, lanes] = jnp.where(low, found[0][0], found[1][0]).astype(bfloat)
        d_key_ref[:, lanes] = jnp.where(low_long, found[0][1], found[1][1]).astype(bfloat)
        d_value_ref[:, lanes] = jnp.where(low_long, found[0][2], found[1][2]).astype(bfloat)
        return carry

    lax.fori_loop(0, query_ref.shape[1] // (2 * HD), one_pair, 0)


def attend_backward(d_attend, key_rows, value_rows, query_rows, allowed, weights):
    length, width = key_rows.shape
    slots = d_attend.shape[0]
    out = lambda rows: ((rows, width), bfloat, None, None)
    return kernel_call(
        attend_back_kernel,
        "attention_backward",
        1,
        [
            whole(d_attend),
            whole(key_rows),
            whole(value_rows),
            whole(query_rows),
            whole(allowed),
            (weights, (width, width), lambda step: (0, 3)),
        ],
        [out(slots), out(length), out(length)],
        (
            2 * slots * width * width + 20 * slots * length * width,
            2 * width * width,
            HEADS * slots * length,
        ),
        [pltpu.VMEM((slots, width), bfloat)],
    )


def project_back_kernel(
    d_pre_ref, d_query_ref, d_key_ref, d_value_ref, slot_ref, hidden_row_ref, small_ref,
    normed_ref, inverse_ref, init_normed_ref, init_inverse_ref, weight_ref, ahead_ref,
    embed_ref, position_ref, sums_ref, d_stream_ref, d_init_ref,
):
    step = pl.program_id(0)

    @pl.when(step == 0)
    def _():
        d_init_ref[...] = d_pre_ref[...] + trans_dot(d_query_ref[...], weight_ref[...])

    @pl.when(step == 1)
    def _():
        d_stream_ref[...] = trans_dot(d_key_ref[...], weight_ref[...])

    @pl.when(step == 2)
    def _():
        gain_row = row_of(small_ref, 0)
        d_stream = d_stream_ref[...] + trans_dot(d_value_ref[...], weight_ref[...])
        d_start, gain_init, bias_init = norm_back(
            d_init_ref[...], init_normed_ref[...], init_inverse_ref[:, :1], gain_row
        )
        d_embed, gain, bias = norm_back(
            d_stream, normed_ref[...], inverse_ref[:, :1], gain_row
        )
        position_ref[...] = d_embed + lax.dot_general(
            slot_ref[...],
            d_start,
            (((0,), (0,)), ((), ())),
            precision=lax.Precision.HIGHEST,
            preferred_element_type=single,
        )
        embed_b = d_embed.astype(bfloat)
        embed_ref[...] = embed_b
        sums_ref[...] = jnp.zeros_like(sums_ref)
        sums_ref[pl.ds(0, 1), :] = (gain_init + gain)[None]
        sums_ref[pl.ds(1, 1), :] = (bias_init + bias)[None]
        sums_ref[pl.ds(2, 1), :] = column_sum(d_query_ref[...])[None]
        sums_ref[pl.ds(3, 1), :] = column_sum(d_value_ref[...])[None]
        sums_ref[pl.ds(4, 1), :] = column_sum(d_pre_ref[...].astype(bfloat))[None]
        masked = jnp.where(hidden_row_ref[:, :1] > 0.0, embed_b.astype(single), 0.0)
        sums_ref[pl.ds(5, 1), :] = jnp.sum(masked, axis=0)[None]


def project_backward(
    d_pre, d_query, d_key, d_value, slot_hot, hidden_rows, small_full,
    normed, inverse, init_normed, init_inverse, weights, ahead,
):
    length, width = normed.shape
    slots = d_pre.shape[0]
    arrays = (
        d_pre, d_query, d_key, d_value, slot_hot, hidden_rows, small_full,
        normed, inverse, init_normed, init_inverse,
    )
    return kernel_call(
        project_back_kernel,
        "projection_backward",
        3,
        [whole(array) for array in arrays]
        + [(weights, (width, width), lambda step: (0, step)), (ahead, "any", None)],
        [
            ((length, width), bfloat, None, None),
            ((length, width), single, None, None),
            ((8, width), single, None, None),
        ],
        (5 * length * width * width, 6 * width * width, 0),
        [pltpu.VMEM((length, width), single), pltpu.VMEM((slots, width), single)],
    )


def adam_direction(weight_arr, new_first, new_second):
    first_scale, second_scale = 1.0 / (1.0 - beta_first**STEP), 1.0 / (1.0 - beta_second**STEP)
    scaled = new_second * second_scale
    return (new_first * first_scale) / (
        scaled * lax.rsqrt(scaled) + adam_eps
    ) + weight_decay * weight_arr


def adam_moments(weight_arr, first_mom, second_mom, gradient, factor):
    clipped = gradient * factor
    new_first = beta_first * first_mom + (1.0 - beta_first) * clipped
    new_second = beta_second * second_mom + (1.0 - beta_second) * clipped * clipped
    return (new_first, new_second, adam_direction(weight_arr, new_first, new_second))


def row_block(count, most=240):
    return most if count % most == 0 else count


def lookup_kernel(pieces, *refs):
    step = pl.program_id(0)
    starts, count = pieces
    runs = len(starts)
    head_refs, refs = refs[: runs * count], refs[runs * count :]
    asked_ref, given_ref, side_ref, grad_ref, square_ref = refs
    rows, width = grad_ref.shape
    base = step * rows
    row_hot = asked_ref[...] == base + lax.broadcasted_iota(
        jnp.int32, (rows, asked_ref.shape[1]), 0
    )
    grad = plain_dot(row_hot.astype(bfloat), given_ref[...])
    for part in range(count):
        head = head_refs[part][...].astype(single)
        for run in range(1, runs):
            later = head_refs[run * count + part][...].astype(single)
            head = jnp.where(step >= starts[run], later, head)
        grad += head
    grad_ref[...] = grad
    place = base + lax.broadcasted_iota(jnp.int32, (rows, width), 0)
    own = (place >= side_ref[0]) & (place < side_ref[1])

    @pl.when(step == 0)
    def _():
        square_ref[...] = jnp.zeros_like(square_ref)

    square_ref[...] += jnp.sum(jnp.where(own, grad * grad, 0.0), axis=0, keepdims=True)


def lookup_grad(heads, count, asked_rows, given, sides):
    width = heads[0].shape[1]
    vrows = sum(head.shape[0] for head in heads) // count
    rows = vrows // 4
    steps = [head.shape[0] // count // rows for head in heads]
    starts = [sum(steps[:run]) for run in range(len(heads))]
    whole_spec = lambda array: pl.BlockSpec(array.shape, lambda step: (0, 0))
    return pl.pallas_call(
        lambda *refs: lookup_kernel((starts, count), *refs),
        grid=(4,),
        in_specs=[
            pl.BlockSpec(
                (rows, width),
                lambda step, run=run, part=part: (
                    part * steps[run] + jnp.clip(step - starts[run], 0, steps[run] - 1),
                    0,
                ),
            )
            for run in range(len(heads))
            for part in range(count)
        ]
        + [
            whole_spec(asked_rows),
            whole_spec(given),
            pl.BlockSpec(memory_space=pltpu.SMEM),
        ],
        out_specs=[
            pl.BlockSpec((rows, width), lambda step: (step, 0)),
            pl.BlockSpec((1, width), lambda step: (0, 0)),
        ],
        out_shape=[
            jax.ShapeDtypeStruct((vrows, width), single),
            jax.ShapeDtypeStruct((1, width), single),
        ],
        cost_estimate=pl.CostEstimate(flops=0, bytes_accessed=0, transcendentals=0),
        name="table_gradient",
    )(*[head for head in heads for _ in range(count)], asked_rows, given, sides)


def full_sum(values):
    return jnp.sum(jnp.sum(values, axis=1, keepdims=True), axis=0, keepdims=True)


def pair_row(weight_sum, dir_sum):
    lane = lax.broadcasted_iota(jnp.int32, (1, 128), 1)
    return jnp.where(lane == 0, weight_sum, dir_sum)


def norms_kernel(offset_ref, *refs):
    total_ref, table_refs, layer_refs, position_refs, small_refs = (
        refs[0], refs[1:5], refs[5:9], refs[9:13], refs[13:17],
    )
    norms_ref, layer_out, position_out, small_out = refs[17], refs[18:21], refs[21:24], refs[24:27]
    sums_ref = refs[27]
    step = pl.program_id(0)
    total_square = jnp.sum(total_ref[...], axis=0, keepdims=True)[:, :1]
    factor = jnp.minimum(1.0, clip_norm / jnp.sqrt(total_square))

    @pl.when(step == 0)
    def _():
        sums_ref[...] = jnp.zeros_like(sums_ref)
        norms_ref[...] = jnp.zeros_like(norms_ref)
        for row, group_refs, outs in ((4, position_refs, position_out), (5, small_refs, small_out)):
            weight_arr = group_refs[0][...]
            first, second, direction = adam_moments(
                weight_arr, group_refs[1][...], group_refs[2][...], group_refs[3][...], factor
            )
            for ref, value in zip(outs, (first, second, direction)):
                ref[...] = value
            norms_ref[pl.ds(row, 1), :] = pair_row(
                full_sum(weight_arr * weight_arr), full_sum(direction * direction)
            )

    @pl.when(step < 3)
    def _():
        weight_arr, first_mom, second_mom, gradient = (ref[0] for ref in layer_refs)
        first, second, direction = adam_moments(
            weight_arr, first_mom, second_mom, gradient, factor
        )
        for ref, value in zip(layer_out, (first, second, direction)):
            ref[0] = value
        norms_ref[pl.ds(1 + step, 1), :] = pair_row(
            full_sum(weight_arr * weight_arr), full_sum(direction * direction)
        )

    weight_arr = table_refs[0][...]
    _, _, direction = adam_moments(
        weight_arr, table_refs[1][...], table_refs[2][...], table_refs[3][...], factor
    )
    sums_ref[pl.ds(0, 1), :] += jnp.sum(weight_arr * weight_arr, axis=0, keepdims=True)
    sums_ref[pl.ds(1, 1), :] += jnp.sum(direction * direction, axis=0, keepdims=True)

    @pl.when(step == pl.num_programs(0) - 1)
    def _():
        norms_ref[pl.ds(0, 1), :] = pair_row(
            full_sum(sums_ref[pl.ds(0, 1), :]), full_sum(sums_ref[pl.ds(1, 1), :])
        )


def update_norms(totals, table, layer, position, small, split, dp_index):
    vrows, width = table[0].shape
    rows = row_block(split, 240)
    if split // rows < 3:
        rows = split // 3
    one_part = pl.BlockSpec(
        (1,) + layer[0].shape[1:], lambda step, offset: (jnp.minimum(step, 2), 0, 0)
    )
    fixed = lambda array: pl.BlockSpec(
        array.shape, lambda step, offset, rank=array.ndim: (0,) * rank
    )
    part = pl.BlockSpec((rows, width), lambda step, offset: (offset[0] + step, 0))
    groups = tuple(layer) + tuple(position) + tuple(small)
    outs = [
        jax.ShapeDtypeStruct(group[0].shape, single)
        for group in (layer, position, small)
        for _ in range(3)
    ]
    norms = jax.ShapeDtypeStruct((8, 128), single)
    return pl.pallas_call(
        norms_kernel,
        grid_spec=pltpu.PrefetchScalarGridSpec(
            num_scalar_prefetch=1,
            grid=(split // rows,),
            in_specs=[fixed(totals)]
            + [part] * 4
            + [one_part] * 4
            + [fixed(array) for array in groups[4:]],
            out_specs=[fixed(norms)] + [one_part] * 3 + [fixed(out) for out in outs[3:]],
            scratch_shapes=[pltpu.VMEM((8, width), single)],
        ),
        out_shape=[norms] + outs,
        cost_estimate=pl.CostEstimate(flops=0, bytes_accessed=0, transcendentals=0),
        name="update_norms",
    )((dp_index * (split // rows)).astype(jnp.int32)[None], totals, *table, *groups)


def final_kernel(
    pairs_ref, weight_ref, first_ref, second_ref,
    layer_ref, layer_dir_ref, position_ref, position_dir_ref, small_ref, small_dir_ref,
    next_ref, layer_next_ref, position_next_ref, small_next_ref,
):
    roots = jnp.sqrt(jnp.sum(pairs_ref[...], axis=0, keepdims=True))

    def rate(group):
        return learn_rate * (
            roots[:, 2 * group : 2 * group + 1] / roots[:, 2 * group + 1 : 2 * group + 2]
        )

    weight_arr = weight_ref[...]
    direction = adam_direction(weight_arr, first_ref[...], second_ref[...])
    next_ref[...] = weight_arr - rate(0) * direction

    step = pl.program_id(0)
    for part in range(3):

        @pl.when(step == part)
        def _():
            layer_next_ref[0] = layer_ref[0] - rate(1 + part) * layer_dir_ref[0]

    @pl.when(step == 0)
    def _():
        position_next_ref[...] = position_ref[...] - rate(4) * position_dir_ref[...]
        small_next_ref[...] = small_ref[...] - rate(5) * small_dir_ref[...]


def final_update(pairs, table, groups):
    vrows, width = table[0].shape
    rows = row_block(vrows, 480)
    if vrows // rows < 3:
        rows = row_block(vrows, 240)
    fixed = lambda array: pl.BlockSpec(array.shape, lambda step, rank=array.ndim: (0,) * rank)
    block = pl.BlockSpec((rows, width), lambda step: (step, 0))
    one_part = pl.BlockSpec((1,) + groups[0].shape[1:], lambda step: (jnp.minimum(step, 2), 0, 0))
    outs = [jax.ShapeDtypeStruct(array.shape, single) for array in groups[::2]]
    return pl.pallas_call(
        final_kernel,
        grid=(vrows // rows,),
        in_specs=[fixed(pairs)]
        + [block] * 3
        + [one_part] * 2
        + [fixed(array) for array in groups[2:]],
        out_specs=[block, one_part] + [fixed(out) for out in outs[1:]],
        out_shape=[jax.ShapeDtypeStruct((vrows, width), single)] + outs,
        cost_estimate=pl.CostEstimate(flops=0, bytes_accessed=0, transcendentals=0),
        name="final_update",
    )(pairs, *table, *groups)


class Exchange:
    def __init__(self):
        self.last = None

    def __call__(self, values, axes):
        if self.last is not None:
            values, _ = lax.optimization_barrier((values, self.last))
        self.last = lax.all_to_all(values, axes, 0, 0, tiled=True)
        return self.last

    def copies(self, values, axes, count):
        return self(jnp.broadcast_to(values[None], (count,) + values.shape), axes)

    def columns(self, values, axes, count):
        rows, width = values.shape
        blocks = values.reshape(rows, count, width // count).transpose(1, 0, 2)
        return self(blocks, axes).reshape(count * rows, -1)

    def rows(self, values, count):
        return self(values.reshape(count, values.shape[0] // count, values.shape[1]), ALL)


def side_by_side(blocks):
    return blocks.transpose(1, 0, 2).reshape(blocks.shape[1], -1)


def after(values, *waits):
    for wait in waits:
        values = values + (wait[(0,) * wait.ndim] > 3.395e38).astype(values.dtype)
    return values


def masked_total(mask, values):
    return jnp.sum(jnp.where(mask, values, 0), axis=-1)


def slot_layout(pred_row, order_row, token_row):
    length = pred_row.shape[0]
    index = jnp.arange(length)
    before = index[None, :] <= index[:, None]
    seen = masked_total(before, pred_row[None, :])
    masked = jnp.sum(pred_row)
    place = jnp.where(pred_row == 1, seen - 1, masked + index - seen)
    slot_hot = place[None, :] == jnp.arange(CAP)[:, None]
    rank_row = masked_total(order_row[None, :] == index[:, None], index[None, :])
    slot_rank = masked_total(slot_hot, rank_row[None, :])
    slot_target = masked_total(slot_hot, token_row[None, :])
    slot_pos = masked_total(slot_hot, index[None, :])
    allowed = rank_row[None, :] <= slot_rank[:, None]
    return slot_hot, slot_pos, slot_target, allowed, masked


def bucket_layout(content, vrows):
    index = jnp.arange(content.shape[0])
    same = content[None, :] == content[:, None]
    first = jnp.min(jnp.where(same, index[None, :], content.shape[0]), axis=1)
    is_first = first == index
    owner = content // vrows
    ahead = (owner[None, :] == owner[:, None]) & is_first[None, :] & (index[None, :] < first[:, None])
    return owner, jnp.sum(ahead.astype(jnp.int32), axis=1)


def bucket_round(content, owner, place, turn, owners, vrows):
    usable = BUCKET - 1
    local = place - turn * usable
    taken = (local >= 0) & (local < usable)
    flat = jnp.where(taken, owner * BUCKET + local, -1)
    hot = flat[None, :] == jnp.arange(owners * BUCKET)[:, None]
    wanted = jnp.max(jnp.where(hot, (content - owner * vrows)[None, :], -1), axis=1)
    return hot.astype(bfloat), wanted.reshape(owners, BUCKET)


def on_device(
    token_ids,
    pred_mask,
    fact_order,
    corpus,
    embed_table,
    table_moment,
    table_square,
    layer_weights,
    layer_moment,
    layer_square,
    position_table,
    position_moment,
    position_square,
    small_params,
    small_moment,
    small_square,
):
    exchange = Exchange()
    dp_devs = lax.axis_size("dp")
    owners = lax.axis_size(VOC)
    devices = dp_devs * owners
    vrows, width = embed_table.shape
    length = token_ids.shape[1]
    feed = layer_weights.shape[2]
    shared = jnp.concatenate([position_table, small_params]).T
    shared_rows = shared.shape[1]
    shared = jnp.pad(shared, ((0, 0), (0, -shared_rows % 128)))
    shard = jnp.concatenate([layer_weights[0], layer_weights[1], layer_weights[2], shared], axis=1)
    shard = lax.all_gather(shard.astype(bfloat), ALL, axis=0, tiled=True)
    table_b = embed_table.astype(bfloat)
    token_row = token_ids[0]
    pred_row = pred_mask[0]
    first_row = lax.axis_index(VOC) * vrows
    content = jnp.where(pred_row == 1, MASK_ID, token_row)
    slot_hot, slot_pos, slot_target, allowed, masked = slot_layout(pred_row, fact_order[0], token_row)
    owner, place = bucket_layout(content, vrows)
    hot, wanted = bucket_round(content, owner, place, 0, owners, vrows)
    note = jnp.concatenate(
        [slot_target, slot_pos, jnp.stack([masked, corpus[0], jnp.max(place)])]
    )
    packet = jnp.concatenate(
        [wanted, jnp.broadcast_to(note[None], (owners, note.shape[0]))], axis=1
    )
    packet = jnp.pad(packet, ((0, 0), (0, 256 - packet.shape[1])))
    packet = jnp.broadcast_to(packet[None], (dp_devs,) + packet.shape)
    packet = exchange(packet.reshape(devices, packet.shape[-1]), ALL)
    asked = packet[:, :BUCKET]
    tail = BUCKET + 2 * CAP
    counts_all = packet[:, tail]
    corpus_all = packet[:, tail + 1]
    rounds = jnp.max(packet[:, tail + 2]) // (BUCKET - 1) + 1
    group = lax.axis_index("dp") * owners
    outer = lax.axis_size("hi")

    def group_order(values):
        return values.reshape(outer, 2, 2, CAP).transpose(2, 1, 0, 3).reshape(-1)

    group_asked = lax.dynamic_slice_in_dim(asked, group, owners, 0)
    group_target = group_order(
        lax.dynamic_slice_in_dim(packet[:, BUCKET : BUCKET + CAP], group, owners, 0)
    )
    corpus_hot = corpus_all[:, None] == jnp.arange(NCORP)[None, :]
    corpus_counts = jnp.sum(jnp.where(corpus_hot, counts_all[:, None], 0), axis=0)
    seq_count = masked_total(corpus_hot, corpus_counts[None, :])
    seq_weight = 1.0 / (NCORP * seq_count.astype(single))
    slot_weight = jnp.where(
        jnp.arange(CAP)[None, :] < counts_all[:, None], seq_weight[:, None], 0.0
    )
    group_weight = group_order(lax.dynamic_slice_in_dim(slot_weight, group, owners, 0))

    def serve(asked_rows):
        served = jnp.take(table_b, jnp.maximum(asked_rows, 0).reshape(-1), axis=0)
        return served.reshape(owners, BUCKET, width)

    arrived = exchange(serve(group_asked), VOC)
    embed_rows = rows_dot(hot, arrived.reshape(-1, width))

    def more_rows(state):
        turn, rows = state
        hot_t, wanted_t = bucket_round(content, owner, place, turn, owners, vrows)
        asked_t = lax.all_to_all(wanted_t, VOC, 0, 0, tiled=True)
        arrived_t = lax.all_to_all(serve(asked_t), VOC, 0, 0, tiled=True)
        return turn + 1, rows + rows_dot(hot_t, arrived_t.reshape(-1, width))

    _, embed_rows = lax.while_loop(
        lambda state: state[0] < rounds, more_rows, (jnp.ones((), rounds.dtype), embed_rows)
    )
    few = devices <= 32
    near = 4
    allowed = allowed.astype(single)
    slot_hot = slot_hot.astype(single)
    (
        key_rows,
        value_rows,
        query_rows,
        mixed_b,
        middle,
        mid_normed,
        mid_inverse,
        stream_b,
        stream_normed,
        stream_inverse,
        query_init,
        init_normed,
        init_inverse,
        position_full,
        small_full,
    ) = attend_forward(embed_rows, slot_hot, allowed, shard, length, small_params.shape[0])
    middle_b, hidden, active_b, output_b, end_normed, end_inverse = feed_forward(
        middle, small_full, shard
    )
    if few:
        kept_rows = jnp.concatenate([mixed_b, middle_b], axis=1)
        kept_all = lax.all_gather(kept_rows, ALL, axis=0, tiled=True)
        stream_all = lax.all_gather(stream_b, NEAR, axis=0, tiled=True)
    group_rows = exchange.copies(output_b, "hi", outer).reshape(-1, width)
    group_rows = exchange.copies(group_rows, "mid", 2).reshape(-1, width)
    group_rows = exchange.copies(group_rows, "core", 2).reshape(-1, width)
    logits = trans_dot(group_rows, table_b)
    local_target = group_target - first_row
    target_hit = jnp.arange(vrows)[None, :] == local_target[:, None]
    row_top = jnp.max(logits, axis=1)
    row_total = jnp.sum(jnp.exp(logits - row_top[:, None]), axis=1)
    row_target = jnp.sum(jnp.where(target_hit, logits, 0.0), axis=1)
    stats = exchange.copies(jnp.stack([row_top, row_total]), VOC, owners)
    top_all = jnp.max(stats[:, 0], axis=0)
    total_all = jnp.sum(stats[:, 1] * jnp.exp(stats[:, 0] - top_all[None]), axis=0)
    log_total = top_all + jnp.log(total_all)
    own_place = lax.axis_index(("core", "mid", "hi"))
    own_total = lax.dynamic_slice_in_dim(log_total * group_weight, own_place * CAP, CAP, 0)
    loss_part = jnp.sum(own_total) - jnp.sum(row_target * group_weight)
    d_logits = (
        group_weight[:, None] * (jnp.exp(logits - log_total[:, None]) - target_hit.astype(single))
    ).astype(bfloat)
    def swapped(axis, kind, part):
        side = lax.axis_index(axis)
        theirs = lax.ppermute(part(1 - side).astype(kind), axis, [(0, 1), (1, 0)])
        return part(side) + theirs.astype(single)

    half = owners * CAP // 2

    def rows_half(side):
        return plain_dot(lax.dynamic_slice_in_dim(d_logits, side * half, half, 0), table_b)

    d_output = swapped("core", single, rows_half)
    quarter = half // 2
    d_half = d_output
    d_output = swapped(
        "mid", bfloat, lambda side: lax.dynamic_slice_in_dim(d_half, side * quarter, quarter, 0)
    )
    grad_head = rows_dot(d_logits, group_rows)
    grad_head = after(grad_head, d_half, *((stream_all,) if few else ()))
    heads = [
        lax.all_gather(half_b, "dp", axis=0, tiled=True)
        for half_b in jnp.split(grad_head.astype(bfloat), [vrows * 3 // 4])
    ]
    d_output = exchange(d_output.astype(bfloat).reshape(outer, CAP, width), "hi")
    if few:
        d_output, kept_all = lax.optimization_barrier((d_output, kept_all))
    d_branch, d_hidden, d_pre, d_attend, sums_feed = feed_backward(
        d_output,
        end_normed,
        end_inverse,
        hidden,
        small_full,
        mid_normed,
        mid_inverse,
        shard,
    )
    if few:
        wide = feed // devices
        both = jnp.concatenate(
            [
                d_hidden.reshape(CAP, devices, -1),
                d_attend.reshape(CAP, devices, -1),
            ],
            axis=2,
        ).reshape(CAP, -1)
        both = exchange.columns(both, ALL, devices)
        branch_all = lax.all_gather(d_branch, ALL, axis=0, tiled=True)
    d_query, d_key, d_value = attend_backward(
        d_attend, key_rows, value_rows, query_rows, allowed, shard
    )
    if few:
        piece = width // near
        pairs = jnp.concatenate(
            [d_key.reshape(length, near, piece), d_value.reshape(length, near, piece)], axis=2
        ).transpose(1, 0, 2)
        asks = d_query.reshape(CAP, near, piece).transpose(1, 0, 2)
        asks = jnp.concatenate([asks[:, : CAP // 2], asks[:, CAP // 2 :]], axis=2)
        pairs = exchange(jnp.concatenate([pairs, asks], axis=1), NEAR)
    hidden_rows = spread((content == MASK_ID).astype(single)[:, None])
    embed_back, grad_position, sums_back = project_backward(
        d_pre,
        d_query,
        d_key,
        d_value,
        slot_hot,
        hidden_rows,
        small_full,
        stream_normed,
        stream_inverse,
        init_normed,
        init_inverse,
        shard,
        heads[0],
    )
    grad_small = jnp.concatenate([sums_back[:5], sums_feed[:9]])
    mask_sum = sums_back[5]
    mask_left = mask_sum - lax.reduce_precision(mask_sum, 8, 7)
    mask_owner = MASK_ID // vrows
    is_left = (jnp.arange(BUCKET) == BUCKET - 1)[None, :] & (
        jnp.arange(owners) == mask_owner
    )[:, None]

    def plain_exchange(values, axes):
        return lax.all_to_all(values, axes, 0, 0, tiled=True)

    def give(hot_rows, extra, send):
        rows = plain_dot(hot_rows, embed_back).reshape(owners, BUCKET, width)
        rows = jnp.where(is_left[:, :, None] & extra, mask_left[None, None, :], rows)
        return send(rows.astype(bfloat), VOC).reshape(-1, width)

    def of_both(rows):
        if dp_devs == 2:
            return jnp.concatenate([rows, lax.ppermute(rows, "dp", [(0, 1), (1, 0)])])
        return lax.all_gather(rows, "dp", axis=0, tiled=True)

    def both_groups(asked_rows):
        if dp_devs == 2:
            return jnp.roll(asked_rows, -group, axis=0)
        return asked_rows

    split = vrows // dp_devs
    sides = lax.axis_index("dp") * split + jnp.array([0, split])

    def into_rows(heads, parts, asked_rows, given, sides):
        return lookup_grad(heads, parts, both_groups(asked_rows).reshape(1, -1), given, sides)

    last = (jnp.arange(BUCKET) == BUCKET - 1)[None, :]
    left_row = jnp.where(lax.axis_index(VOC) == mask_owner, MASK_ID - first_row, -1)
    given = of_both(give(hot, True, exchange))

    if few:
        near_pos = packet[:, BUCKET + CAP : tail].reshape(dp_devs * outer, near * CAP)
        near_pos = lax.dynamic_index_in_dim(
            near_pos, lax.axis_index(("dp", "hi")), 0, False
        )
        init_rows = norm_forward(position_full, small_full[0], small_full[1])[0].astype(bfloat)
        init_hot = near_pos[:, None] == jnp.arange(length)[None, :]
        init_all = plain_dot(init_hot.astype(bfloat), init_rows).astype(bfloat)
        asks = pairs[:, length:]
        asks = jnp.concatenate([asks[..., :piece], asks[..., piece:]], axis=1)
        grad_pair = rows_dot(stream_all, pairs[:, :length].reshape(near * length, -1))
        grad_ask = rows_dot(init_all, asks.reshape(near * CAP, piece))
        share = width // devices
        active_mine = exchange.columns(active_b, ALL, devices)
        grad_up = rows_dot(kept_all[:, width:], both[:, :wide])
        grad_out = rows_dot(kept_all[:, :width], both[:, wide:])
        grad_down = rows_dot(branch_all, active_mine)
        shared_grad = jnp.concatenate([grad_position, grad_small]).T
        results = jnp.concatenate(
            [grad_pair, grad_ask, grad_up, grad_down, grad_out, shared_grad], axis=1
        )
        results = after(results.astype(bfloat), given[-1:])
        results = exchange.rows(results, devices).astype(single)
        sides = after(sides, results)
        pieces = 3 * piece
        attn = jnp.sum(
            results[..., :pieces].reshape(dp_devs * outer, near, share, pieces), axis=0
        )
        shared_grad = jnp.sum(results[..., -shared_rows:], axis=0)
        single_parts = results[..., pieces:-shared_rows]
        part_square = (
            jnp.sum(attn * attn)
            + jnp.sum(single_parts * single_parts)
            + jnp.sum(shared_grad * shared_grad)
        )
        shared_grad = shared_grad.T
        position_grad, small_grad = shared_grad[:length], shared_grad[length:]
        grad_key, grad_value, grad_query = (
            side_by_side(attn[..., part * piece : (part + 1) * piece]) for part in range(3)
        )
        grad_up, grad_down, grad_out = (
            side_by_side(single_parts[..., low:high])
            for low, high in ((0, wide), (wide, 2 * wide), (2 * wide, None))
        )
        layer_grad = jnp.stack(
            [
                jnp.concatenate([grad_query, grad_key, grad_value, grad_out], axis=1),
                grad_up,
                grad_down,
            ]
        )
    else:
        whole = (
            jnp.concatenate(
                [
                    rows_dot(query_init.astype(bfloat), d_query),
                    rows_dot(stream_b, d_key),
                    rows_dot(stream_b, d_value),
                    rows_dot(mixed_b, d_attend),
                ],
                axis=1,
            ),
            rows_dot(middle_b, d_hidden),
            rows_dot(d_branch, active_b),
        )
        layer_grad = jnp.stack(
            [lax.psum_scatter(part, ALL, scatter_dimension=0, tiled=True) for part in whole]
        )
        shared_grad = jnp.concatenate([grad_position, grad_small]).T
        shared_grad = lax.psum_scatter(shared_grad, ALL, scatter_dimension=0, tiled=True).T
        position_grad, small_grad = shared_grad[:length], shared_grad[length:]
        part_square = jnp.sum(layer_grad * layer_grad) + jnp.sum(shared_grad * shared_grad)
    table_grad, table_square_sum = into_rows(
        heads, dp_devs, jnp.where(last, left_row, asked), given, sides
    )

    def more_grads(state):
        turn, grads, _ = state
        hot_t, wanted_t = bucket_round(content, owner, place, turn, owners, vrows)
        wanted_t = jnp.broadcast_to(wanted_t[None], (dp_devs,) + wanted_t.shape)
        asked_t = lax.all_to_all(
            wanted_t.reshape(devices, BUCKET), ALL, 0, 0, tiled=True
        )
        given_t = of_both(give(hot_t, False, plain_exchange))
        return (turn + 1,) + tuple(into_rows([grads], 1, asked_t, given_t, sides))

    _, table_grad, table_square_sum = lax.while_loop(
        lambda state: state[0] < rounds,
        more_grads,
        (jnp.ones((), rounds.dtype), table_grad, table_square_sum),
    )
    square_part = jnp.sum(table_square_sum) + part_square
    totals = exchange.copies(jnp.stack([square_part, loss_part]), ALL, devices)
    total_square, loss_value = jnp.sum(totals, axis=0)
    grad_norm = jnp.sqrt(total_square)
    factor = jnp.minimum(1.0, clip_norm / grad_norm)
    (
        norms,
        layer_first,
        layer_second,
        layer_dir,
        position_first,
        position_second,
        position_dir,
        small_first,
        small_second,
        small_dir,
    ) = update_norms(
        totals,
        (embed_table, table_moment, table_square, table_grad),
        (layer_weights, layer_moment, layer_square, layer_grad),
        (position_table, position_moment, position_square, position_grad),
        (small_params, small_moment, small_square, small_grad),
        split,
        lax.axis_index("dp"),
    )
    factor_late, norms = lax.optimization_barrier((factor, norms))
    pairs = exchange.copies(norms[:6, :2].reshape(-1), ALL, devices)
    table_first, table_second, _ = adam_moments(
        embed_table, table_moment, table_square, table_grad, factor_late
    )
    trust_norms = jnp.sqrt(jnp.sum(pairs, axis=0)).reshape(6, 2)
    table_next, layer_next, position_next, small_next = final_update(
        pairs,
        (embed_table, table_first, table_second),
        (
            layer_weights,
            layer_dir,
            position_table,
            position_dir,
            small_params,
            small_dir,
        ),
    )
    return (
        loss_value,
        grad_norm,
        table_next,
        table_first,
        table_second,
        layer_next,
        layer_first,
        layer_second,
        position_next,
        position_first,
        position_second,
        small_next,
        small_first,
        small_second,
        trust_norms,
    )


def solution(mesh):
    dp_devs, owners = mesh.devices.shape
    fine = Mesh(mesh.devices.reshape(dp_devs, owners // 4, 2, 2), ALL)
    rows, inner = P(ALL, None), P(None, ALL)
    table, layer = P(VOC, None), P(None, ALL, None)
    return jax.shard_map(
        on_device,
        mesh=fine,
        in_specs=(rows,) * 3 + (P(ALL),) + (table,) * 3 + (layer,) * 3 + (inner,) * 6,
        out_specs=(P(), P()) + (table,) * 3 + (layer,) * 3 + (inner,) * 6 + (P(),),
        check_vma=False,
    )
```

```python
import jax
import jax.numpy as jnp
from jax import lax
from jax.experimental import pallas as pl
from jax.experimental.pallas import tpu as pltpu
from jax.sharding import Mesh
from jax.sharding import PartitionSpec as P

HEADS = 12
HD = 64
MASK_ID = 103
NCORP = 4
STEP = 5
CAP = 64


clip_norm = 0.1
learn_rate = 0.3
beta_first = 0.9
beta_second = 0.999
adam_eps = 1e-06
weight_decay = 0.01
norm_eps = 1e-05
masked_score = -1e30
BUCKET = 32
ALL = ("dp", "hi", "mid", "core")
VOC = ("hi", "mid", "core")
NEAR = ("mid", "core")
bfloat = jnp.bfloat16
single = jnp.float32


def plain_dot(left_op, right_op):
    return jnp.dot(left_op, right_op, preferred_element_type=single)


def trans_dot(left_op, right_op):
    return lax.dot_general(
        left_op, right_op, (((1,), (1,)), ((), ())), preferred_element_type=single
    )


def rows_dot(left_op, right_op):
    return lax.dot_general(
        left_op, right_op, (((0,), (0,)), ((), ())), preferred_element_type=single
    )


def column_sum(values):
    return jnp.sum(values.astype(single), axis=0)


def norm_forward(values, gain_row, bias_row):
    center = values - jnp.mean(values, axis=-1, keepdims=True)
    inverse = lax.rsqrt(jnp.mean(center * center, axis=-1, keepdims=True) + norm_eps)
    normed = center * inverse
    return (normed * gain_row + bias_row, (normed, inverse))


def norm_backward(upstream, kept_norm, gain_row):
    normed, inverse = kept_norm
    scaled = upstream * gain_row
    inner = (
        scaled
        - jnp.mean(scaled, axis=-1, keepdims=True)
        - normed * jnp.mean(scaled * normed, axis=-1, keepdims=True)
    )
    return (inner * inverse, jnp.sum(upstream * normed, axis=0), jnp.sum(upstream, axis=0))


def pair_masks(rows):
    lane = lax.broadcasted_iota(jnp.int32, (rows, 2 * HD), 1)
    return lane < HD, lane >= HD


def head_probs(query_pair, key_pair, head_lanes, blocked):
    scores = trans_dot(jnp.where(head_lanes, query_pair, jnp.zeros_like(query_pair)), key_pair)
    scores = jnp.where(blocked, masked_score, scores * HD ** (-0.5))
    row_top = jnp.max(scores, axis=-1, keepdims=True)
    powers = jnp.exp(scores - row_top)
    return powers / jnp.sum(powers, axis=-1, keepdims=True)


def spread(column, lanes=128):
    return jnp.broadcast_to(column, (column.shape[0], lanes))


def row_of(ref, row):
    return ref[pl.ds(row, 1), :]


def attend_kernel(
    embed_ref, slot_ref, allowed_ref, shared_ref, weight_ref,
    key_ref, value_ref, query_ref, mixed_ref, middle_ref, normed_ref, inverse_ref,
    stream_ref, stream_normed_ref, stream_inverse_ref,
    init_ref, init_normed_ref, init_inverse_ref, position_ref, small_ref,
):
    step = pl.program_id(0)
    length = position_ref.shape[0]

    @pl.when(step == 0)
    def _():
        shared = shared_ref[...].astype(single).T
        position_ref[...] = shared[:length]
        small_ref[...] = shared[length : length + small_ref.shape[0]]
        gain, bias = row_of(small_ref, 0), row_of(small_ref, 1)
        stream, (normed, inverse) = norm_forward(embed_ref[...] + position_ref[...], gain, bias)
        stream_ref[...] = stream.astype(bfloat)
        stream_normed_ref[...] = normed
        stream_inverse_ref[...] = spread(inverse)
        chosen = plain_dot(slot_ref[...].astype(bfloat), position_ref[...].astype(bfloat))
        init, (normed, inverse) = norm_forward(chosen, gain, bias)
        init_ref[...] = init
        init_normed_ref[...] = normed
        init_inverse_ref[...] = spread(inverse)
        key_ref[...] = plain_dot(stream_ref[...], weight_ref[...]).astype(bfloat)

    @pl.when(step == 1)
    def _():
        value_ref[...] = (
            plain_dot(stream_ref[...], weight_ref[...]) + row_of(small_ref, 3)
        ).astype(bfloat)

    @pl.when(step == 2)
    def _():
        query_ref[...] = (
            plain_dot(init_ref[...].astype(bfloat), weight_ref[...]) + row_of(small_ref, 2)
        ).astype(bfloat)
        blocked = allowed_ref[...] == 0.0
        low, high = pair_masks(query_ref.shape[0])

        def one_pair(pair, carry):
            lanes = pl.ds(pl.multiple_of(pair * 2 * HD, 2 * HD), 2 * HD)
            query_pair, key_pair, value_pair = query_ref[:, lanes], key_ref[:, lanes], value_ref[:, lanes]
            left, right = (
                plain_dot(
                    head_probs(query_pair, key_pair, head_lanes, blocked).astype(bfloat), value_pair
                )
                for head_lanes in (low, high)
            )
            mixed_ref[:, lanes] = jnp.where(low, left, right).astype(bfloat)
            return carry

        lax.fori_loop(0, query_ref.shape[1] // (2 * HD), one_pair, 0)

    @pl.when(step == 3)
    def _():
        attend = plain_dot(mixed_ref[...], weight_ref[...]) + row_of(small_ref, 4)
        middle, (normed, inverse) = norm_forward(
            init_ref[...] + attend, row_of(small_ref, 5), row_of(small_ref, 6)
        )
        middle_ref[...] = middle
        normed_ref[...] = normed
        inverse_ref[...] = spread(inverse)


def kernel_call(body, name, steps, inputs, shapes, cost, scratch=()):
    fixed = lambda rank: lambda step: (0,) * rank

    def spec(shape, block, index):
        if block is None:
            return pl.BlockSpec(shape, fixed(len(shape)))
        if block == "any":
            return pl.BlockSpec(memory_space=pl.ANY)
        return pl.BlockSpec(block, index)

    return pl.pallas_call(
        body,
        grid=(steps,),
        in_specs=[spec(array.shape, block, index) for array, block, index in inputs],
        out_specs=[spec(shape, block, index) for shape, _, block, index in shapes],
        out_shape=[jax.ShapeDtypeStruct(shape, kind) for shape, kind, _, _ in shapes],
        scratch_shapes=list(scratch),
        cost_estimate=pl.CostEstimate(flops=cost[0] // 64, bytes_accessed=cost[1] // 64, transcendentals=0),
        name=name,
    )(*(array for array, _, _ in inputs))


def whole(array):
    return array, None, None


def attend_forward(embed_rows, slot_hot, allowed, weights, length, small_count):
    width = embed_rows.shape[1]
    slots = slot_hot.shape[0]
    out = lambda rows, kind, columns=width: ((rows, columns), kind, None, None)
    shared = weights.shape[1] - 12 * width
    return kernel_call(
        attend_kernel,
        "attention_forward",
        4,
        [
            whole(embed_rows),
            whole(slot_hot),
            whole(allowed),
            (weights, (width, shared), lambda step: (0, 12 * width // shared)),
            (
                weights,
                (width, width),
                lambda step: (0, jnp.where(step == 3, 3, (step + 1) % 3)),
            ),
        ],
        [
            out(length, bfloat), out(length, bfloat), out(slots, bfloat), out(slots, bfloat),
            out(slots, single), out(slots, single), out(slots, single, 128),
            out(length, bfloat), out(length, single), out(length, single, 128),
            out(slots, single), out(slots, single), out(slots, single, 128),
            out(length, single), out(small_count, single),
        ],
        (
            4 * length * width * width + 8 * slots * length * width,
            8 * width * width,
            HEADS * slots * length,
        ),
    )


def erf_half(hidden):
    return 0.5 * (1.0 + lax.erf(hidden * 0.5**0.5))


def feed_kernel(
    middle_ref, small_ref, up_ref, down_ref,
    middle_b_ref, hidden_ref, active_ref, output_ref, normed_ref, inverse_ref, total_ref,
):
    step = pl.program_id(0)

    @pl.when(step == 0)
    def _():
        middle_b_ref[...] = middle_ref[...].astype(bfloat)
        total_ref[...] = middle_ref[...] + row_of(small_ref, 11)

    hidden = plain_dot(middle_b_ref[...], up_ref[...]) + row_of(small_ref, 7 + step)
    hidden_ref[...] = hidden
    active = (hidden * erf_half(hidden)).astype(bfloat)
    active_ref[...] = active
    total_ref[...] += trans_dot(active, down_ref[...])

    @pl.when(step == pl.num_programs(0) - 1)
    def _():
        output, (normed, inverse) = norm_forward(
            total_ref[...], row_of(small_ref, 12), row_of(small_ref, 13)
        )
        output_ref[...] = output.astype(bfloat)
        normed_ref[...] = normed
        inverse_ref[...] = spread(inverse)


def feed_forward(middle, small_full, weights):
    slots, width = middle.shape
    wide = lambda kind: ((slots, 4 * width), kind, (slots, width), lambda step: (0, step))
    out = lambda kind, columns=width: ((slots, columns), kind, None, None)
    return kernel_call(
        feed_kernel,
        "feed_forward",
        4,
        [
            whole(middle),
            whole(small_full),
            (weights, (width, width), lambda step: (0, 4 + step)),
            (weights, (width, width), lambda step: (0, 8 + step)),
        ],
        [
            out(bfloat), wide(single), wide(bfloat), out(bfloat), out(single), out(single, 128),
        ],
        (16 * slots * width * width, 16 * width * width, 4 * slots * width),
        [pltpu.VMEM((slots, width), single)],
    )


def norm_back(upstream, normed, inverse, gain_row):
    return norm_backward(upstream, (normed, inverse), gain_row)


def feed_back_kernel(
    parts_ref, normed_ref, inverse_ref, hidden_ref, small_ref, mid_normed_ref, mid_inverse_ref,
    up_ref, down_ref,
    d_branch_ref, d_hidden_ref, d_pre_ref, d_attend_ref, sums_ref, d_middle_ref,
):
    step = pl.program_id(0)

    @pl.when(step == 0)
    def _():
        sums_ref[...] = jnp.zeros_like(sums_ref)
        d_sum, gain, bias = norm_back(
            jnp.sum(parts_ref[...].astype(single), axis=0), normed_ref[...], inverse_ref[:, :1], row_of(small_ref, 12)
        )
        d_branch = d_sum.astype(bfloat)
        d_branch_ref[...] = d_branch
        d_middle_ref[...] = d_sum
        sums_ref[pl.ds(6, 1), :] = column_sum(d_branch)[None]
        sums_ref[pl.ds(7, 1), :] = gain[None]
        sums_ref[pl.ds(8, 1), :] = bias[None]

    hidden = hidden_ref[...]
    slope = erf_half(hidden) + hidden * jnp.exp(-0.5 * hidden * hidden) * (2.0 * jnp.pi) ** (-0.5)
    d_hidden = (plain_dot(d_branch_ref[...], down_ref[...]) * slope).astype(bfloat)
    d_hidden_ref[...] = d_hidden
    sums_ref[pl.ds(2 + step, 1), :] = column_sum(d_hidden)[None]
    d_middle_ref[...] += trans_dot(d_hidden, up_ref[...])

    @pl.when(step == pl.num_programs(0) - 1)
    def _():
        d_pre, gain, bias = norm_back(
            d_middle_ref[...], mid_normed_ref[...], mid_inverse_ref[:, :1], row_of(small_ref, 5)
        )
        d_pre_ref[...] = d_pre
        d_attend_ref[...] = d_pre.astype(bfloat)
        sums_ref[pl.ds(0, 1), :] = gain[None]
        sums_ref[pl.ds(1, 1), :] = bias[None]


def feed_backward(parts, normed, inverse, hidden, small_full, mid_normed, mid_inverse, weights):
    slots, width = normed.shape
    block = (slots, width), lambda step: (0, step)
    out = lambda kind, rows=slots: ((rows, width), kind, None, None)
    return kernel_call(
        feed_back_kernel,
        "feed_backward",
        4,
        [
            whole(parts),
            whole(normed),
            whole(inverse),
            (hidden,) + block,
            whole(small_full),
            whole(mid_normed),
            whole(mid_inverse),
            (weights, (width, width), lambda step: (0, 4 + step)),
            (weights, (width, width), lambda step: (0, 8 + step)),
        ],
        [
            out(bfloat), ((slots, 4 * width), bfloat) + block, out(single), out(bfloat),
            out(single, 16),
        ],
        (16 * slots * width * width, 16 * width * width, 8 * slots * width),
        [pltpu.VMEM((slots, width), single)],
    )


def attend_back_kernel(
    d_attend_ref, key_ref, value_ref, query_ref, allowed_ref, weight_ref,
    d_query_ref, d_key_ref, d_value_ref, d_mixed_ref,
):
    d_mixed_ref[...] = trans_dot(d_attend_ref[...], weight_ref[...]).astype(bfloat)
    blocked = allowed_ref[...] == 0.0
    slots, length = blocked.shape
    low, high = pair_masks(slots)
    low_long, _ = pair_masks(length)
    scale = HD ** (-0.5)

    def one_pair(pair, carry):
        lanes = pl.ds(pl.multiple_of(pair * 2 * HD, 2 * HD), 2 * HD)
        query_pair, key_pair, value_pair = query_ref[:, lanes], key_ref[:, lanes], value_ref[:, lanes]
        mixed_pair = d_mixed_ref[:, lanes]
        found = []
        for head_lanes in (low, high):
            probs = head_probs(query_pair, key_pair, head_lanes, blocked)
            d_probs = trans_dot(
                jnp.where(head_lanes, mixed_pair, jnp.zeros_like(mixed_pair)), value_pair
            )
            inner = jnp.sum(probs * d_probs, axis=-1, keepdims=True)
            d_scores = (probs * (d_probs - inner)).astype(bfloat)
            found.append(
                (
                    plain_dot(d_scores, key_pair) * scale,
                    rows_dot(d_scores, query_pair) * scale,
                    rows_dot(probs.astype(bfloat), mixed_pair),
                )
            )
        d_query_ref[:, lanes] = jnp.where(low, found[0][0], found[1][0]).astype(bfloat)
        d_key_ref[:, lanes] = jnp.where(low_long, found[0][1], found[1][1]).astype(bfloat)
        d_value_ref[:, lanes] = jnp.where(low_long, found[0][2], found[1][2]).astype(bfloat)
        return carry

    lax.fori_loop(0, query_ref.shape[1] // (2 * HD), one_pair, 0)


def attend_backward(d_attend, key_rows, value_rows, query_rows, allowed, weights):
    length, width = key_rows.shape
    slots = d_attend.shape[0]
    out = lambda rows: ((rows, width), bfloat, None, None)
    return kernel_call(
        attend_back_kernel,
        "attention_backward",
        1,
        [
            whole(d_attend),
            whole(key_rows),
            whole(value_rows),
            whole(query_rows),
            whole(allowed),
            (weights, (width, width), lambda step: (0, 3)),
        ],
        [out(slots), out(length), out(length)],
        (
            2 * slots * width * width + 20 * slots * length * width,
            2 * width * width,
            HEADS * slots * length,
        ),
        [pltpu.VMEM((slots, width), bfloat)],
    )


def project_back_kernel(
    d_pre_ref, d_query_ref, d_key_ref, d_value_ref, slot_ref, hidden_row_ref, small_ref,
    normed_ref, inverse_ref, init_normed_ref, init_inverse_ref, weight_ref, ahead_ref,
    embed_ref, position_ref, sums_ref, d_stream_ref, d_init_ref,
):
    step = pl.program_id(0)

    @pl.when(step == 0)
    def _():
        d_init_ref[...] = d_pre_ref[...] + trans_dot(d_query_ref[...], weight_ref[...])

    @pl.when(step == 1)
    def _():
        d_stream_ref[...] = trans_dot(d_key_ref[...], weight_ref[...])

    @pl.when(step == 2)
    def _():
        gain_row = row_of(small_ref, 0)
        d_stream = d_stream_ref[...] + trans_dot(d_value_ref[...], weight_ref[...])
        d_start, gain_init, bias_init = norm_back(
            d_init_ref[...], init_normed_ref[...], init_inverse_ref[:, :1], gain_row
        )
        d_embed, gain, bias = norm_back(
            d_stream, normed_ref[...], inverse_ref[:, :1], gain_row
        )
        position_ref[...] = d_embed + lax.dot_general(
            slot_ref[...],
            d_start,
            (((0,), (0,)), ((), ())),
            precision=lax.Precision.HIGHEST,
            preferred_element_type=single,
        )
        embed_b = d_embed.astype(bfloat)
        embed_ref[...] = embed_b
        sums_ref[...] = jnp.zeros_like(sums_ref)
        sums_ref[pl.ds(0, 1), :] = (gain_init + gain)[None]
        sums_ref[pl.ds(1, 1), :] = (bias_init + bias)[None]
        sums_ref[pl.ds(2, 1), :] = column_sum(d_query_ref[...])[None]
        sums_ref[pl.ds(3, 1), :] = column_sum(d_value_ref[...])[None]
        sums_ref[pl.ds(4, 1), :] = column_sum(d_pre_ref[...].astype(bfloat))[None]
        masked = jnp.where(hidden_row_ref[:, :1] > 0.0, embed_b.astype(single), 0.0)
        sums_ref[pl.ds(5, 1), :] = jnp.sum(masked, axis=0)[None]


def project_backward(
    d_pre, d_query, d_key, d_value, slot_hot, hidden_rows, small_full,
    normed, inverse, init_normed, init_inverse, weights, ahead,
):
    length, width = normed.shape
    slots = d_pre.shape[0]
    arrays = (
        d_pre, d_query, d_key, d_value, slot_hot, hidden_rows, small_full,
        normed, inverse, init_normed, init_inverse,
    )
    return kernel_call(
        project_back_kernel,
        "projection_backward",
        3,
        [whole(array) for array in arrays]
        + [(weights, (width, width), lambda step: (0, step)), (ahead, "any", None)],
        [
            ((length, width), bfloat, None, None),
            ((length, width), single, None, None),
            ((8, width), single, None, None),
        ],
        (5 * length * width * width, 6 * width * width, 0),
        [pltpu.VMEM((length, width), single), pltpu.VMEM((slots, width), single)],
    )


def adam_direction(weight_arr, new_first, new_second):
    first_scale, second_scale = 1.0 / (1.0 - beta_first**STEP), 1.0 / (1.0 - beta_second**STEP)
    scaled = new_second * second_scale
    return (new_first * first_scale) / (
        scaled * lax.rsqrt(scaled) + adam_eps
    ) + weight_decay * weight_arr


def adam_moments(weight_arr, first_mom, second_mom, gradient, factor):
    clipped = gradient * factor
    new_first = beta_first * first_mom + (1.0 - beta_first) * clipped
    new_second = beta_second * second_mom + (1.0 - beta_second) * clipped * clipped
    return (new_first, new_second, adam_direction(weight_arr, new_first, new_second))


def row_block(count, most=240):
    return most if count % most == 0 else count


def lookup_kernel(pieces, *refs):
    step = pl.program_id(0)
    starts, count = pieces
    runs = len(starts)
    head_refs, refs = refs[: runs * count], refs[runs * count :]
    asked_ref, given_ref, side_ref, grad_ref, square_ref = refs
    rows, width = grad_ref.shape
    base = step * rows
    row_hot = asked_ref[...] == base + lax.broadcasted_iota(
        jnp.int32, (rows, asked_ref.shape[1]), 0
    )
    grad = plain_dot(row_hot.astype(bfloat), given_ref[...])
    for part in range(count):
        head = head_refs[part][...].astype(single)
        for run in range(1, runs):
            later = head_refs[run * count + part][...].astype(single)
            head = jnp.where(step >= starts[run], later, head)
        grad += head
    grad_ref[...] = grad
    place = base + lax.broadcasted_iota(jnp.int32, (rows, width), 0)
    own = (place >= side_ref[0]) & (place < side_ref[1])

    @pl.when(step == 0)
    def _():
        square_ref[...] = jnp.zeros_like(square_ref)

    square_ref[...] += jnp.sum(jnp.where(own, grad * grad, 0.0), axis=0, keepdims=True)


def lookup_grad(heads, count, asked_rows, given, sides):
    width = heads[0].shape[1]
    vrows = sum(head.shape[0] for head in heads) // count
    rows = vrows // 4
    steps = [head.shape[0] // count // rows for head in heads]
    starts = [sum(steps[:run]) for run in range(len(heads))]
    whole_spec = lambda array: pl.BlockSpec(array.shape, lambda step: (0, 0))
    return pl.pallas_call(
        lambda *refs: lookup_kernel((starts, count), *refs),
        grid=(4,),
        in_specs=[
            pl.BlockSpec(
                (rows, width),
                lambda step, run=run, part=part: (
                    part * steps[run] + jnp.clip(step - starts[run], 0, steps[run] - 1),
                    0,
                ),
            )
            for run in range(len(heads))
            for part in range(count)
        ]
        + [
            whole_spec(asked_rows),
            whole_spec(given),
            pl.BlockSpec(memory_space=pltpu.SMEM),
        ],
        out_specs=[
            pl.BlockSpec((rows, width), lambda step: (step, 0)),
            pl.BlockSpec((1, width), lambda step: (0, 0)),
        ],
        out_shape=[
            jax.ShapeDtypeStruct((vrows, width), single),
            jax.ShapeDtypeStruct((1, width), single),
        ],
        cost_estimate=pl.CostEstimate(flops=0, bytes_accessed=0, transcendentals=0),
        name="table_gradient",
    )(*[head for head in heads for _ in range(count)], asked_rows, given, sides)


def full_sum(values):
    return jnp.sum(jnp.sum(values, axis=1, keepdims=True), axis=0, keepdims=True)


def pair_row(weight_sum, dir_sum):
    lane = lax.broadcasted_iota(jnp.int32, (1, 128), 1)
    return jnp.where(lane == 0, weight_sum, dir_sum)


def norms_kernel(offset_ref, *refs):
    total_ref, table_refs, layer_refs, position_refs, small_refs = (
        refs[0], refs[1:5], refs[5:9], refs[9:13], refs[13:17],
    )
    norms_ref, layer_out, position_out, small_out = refs[17], refs[18:21], refs[21:24], refs[24:27]
    sums_ref = refs[27]
    step = pl.program_id(0)
    total_square = jnp.sum(total_ref[...], axis=0, keepdims=True)[:, :1]
    factor = jnp.minimum(1.0, clip_norm / jnp.sqrt(total_square))

    @pl.when(step == 0)
    def _():
        sums_ref[...] = jnp.zeros_like(sums_ref)
        norms_ref[...] = jnp.zeros_like(norms_ref)
        for row, group_refs, outs in ((4, position_refs, position_out), (5, small_refs, small_out)):
            weight_arr = group_refs[0][...]
            first, second, direction = adam_moments(
                weight_arr, group_refs[1][...], group_refs[2][...], group_refs[3][...], factor
            )
            for ref, value in zip(outs, (first, second, direction)):
                ref[...] = value
            norms_ref[pl.ds(row, 1), :] = pair_row(
                full_sum(weight_arr * weight_arr), full_sum(direction * direction)
            )

    @pl.when(step < 3)
    def _():
        weight_arr, first_mom, second_mom, gradient = (ref[0] for ref in layer_refs)
        first, second, direction = adam_moments(
            weight_arr, first_mom, second_mom, gradient, factor
        )
        for ref, value in zip(layer_out, (first, second, direction)):
            ref[0] = value
        norms_ref[pl.ds(1 + step, 1), :] = pair_row(
            full_sum(weight_arr * weight_arr), full_sum(direction * direction)
        )

    weight_arr = table_refs[0][...]
    _, _, direction = adam_moments(
        weight_arr, table_refs[1][...], table_refs[2][...], table_refs[3][...], factor
    )
    sums_ref[pl.ds(0, 1), :] += jnp.sum(weight_arr * weight_arr, axis=0, keepdims=True)
    sums_ref[pl.ds(1, 1), :] += jnp.sum(direction * direction, axis=0, keepdims=True)

    @pl.when(step == pl.num_programs(0) - 1)
    def _():
        norms_ref[pl.ds(0, 1), :] = pair_row(
            full_sum(sums_ref[pl.ds(0, 1), :]), full_sum(sums_ref[pl.ds(1, 1), :])
        )


def update_norms(totals, table, layer, position, small, split, dp_index):
    vrows, width = table[0].shape
    rows = row_block(split, 240)
    if split // rows < 3:
        rows = split // 3
    one_part = pl.BlockSpec(
        (1,) + layer[0].shape[1:], lambda step, offset: (jnp.minimum(step, 2), 0, 0)
    )
    fixed = lambda array: pl.BlockSpec(
        array.shape, lambda step, offset, rank=array.ndim: (0,) * rank
    )
    part = pl.BlockSpec((rows, width), lambda step, offset: (offset[0] + step, 0))
    groups = tuple(layer) + tuple(position) + tuple(small)
    outs = [
        jax.ShapeDtypeStruct(group[0].shape, single)
        for group in (layer, position, small)
        for _ in range(3)
    ]
    norms = jax.ShapeDtypeStruct((8, 128), single)
    return pl.pallas_call(
        norms_kernel,
        grid_spec=pltpu.PrefetchScalarGridSpec(
            num_scalar_prefetch=1,
            grid=(split // rows,),
            in_specs=[fixed(totals)]
            + [part] * 4
            + [one_part] * 4
            + [fixed(array) for array in groups[4:]],
            out_specs=[fixed(norms)] + [one_part] * 3 + [fixed(out) for out in outs[3:]],
            scratch_shapes=[pltpu.VMEM((8, width), single)],
        ),
        out_shape=[norms] + outs,
        cost_estimate=pl.CostEstimate(flops=0, bytes_accessed=0, transcendentals=0),
        name="update_norms",
    )((dp_index * (split // rows)).astype(jnp.int32)[None], totals, *table, *groups)


def final_kernel(
    pairs_ref, totals_ref, weight_ref, first_ref, old_ref, grad_ref,
    layer_ref, layer_dir_ref, position_ref, position_dir_ref, small_ref, small_dir_ref,
    next_ref, second_ref, layer_next_ref, position_next_ref, small_next_ref,
):
    roots = jnp.sqrt(jnp.sum(pairs_ref[...], axis=0, keepdims=True))

    def rate(group):
        return learn_rate * (
            roots[:, 2 * group : 2 * group + 1] / roots[:, 2 * group + 1 : 2 * group + 2]
        )

    total_square = jnp.sum(totals_ref[...], axis=0, keepdims=True)[:, :1]
    factor = jnp.minimum(1.0, clip_norm / jnp.sqrt(total_square))
    weight_arr, clipped = weight_ref[...], grad_ref[...] * factor
    second = beta_second * old_ref[...] + (1.0 - beta_second) * clipped * clipped
    second_ref[...] = second
    direction = adam_direction(weight_arr, first_ref[...], second)
    next_ref[...] = weight_arr - rate(0) * direction

    step = pl.program_id(0)
    for part in range(3):

        @pl.when(step == part)
        def _():
            layer_next_ref[0] = layer_ref[0] - rate(1 + part) * layer_dir_ref[0]

    @pl.when(step == 0)
    def _():
        position_next_ref[...] = position_ref[...] - rate(4) * position_dir_ref[...]
        small_next_ref[...] = small_ref[...] - rate(5) * small_dir_ref[...]


def final_update(pairs, totals, table, groups):
    vrows, width = table[0].shape
    rows = row_block(vrows, 480)
    if vrows // rows < 3:
        rows = row_block(vrows, 240)
    fixed = lambda array: pl.BlockSpec(array.shape, lambda step, rank=array.ndim: (0,) * rank)
    block = pl.BlockSpec((rows, width), lambda step: (step, 0))
    one_part = pl.BlockSpec((1,) + groups[0].shape[1:], lambda step: (jnp.minimum(step, 2), 0, 0))
    outs = [jax.ShapeDtypeStruct(array.shape, single) for array in groups[::2]]
    return pl.pallas_call(
        final_kernel,
        grid=(vrows // rows,),
        in_specs=[fixed(pairs), fixed(totals)]
        + [block] * 4
        + [one_part] * 2
        + [fixed(array) for array in groups[2:]],
        out_specs=[block, block, one_part] + [fixed(out) for out in outs[1:]],
        out_shape=[jax.ShapeDtypeStruct((vrows, width), single)] * 2 + outs,
        cost_estimate=pl.CostEstimate(flops=0, bytes_accessed=0, transcendentals=0),
        name="final_update",
    )(pairs, totals, *table, *groups)


class Exchange:
    def __init__(self):
        self.last = None

    def __call__(self, values, axes):
        if self.last is not None:
            values, _ = lax.optimization_barrier((values, self.last))
        self.last = lax.all_to_all(values, axes, 0, 0, tiled=True)
        return self.last

    def copies(self, values, axes, count):
        return self(jnp.broadcast_to(values[None], (count,) + values.shape), axes)

    def columns(self, values, axes, count):
        rows, width = values.shape
        blocks = values.reshape(rows, count, width // count).transpose(1, 0, 2)
        return self(blocks, axes).reshape(count * rows, -1)

    def rows(self, values, count):
        return self(values.reshape(count, values.shape[0] // count, values.shape[1]), ALL)


def side_by_side(blocks):
    return blocks.transpose(1, 0, 2).reshape(blocks.shape[1], -1)


def after(values, *waits):
    for wait in waits:
        values = values + (wait[(0,) * wait.ndim] > 3.395e38).astype(values.dtype)
    return values


def masked_total(mask, values):
    return jnp.sum(jnp.where(mask, values, 0), axis=-1)


def slot_layout(pred_row, order_row, token_row):
    length = pred_row.shape[0]
    index = jnp.arange(length)
    before = index[None, :] <= index[:, None]
    seen = masked_total(before, pred_row[None, :])
    masked = jnp.sum(pred_row)
    place = jnp.where(pred_row == 1, seen - 1, masked + index - seen)
    slot_hot = place[None, :] == jnp.arange(CAP)[:, None]
    rank_row = masked_total(order_row[None, :] == index[:, None], index[None, :])
    slot_rank = masked_total(slot_hot, rank_row[None, :])
    slot_target = masked_total(slot_hot, token_row[None, :])
    slot_pos = masked_total(slot_hot, index[None, :])
    allowed = rank_row[None, :] <= slot_rank[:, None]
    return slot_hot, slot_pos, slot_target, allowed, masked


def bucket_layout(content, vrows):
    index = jnp.arange(content.shape[0])
    same = content[None, :] == content[:, None]
    first = jnp.min(jnp.where(same, index[None, :], content.shape[0]), axis=1)
    is_first = first == index
    owner = content // vrows
    ahead = (owner[None, :] == owner[:, None]) & is_first[None, :] & (index[None, :] < first[:, None])
    return owner, jnp.sum(ahead.astype(jnp.int32), axis=1)


def bucket_round(content, owner, place, turn, owners, vrows):
    usable = BUCKET - 1
    local = place - turn * usable
    taken = (local >= 0) & (local < usable)
    flat = jnp.where(taken, owner * BUCKET + local, -1)
    hot = flat[None, :] == jnp.arange(owners * BUCKET)[:, None]
    wanted = jnp.max(jnp.where(hot, (content - owner * vrows)[None, :], -1), axis=1)
    return hot.astype(bfloat), wanted.reshape(owners, BUCKET)


def on_device(
    token_ids,
    pred_mask,
    fact_order,
    corpus,
    embed_table,
    table_moment,
    table_square,
    layer_weights,
    layer_moment,
    layer_square,
    position_table,
    position_moment,
    position_square,
    small_params,
    small_moment,
    small_square,
):
    exchange = Exchange()
    dp_devs = lax.axis_size("dp")
    owners = lax.axis_size(VOC)
    devices = dp_devs * owners
    vrows, width = embed_table.shape
    length = token_ids.shape[1]
    feed = layer_weights.shape[2]
    shared = jnp.concatenate([position_table, small_params]).T
    shared_rows = shared.shape[1]
    shared = jnp.pad(shared, ((0, 0), (0, -shared_rows % 128)))
    shard = jnp.concatenate([layer_weights[0], layer_weights[1], layer_weights[2], shared], axis=1)
    shard = lax.all_gather(shard.astype(bfloat), ALL, axis=0, tiled=True)
    table_b = embed_table.astype(bfloat)
    token_row = token_ids[0]
    pred_row = pred_mask[0]
    first_row = lax.axis_index(VOC) * vrows
    content = jnp.where(pred_row == 1, MASK_ID, token_row)
    slot_hot, slot_pos, slot_target, allowed, masked = slot_layout(pred_row, fact_order[0], token_row)
    owner, place = bucket_layout(content, vrows)
    hot, wanted = bucket_round(content, owner, place, 0, owners, vrows)
    note = jnp.concatenate(
        [slot_target, slot_pos, jnp.stack([masked, corpus[0], jnp.max(place)])]
    )
    packet = jnp.concatenate(
        [wanted, jnp.broadcast_to(note[None], (owners, note.shape[0]))], axis=1
    )
    packet = jnp.pad(packet, ((0, 0), (0, 256 - packet.shape[1])))
    packet = jnp.broadcast_to(packet[None], (dp_devs,) + packet.shape)
    packet = exchange(packet.reshape(devices, packet.shape[-1]), ALL)
    asked = packet[:, :BUCKET]
    tail = BUCKET + 2 * CAP
    counts_all = packet[:, tail]
    corpus_all = packet[:, tail + 1]
    rounds = jnp.max(packet[:, tail + 2]) // (BUCKET - 1) + 1
    group = lax.axis_index("dp") * owners
    outer = lax.axis_size("hi")

    def group_order(values):
        return values.reshape(outer, 2, 2, CAP).transpose(2, 1, 0, 3).reshape(-1)

    group_asked = lax.dynamic_slice_in_dim(asked, group, owners, 0)
    group_target = group_order(
        lax.dynamic_slice_in_dim(packet[:, BUCKET : BUCKET + CAP], group, owners, 0)
    )
    corpus_hot = corpus_all[:, None] == jnp.arange(NCORP)[None, :]
    corpus_counts = jnp.sum(jnp.where(corpus_hot, counts_all[:, None], 0), axis=0)
    seq_count = masked_total(corpus_hot, corpus_counts[None, :])
    seq_weight = 1.0 / (NCORP * seq_count.astype(single))
    slot_weight = jnp.where(
        jnp.arange(CAP)[None, :] < counts_all[:, None], seq_weight[:, None], 0.0
    )
    group_weight = group_order(lax.dynamic_slice_in_dim(slot_weight, group, owners, 0))

    def serve(asked_rows):
        served = jnp.take(table_b, jnp.maximum(asked_rows, 0).reshape(-1), axis=0)
        return served.reshape(owners, BUCKET, width)

    arrived = exchange(serve(group_asked), VOC)
    embed_rows = rows_dot(hot, arrived.reshape(-1, width))

    def more_rows(state):
        turn, rows = state
        hot_t, wanted_t = bucket_round(content, owner, place, turn, owners, vrows)
        asked_t = lax.all_to_all(wanted_t, VOC, 0, 0, tiled=True)
        arrived_t = lax.all_to_all(serve(asked_t), VOC, 0, 0, tiled=True)
        return turn + 1, rows + rows_dot(hot_t, arrived_t.reshape(-1, width))

    _, embed_rows = lax.while_loop(
        lambda state: state[0] < rounds, more_rows, (jnp.ones((), rounds.dtype), embed_rows)
    )
    few = devices <= 32
    near = 4
    allowed = allowed.astype(single)
    slot_hot = slot_hot.astype(single)
    (
        key_rows,
        value_rows,
        query_rows,
        mixed_b,
        middle,
        mid_normed,
        mid_inverse,
        stream_b,
        stream_normed,
        stream_inverse,
        query_init,
        init_normed,
        init_inverse,
        position_full,
        small_full,
    ) = attend_forward(embed_rows, slot_hot, allowed, shard, length, small_params.shape[0])
    middle_b, hidden, active_b, output_b, end_normed, end_inverse = feed_forward(
        middle, small_full, shard
    )
    if few:
        kept_rows = jnp.concatenate([mixed_b, middle_b], axis=1)
        kept_all = lax.all_gather(kept_rows, ALL, axis=0, tiled=True)
        stream_all = lax.all_gather(stream_b, NEAR, axis=0, tiled=True)
    group_rows = exchange.copies(output_b, "hi", outer).reshape(-1, width)
    group_rows = exchange.copies(group_rows, "mid", 2).reshape(-1, width)
    group_rows = exchange.copies(group_rows, "core", 2).reshape(-1, width)
    logits = trans_dot(group_rows, table_b)
    local_target = group_target - first_row
    target_hit = jnp.arange(vrows)[None, :] == local_target[:, None]
    row_top = jnp.max(logits, axis=1)
    row_total = jnp.sum(jnp.exp(logits - row_top[:, None]), axis=1)
    row_target = jnp.sum(jnp.where(target_hit, logits, 0.0), axis=1)
    stats = exchange.copies(jnp.stack([row_top, row_total]), VOC, owners)
    top_all = jnp.max(stats[:, 0], axis=0)
    total_all = jnp.sum(stats[:, 1] * jnp.exp(stats[:, 0] - top_all[None]), axis=0)
    log_total = top_all + jnp.log(total_all)
    own_place = lax.axis_index(("core", "mid", "hi"))
    own_total = lax.dynamic_slice_in_dim(log_total * group_weight, own_place * CAP, CAP, 0)
    loss_part = jnp.sum(own_total) - jnp.sum(row_target * group_weight)
    d_logits = (
        group_weight[:, None] * (jnp.exp(logits - log_total[:, None]) - target_hit.astype(single))
    ).astype(bfloat)
    def swapped(axis, kind, part):
        side = lax.axis_index(axis)
        theirs = lax.ppermute(part(1 - side).astype(kind), axis, [(0, 1), (1, 0)])
        return part(side) + theirs.astype(single)

    half = owners * CAP // 2

    def rows_half(side):
        return plain_dot(lax.dynamic_slice_in_dim(d_logits, side * half, half, 0), table_b)

    d_output = swapped("core", single, rows_half)
    quarter = half // 2
    d_half = d_output
    d_output = swapped(
        "mid", bfloat, lambda side: lax.dynamic_slice_in_dim(d_half, side * quarter, quarter, 0)
    )
    grad_head = rows_dot(d_logits, group_rows)
    grad_head = after(grad_head, d_half, *((stream_all,) if few else ()))
    heads = [
        lax.all_gather(half_b, "dp", axis=0, tiled=True)
        for half_b in jnp.split(grad_head.astype(bfloat), [vrows * 3 // 4])
    ]
    d_output = exchange(d_output.astype(bfloat).reshape(outer, CAP, width), "hi")
    if few:
        d_output, kept_all = lax.optimization_barrier((d_output, kept_all))
    d_branch, d_hidden, d_pre, d_attend, sums_feed = feed_backward(
        d_output,
        end_normed,
        end_inverse,
        hidden,
        small_full,
        mid_normed,
        mid_inverse,
        shard,
    )
    if few:
        wide = feed // devices
        both = jnp.concatenate(
            [
                d_hidden.reshape(CAP, devices, -1),
                d_attend.reshape(CAP, devices, -1),
            ],
            axis=2,
        ).reshape(CAP, -1)
        both = exchange.columns(both, ALL, devices)
        branch_all = lax.all_gather(d_branch, ALL, axis=0, tiled=True)
    d_query, d_key, d_value = attend_backward(
        d_attend, key_rows, value_rows, query_rows, allowed, shard
    )
    if few:
        piece = width // near
        pairs = jnp.concatenate(
            [d_key.reshape(length, near, piece), d_value.reshape(length, near, piece)], axis=2
        ).transpose(1, 0, 2)
        asks = d_query.reshape(CAP, near, piece).transpose(1, 0, 2)
        asks = jnp.concatenate([asks[:, : CAP // 2], asks[:, CAP // 2 :]], axis=2)
        pairs = exchange(jnp.concatenate([pairs, asks], axis=1), NEAR)
    hidden_rows = spread((content == MASK_ID).astype(single)[:, None])
    embed_back, grad_position, sums_back = project_backward(
        d_pre,
        d_query,
        d_key,
        d_value,
        slot_hot,
        hidden_rows,
        small_full,
        stream_normed,
        stream_inverse,
        init_normed,
        init_inverse,
        shard,
        heads[0],
    )
    grad_small = jnp.concatenate([sums_back[:5], sums_feed[:9]])
    mask_sum = sums_back[5]
    mask_left = mask_sum - lax.reduce_precision(mask_sum, 8, 7)
    mask_owner = MASK_ID // vrows
    is_left = (jnp.arange(BUCKET) == BUCKET - 1)[None, :] & (
        jnp.arange(owners) == mask_owner
    )[:, None]

    def plain_exchange(values, axes):
        return lax.all_to_all(values, axes, 0, 0, tiled=True)

    def give(hot_rows, extra, send):
        rows = plain_dot(hot_rows, embed_back).reshape(owners, BUCKET, width)
        rows = jnp.where(is_left[:, :, None] & extra, mask_left[None, None, :], rows)
        return send(rows.astype(bfloat), VOC).reshape(-1, width)

    def of_both(rows):
        if dp_devs == 2:
            return jnp.concatenate([rows, lax.ppermute(rows, "dp", [(0, 1), (1, 0)])])
        return lax.all_gather(rows, "dp", axis=0, tiled=True)

    def both_groups(asked_rows):
        if dp_devs == 2:
            return jnp.roll(asked_rows, -group, axis=0)
        return asked_rows

    split = vrows // dp_devs
    sides = lax.axis_index("dp") * split + jnp.array([0, split])

    def into_rows(heads, parts, asked_rows, given, sides):
        return lookup_grad(heads, parts, both_groups(asked_rows).reshape(1, -1), given, sides)

    last = (jnp.arange(BUCKET) == BUCKET - 1)[None, :]
    left_row = jnp.where(lax.axis_index(VOC) == mask_owner, MASK_ID - first_row, -1)
    given = of_both(give(hot, True, exchange))

    if few:
        near_pos = packet[:, BUCKET + CAP : tail].reshape(dp_devs * outer, near * CAP)
        near_pos = lax.dynamic_index_in_dim(
            near_pos, lax.axis_index(("dp", "hi")), 0, False
        )
        init_rows = norm_forward(position_full, small_full[0], small_full[1])[0].astype(bfloat)
        init_hot = near_pos[:, None] == jnp.arange(length)[None, :]
        init_all = plain_dot(init_hot.astype(bfloat), init_rows).astype(bfloat)
        asks = pairs[:, length:]
        asks = jnp.concatenate([asks[..., :piece], asks[..., piece:]], axis=1)
        grad_pair = rows_dot(stream_all, pairs[:, :length].reshape(near * length, -1))
        grad_ask = rows_dot(init_all, asks.reshape(near * CAP, piece))
        share = width // devices
        active_mine = exchange.columns(active_b, ALL, devices)
        grad_up = rows_dot(kept_all[:, width:], both[:, :wide])
        grad_out = rows_dot(kept_all[:, :width], both[:, wide:])
        grad_down = rows_dot(branch_all, active_mine)
        shared_grad = jnp.concatenate([grad_position, grad_small]).T
        results = jnp.concatenate(
            [grad_pair, grad_ask, grad_up, grad_down, grad_out, shared_grad], axis=1
        )
        results = after(results.astype(bfloat), given[-1:])
        results = exchange.rows(results, devices).astype(single)
        sides = after(sides, results)
        pieces = 3 * piece
        attn = jnp.sum(
            results[..., :pieces].reshape(dp_devs * outer, near, share, pieces), axis=0
        )
        shared_grad = jnp.sum(results[..., -shared_rows:], axis=0)
        single_parts = results[..., pieces:-shared_rows]
        part_square = (
            jnp.sum(attn * attn)
            + jnp.sum(single_parts * single_parts)
            + jnp.sum(shared_grad * shared_grad)
        )
        shared_grad = shared_grad.T
        position_grad, small_grad = shared_grad[:length], shared_grad[length:]
        grad_key, grad_value, grad_query = (
            side_by_side(attn[..., part * piece : (part + 1) * piece]) for part in range(3)
        )
        grad_up, grad_down, grad_out = (
            side_by_side(single_parts[..., low:high])
            for low, high in ((0, wide), (wide, 2 * wide), (2 * wide, None))
        )
        layer_grad = jnp.stack(
            [
                jnp.concatenate([grad_query, grad_key, grad_value, grad_out], axis=1),
                grad_up,
                grad_down,
            ]
        )
    else:
        whole = (
            jnp.concatenate(
                [
                    rows_dot(query_init.astype(bfloat), d_query),
                    rows_dot(stream_b, d_key),
                    rows_dot(stream_b, d_value),
                    rows_dot(mixed_b, d_attend),
                ],
                axis=1,
            ),
            rows_dot(middle_b, d_hidden),
            rows_dot(d_branch, active_b),
        )
        layer_grad = jnp.stack(
            [lax.psum_scatter(part, ALL, scatter_dimension=0, tiled=True) for part in whole]
        )
        shared_grad = jnp.concatenate([grad_position, grad_small]).T
        shared_grad = lax.psum_scatter(shared_grad, ALL, scatter_dimension=0, tiled=True).T
        position_grad, small_grad = shared_grad[:length], shared_grad[length:]
        part_square = jnp.sum(layer_grad * layer_grad) + jnp.sum(shared_grad * shared_grad)
    table_grad, table_square_sum = into_rows(
        heads, dp_devs, jnp.where(last, left_row, asked), given, sides
    )

    def more_grads(state):
        turn, grads, _ = state
        hot_t, wanted_t = bucket_round(content, owner, place, turn, owners, vrows)
        wanted_t = jnp.broadcast_to(wanted_t[None], (dp_devs,) + wanted_t.shape)
        asked_t = lax.all_to_all(
            wanted_t.reshape(devices, BUCKET), ALL, 0, 0, tiled=True
        )
        given_t = of_both(give(hot_t, False, plain_exchange))
        return (turn + 1,) + tuple(into_rows([grads], 1, asked_t, given_t, sides))

    _, table_grad, table_square_sum = lax.while_loop(
        lambda state: state[0] < rounds,
        more_grads,
        (jnp.ones((), rounds.dtype), table_grad, table_square_sum),
    )
    square_part = jnp.sum(table_square_sum) + part_square
    totals = exchange.copies(jnp.stack([square_part, loss_part]), ALL, devices)
    total_square, loss_value = jnp.sum(totals, axis=0)
    grad_norm = jnp.sqrt(total_square)
    factor = jnp.minimum(1.0, clip_norm / grad_norm)
    (
        norms,
        layer_first,
        layer_second,
        layer_dir,
        position_first,
        position_second,
        position_dir,
        small_first,
        small_second,
        small_dir,
    ) = update_norms(
        totals,
        (embed_table, table_moment, table_square, table_grad),
        (layer_weights, layer_moment, layer_square, layer_grad),
        (position_table, position_moment, position_square, position_grad),
        (small_params, small_moment, small_square, small_grad),
        split,
        lax.axis_index("dp"),
    )
    factor_late, norms = lax.optimization_barrier((factor, norms))
    pairs = exchange.copies(norms[:6, :2].reshape(-1), ALL, devices)
    table_first = beta_first * table_moment + (1.0 - beta_first) * (table_grad * factor_late)
    trust_norms = jnp.sqrt(jnp.sum(pairs, axis=0)).reshape(6, 2)
    table_next, table_second, layer_next, position_next, small_next = final_update(
        pairs,
        totals,
        (embed_table, table_first, table_square, table_grad),
        (
            layer_weights,
            layer_dir,
            position_table,
            position_dir,
            small_params,
            small_dir,
        ),
    )
    return (
        loss_value,
        grad_norm,
        table_next,
        table_first,
        table_second,
        layer_next,
        layer_first,
        layer_second,
        position_next,
        position_first,
        position_second,
        small_next,
        small_first,
        small_second,
        trust_norms,
    )


def solution(mesh):
    dp_devs, owners = mesh.devices.shape
    fine = Mesh(mesh.devices.reshape(dp_devs, owners // 4, 2, 2), ALL)
    rows, inner = P(ALL, None), P(None, ALL)
    table, layer = P(VOC, None), P(None, ALL, None)
    return jax.shard_map(
        on_device,
        mesh=fine,
        in_specs=(rows,) * 3 + (P(ALL),) + (table,) * 3 + (layer,) * 3 + (inner,) * 6,
        out_specs=(P(), P()) + (table,) * 3 + (layer,) * 3 + (inner,) * 6 + (P(),),
        check_vma=False,
    )
```

```python
import jax
import jax.numpy as jnp
from jax import lax
from jax.experimental import pallas as pl
from jax.experimental.pallas import tpu as pltpu
from jax.sharding import Mesh
from jax.sharding import PartitionSpec as P

HEADS = 12
HD = 64
MASK_ID = 103
NCORP = 4
STEP = 5
CAP = 64


clip_norm = 0.1
learn_rate = 0.3
beta_first = 0.9
beta_second = 0.999
adam_eps = 1e-06
weight_decay = 0.01
norm_eps = 1e-05
masked_score = -1e30
BUCKET = 32
ALL = ("dp", "hi", "mid", "core")
VOC = ("hi", "mid", "core")
NEAR = ("mid", "core")
bfloat = jnp.bfloat16
single = jnp.float32


def plain_dot(left_op, right_op):
    return jnp.dot(left_op, right_op, preferred_element_type=single)


def trans_dot(left_op, right_op):
    return lax.dot_general(
        left_op, right_op, (((1,), (1,)), ((), ())), preferred_element_type=single
    )


def rows_dot(left_op, right_op):
    return lax.dot_general(
        left_op, right_op, (((0,), (0,)), ((), ())), preferred_element_type=single
    )


def column_sum(values):
    return jnp.sum(values.astype(single), axis=0)


def norm_forward(values, gain_row, bias_row):
    center = values - jnp.mean(values, axis=-1, keepdims=True)
    inverse = lax.rsqrt(jnp.mean(center * center, axis=-1, keepdims=True) + norm_eps)
    normed = center * inverse
    return (normed * gain_row + bias_row, (normed, inverse))


def norm_backward(upstream, kept_norm, gain_row):
    normed, inverse = kept_norm
    scaled = upstream * gain_row
    inner = (
        scaled
        - jnp.mean(scaled, axis=-1, keepdims=True)
        - normed * jnp.mean(scaled * normed, axis=-1, keepdims=True)
    )
    return (inner * inverse, jnp.sum(upstream * normed, axis=0), jnp.sum(upstream, axis=0))


def pair_masks(rows):
    lane = lax.broadcasted_iota(jnp.int32, (rows, 2 * HD), 1)
    return lane < HD, lane >= HD


def head_probs(query_pair, key_pair, head_lanes, blocked):
    scores = trans_dot(jnp.where(head_lanes, query_pair, jnp.zeros_like(query_pair)), key_pair)
    scores = jnp.where(blocked, masked_score, scores * HD ** (-0.5))
    row_top = jnp.max(scores, axis=-1, keepdims=True)
    powers = jnp.exp(scores - row_top)
    return powers / jnp.sum(powers, axis=-1, keepdims=True)


def spread(column, lanes=128):
    return jnp.broadcast_to(column, (column.shape[0], lanes))


def row_of(ref, row):
    return ref[pl.ds(row, 1), :]


def attend_kernel(
    embed_ref, slot_ref, allowed_ref, shared_ref, weight_ref,
    key_ref, value_ref, query_ref, mixed_ref, middle_ref, normed_ref, inverse_ref,
    stream_ref, stream_normed_ref, stream_inverse_ref,
    init_ref, init_normed_ref, init_inverse_ref, position_ref, small_ref,
):
    step = pl.program_id(0)
    length = position_ref.shape[0]

    @pl.when(step == 0)
    def _():
        shared = shared_ref[...].astype(single).T
        position_ref[...] = shared[:length]
        small_ref[...] = shared[length : length + small_ref.shape[0]]
        gain, bias = row_of(small_ref, 0), row_of(small_ref, 1)
        stream, (normed, inverse) = norm_forward(embed_ref[...] + position_ref[...], gain, bias)
        stream_ref[...] = stream.astype(bfloat)
        stream_normed_ref[...] = normed
        stream_inverse_ref[...] = spread(inverse)
        chosen = plain_dot(slot_ref[...].astype(bfloat), position_ref[...].astype(bfloat))
        init, (normed, inverse) = norm_forward(chosen, gain, bias)
        init_ref[...] = init
        init_normed_ref[...] = normed
        init_inverse_ref[...] = spread(inverse)
        key_ref[...] = plain_dot(stream_ref[...], weight_ref[...]).astype(bfloat)

    @pl.when(step == 1)
    def _():
        value_ref[...] = (
            plain_dot(stream_ref[...], weight_ref[...]) + row_of(small_ref, 3)
        ).astype(bfloat)

    @pl.when(step == 2)
    def _():
        query_ref[...] = (
            plain_dot(init_ref[...].astype(bfloat), weight_ref[...]) + row_of(small_ref, 2)
        ).astype(bfloat)
        blocked = allowed_ref[...] == 0.0
        low, high = pair_masks(query_ref.shape[0])

        def one_pair(pair, carry):
            lanes = pl.ds(pl.multiple_of(pair * 2 * HD, 2 * HD), 2 * HD)
            query_pair, key_pair, value_pair = query_ref[:, lanes], key_ref[:, lanes], value_ref[:, lanes]
            left, right = (
                plain_dot(
                    head_probs(query_pair, key_pair, head_lanes, blocked).astype(bfloat), value_pair
                )
                for head_lanes in (low, high)
            )
            mixed_ref[:, lanes] = jnp.where(low, left, right).astype(bfloat)
            return carry

        lax.fori_loop(0, query_ref.shape[1] // (2 * HD), one_pair, 0)

    @pl.when(step == 3)
    def _():
        attend = plain_dot(mixed_ref[...], weight_ref[...]) + row_of(small_ref, 4)
        middle, (normed, inverse) = norm_forward(
            init_ref[...] + attend, row_of(small_ref, 5), row_of(small_ref, 6)
        )
        middle_ref[...] = middle
        normed_ref[...] = normed
        inverse_ref[...] = spread(inverse)


def kernel_call(body, name, steps, inputs, shapes, cost, scratch=()):
    fixed = lambda rank: lambda step: (0,) * rank

    def spec(shape, block, index):
        if block is None:
            return pl.BlockSpec(shape, fixed(len(shape)))
        if block == "any":
            return pl.BlockSpec(memory_space=pl.ANY)
        return pl.BlockSpec(block, index)

    return pl.pallas_call(
        body,
        grid=(steps,),
        in_specs=[spec(array.shape, block, index) for array, block, index in inputs],
        out_specs=[spec(shape, block, index) for shape, _, block, index in shapes],
        out_shape=[jax.ShapeDtypeStruct(shape, kind) for shape, kind, _, _ in shapes],
        scratch_shapes=list(scratch),
        cost_estimate=pl.CostEstimate(flops=cost[0] // 64, bytes_accessed=cost[1] // 64, transcendentals=0),
        name=name,
    )(*(array for array, _, _ in inputs))


def whole(array):
    return array, None, None


def attend_forward(embed_rows, slot_hot, allowed, weights, length, small_count):
    width = embed_rows.shape[1]
    slots = slot_hot.shape[0]
    out = lambda rows, kind, columns=width: ((rows, columns), kind, None, None)
    shared = weights.shape[1] - 12 * width
    return kernel_call(
        attend_kernel,
        "attention_forward",
        4,
        [
            whole(embed_rows),
            whole(slot_hot),
            whole(allowed),
            (weights, (width, shared), lambda step: (0, 12 * width // shared)),
            (
                weights,
                (width, width),
                lambda step: (0, jnp.where(step == 3, 3, (step + 1) % 3)),
            ),
        ],
        [
            out(length, bfloat), out(length, bfloat), out(slots, bfloat), out(slots, bfloat),
            out(slots, single), out(slots, single), out(slots, single, 128),
            out(length, bfloat), out(length, single), out(length, single, 128),
            out(slots, single), out(slots, single), out(slots, single, 128),
            out(length, single), out(small_count, single),
        ],
        (
            4 * length * width * width + 8 * slots * length * width,
            8 * width * width,
            HEADS * slots * length,
        ),
    )


def erf_half(hidden):
    return 0.5 * (1.0 + lax.erf(hidden * 0.5**0.5))


def feed_kernel(
    middle_ref, small_ref, up_ref, down_ref,
    middle_b_ref, hidden_ref, active_ref, output_ref, normed_ref, inverse_ref, total_ref,
):
    step = pl.program_id(0)

    @pl.when(step == 0)
    def _():
        middle_b_ref[...] = middle_ref[...].astype(bfloat)
        total_ref[...] = middle_ref[...] + row_of(small_ref, 11)

    hidden = plain_dot(middle_b_ref[...], up_ref[...]) + row_of(small_ref, 7 + step)
    hidden_ref[...] = hidden
    active = (hidden * erf_half(hidden)).astype(bfloat)
    active_ref[...] = active
    total_ref[...] += trans_dot(active, down_ref[...])

    @pl.when(step == pl.num_programs(0) - 1)
    def _():
        output, (normed, inverse) = norm_forward(
            total_ref[...], row_of(small_ref, 12), row_of(small_ref, 13)
        )
        output_ref[...] = output.astype(bfloat)
        normed_ref[...] = normed
        inverse_ref[...] = spread(inverse)


def feed_forward(middle, small_full, weights):
    slots, width = middle.shape
    wide = lambda kind: ((slots, 4 * width), kind, (slots, width), lambda step: (0, step))
    out = lambda kind, columns=width: ((slots, columns), kind, None, None)
    return kernel_call(
        feed_kernel,
        "feed_forward",
        4,
        [
            whole(middle),
            whole(small_full),
            (weights, (width, width), lambda step: (0, 4 + step)),
            (weights, (width, width), lambda step: (0, 8 + step)),
        ],
        [
            out(bfloat), wide(single), wide(bfloat), out(bfloat), out(single), out(single, 128),
        ],
        (16 * slots * width * width, 16 * width * width, 4 * slots * width),
        [pltpu.VMEM((slots, width), single)],
    )


def norm_back(upstream, normed, inverse, gain_row):
    return norm_backward(upstream, (normed, inverse), gain_row)


def feed_back_kernel(
    parts_ref, normed_ref, inverse_ref, hidden_ref, small_ref, mid_normed_ref, mid_inverse_ref,
    up_ref, down_ref,
    d_branch_ref, d_hidden_ref, d_pre_ref, d_attend_ref, sums_ref, d_middle_ref,
):
    step = pl.program_id(0)

    @pl.when(step == 0)
    def _():
        sums_ref[...] = jnp.zeros_like(sums_ref)
        d_sum, gain, bias = norm_back(
            jnp.sum(parts_ref[...].astype(single), axis=0), normed_ref[...], inverse_ref[:, :1], row_of(small_ref, 12)
        )
        d_branch = d_sum.astype(bfloat)
        d_branch_ref[...] = d_branch
        d_middle_ref[...] = d_sum
        sums_ref[pl.ds(6, 1), :] = column_sum(d_branch)[None]
        sums_ref[pl.ds(7, 1), :] = gain[None]
        sums_ref[pl.ds(8, 1), :] = bias[None]

    hidden = hidden_ref[...]
    slope = erf_half(hidden) + hidden * jnp.exp(-0.5 * hidden * hidden) * (2.0 * jnp.pi) ** (-0.5)
    d_hidden = (plain_dot(d_branch_ref[...], down_ref[...]) * slope).astype(bfloat)
    d_hidden_ref[...] = d_hidden
    sums_ref[pl.ds(2 + step, 1), :] = column_sum(d_hidden)[None]
    d_middle_ref[...] += trans_dot(d_hidden, up_ref[...])

    @pl.when(step == pl.num_programs(0) - 1)
    def _():
        d_pre, gain, bias = norm_back(
            d_middle_ref[...], mid_normed_ref[...], mid_inverse_ref[:, :1], row_of(small_ref, 5)
        )
        d_pre_ref[...] = d_pre
        d_attend_ref[...] = d_pre.astype(bfloat)
        sums_ref[pl.ds(0, 1), :] = gain[None]
        sums_ref[pl.ds(1, 1), :] = bias[None]


def feed_backward(parts, normed, inverse, hidden, small_full, mid_normed, mid_inverse, weights):
    slots, width = normed.shape
    block = (slots, width), lambda step: (0, step)
    out = lambda kind, rows=slots: ((rows, width), kind, None, None)
    return kernel_call(
        feed_back_kernel,
        "feed_backward",
        4,
        [
            whole(parts),
            whole(normed),
            whole(inverse),
            (hidden,) + block,
            whole(small_full),
            whole(mid_normed),
            whole(mid_inverse),
            (weights, (width, width), lambda step: (0, 4 + step)),
            (weights, (width, width), lambda step: (0, 8 + step)),
        ],
        [
            out(bfloat), ((slots, 4 * width), bfloat) + block, out(single), out(bfloat),
            out(single, 16),
        ],
        (16 * slots * width * width, 16 * width * width, 8 * slots * width),
        [pltpu.VMEM((slots, width), single)],
    )


def attend_back_kernel(
    d_attend_ref, key_ref, value_ref, query_ref, allowed_ref, weight_ref,
    d_query_ref, d_key_ref, d_value_ref, d_mixed_ref,
):
    d_mixed_ref[...] = trans_dot(d_attend_ref[...], weight_ref[...]).astype(bfloat)
    blocked = allowed_ref[...] == 0.0
    slots, length = blocked.shape
    low, high = pair_masks(slots)
    low_long, _ = pair_masks(length)
    scale = HD ** (-0.5)

    def one_pair(pair, carry):
        lanes = pl.ds(pl.multiple_of(pair * 2 * HD, 2 * HD), 2 * HD)
        query_pair, key_pair, value_pair = query_ref[:, lanes], key_ref[:, lanes], value_ref[:, lanes]
        mixed_pair = d_mixed_ref[:, lanes]
        found = []
        for head_lanes in (low, high):
            probs = head_probs(query_pair, key_pair, head_lanes, blocked)
            d_probs = trans_dot(
                jnp.where(head_lanes, mixed_pair, jnp.zeros_like(mixed_pair)), value_pair
            )
            inner = jnp.sum(probs * d_probs, axis=-1, keepdims=True)
            d_scores = (probs * (d_probs - inner)).astype(bfloat)
            found.append(
                (
                    plain_dot(d_scores, key_pair) * scale,
                    rows_dot(d_scores, query_pair) * scale,
                    rows_dot(probs.astype(bfloat), mixed_pair),
                )
            )
        d_query_ref[:, lanes] = jnp.where(low, found[0][0], found[1][0]).astype(bfloat)
        d_key_ref[:, lanes] = jnp.where(low_long, found[0][1], found[1][1]).astype(bfloat)
        d_value_ref[:, lanes] = jnp.where(low_long, found[0][2], found[1][2]).astype(bfloat)
        return carry

    lax.fori_loop(0, query_ref.shape[1] // (2 * HD), one_pair, 0)


def attend_backward(d_attend, key_rows, value_rows, query_rows, allowed, weights):
    length, width = key_rows.shape
    slots = d_attend.shape[0]
    out = lambda rows: ((rows, width), bfloat, None, None)
    return kernel_call(
        attend_back_kernel,
        "attention_backward",
        1,
        [
            whole(d_attend),
            whole(key_rows),
            whole(value_rows),
            whole(query_rows),
            whole(allowed),
            (weights, (width, width), lambda step: (0, 3)),
        ],
        [out(slots), out(length), out(length)],
        (
            2 * slots * width * width + 20 * slots * length * width,
            2 * width * width,
            HEADS * slots * length,
        ),
        [pltpu.VMEM((slots, width), bfloat)],
    )


def project_back_kernel(
    d_pre_ref, d_query_ref, d_key_ref, d_value_ref, slot_ref, hidden_row_ref, small_ref,
    normed_ref, inverse_ref, init_normed_ref, init_inverse_ref, weight_ref, ahead_ref,
    embed_ref, position_ref, sums_ref, d_stream_ref, d_init_ref,
):
    step = pl.program_id(0)

    @pl.when(step == 0)
    def _():
        d_init_ref[...] = d_pre_ref[...] + trans_dot(d_query_ref[...], weight_ref[...])

    @pl.when(step == 1)
    def _():
        d_stream_ref[...] = trans_dot(d_key_ref[...], weight_ref[...])

    @pl.when(step == 2)
    def _():
        gain_row = row_of(small_ref, 0)
        d_stream = d_stream_ref[...] + trans_dot(d_value_ref[...], weight_ref[...])
        d_start, gain_init, bias_init = norm_back(
            d_init_ref[...], init_normed_ref[...], init_inverse_ref[:, :1], gain_row
        )
        d_embed, gain, bias = norm_back(
            d_stream, normed_ref[...], inverse_ref[:, :1], gain_row
        )
        position_ref[...] = d_embed + lax.dot_general(
            slot_ref[...],
            d_start,
            (((0,), (0,)), ((), ())),
            precision=lax.Precision.HIGHEST,
            preferred_element_type=single,
        )
        embed_b = d_embed.astype(bfloat)
        embed_ref[...] = embed_b
        sums_ref[...] = jnp.zeros_like(sums_ref)
        sums_ref[pl.ds(0, 1), :] = (gain_init + gain)[None]
        sums_ref[pl.ds(1, 1), :] = (bias_init + bias)[None]
        sums_ref[pl.ds(2, 1), :] = column_sum(d_query_ref[...])[None]
        sums_ref[pl.ds(3, 1), :] = column_sum(d_value_ref[...])[None]
        sums_ref[pl.ds(4, 1), :] = column_sum(d_pre_ref[...].astype(bfloat))[None]
        masked = jnp.where(hidden_row_ref[:, :1] > 0.0, embed_b.astype(single), 0.0)
        sums_ref[pl.ds(5, 1), :] = jnp.sum(masked, axis=0)[None]


def project_backward(
    d_pre, d_query, d_key, d_value, slot_hot, hidden_rows, small_full,
    normed, inverse, init_normed, init_inverse, weights, ahead,
):
    length, width = normed.shape
    slots = d_pre.shape[0]
    arrays = (
        d_pre, d_query, d_key, d_value, slot_hot, hidden_rows, small_full,
        normed, inverse, init_normed, init_inverse,
    )
    return kernel_call(
        project_back_kernel,
        "projection_backward",
        3,
        [whole(array) for array in arrays]
        + [(weights, (width, width), lambda step: (0, step)), (ahead, "any", None)],
        [
            ((length, width), bfloat, None, None),
            ((length, width), single, None, None),
            ((8, width), single, None, None),
        ],
        (5 * length * width * width, 6 * width * width, 0),
        [pltpu.VMEM((length, width), single), pltpu.VMEM((slots, width), single)],
    )


def adam_direction(weight_arr, new_first, new_second):
    first_scale, second_scale = 1.0 / (1.0 - beta_first**STEP), 1.0 / (1.0 - beta_second**STEP)
    scaled = new_second * second_scale
    return (new_first * first_scale) / (
        scaled * lax.rsqrt(scaled) + adam_eps
    ) + weight_decay * weight_arr


def adam_moments(weight_arr, first_mom, second_mom, gradient, factor):
    clipped = gradient * factor
    new_first = beta_first * first_mom + (1.0 - beta_first) * clipped
    new_second = beta_second * second_mom + (1.0 - beta_second) * clipped * clipped
    return (new_first, new_second, adam_direction(weight_arr, new_first, new_second))


def row_block(count, most=240):
    return most if count % most == 0 else count


def lookup_kernel(pieces, *refs):
    step = pl.program_id(0)
    starts, count = pieces
    runs = len(starts)
    head_refs, refs = refs[: runs * count], refs[runs * count :]
    asked_ref, given_ref, side_ref, grad_ref, square_ref = refs
    rows, width = grad_ref.shape
    base = step * rows
    row_hot = asked_ref[...] == base + lax.broadcasted_iota(
        jnp.int32, (rows, asked_ref.shape[1]), 0
    )
    grad = plain_dot(row_hot.astype(bfloat), given_ref[...])
    for part in range(count):
        head = head_refs[part][...].astype(single)
        for run in range(1, runs):
            later = head_refs[run * count + part][...].astype(single)
            head = jnp.where(step >= starts[run], later, head)
        grad += head
    grad_ref[...] = grad
    place = base + lax.broadcasted_iota(jnp.int32, (rows, width), 0)
    own = (place >= side_ref[0]) & (place < side_ref[1])

    @pl.when(step == 0)
    def _():
        square_ref[...] = jnp.zeros_like(square_ref)

    square_ref[...] += jnp.sum(jnp.where(own, grad * grad, 0.0), axis=0, keepdims=True)


def lookup_grad(heads, count, asked_rows, given, sides):
    width = heads[0].shape[1]
    vrows = sum(head.shape[0] for head in heads) // count
    rows = vrows // 4
    steps = [head.shape[0] // count // rows for head in heads]
    starts = [sum(steps[:run]) for run in range(len(heads))]
    whole_spec = lambda array: pl.BlockSpec(array.shape, lambda step: (0, 0))
    return pl.pallas_call(
        lambda *refs: lookup_kernel((starts, count), *refs),
        grid=(4,),
        in_specs=[
            pl.BlockSpec(
                (rows, width),
                lambda step, run=run, part=part: (
                    part * steps[run] + jnp.clip(step - starts[run], 0, steps[run] - 1),
                    0,
                ),
            )
            for run in range(len(heads))
            for part in range(count)
        ]
        + [
            whole_spec(asked_rows),
            whole_spec(given),
            pl.BlockSpec(memory_space=pltpu.SMEM),
        ],
        out_specs=[
            pl.BlockSpec((rows, width), lambda step: (step, 0)),
            pl.BlockSpec((1, width), lambda step: (0, 0)),
        ],
        out_shape=[
            jax.ShapeDtypeStruct((vrows, width), single),
            jax.ShapeDtypeStruct((1, width), single),
        ],
        cost_estimate=pl.CostEstimate(flops=0, bytes_accessed=0, transcendentals=0),
        name="table_gradient",
    )(*[head for head in heads for _ in range(count)], asked_rows, given, sides)


def full_sum(values):
    return jnp.sum(jnp.sum(values, axis=1, keepdims=True), axis=0, keepdims=True)


def pair_row(weight_sum, dir_sum):
    lane = lax.broadcasted_iota(jnp.int32, (1, 128), 1)
    return jnp.where(lane == 0, weight_sum, dir_sum)


def norms_kernel(offset_ref, *refs):
    total_ref, table_refs, layer_refs, position_refs, small_refs = (
        refs[0], refs[1:5], refs[5:9], refs[9:13], refs[13:17],
    )
    norms_ref, layer_out, position_out, small_out = refs[17], refs[18:21], refs[21:24], refs[24:27]
    sums_ref = refs[27]
    step = pl.program_id(0)
    total_square = jnp.sum(total_ref[...], axis=0, keepdims=True)[:, :1]
    factor = jnp.minimum(1.0, clip_norm / jnp.sqrt(total_square))

    @pl.when(step == 0)
    def _():
        sums_ref[...] = jnp.zeros_like(sums_ref)
        norms_ref[...] = jnp.zeros_like(norms_ref)
        for row, group_refs, outs in ((4, position_refs, position_out), (5, small_refs, small_out)):
            weight_arr = group_refs[0][...]
            first, second, direction = adam_moments(
                weight_arr, group_refs[1][...], group_refs[2][...], group_refs[3][...], factor
            )
            for ref, value in zip(outs, (first, second, direction)):
                ref[...] = value
            norms_ref[pl.ds(row, 1), :] = pair_row(
                full_sum(weight_arr * weight_arr), full_sum(direction * direction)
            )

    @pl.when(step < 3)
    def _():
        weight_arr, first_mom, second_mom, gradient = (ref[0] for ref in layer_refs)
        first, second, direction = adam_moments(
            weight_arr, first_mom, second_mom, gradient, factor
        )
        for ref, value in zip(layer_out, (first, second, direction)):
            ref[0] = value
        norms_ref[pl.ds(1 + step, 1), :] = pair_row(
            full_sum(weight_arr * weight_arr), full_sum(direction * direction)
        )

    weight_arr = table_refs[0][...]
    _, _, direction = adam_moments(
        weight_arr, table_refs[1][...], table_refs[2][...], table_refs[3][...], factor
    )
    sums_ref[pl.ds(0, 1), :] += jnp.sum(weight_arr * weight_arr, axis=0, keepdims=True)
    sums_ref[pl.ds(1, 1), :] += jnp.sum(direction * direction, axis=0, keepdims=True)

    @pl.when(step == pl.num_programs(0) - 1)
    def _():
        norms_ref[pl.ds(0, 1), :] = pair_row(
            full_sum(sums_ref[pl.ds(0, 1), :]), full_sum(sums_ref[pl.ds(1, 1), :])
        )


def update_norms(totals, table, layer, position, small, split, dp_index):
    vrows, width = table[0].shape
    rows = row_block(split, 240)
    if split // rows < 3:
        rows = split // 3
    one_part = pl.BlockSpec(
        (1,) + layer[0].shape[1:], lambda step, offset: (jnp.minimum(step, 2), 0, 0)
    )
    fixed = lambda array: pl.BlockSpec(
        array.shape, lambda step, offset, rank=array.ndim: (0,) * rank
    )
    part = pl.BlockSpec((rows, width), lambda step, offset: (offset[0] + step, 0))
    groups = tuple(layer) + tuple(position) + tuple(small)
    outs = [
        jax.ShapeDtypeStruct(group[0].shape, single)
        for group in (layer, position, small)
        for _ in range(3)
    ]
    norms = jax.ShapeDtypeStruct((8, 128), single)
    return pl.pallas_call(
        norms_kernel,
        grid_spec=pltpu.PrefetchScalarGridSpec(
            num_scalar_prefetch=1,
            grid=(split // rows,),
            in_specs=[fixed(totals)]
            + [part] * 4
            + [one_part] * 4
            + [fixed(array) for array in groups[4:]],
            out_specs=[fixed(norms)] + [one_part] * 3 + [fixed(out) for out in outs[3:]],
            scratch_shapes=[pltpu.VMEM((8, width), single)],
        ),
        out_shape=[norms] + outs,
        cost_estimate=pl.CostEstimate(flops=0, bytes_accessed=0, transcendentals=0),
        name="update_norms",
    )((dp_index * (split // rows)).astype(jnp.int32)[None], totals, *table, *groups)


def final_kernel(
    pairs_ref, weight_ref, first_ref, second_ref,
    layer_ref, layer_dir_ref, position_ref, position_dir_ref, small_ref, small_dir_ref,
    next_ref, layer_next_ref, position_next_ref, small_next_ref,
):
    roots = jnp.sqrt(jnp.sum(pairs_ref[...], axis=0, keepdims=True))

    def rate(group):
        return learn_rate * (
            roots[:, 2 * group : 2 * group + 1] / roots[:, 2 * group + 1 : 2 * group + 2]
        )

    weight_arr = weight_ref[...]
    direction = adam_direction(weight_arr, first_ref[...], second_ref[...])
    next_ref[...] = weight_arr - rate(0) * direction

    step = pl.program_id(0)
    for part in range(3):

        @pl.when(step == part)
        def _():
            layer_next_ref[0] = layer_ref[0] - rate(1 + part) * layer_dir_ref[0]

    @pl.when(step == 0)
    def _():
        position_next_ref[...] = position_ref[...] - rate(4) * position_dir_ref[...]
        small_next_ref[...] = small_ref[...] - rate(5) * small_dir_ref[...]


def final_update(pairs, table, groups):
    vrows, width = table[0].shape
    rows = row_block(vrows, 480)
    if vrows // rows < 3:
        rows = row_block(vrows, 240)
    fixed = lambda array: pl.BlockSpec(array.shape, lambda step, rank=array.ndim: (0,) * rank)
    block = pl.BlockSpec((rows, width), lambda step: (step, 0))
    one_part = pl.BlockSpec((1,) + groups[0].shape[1:], lambda step: (jnp.minimum(step, 2), 0, 0))
    outs = [jax.ShapeDtypeStruct(array.shape, single) for array in groups[::2]]
    return pl.pallas_call(
        final_kernel,
        grid=(vrows // rows,),
        in_specs=[fixed(pairs)]
        + [block] * 3
        + [one_part] * 2
        + [fixed(array) for array in groups[2:]],
        out_specs=[block, one_part] + [fixed(out) for out in outs[1:]],
        out_shape=[jax.ShapeDtypeStruct((vrows, width), single)] + outs,
        cost_estimate=pl.CostEstimate(flops=0, bytes_accessed=0, transcendentals=0),
        name="final_update",
    )(pairs, *table, *groups)


class Exchange:
    def __init__(self):
        self.last = None

    def __call__(self, values, axes):
        if self.last is not None:
            values, _ = lax.optimization_barrier((values, self.last))
        self.last = lax.all_to_all(values, axes, 0, 0, tiled=True)
        return self.last

    def copies(self, values, axes, count):
        return self(jnp.broadcast_to(values[None], (count,) + values.shape), axes)

    def columns(self, values, axes, count):
        rows, width = values.shape
        blocks = values.reshape(rows, count, width // count).transpose(1, 0, 2)
        return self(blocks, axes).reshape(count * rows, -1)

    def rows(self, values, count):
        return self(values.reshape(count, values.shape[0] // count, values.shape[1]), ALL)


def side_by_side(blocks):
    return blocks.transpose(1, 0, 2).reshape(blocks.shape[1], -1)


def after(values, *waits):
    for wait in waits:
        values = values + (wait[(0,) * wait.ndim] > 3.395e38).astype(values.dtype)
    return values


def masked_total(mask, values):
    return jnp.sum(jnp.where(mask, values, 0), axis=-1)


def slot_layout(pred_row, order_row, token_row):
    length = pred_row.shape[0]
    index = jnp.arange(length)
    before = index[None, :] <= index[:, None]
    seen = masked_total(before, pred_row[None, :])
    masked = jnp.sum(pred_row)
    place = jnp.where(pred_row == 1, seen - 1, masked + index - seen)
    slot_hot = place[None, :] == jnp.arange(CAP)[:, None]
    rank_row = masked_total(order_row[None, :] == index[:, None], index[None, :])
    slot_rank = masked_total(slot_hot, rank_row[None, :])
    slot_target = masked_total(slot_hot, token_row[None, :])
    slot_pos = masked_total(slot_hot, index[None, :])
    allowed = rank_row[None, :] <= slot_rank[:, None]
    return slot_hot, slot_pos, slot_target, allowed, masked


def bucket_layout(content, vrows):
    index = jnp.arange(content.shape[0])
    same = content[None, :] == content[:, None]
    first = jnp.min(jnp.where(same, index[None, :], content.shape[0]), axis=1)
    is_first = first == index
    owner = content // vrows
    ahead = (owner[None, :] == owner[:, None]) & is_first[None, :] & (index[None, :] < first[:, None])
    return owner, jnp.sum(ahead.astype(jnp.int32), axis=1)


def bucket_round(content, owner, place, turn, owners, vrows):
    usable = BUCKET - 1
    local = place - turn * usable
    taken = (local >= 0) & (local < usable)
    flat = jnp.where(taken, owner * BUCKET + local, -1)
    hot = flat[None, :] == jnp.arange(owners * BUCKET)[:, None]
    wanted = jnp.max(jnp.where(hot, (content - owner * vrows)[None, :], -1), axis=1)
    return hot.astype(bfloat), wanted.reshape(owners, BUCKET)


def on_device(
    token_ids,
    pred_mask,
    fact_order,
    corpus,
    embed_table,
    table_moment,
    table_square,
    layer_weights,
    layer_moment,
    layer_square,
    position_table,
    position_moment,
    position_square,
    small_params,
    small_moment,
    small_square,
):
    exchange = Exchange()
    dp_devs = lax.axis_size("dp")
    owners = lax.axis_size(VOC)
    devices = dp_devs * owners
    vrows, width = embed_table.shape
    length = token_ids.shape[1]
    feed = layer_weights.shape[2]
    shared = jnp.concatenate([position_table, small_params]).T
    shared_rows = shared.shape[1]
    shared = jnp.pad(shared, ((0, 0), (0, -shared_rows % 128)))
    shard = jnp.concatenate([layer_weights[0], layer_weights[1], layer_weights[2], shared], axis=1)
    shard = lax.all_gather(shard.astype(bfloat), ALL, axis=0, tiled=True)
    table_b = embed_table.astype(bfloat)
    token_row = token_ids[0]
    pred_row = pred_mask[0]
    first_row = lax.axis_index(VOC) * vrows
    content = jnp.where(pred_row == 1, MASK_ID, token_row)
    slot_hot, slot_pos, slot_target, allowed, masked = slot_layout(pred_row, fact_order[0], token_row)
    owner, place = bucket_layout(content, vrows)
    hot, wanted = bucket_round(content, owner, place, 0, owners, vrows)
    note = jnp.concatenate(
        [slot_target, slot_pos, jnp.stack([masked, corpus[0], jnp.max(place)])]
    )
    packet = jnp.concatenate(
        [wanted, jnp.broadcast_to(note[None], (owners, note.shape[0]))], axis=1
    )
    packet = jnp.pad(packet, ((0, 0), (0, 256 - packet.shape[1])))
    packet = jnp.broadcast_to(packet[None], (dp_devs,) + packet.shape)
    packet = exchange(packet.reshape(devices, packet.shape[-1]), ALL)
    asked = packet[:, :BUCKET]
    tail = BUCKET + 2 * CAP
    counts_all = packet[:, tail]
    corpus_all = packet[:, tail + 1]
    rounds = jnp.max(packet[:, tail + 2]) // (BUCKET - 1) + 1
    group = lax.axis_index("dp") * owners
    outer = lax.axis_size("hi")

    def group_order(values):
        return values.reshape(outer, 2, 2, CAP).transpose(2, 1, 0, 3).reshape(-1)

    group_asked = lax.dynamic_slice_in_dim(asked, group, owners, 0)
    group_target = group_order(
        lax.dynamic_slice_in_dim(packet[:, BUCKET : BUCKET + CAP], group, owners, 0)
    )
    corpus_hot = corpus_all[:, None] == jnp.arange(NCORP)[None, :]
    corpus_counts = jnp.sum(jnp.where(corpus_hot, counts_all[:, None], 0), axis=0)
    seq_count = masked_total(corpus_hot, corpus_counts[None, :])
    seq_weight = 1.0 / (NCORP * seq_count.astype(single))
    slot_weight = jnp.where(
        jnp.arange(CAP)[None, :] < counts_all[:, None], seq_weight[:, None], 0.0
    )
    group_weight = group_order(lax.dynamic_slice_in_dim(slot_weight, group, owners, 0))

    def serve(asked_rows):
        served = jnp.take(table_b, jnp.maximum(asked_rows, 0).reshape(-1), axis=0)
        return served.reshape(owners, BUCKET, width)

    arrived = exchange(serve(group_asked), VOC)
    embed_rows = rows_dot(hot, arrived.reshape(-1, width))

    def more_rows(state):
        turn, rows = state
        hot_t, wanted_t = bucket_round(content, owner, place, turn, owners, vrows)
        asked_t = lax.all_to_all(wanted_t, VOC, 0, 0, tiled=True)
        arrived_t = lax.all_to_all(serve(asked_t), VOC, 0, 0, tiled=True)
        return turn + 1, rows + rows_dot(hot_t, arrived_t.reshape(-1, width))

    _, embed_rows = lax.while_loop(
        lambda state: state[0] < rounds, more_rows, (jnp.ones((), rounds.dtype), embed_rows)
    )
    few = devices <= 32
    near = 4
    allowed = allowed.astype(single)
    slot_hot = slot_hot.astype(single)
    (
        key_rows,
        value_rows,
        query_rows,
        mixed_b,
        middle,
        mid_normed,
        mid_inverse,
        stream_b,
        stream_normed,
        stream_inverse,
        query_init,
        init_normed,
        init_inverse,
        position_full,
        small_full,
    ) = attend_forward(embed_rows, slot_hot, allowed, shard, length, small_params.shape[0])
    middle_b, hidden, active_b, output_b, end_normed, end_inverse = feed_forward(
        middle, small_full, shard
    )
    if few:
        kept_rows = jnp.concatenate([mixed_b, middle_b], axis=1)
        kept_all = lax.all_gather(kept_rows, ALL, axis=0, tiled=True)
        stream_all = lax.all_gather(stream_b, NEAR, axis=0, tiled=True)
    group_rows = exchange.copies(output_b, "hi", outer).reshape(-1, width)
    group_rows = exchange.copies(group_rows, "mid", 2).reshape(-1, width)
    group_rows = exchange.copies(group_rows, "core", 2).reshape(-1, width)
    logits = trans_dot(group_rows, table_b)
    local_target = group_target - first_row
    target_hit = jnp.arange(vrows)[None, :] == local_target[:, None]
    row_top = jnp.max(logits, axis=1)
    row_total = jnp.sum(jnp.exp(logits - row_top[:, None]), axis=1)
    row_target = jnp.sum(jnp.where(target_hit, logits, 0.0), axis=1)
    stats = exchange.copies(jnp.stack([row_top, row_total]), VOC, owners)
    top_all = jnp.max(stats[:, 0], axis=0)
    total_all = jnp.sum(stats[:, 1] * jnp.exp(stats[:, 0] - top_all[None]), axis=0)
    log_total = top_all + jnp.log(total_all)
    own_place = lax.axis_index(("core", "mid", "hi"))
    own_total = lax.dynamic_slice_in_dim(log_total * group_weight, own_place * CAP, CAP, 0)
    loss_part = jnp.sum(own_total) - jnp.sum(row_target * group_weight)
    d_logits = (
        group_weight[:, None] * (jnp.exp(logits - log_total[:, None]) - target_hit.astype(single))
    ).astype(bfloat)
    def swapped(axis, kind, part):
        side = lax.axis_index(axis)
        theirs = lax.ppermute(part(1 - side).astype(kind), axis, [(0, 1), (1, 0)])
        return part(side) + theirs.astype(single)

    half = owners * CAP // 2

    def rows_half(side):
        return plain_dot(lax.dynamic_slice_in_dim(d_logits, side * half, half, 0), table_b)

    d_output = swapped("core", single, rows_half)
    quarter = half // 2
    d_half = d_output
    d_output = swapped(
        "mid", bfloat, lambda side: lax.dynamic_slice_in_dim(d_half, side * quarter, quarter, 0)
    )
    grad_head = rows_dot(d_logits, group_rows)
    grad_head = after(grad_head, d_half, *((stream_all,) if few else ()))
    heads = [
        lax.all_gather(half_b, "dp", axis=0, tiled=True)
        for half_b in jnp.split(grad_head.astype(bfloat), [vrows // 2])
    ]
    d_output = exchange(d_output.astype(bfloat).reshape(outer, CAP, width), "hi")
    if few:
        d_output, kept_all = lax.optimization_barrier((d_output, kept_all))
    d_branch, d_hidden, d_pre, d_attend, sums_feed = feed_backward(
        d_output,
        end_normed,
        end_inverse,
        hidden,
        small_full,
        mid_normed,
        mid_inverse,
        shard,
    )
    if few:
        wide = feed // devices
        both = jnp.concatenate(
            [
                d_hidden.reshape(CAP, devices, -1),
                d_attend.reshape(CAP, devices, -1),
            ],
            axis=2,
        ).reshape(CAP, -1)
        both = exchange.columns(both, ALL, devices)
        branch_all = lax.all_gather(d_branch, ALL, axis=0, tiled=True)
    d_query, d_key, d_value = attend_backward(
        d_attend, key_rows, value_rows, query_rows, allowed, shard
    )
    if few:
        piece = width // near
        pairs = jnp.concatenate(
            [d_key.reshape(length, near, piece), d_value.reshape(length, near, piece)], axis=2
        ).transpose(1, 0, 2)
        asks = d_query.reshape(CAP, near, piece).transpose(1, 0, 2)
        asks = jnp.concatenate([asks[:, : CAP // 2], asks[:, CAP // 2 :]], axis=2)
        pairs = exchange(jnp.concatenate([pairs, asks], axis=1), NEAR)
    hidden_rows = spread((content == MASK_ID).astype(single)[:, None])
    embed_back, grad_position, sums_back = project_backward(
        d_pre,
        d_query,
        d_key,
        d_value,
        slot_hot,
        hidden_rows,
        small_full,
        stream_normed,
        stream_inverse,
        init_normed,
        init_inverse,
        shard,
        heads[0],
    )
    grad_small = jnp.concatenate([sums_back[:5], sums_feed[:9]])
    mask_sum = sums_back[5]
    mask_left = mask_sum - lax.reduce_precision(mask_sum, 8, 7)
    mask_owner = MASK_ID // vrows
    is_left = (jnp.arange(BUCKET) == BUCKET - 1)[None, :] & (
        jnp.arange(owners) == mask_owner
    )[:, None]

    def plain_exchange(values, axes):
        return lax.all_to_all(values, axes, 0, 0, tiled=True)

    def give(hot_rows, extra, send):
        rows = plain_dot(hot_rows, embed_back).reshape(owners, BUCKET, width)
        rows = jnp.where(is_left[:, :, None] & extra, mask_left[None, None, :], rows)
        return send(rows.astype(bfloat), VOC).reshape(-1, width)

    def of_both(rows):
        if dp_devs == 2:
            return jnp.concatenate([rows, lax.ppermute(rows, "dp", [(0, 1), (1, 0)])])
        return lax.all_gather(rows, "dp", axis=0, tiled=True)

    def both_groups(asked_rows):
        if dp_devs == 2:
            return jnp.roll(asked_rows, -group, axis=0)
        return asked_rows

    split = vrows // dp_devs
    sides = lax.axis_index("dp") * split + jnp.array([0, split])

    def into_rows(heads, parts, asked_rows, given, sides):
        return lookup_grad(heads, parts, both_groups(asked_rows).reshape(1, -1), given, sides)

    last = (jnp.arange(BUCKET) == BUCKET - 1)[None, :]
    left_row = jnp.where(lax.axis_index(VOC) == mask_owner, MASK_ID - first_row, -1)
    given = of_both(give(hot, True, exchange))

    if few:
        near_pos = packet[:, BUCKET + CAP : tail].reshape(dp_devs * outer, near * CAP)
        near_pos = lax.dynamic_index_in_dim(
            near_pos, lax.axis_index(("dp", "hi")), 0, False
        )
        init_rows = norm_forward(position_full, small_full[0], small_full[1])[0].astype(bfloat)
        init_hot = near_pos[:, None] == jnp.arange(length)[None, :]
        init_all = plain_dot(init_hot.astype(bfloat), init_rows).astype(bfloat)
        asks = pairs[:, length:]
        asks = jnp.concatenate([asks[..., :piece], asks[..., piece:]], axis=1)
        grad_pair = rows_dot(stream_all, pairs[:, :length].reshape(near * length, -1))
        grad_ask = rows_dot(init_all, asks.reshape(near * CAP, piece))
        share = width // devices
        active_mine = exchange.columns(active_b, ALL, devices)
        grad_up = rows_dot(kept_all[:, width:], both[:, :wide])
        grad_out = rows_dot(kept_all[:, :width], both[:, wide:])
        grad_down = rows_dot(branch_all, active_mine)
        shared_grad = jnp.concatenate([grad_position, grad_small]).T
        results = jnp.concatenate(
            [grad_pair, grad_ask, grad_up, grad_down, grad_out, shared_grad], axis=1
        )
        results = after(results.astype(bfloat), given[-1:])
        results = exchange.rows(results, devices).astype(single)
        sides = after(sides, results)
        pieces = 3 * piece
        attn = jnp.sum(
            results[..., :pieces].reshape(dp_devs * outer, near, share, pieces), axis=0
        )
        shared_grad = jnp.sum(results[..., -shared_rows:], axis=0)
        single_parts = results[..., pieces:-shared_rows]
        part_square = (
            jnp.sum(attn * attn)
            + jnp.sum(single_parts * single_parts)
            + jnp.sum(shared_grad * shared_grad)
        )
        shared_grad = shared_grad.T
        position_grad, small_grad = shared_grad[:length], shared_grad[length:]
        grad_key, grad_value, grad_query = (
            side_by_side(attn[..., part * piece : (part + 1) * piece]) for part in range(3)
        )
        grad_up, grad_down, grad_out = (
            side_by_side(single_parts[..., low:high])
            for low, high in ((0, wide), (wide, 2 * wide), (2 * wide, None))
        )
        layer_grad = jnp.stack(
            [
                jnp.concatenate([grad_query, grad_key, grad_value, grad_out], axis=1),
                grad_up,
                grad_down,
            ]
        )
    else:
        whole = (
            jnp.concatenate(
                [
                    rows_dot(query_init.astype(bfloat), d_query),
                    rows_dot(stream_b, d_key),
                    rows_dot(stream_b, d_value),
                    rows_dot(mixed_b, d_attend),
                ],
                axis=1,
            ),
            rows_dot(middle_b, d_hidden),
            rows_dot(d_branch, active_b),
        )
        layer_grad = jnp.stack(
            [lax.psum_scatter(part, ALL, scatter_dimension=0, tiled=True) for part in whole]
        )
        shared_grad = jnp.concatenate([grad_position, grad_small]).T
        shared_grad = lax.psum_scatter(shared_grad, ALL, scatter_dimension=0, tiled=True).T
        position_grad, small_grad = shared_grad[:length], shared_grad[length:]
        part_square = jnp.sum(layer_grad * layer_grad) + jnp.sum(shared_grad * shared_grad)
    table_grad, table_square_sum = into_rows(
        heads, dp_devs, jnp.where(last, left_row, asked), given, sides
    )

    def more_grads(state):
        turn, grads, _ = state
        hot_t, wanted_t = bucket_round(content, owner, place, turn, owners, vrows)
        wanted_t = jnp.broadcast_to(wanted_t[None], (dp_devs,) + wanted_t.shape)
        asked_t = lax.all_to_all(
            wanted_t.reshape(devices, BUCKET), ALL, 0, 0, tiled=True
        )
        given_t = of_both(give(hot_t, False, plain_exchange))
        return (turn + 1,) + tuple(into_rows([grads], 1, asked_t, given_t, sides))

    _, table_grad, table_square_sum = lax.while_loop(
        lambda state: state[0] < rounds,
        more_grads,
        (jnp.ones((), rounds.dtype), table_grad, table_square_sum),
    )
    square_part = jnp.sum(table_square_sum) + part_square
    totals = exchange.copies(jnp.stack([square_part, loss_part]), ALL, devices)
    total_square, loss_value = jnp.sum(totals, axis=0)
    grad_norm = jnp.sqrt(total_square)
    factor = jnp.minimum(1.0, clip_norm / grad_norm)
    (
        norms,
        layer_first,
        layer_second,
        layer_dir,
        position_first,
        position_second,
        position_dir,
        small_first,
        small_second,
        small_dir,
    ) = update_norms(
        totals,
        (embed_table, table_moment, table_square, table_grad),
        (layer_weights, layer_moment, layer_square, layer_grad),
        (position_table, position_moment, position_square, position_grad),
        (small_params, small_moment, small_square, small_grad),
        split,
        lax.axis_index("dp"),
    )
    factor_late, norms = lax.optimization_barrier((factor, norms))
    pairs = exchange.copies(norms[:6, :2].reshape(-1), ALL, devices)
    table_first, table_second, _ = adam_moments(
        embed_table, table_moment, table_square, table_grad, factor_late
    )
    trust_norms = jnp.sqrt(jnp.sum(pairs, axis=0)).reshape(6, 2)
    table_next, layer_next, position_next, small_next = final_update(
        pairs,
        (embed_table, table_first, table_second),
        (
            layer_weights,
            layer_dir,
            position_table,
            position_dir,
            small_params,
            small_dir,
        ),
    )
    return (
        loss_value,
        grad_norm,
        table_next,
        table_first,
        table_second,
        layer_next,
        layer_first,
        layer_second,
        position_next,
        position_first,
        position_second,
        small_next,
        small_first,
        small_second,
        trust_norms,
    )


def solution(mesh):
    dp_devs, owners = mesh.devices.shape
    fine = Mesh(mesh.devices.reshape(dp_devs, owners // 4, 2, 2), ALL)
    rows, inner = P(ALL, None), P(None, ALL)
    table, layer = P(VOC, None), P(None, ALL, None)
    return jax.shard_map(
        on_device,
        mesh=fine,
        in_specs=(rows,) * 3 + (P(ALL),) + (table,) * 3 + (layer,) * 3 + (inner,) * 6,
        out_specs=(P(), P()) + (table,) * 3 + (layer,) * 3 + (inner,) * 6 + (P(),),
        check_vma=False,
    )
```
